32 devices in a mesh: dp: 16 (over z, x, core), hd: 2 (over y).
Axes of the slice: x: 2, y: 2, z: 4, core: 2. Of those that a mesh axis runs over, the one named last changes fastest.
Arguments:
- tokens: bfloat16 [64, 64, 768], P(('dp', 'hd')), may hold values from -6 to 6
- encoder: bfloat16 [64, 576, 768], P(('dp', 'hd')), may hold values from -6 to 6
- patch_count: int32 [64], P(('dp', 'hd')), may hold values from 196 to 576, as said below
- out_grad: bfloat16 [64, 64, 768], P(('dp', 'hd')), may hold values from -6 to 6
- uni_attn_gain: bfloat16 [768], P(('dp', 'hd')), may hold values from 0.099609375 to 1.8984375
- uni_attn_shift: bfloat16 [768], P(('dp', 'hd')), may hold values from -2 to 2
- uni_qkv: bfloat16 [768, 2304], P(('dp', 'hd')), may hold values from -0.21875 to 0.21875
- uni_out: bfloat16 [768, 768], P(('dp', 'hd')), may hold values from -0.875 to 0.875
- uni_mlp_gain: bfloat16 [768], P(('dp', 'hd')), may hold values from 0.099609375 to 1.8984375
- uni_mlp_shift: bfloat16 [768], P(('dp', 'hd')), may hold values from -2 to 2
- uni_up: bfloat16 [768, 3072], P(('dp', 'hd')), may hold values from -0.21875 to 0.21875
- uni_down: bfloat16 [3072, 768], P(('dp', 'hd')), may hold values from -0.109375 to 0.109375
- multi_attn_gain: bfloat16 [768], P(('dp', 'hd')), may hold values from 0.099609375 to 1.8984375
- multi_attn_shift: bfloat16 [768], P(('dp', 'hd')), may hold values from -2 to 2
- multi_qkv: bfloat16 [768, 2304], P(('dp', 'hd')), may hold values from -0.21875 to 0.21875
- multi_out: bfloat16 [768, 768], P(('dp', 'hd')), may hold values from -0.875 to 0.875
- cross_gain: bfloat16 [768], P(('dp', 'hd')), may hold values from 0.099609375 to 1.8984375
- cross_shift: bfloat16 [768], P(('dp', 'hd')), may hold values from -2 to 2
- cross_query: bfloat16 [768, 768], P(('dp', 'hd')), may hold values from -0.21875 to 0.21875
- cross_pair: bfloat16 [768, 1536], P(('dp', 'hd')), may hold values from -0.21875 to 0.21875
- cross_out: bfloat16 [768, 768], P(('dp', 'hd')), may hold values from -1.75 to 1.75
- multi_mlp_gain: bfloat16 [768], P(('dp', 'hd')), may hold values from 0.099609375 to 1.8984375
- multi_mlp_shift: bfloat16 [768], P(('dp', 'hd')), may hold values from -2 to 2
- multi_up: bfloat16 [768, 3072], P(('dp', 'hd')), may hold values from -0.21875 to 0.21875
- multi_down: bfloat16 [3072, 768], P(('dp', 'hd')), may hold values from -0.109375 to 0.109375
Outputs:
- activations: bfloat16 [64, 64, 768], P(('dp', 'hd'))
- grad_tokens: bfloat16 [64, 64, 768], P(('dp', 'hd'))
- grad_encoder: bfloat16 [64, 576, 768], P(('dp', 'hd'))
- grad_uni_attn_gain: float32 [768], P(('dp', 'hd'))
- grad_uni_attn_shift: float32 [768], P(('dp', 'hd'))
- grad_uni_qkv: float32 [768, 2304], P(('dp', 'hd'))
- grad_uni_out: float32 [768, 768], P(('dp', 'hd'))
- grad_uni_mlp_gain: float32 [768], P(('dp', 'hd'))
- grad_uni_mlp_shift: float32 [768], P(('dp', 'hd'))
- grad_uni_up: float32 [768, 3072], P(('dp', 'hd'))
- grad_uni_down: float32 [3072, 768], P(('dp', 'hd'))
- grad_multi_attn_gain: float32 [768], P(('dp', 'hd'))
- grad_multi_attn_shift: float32 [768], P(('dp', 'hd'))
- grad_multi_qkv: float32 [768, 2304], P(('dp', 'hd'))
- grad_multi_out: float32 [768, 768], P(('dp', 'hd'))
- grad_cross_gain: float32 [768], P(('dp', 'hd'))
- grad_cross_shift: float32 [768], P(('dp', 'hd'))
- grad_cross_query: float32 [768, 768], P(('dp', 'hd'))
- grad_cross_pair: float32 [768, 1536], P(('dp', 'hd'))
- grad_cross_out: float32 [768, 768], P(('dp', 'hd'))
- grad_multi_mlp_gain: float32 [768], P(('dp', 'hd'))
- grad_multi_mlp_shift: float32 [768], P(('dp', 'hd'))
- grad_multi_up: float32 [768, 3072], P(('dp', 'hd'))
- grad_multi_down: float32 [3072, 768], P(('dp', 'hd'))
The draws below stay inside these ranges and needn't reach their ends.
Inputs may be any that keep to these rules, and one draw needn't show every extreme that they name: Caption c's valid patches are slots 0 to patch_count[c] - 1; every count is 196 or 576, and both occur in every draw.
All inputs are finite; a program needn't handle non-finite values.
Results may differ from the reference program's by a relative error of at most 0.025.
Values may be sent and summed in bfloat16 or wider, within the bound.
No kernel may reach another device: no remote copies, remote signals or barrier semaphores. Data moves between devices by JAX's collectives and lax.ppermute only.
A program may use at most 256 MiB of HBM per device.

```python
import math
import jax
import jax.numpy as jnp
from jax import lax

D = 768
HEADS = 12
DH = 64
FF = 3072
E = 768
SEQ = 64
PATCHES = 576
SHORT = 196
CAPTIONS = 64


def draw_patch_count(key, part):
    key_pick = jax.random.fold_in(key, 11)
    key_first = jax.random.fold_in(key, 12)
    key_second = jax.random.fold_in(key, 13)
    choose_long = jax.random.randint(key_pick, (CAPTIONS,), 0, 2)
    counts = jnp.where(choose_long == 1, PATCHES, SHORT).astype(jnp.int32)
    first_slot = jax.random.randint(key_first, (), 0, CAPTIONS)
    second = (first_slot + 1 + jax.random.randint(key_second, (), 0, CAPTIONS - 1)) % CAPTIONS
    counts = counts.at[first_slot].set(PATCHES)
    counts = counts.at[second].set(SHORT)
    return counts.astype(jnp.int32)


def steps_of(key, shape, cuts, low, top_value):
    def one(dim, shards_of):
        draws = jax.random.uniform(jax.random.fold_in(jax.random.fold_in(key, 6), dim), (shards_of,), jnp.float32, low / len(cuts), top_value / len(cuts))
        return jnp.repeat(jnp.exp(draws), shape[dim] // shards_of).reshape((-1,) + (1,) * (len(shape) - dim - 1))

    gain = one(*cuts[0])
    for cut in cuts[1:]:
        gain = gain * one(*cut)
    return gain


def noise(key, dims, scale, bound, cuts=(), held_as=jnp.bfloat16):
    values = jax.random.normal(key, dims, jnp.float32) * scale
    if len(cuts) > 0:
        values = steps_of(key, dims, cuts, -0.22, 0.18) * values
    return jnp.clip(values, min=-bound, max=bound).astype(held_as)


def setup_inputs(seed: int = 0) -> dict:
    seeds = jax.random.split(jax.random.key(seed), 26)
    return {
        "tokens": noise(seeds[0], (CAPTIONS, SEQ, D), 1.0, 6.0, ((0, 32),)),
        "encoder": noise(seeds[1], (CAPTIONS, PATCHES, E), 1.0, 6.0, ((0, 32),)),
        "patch_count": draw_patch_count(jax.random.fold_in(seeds[25], 71), 0),
        "out_grad": noise(seeds[3], (CAPTIONS, SEQ, D), 1.0, 6.0, ((0, 32),)),
        "uni_attn_gain": jnp.clip(1.0 + 0.18 * jax.random.normal(seeds[4], (D,), jnp.float32), 0.099609375, 1.8984375).astype(jnp.bfloat16),
        "uni_attn_shift": noise(seeds[5], (D,), 0.3, 2.0, ((0, 32),)),
        "uni_qkv": noise(seeds[6], (D, 3 * D), D ** -0.5, 0.21875, ((0, 32),)),
        "uni_out": noise(seeds[7], (D, D), (D // 16) ** -0.5, 0.875, ((0, 32),)),
        "uni_mlp_gain": jnp.clip(1.0 + 0.18 * jax.random.normal(seeds[8], (D,), jnp.float32), 0.099609375, 1.8984375).astype(jnp.bfloat16),
        "uni_mlp_shift": noise(seeds[9], (D,), 0.3, 2.0, ((0, 32),)),
        "uni_up": noise(seeds[10], (D, FF), D ** -0.5, 0.21875, ((0, 32),)),
        "uni_down": noise(seeds[11], (FF, D), FF ** -0.5, 0.109375, ((0, 32),)),
        "multi_attn_gain": jnp.clip(1.0 + 0.18 * jax.random.normal(seeds[12], (D,), jnp.float32), 0.099609375, 1.8984375).astype(jnp.bfloat16),
        "multi_attn_shift": noise(seeds[13], (D,), 0.3, 2.0, ((0, 32),)),
        "multi_qkv": noise(seeds[14], (D, 3 * D), D ** -0.5, 0.21875, ((0, 32),)),
        "multi_out": noise(seeds[15], (D, D), (D // 16) ** -0.5, 0.875, ((0, 32),)),
        "cross_gain": jnp.clip(1.0 + 0.18 * jax.random.normal(seeds[16], (D,), jnp.float32), 0.099609375, 1.8984375).astype(jnp.bfloat16),
        "cross_shift": noise(seeds[17], (D,), 0.3, 2.0, ((0, 32),)),
        "cross_query": noise(seeds[18], (D, D), D ** -0.5, 0.21875, ((0, 32),)),
        "cross_pair": noise(seeds[19], (E, 2 * D), E ** -0.5, 0.21875, ((0, 32),)),
        "cross_out": noise(seeds[20], (D, D), (D // 64) ** -0.5, 1.75, ((0, 32),)),
        "multi_mlp_gain": jnp.clip(1.0 + 0.18 * jax.random.normal(seeds[21], (D,), jnp.float32), 0.099609375, 1.8984375).astype(jnp.bfloat16),
        "multi_mlp_shift": noise(seeds[22], (D,), 0.3, 2.0, ((0, 32),)),
        "multi_up": noise(seeds[23], (D, FF), D ** -0.5, 0.21875, ((0, 32),)),
        "multi_down": noise(seeds[24], (FF, D), FF ** -0.5, 0.109375, ((0, 32),)),
    }


@jax.custom_vjp
def low(v):
    return lax.optimization_barrier(v.astype(jnp.bfloat16)).astype(jnp.float32)

@jax.custom_vjp
def low_back(v):
    return v

def low_keep(v):
    return (low(v), None)

def low_pass(kept, grad):
    return (grad,)

def back_keep(v):
    return (v, None)

def back_low(kept, grad):
    return (low(grad),)
low.defvjp(low_keep, low_pass)
low_back.defvjp(back_keep, back_low)
epsilon = 1e-05
highest = lax.Precision.HIGHEST
masked_value = -1e+30

def layer_norm(hidden, norm_gain, norm_shift):
    centred = hidden - lax.optimization_barrier(jnp.mean(hidden, axis=-1, keepdims=True))
    spread = lax.optimization_barrier(jnp.mean(centred * centred, axis=-1, keepdims=True))
    return centred * lax.rsqrt(spread + epsilon) * norm_gain + norm_shift

def project(inputs, weight):
    return jnp.einsum('...i,ij->...j', inputs, weight, precision=highest)

def attend(queries, keys_in, values_in, allowed):
    groups, length, model_width = queries.shape
    query_heads = queries.reshape(groups, length, HEADS, DH)
    key_heads = keys_in.reshape(groups, keys_in.shape[1], HEADS, DH)
    value_heads = values_in.reshape(groups, values_in.shape[1], HEADS, DH)
    scores = low_back(jnp.einsum('gqhd,gkhd->ghqk', query_heads, key_heads, precision=highest) * DH ** (-0.5))
    masked = jnp.where(allowed, scores, masked_value)
    attn_weights = low(jax.nn.softmax(masked, axis=-1))
    attended = jnp.einsum('ghqk,gkhd->gqhd', attn_weights, value_heads, precision=highest)
    return low(low_back(attended.reshape(groups, length, model_width)))

def self_layer(hidden, norm_gain, norm_shift, w_qkv, w_out):
    normed = low(layer_norm(hidden, norm_gain, norm_shift))
    mixed = project(normed, w_qkv)
    queries = low(low_back(mixed[..., :D]))
    keys_in = low(low_back(mixed[..., D:2 * D]))
    values_in = low(low_back(mixed[..., 2 * D:]))
    length = hidden.shape[1]
    causal = (jnp.arange(length)[:, None] >= jnp.arange(length)[None, :])[None, None]
    attended = attend(queries, keys_in, values_in, causal)
    return hidden + low_back(project(attended, w_out))

def cross_layer(hidden, encoded, allowed, norm_gain, norm_shift, w_query, w_pair, w_out):
    normed = low(layer_norm(hidden, norm_gain, norm_shift))
    queries = low(low_back(project(normed, w_query)))
    pair_rows = project(encoded, w_pair)
    keys_in = low(low_back(pair_rows[..., :D]))
    values_in = low(low_back(pair_rows[..., D:]))
    attended = attend(queries, keys_in, values_in, allowed[:, None, None, :])
    return hidden + low_back(project(attended, w_out))

def feed_layer(hidden, norm_gain, norm_shift, w_up, w_down):
    normed = low(layer_norm(hidden, norm_gain, norm_shift))
    upward = low_back(project(normed, w_up))
    active = low(jax.nn.gelu(upward))
    return hidden + low_back(project(active, w_down))

def forward(tokens_in, encoded, allowed, params):
    hidden = self_layer(tokens_in, params[0], params[1], params[2], params[3])
    hidden = feed_layer(hidden, params[4], params[5], params[6], params[7])
    hidden = self_layer(hidden, params[8], params[9], params[10], params[11])
    hidden = cross_layer(hidden, encoded, allowed, params[12], params[13], params[14], params[15], params[16])
    return feed_layer(hidden, params[17], params[18], params[19], params[20])

def reference(tokens, encoder, patch_count, out_grad, uni_attn_gain, uni_attn_shift, uni_qkv, uni_out, uni_mlp_gain, uni_mlp_shift, uni_up, uni_down, multi_attn_gain, multi_attn_shift, multi_qkv, multi_out, cross_gain, cross_shift, cross_query, cross_pair, cross_out, multi_mlp_gain, multi_mlp_shift, multi_up, multi_down):
    params = tuple((member.astype(jnp.float32) for member in (uni_attn_gain, uni_attn_shift, uni_qkv, uni_out, uni_mlp_gain, uni_mlp_shift, uni_up, uni_down, multi_attn_gain, multi_attn_shift, multi_qkv, multi_out, cross_gain, cross_shift, cross_query, cross_pair, cross_out, multi_mlp_gain, multi_mlp_shift, multi_up, multi_down)))
    group_size = math.gcd(CAPTIONS, 32)
    steps_count = CAPTIONS // group_size
    patch_slots = jnp.arange(PATCHES, dtype=jnp.int32)
    allowed = patch_slots[None, :] < patch_count[:, None].astype(jnp.int32)
    token_groups = tokens.astype(jnp.float32).reshape(steps_count, group_size, SEQ, D)
    encoder_groups = encoder.astype(jnp.float32).reshape(steps_count, group_size, PATCHES, E)
    allowed_groups = allowed.reshape(steps_count, group_size, PATCHES)
    grad_groups = out_grad.astype(jnp.float32).reshape(steps_count, group_size, SEQ, D)

    def one_group(totals, pieces):
        tokens_part, encoded, allowed_part, cotangent = pieces

        def run_forward(tokens_in, encoded_in, weights_in):
            return forward(tokens_in, encoded_in, allowed_part, weights_in)
        result, pull_back = jax.vjp(run_forward, tokens_part, encoded, params)
        grad_part, grad_encoded, grad_params = pull_back(cotangent)
        totals = jax.tree.map(jnp.add, totals, grad_params)
        return (totals, (result.astype(jnp.bfloat16), grad_part.astype(jnp.bfloat16), grad_encoded.astype(jnp.bfloat16)))
    initial = tuple((jnp.zeros_like(member) for member in params))
    totals, (results, grad_inputs, grad_encodes) = lax.scan(one_group, initial, (token_groups, encoder_groups, allowed_groups, grad_groups))
    return (results.reshape(CAPTIONS, SEQ, D), grad_inputs.reshape(CAPTIONS, SEQ, D), grad_encodes.reshape(CAPTIONS, PATCHES, E), totals[0], totals[1], totals[2], totals[3], totals[4], totals[5], totals[6], totals[7], totals[8], totals[9], totals[10], totals[11], totals[12], totals[13], totals[14], totals[15], totals[16], totals[17], totals[18], totals[19], totals[20])
```

```python
import jax
import jax.numpy as jnp
from jax import lax
from jax.sharding import PartitionSpec as P

DH = 64
AXES = ("dp", "hd")
EPS = 1e-05
MASKED = -1e30
bf16 = jnp.bfloat16
f32 = jnp.float32


BIT_PAIR, BIT_CORE, BIT_NEAR = 1, 2, 4


class Place:
    def __init__(self):
        self.count = lax.axis_size("dp") * lax.axis_size("hd")
        self.outer_size = self.count // 8
        index = lax.axis_index("dp") * lax.axis_size("hd") + lax.axis_index("hd")
        self.pair = index % 2
        self.core = (index // 2) % 2
        self.near = (index // 4) % 2
        self.outer = index // 8

    def swap(self, x, bit):
        return lax.ppermute(x, AXES, [(i, i ^ bit) for i in range(self.count)])

    def shift(self, x, k):
        n = self.count
        return lax.ppermute(x, AXES, [(i, (i + 8 * k) % n) for i in range(n)])


def pick(x, index, axis):
    return lax.dynamic_index_in_dim(x, index, axis, keepdims=False)


def join(own, got, index, axis):
    shape = own.shape[:axis] + (2,) + own.shape[axis:]
    out = jnp.zeros(shape, own.dtype)
    out = lax.dynamic_update_index_in_dim(out, own, index, axis)
    return lax.dynamic_update_index_in_dim(out, got, 1 - index, axis)


def gather_rows(place, shard, near_last):
    n = place.outer_size
    got = [place.shift(shard, k) for k in range(1, n)]
    block = jnp.zeros((n,) + shard.shape, shard.dtype)
    block = lax.dynamic_update_index_in_dim(block, shard, place.outer, 0)
    for k in range(1, n):
        block = lax.dynamic_update_index_in_dim(block, got[k - 1], (place.outer - k) % n, 0)
    if near_last:
        block = join(block, place.swap(block, BIT_PAIR), place.pair, 1)
        block = join(block, place.swap(block, BIT_NEAR), place.near, 1)
    else:
        block = join(block, place.swap(block, BIT_NEAR), place.near, 1)
        block = join(block, place.swap(block, BIT_PAIR), place.pair, 2)
    block = join(block, place.swap(block, BIT_CORE), place.core, 2)
    return block.reshape(place.count * shard.shape[0], shard.shape[1])


def scatter_rows(place, full, near_first):
    n = place.outer_size
    rows = full.shape[0] // place.count
    t = full.astype(bf16).reshape(n, 2, 2, 2, rows, full.shape[1])

    def halve(t, index, bit, axis):
        got = place.swap(pick(t, 1 - index, axis), bit)
        return (pick(t, index, axis).astype(f32) + got.astype(f32)).astype(bf16)

    t = halve(t, place.core, BIT_CORE, 2)
    if near_first:
        t = halve(t, place.near, BIT_NEAR, 1)
        t = halve(t, place.pair, BIT_PAIR, 1)
    else:
        t = halve(t, place.pair, BIT_PAIR, 2)
        t = halve(t, place.near, BIT_NEAR, 1)
    total = pick(t, place.outer, 0).astype(f32)
    for k in range(1, n):
        got = place.shift(pick(t, (place.outer + k) % n, 0), k)
        total = total + got.astype(f32)
    return total


def dot(a, b):
    return jnp.dot(a, b, preferred_element_type=f32)


def dot_rows(a, b):
    return lax.dot_general(a, b, (((0,), (0,)), ((), ())), preferred_element_type=f32)


def dot_back(a, w):
    return lax.dot_general(a, w, (((1,), (1,)), ((), ())), preferred_element_type=f32)


def norm_forward(x, gain, shift):
    centred = x - jnp.mean(x, axis=-1, keepdims=True)
    inv = lax.rsqrt(jnp.mean(centred * centred, axis=-1, keepdims=True) + EPS)
    unit = centred * inv
    return (unit * gain + shift).astype(bf16), unit, inv


def norm_backward(grad, unit, inv, gain):
    du = grad * gain
    dx = inv * (
        du
        - jnp.mean(du, axis=-1, keepdims=True)
        - unit * jnp.mean(du * unit, axis=-1, keepdims=True)
    )
    return dx, jnp.sum(grad * unit, axis=0), jnp.sum(grad, axis=0)


GELU_A = 0.7978845608028654
GELU_B = 0.044715


def gelu_forward(u):
    return 0.5 * u * (1.0 + jnp.tanh(GELU_A * (u + GELU_B * u * u * u)))


def gelu_slope(u):
    t = jnp.tanh(GELU_A * (u + GELU_B * u * u * u))
    return 0.5 * (1.0 + t) + 0.5 * u * (1.0 - t * t) * GELU_A * (1.0 + 3.0 * GELU_B * u * u)


def heads(x, captions):
    return x.reshape(captions, x.shape[0] // captions, x.shape[1] // DH, DH)


def attend_forward(q, k, v, allowed, captions):
    s = jnp.einsum(
        "bqhd,bkhd->bhqk", heads(q, captions), heads(k, captions), preferred_element_type=f32
    ) * DH ** (-0.5)
    s = jnp.where(allowed, s, MASKED)
    s = s - jnp.max(s, axis=-1, keepdims=True)
    e = jnp.exp(s)
    p = e / jnp.sum(e, axis=-1, keepdims=True)
    o = jnp.einsum("bhqk,bkhd->bqhd", p.astype(bf16), heads(v, captions), preferred_element_type=f32)
    return o.reshape(q.shape).astype(bf16), p


def attend_backward(q, k, v, p, do, captions):
    doh = heads(do, captions)
    dp = jnp.einsum("bqhd,bkhd->bhqk", doh, heads(v, captions), preferred_element_type=f32)
    ds = (p * (dp - jnp.sum(p * dp, axis=-1, keepdims=True))).astype(bf16)
    scale = DH ** (-0.5)
    dq = jnp.einsum("bhqk,bkhd->bqhd", ds, heads(k, captions), preferred_element_type=f32) * scale
    dk = jnp.einsum("bhqk,bqhd->bkhd", ds, heads(q, captions), preferred_element_type=f32) * scale
    dv = jnp.einsum("bhqk,bqhd->bkhd", p.astype(bf16), doh, preferred_element_type=f32)
    return (
        dq.reshape(q.shape).astype(bf16),
        dk.reshape(k.shape).astype(bf16),
        dv.reshape(v.shape).astype(bf16),
    )


def self_forward(x, gain, shift, w_qkv, w_out, captions):
    d = x.shape[1]
    a, unit, inv = norm_forward(x, gain, shift)
    mixed = dot(a, w_qkv).astype(bf16)
    q, k, v = mixed[:, :d], mixed[:, d : 2 * d], mixed[:, 2 * d :]
    length = x.shape[0] // captions
    causal = jnp.arange(length)[:, None] >= jnp.arange(length)[None, :]
    o, p = attend_forward(q, k, v, causal[None, None], captions)
    return x + dot(o, w_out), (a, unit, inv, q, k, v, p, o)


def self_backward(kept, gain, w_qkv, w_out, dx, captions):
    a, unit, inv, q, k, v, p, o = kept
    dy = dx.astype(bf16)
    g_out = dot_rows(o, dy)
    do = dot_back(dy, w_out).astype(bf16)
    dmixed = jnp.concatenate(attend_backward(q, k, v, p, do, captions), axis=1)
    g_qkv = dot_rows(a, dmixed)
    dn, g_gain, g_shift = norm_backward(dot_back(dmixed, w_qkv), unit, inv, gain)
    return dx + dn, g_gain, g_shift, g_qkv, g_out


def cross_forward(x, enc, allowed, gain, shift, w_q, w_pair, w_out, captions):
    d = x.shape[1]
    c, unit, inv = norm_forward(x, gain, shift)
    q = dot(c, w_q).astype(bf16)
    pair = dot(enc, w_pair).astype(bf16)
    k, v = pair[:, :d], pair[:, d:]
    o, p = attend_forward(q, k, v, allowed, captions)
    return x + dot(o, w_out), (c, unit, inv, q, k, v, p, o)


def cross_backward(kept, enc, gain, w_q, w_pair, w_out, dx, captions):
    c, unit, inv, q, k, v, p, o = kept
    dy = dx.astype(bf16)
    g_out = dot_rows(o, dy)
    do = dot_back(dy, w_out).astype(bf16)
    dq, dk, dv = attend_backward(q, k, v, p, do, captions)
    dpair = jnp.concatenate((dk, dv), axis=1)
    g_pair = dot_rows(enc, dpair)
    denc = dot_back(dpair, w_pair)
    g_q = dot_rows(c, dq)
    dn, g_gain, g_shift = norm_backward(dot_back(dq, w_q), unit, inv, gain)
    return dx + dn, denc, g_gain, g_shift, g_q, g_pair, g_out


def feed_forward(x, gain, shift, w_up, w_down):
    b, unit, inv = norm_forward(x, gain, shift)
    u = dot(b, w_up)
    g = gelu_forward(u).astype(bf16)
    return x + dot(g, w_down), (b, unit, inv, u, g)


def feed_backward(kept, gain, w_up, w_down, dx):
    b, unit, inv, u, g = kept
    dz = dx.astype(bf16)
    g_down = dot_rows(g, dz)
    du = (gelu_slope(u) * dot_back(dz, w_down)).astype(bf16)
    g_up = dot_rows(b, du)
    dn, g_gain, g_shift = norm_backward(dot_back(du, w_up), unit, inv, gain)
    return dx + dn, g_gain, g_shift, g_up, g_down


LANES = 128


def pack(matrices, vectors):
    rows = matrices[0].shape[0]
    cols = jnp.stack(vectors, axis=1).astype(matrices[0].dtype)
    cols = jnp.pad(cols, ((0, 0), (0, LANES - cols.shape[1])))
    return jnp.concatenate(tuple(matrices) + (cols,), axis=1)


def unpack(packed, widths, count):
    out, at = [], 0
    for w in widths:
        out.append(packed[:, at : at + w])
        at += w
    vectors = packed[:, at : at + LANES].astype(f32)
    return out, [vectors[:, i] for i in range(count)]


def local(
    tokens, encoder, patch_count, out_grad,
    u_ag, u_as, u_qkv, u_out, u_mg, u_ms, u_up, u_down,
    m_ag, m_as, m_qkv, m_out, c_g, c_s, c_q, c_pair, c_out, m_mg, m_ms, m_up, m_down,
):
    place = Place()
    captions, length, d = tokens.shape
    patches = encoder.shape[1]
    x0 = tokens.reshape(-1, d).astype(f32)
    enc = encoder.reshape(-1, d)
    slots = lax.broadcasted_iota(jnp.int32, (captions, patches), 1)
    allowed = (slots < patch_count[:, None])[:, None, None, :]

    self_w, cross_w = (3 * d, d), (d, 2 * d, d)
    pu = gather_rows(place, pack((u_qkv, u_out), (u_ag, u_as, u_mg, u_ms)), True)
    uup = gather_rows(place, u_up, True)
    udown = gather_rows(place, u_down, False)
    pm = gather_rows(place, pack((m_qkv, m_out), (m_ag, m_as, m_mg, m_ms)), False)
    pc = gather_rows(place, pack((c_q, c_pair, c_out), (c_g, c_s)), True)
    mup = gather_rows(place, m_up, True)
    mdown = gather_rows(place, m_down, False)
    (uqkv, uout), (uag, uas, umg, ums) = unpack(pu, self_w, 4)
    (mqkv, mout), (mag, mas, mmg, mms) = unpack(pm, self_w, 4)
    (cq, cpair, cout), (cg, cs) = unpack(pc, cross_w, 2)

    x0a, k_us = self_forward(x0, uag, uas, uqkv, uout, captions)
    x1, k_uf = feed_forward(x0a, umg, ums, uup, udown)
    x1a, k_ms = self_forward(x1, mag, mas, mqkv, mout, captions)
    x1b, k_mc = cross_forward(x1a, enc, allowed, cg, cs, cq, cpair, cout, captions)
    x2, k_mf = feed_forward(x1b, mmg, mms, mup, mdown)

    dx = out_grad.reshape(-1, d).astype(f32)
    dx, g_mmg, g_mms, g_mup, g_mdown = feed_backward(k_mf, mmg, mup, mdown, dx)
    r_mup = scatter_rows(place, g_mup, True)
    r_mdown = scatter_rows(place, g_mdown, False)
    dx, denc, g_cg, g_cs, g_cq, g_cpair, g_cout = cross_backward(
        k_mc, enc, cg, cq, cpair, cout, dx, captions
    )
    r_c = scatter_rows(place, pack((g_cq, g_cpair, g_cout), (g_cg, g_cs)), True)
    dx, g_mag, g_mas, g_mqkv, g_mout = self_backward(k_ms, mag, mqkv, mout, dx, captions)
    r_m = scatter_rows(place, pack((g_mqkv, g_mout), (g_mag, g_mas, g_mmg, g_mms)), False)
    dx, g_umg, g_ums, g_uup, g_udown = feed_backward(k_uf, umg, uup, udown, dx)
    r_uup = scatter_rows(place, g_uup, True)
    r_udown = scatter_rows(place, g_udown, False)
    dx, g_uag, g_uas, g_uqkv, g_uout = self_backward(k_us, uag, uqkv, uout, dx, captions)
    r_u = scatter_rows(place, pack((g_uqkv, g_uout), (g_uag, g_uas, g_umg, g_ums)), True)

    (r_uqkv, r_uout), (r_uag, r_uas, r_umg, r_ums) = unpack(r_u, self_w, 4)
    (r_mqkv, r_mout), (r_mag, r_mas, r_mmg, r_mms) = unpack(r_m, self_w, 4)
    (r_cq, r_cpair, r_cout), (r_cg, r_cs) = unpack(r_c, cross_w, 2)
    return (
        x2.astype(bf16).reshape(tokens.shape),
        dx.astype(bf16).reshape(tokens.shape),
        denc.astype(bf16).reshape(encoder.shape),
        r_uag, r_uas, r_uqkv, r_uout, r_umg, r_ums, r_uup, r_udown,
        r_mag, r_mas, r_mqkv, r_mout, r_cg, r_cs, r_cq, r_cpair, r_cout,
        r_mmg, r_mms, r_mup, r_mdown,
    )


def solution(mesh):
    rows1 = P(AXES)
    rows2 = P(AXES, None)
    rows3 = P(AXES, None, None)
    block = (rows1, rows1, rows2, rows2)
    weights = block * 2 + block + (rows1, rows1, rows2, rows2, rows2) + block
    return jax.shard_map(
        local,
        mesh=mesh,
        in_specs=(rows3, rows3, rows1, rows3) + weights,
        out_specs=(rows3, rows3, rows3) + weights,
        check_vma=False,
    )
```

```python
import functools

import jax
import jax.numpy as jnp
from jax import lax
from jax.experimental import pallas as pl
from jax.experimental.pallas import tpu as pltpu
from jax.sharding import PartitionSpec as P

DH = 64
AXES = ("dp", "hd")
EPS = 1e-05
MASKED = -1e30
LANES = 128
bf16 = jnp.bfloat16
f32 = jnp.float32
sds = jax.ShapeDtypeStruct


BIT_PAIR, BIT_CORE, BIT_NEAR = 1, 2, 4


class Place:
    def __init__(self):
        self.count = lax.axis_size("dp") * lax.axis_size("hd")
        self.outer_size = self.count // 8
        index = lax.axis_index("dp") * lax.axis_size("hd") + lax.axis_index("hd")
        self.pair = index % 2
        self.core = (index // 2) % 2
        self.near = (index // 4) % 2
        self.outer = index // 8

    def swap(self, x, bit):
        return lax.ppermute(x, AXES, [(i, i ^ bit) for i in range(self.count)])

    def shift(self, x, k):
        n = self.count
        return lax.ppermute(x, AXES, [(i, (i + 8 * k) % n) for i in range(n)])

    def order(self, d):
        n, rows = self.outer_size, d // self.count
        k = lax.broadcasted_iota(jnp.int32, (d, 1), 0)
        row = k % rows
        outer = (self.outer + (k // rows) % n) % n
        rest = k // (rows * n)
        pair = (self.pair + rest % 2) % 2
        near = (self.near + (rest // 2) % 2) % 2
        core = (self.core + rest // 4) % 2
        feature = (((outer * 2 + near) * 2 + core) * 2 + pair) * rows + row
        return (feature == lax.broadcasted_iota(jnp.int32, (d, d), 1)).astype(bf16)


def plus(a, b):
    return (a.astype(f32) + b.astype(f32)).astype(bf16)


def scatter_rows(place, kept, got):
    n = place.outer_size
    half = kept[0].shape[0]
    rows = half // (4 * n)

    def view(x):
        return x.reshape(2, 2, n * rows, x.shape[1])

    ka, ga = view(kept[0]), view(got[0])
    kb, gb = view(kept[1]), view(got[1])
    got_a = place.swap(plus(ka[1], ga[1]), BIT_NEAR)
    got_b = place.swap(plus(kb[:, 1], gb[:, 1]), BIT_PAIR)
    keep_a = plus(ka[0], ga[0])
    keep_b = plus(kb[:, 0], gb[:, 0])
    got_a2 = place.swap(plus(keep_a[1], got_a[1]), BIT_PAIR)
    got_b2 = place.swap(plus(keep_b[1], got_b[1]), BIT_NEAR)
    a = plus(plus(keep_a[0], got_a[0]), got_a2)
    b = plus(plus(keep_b[0], got_b[0]), got_b2)
    t = jnp.concatenate((a, b), axis=1).reshape(n, rows, -1)
    total = t[0].astype(f32)
    for k in range(1, n):
        total = total + place.shift(t[k], k).astype(f32)
    return total


def nn(a, b):
    return jnp.dot(a, b, preferred_element_type=f32)


def nt(a, b):
    return lax.dot_general(a, b, (((1,), (1,)), ((), ())), preferred_element_type=f32)


def tn(a, b):
    return lax.dot_general(a, b, (((0,), (0,)), ((), ())), preferred_element_type=f32)


def unit_norm(x):
    centred = x - jnp.mean(x, axis=-1, keepdims=True)
    inv = lax.rsqrt(jnp.mean(centred * centred, axis=-1, keepdims=True) + EPS)
    return centred * inv, inv


def norm_backward(grad, x, gain):
    unit, inv = unit_norm(x)
    du = grad * gain
    dx = inv * (
        du
        - jnp.mean(du, axis=-1, keepdims=True)
        - unit * jnp.mean(du * unit, axis=-1, keepdims=True)
    )
    return dx, jnp.sum(grad * unit, axis=0, keepdims=True), jnp.sum(grad, axis=0, keepdims=True)


GELU_A = 0.7978845608028654
GELU_B = 0.044715


def two_heads(x):
    first = lax.broadcasted_iota(jnp.int32, x.shape, 1) < DH
    zero = jnp.zeros_like(x)
    return jnp.concatenate((jnp.where(first, x, zero), jnp.where(first, zero, x)), axis=0)


def side_by_side(x):
    n = x.shape[0] // 2
    first = lax.broadcasted_iota(jnp.int32, (n, LANES), 1) < DH
    return jnp.where(first, x[:n], x[n:])


def probabilities(qs, k2, allowed):
    s = jnp.where(allowed, nt(qs, k2) * DH ** (-0.5), MASKED)
    e = jnp.exp(s - jnp.max(s, axis=-1, keepdims=True))
    return e / jnp.sum(e, axis=-1, keepdims=True)


def causal_mask(length):
    row = lax.broadcasted_iota(jnp.int32, (2 * length, length), 0)
    col = lax.broadcasted_iota(jnp.int32, (2 * length, length), 1)
    return jnp.where(row >= length, row - length, row) >= col


def attend_back(q2, k2, v2, do2, allowed):
    scale = DH ** (-0.5)
    qs, dos = two_heads(q2), two_heads(do2)
    p = probabilities(qs, k2, allowed)
    dp = nt(dos, v2)
    ds = (p * (dp - jnp.sum(p * dp, axis=-1, keepdims=True))).astype(bf16)
    dq = side_by_side(nn(ds, k2)) * scale
    dk = tn(ds, qs) * scale
    dv = tn(p.astype(bf16), dos)
    return dq.astype(bf16), dk.astype(bf16), dv.astype(bf16)


def self_forward_kernel(captions, row, x_ref, vec_ref, w_ref, y_ref, a_ref, qkv_ref, o_ref):
    j = pl.program_id(0)

    @pl.when(j == 0)
    def _():
        unit, _inv = unit_norm(x_ref[...])
        a_ref[...] = (unit * vec_ref[row : row + 1] + vec_ref[row + 1 : row + 2]).astype(bf16)

    @pl.when(j < 3)
    def _():
        qkv_ref[j] = nn(a_ref[...], w_ref[...]).astype(bf16)

    @pl.when(j == 3)
    def _():
        length = x_ref.shape[0] // captions
        allowed = causal_mask(length)
        for c in range(captions):
            at = slice(c * length, (c + 1) * length)
            for h in range(0, x_ref.shape[1], LANES):
                cols = slice(h, h + LANES)
                p = probabilities(two_heads(qkv_ref[0, at, cols]), qkv_ref[1, at, cols], allowed)
                o_ref[at, cols] = side_by_side(nn(p.astype(bf16), qkv_ref[2, at, cols])).astype(bf16)
        y_ref[...] = x_ref[...] + nn(o_ref[...], w_ref[...])


def self_backward_kernel(
    captions, row, x_ref, vec_ref, order_ref, a_ref, qkv_ref, o_ref, dx_ref, w_ref,
    out_ref, vg_ref, keep_ref, send_ref, dqkv_ref, at_ref, acc_ref,
):
    j = pl.program_id(0)
    half = keep_ref.shape[0]

    def emit(g):
        keep_ref[...] = g[:half].astype(bf16)
        send_ref[...] = g[half:].astype(bf16)

    @pl.when(j == 0)
    def _():
        dy = dx_ref[...].astype(bf16)
        emit(nn(nt(order_ref[...], o_ref[...]).astype(bf16), dy))
        do = nt(dy, w_ref[...]).astype(bf16)
        length = x_ref.shape[0] // captions
        allowed = causal_mask(length)
        for c in range(captions):
            at = slice(c * length, (c + 1) * length)
            for h in range(0, x_ref.shape[1], LANES):
                cols = slice(h, h + LANES)
                dq, dk, dv = attend_back(
                    qkv_ref[0, at, cols], qkv_ref[1, at, cols], qkv_ref[2, at, cols],
                    do[at, cols], allowed,
                )
                dqkv_ref[0, at, cols] = dq
                dqkv_ref[1, at, cols] = dk
                dqkv_ref[2, at, cols] = dv
        at_ref[...] = nt(order_ref[...], a_ref[...]).astype(bf16)
        acc_ref[...] = jnp.zeros_like(acc_ref)

    @pl.when(j > 0)
    def _():
        d = dqkv_ref[j - 1]
        emit(nn(at_ref[...], d))
        acc_ref[...] += nt(d, w_ref[...])

    @pl.when(j == 3)
    def _():
        dn, gg, gs = norm_backward(acc_ref[...], x_ref[...], vec_ref[row : row + 1])
        out_ref[...] = dx_ref[...] + dn
        vg_ref[0:1] = gg
        vg_ref[1:2] = gs


def cross_forward_kernel(
    captions, row, count_ref, x_ref, vec_ref, kv_ref, w_ref, y_ref, c_ref, q_ref, o_ref
):
    j = pl.program_id(0)
    d = x_ref.shape[1]

    @pl.when(j == 0)
    def _():
        unit, _inv = unit_norm(x_ref[...])
        c = (unit * vec_ref[row : row + 1] + vec_ref[row + 1 : row + 2]).astype(bf16)
        c_ref[...] = c
        q_ref[...] = nn(c, w_ref[...]).astype(bf16)

    @pl.when(j == 1)
    def _():
        length = x_ref.shape[0] // captions
        patches = kv_ref.shape[0] // captions
        slot = lax.broadcasted_iota(jnp.int32, (2 * length, patches), 1)
        for c in range(captions):
            at = slice(c * length, (c + 1) * length)
            keys = slice(c * patches, (c + 1) * patches)
            allowed = slot < count_ref[c]
            for h in range(0, d, LANES):
                cols = slice(h, h + LANES)
                vcols = slice(d + h, d + h + LANES)
                p = probabilities(two_heads(q_ref[at, cols]), kv_ref[keys, cols], allowed)
                o_ref[at, cols] = side_by_side(nn(p.astype(bf16), kv_ref[keys, vcols])).astype(bf16)
        y_ref[...] = x_ref[...] + nn(o_ref[...], w_ref[...])


def cross_backward_kernel(
    captions, row, count_ref, x_ref, vec_ref, order_ref, c_ref, q_ref, o_ref, kv_ref, dx_ref, w_ref,
    out_ref, vg_ref, keep_ref, send_ref, dkv_ref, dq_ref,
):
    j = pl.program_id(0)
    half = keep_ref.shape[0]
    d = x_ref.shape[1]

    def emit(g):
        keep_ref[...] = g[:half].astype(bf16)
        send_ref[...] = g[half:].astype(bf16)

    @pl.when(j == 0)
    def _():
        dy = dx_ref[...].astype(bf16)
        emit(nn(nt(order_ref[...], o_ref[...]).astype(bf16), dy))
        do = nt(dy, w_ref[...]).astype(bf16)
        length = x_ref.shape[0] // captions
        patches = kv_ref.shape[0] // captions
        slot = lax.broadcasted_iota(jnp.int32, (2 * length, patches), 1)
        for c in range(captions):
            at = slice(c * length, (c + 1) * length)
            keys = slice(c * patches, (c + 1) * patches)
            allowed = slot < count_ref[c]
            for h in range(0, d, LANES):
                cols = slice(h, h + LANES)
                vcols = slice(d + h, d + h + LANES)
                dq, dk, dv = attend_back(
                    q_ref[at, cols], kv_ref[keys, cols], kv_ref[keys, vcols], do[at, cols], allowed
                )
                dq_ref[at, cols] = dq
                dkv_ref[keys, cols] = dk
                dkv_ref[keys, vcols] = dv

    @pl.when(j == 1)
    def _():
        dq = dq_ref[...]
        emit(nn(nt(order_ref[...], c_ref[...]).astype(bf16), dq))
        dn, gg, gs = norm_backward(nt(dq, w_ref[...]), x_ref[...], vec_ref[row : row + 1])
        out_ref[...] = dx_ref[...] + dn
        vg_ref[0:1] = gg
        vg_ref[1:2] = gs


def feed_forward_kernel(row, x_ref, vec_ref, up_ref, down_ref, y_ref, b_ref, u_ref):
    @pl.when(pl.program_id(0) == 0)
    def _():
        unit, _inv = unit_norm(x_ref[...])
        b_ref[...] = (unit * vec_ref[row : row + 1] + vec_ref[row + 1 : row + 2]).astype(bf16)
        y_ref[...] = x_ref[...]

    u = nn(b_ref[...], up_ref[...])
    u_ref[...] = u
    g = 0.5 * u * (1.0 + jnp.tanh(GELU_A * (u + GELU_B * u * u * u)))
    y_ref[...] += nn(g.astype(bf16), down_ref[...])


def feed_backward_kernel(
    row, x_ref, vec_ref, order_ref, b_ref, u_ref, dx_ref, up_ref, down_ref,
    out_ref, vg_ref, keep_ref, send_ref, bt_ref, acc_ref,
):
    j = pl.program_id(0)
    half = keep_ref.shape[0]
    d = x_ref.shape[1]

    @pl.when(j == 0)
    def _():
        bt_ref[...] = nt(order_ref[...], b_ref[...]).astype(bf16)
        acc_ref[...] = jnp.zeros_like(acc_ref)

    u = u_ref[...]
    t = jnp.tanh(GELU_A * (u + GELU_B * u * u * u))
    g = (0.5 * u * (1.0 + t)).astype(bf16)
    slope = 0.5 * (1.0 + t) + 0.5 * u * (1.0 - t * t) * GELU_A * (1.0 + 3.0 * GELU_B * u * u)
    dz = dx_ref[...].astype(bf16)
    du = (slope * nt(dz, down_ref[...])).astype(bf16)
    acc_ref[...] += nt(du, up_ref[...])
    g_up = nn(bt_ref[...], du)
    keep_ref[:, :d] = g_up[:half].astype(bf16)
    send_ref[:, :d] = g_up[half:].astype(bf16)
    g_down = nn(nt(order_ref[...], g).astype(bf16), dz)
    keep_ref[:, d:] = g_down[:half].astype(bf16)
    send_ref[:, d:] = g_down[half:].astype(bf16)

    @pl.when(j == 3)
    def _():
        dn, gg, gs = norm_backward(acc_ref[...], x_ref[...], vec_ref[row : row + 1])
        out_ref[...] = dx_ref[...] + dn
        vg_ref[0:1] = gg
        vg_ref[1:2] = gs


def whole(x):
    return pl.BlockSpec(x.shape, lambda *_: (0,) * len(x.shape))


def call(kernel, steps, ins, in_specs, outs, out_specs, scratch=(), scalars=0, flops=0):
    size = sum(x.size * x.dtype.itemsize for x in outs)
    return pl.pallas_call(
        kernel,
        out_shape=outs,
        grid_spec=pltpu.PrefetchScalarGridSpec(
            num_scalar_prefetch=scalars,
            grid=(steps,),
            in_specs=in_specs,
            out_specs=out_specs,
            scratch_shapes=scratch,
        ),
        compiler_params=pltpu.CompilerParams(
            dimension_semantics=("arbitrary",), vmem_limit_bytes=40 << 20
        ),
        cost_estimate=pl.CostEstimate(flops=flops, bytes_accessed=2 * size, transcendentals=0),
    )(*ins)


class Layers:
    def __init__(self, captions, tokens, d, w, vec, order, count):
        self.captions, self.t, self.d = captions, tokens, d
        self.w, self.vec, self.order, self.count = w, vec, order, count
        self.xs = sds((tokens, d), f32)
        self.hs = sds((tokens, d), bf16)

    def weight(self, index):
        return pl.BlockSpec((self.d, self.d), lambda j, *_: (0, index(j)))

    def self_forward(self, x, at, row):
        outs = (self.xs, self.hs, sds((3, self.t, self.d), bf16), self.hs)
        return call(
            functools.partial(self_forward_kernel, self.captions, row), 4,
            (x, self.vec, self.w),
            [whole(x), whole(self.vec), self.weight(lambda j: at + j)],
            outs, [whole(o) for o in outs], flops=8 * self.t * self.d * self.d,
        )

    def self_backward(self, x, kept, dx, at, row):
        d, t = self.d, self.t
        a, qkv, o = kept
        outs = (self.xs, sds((8, d), f32), sds((d // 2, 4 * d), bf16), sds((d // 2, 4 * d), bf16))
        grad = pl.BlockSpec((d // 2, d), lambda j: (0, (j + 3) % 4))
        ins = (x, self.vec, self.order, a, qkv, o, dx)
        return call(
            functools.partial(self_backward_kernel, self.captions, row), 4,
            ins + (self.w,),
            [whole(i) for i in ins] + [self.weight(lambda j: at + (j + 3) % 4)],
            outs, [whole(outs[0]), whole(outs[1]), grad, grad],
            scratch=[pltpu.VMEM((3, t, d), bf16), pltpu.VMEM((d, t), bf16), pltpu.VMEM((t, d), f32)],
            flops=20 * t * d * d,
        )

    def cross_forward(self, x, kv, at, row):
        outs = (self.xs, self.hs, self.hs, self.hs)
        return call(
            functools.partial(cross_forward_kernel, self.captions, row), 2,
            (self.count, x, self.vec, kv, self.w),
            [whole(x), whole(self.vec), whole(kv), self.weight(lambda j: at + 3 * j)],
            outs, [whole(o) for o in outs], scalars=1, flops=10 * self.t * self.d * self.d,
        )

    def cross_backward(self, x, kept, kv, dx, at, row):
        d, t = self.d, self.t
        c, q, o = kept
        outs = (
            self.xs, sds((8, d), f32), sds((d // 2, 2 * d), bf16), sds((d // 2, 2 * d), bf16),
            sds(kv.shape, bf16),
        )
        grad = pl.BlockSpec((d // 2, d), lambda j, *_: (0, 1 - j))
        ins = (x, self.vec, self.order, c, q, o, kv, dx)
        return call(
            functools.partial(cross_backward_kernel, self.captions, row), 2,
            (self.count,) + ins + (self.w,),
            [whole(i) for i in ins] + [self.weight(lambda j: at + 3 - 3 * j)],
            outs, [whole(outs[0]), whole(outs[1]), grad, grad, whole(outs[4])],
            scratch=[pltpu.VMEM((t, d), bf16)], scalars=1, flops=30 * t * d * d,
        )

    def feed_forward(self, x, at, row):
        d, t = self.d, self.t
        outs = (self.xs, self.hs, sds((t, 4 * d), f32))
        return call(
            functools.partial(feed_forward_kernel, row), 4,
            (x, self.vec, self.w, self.w),
            [whole(x), whole(self.vec), self.weight(lambda j: at + j), self.weight(lambda j: at + 4 + j)],
            outs, [whole(outs[0]), whole(outs[1]), pl.BlockSpec((t, d), lambda j: (0, j))],
            flops=16 * t * d * d,
        )

    def feed_backward(self, x, kept, dx, at, row):
        d, t = self.d, self.t
        b, u = kept
        outs = (self.xs, sds((8, d), f32), sds((d // 2, 8 * d), bf16), sds((d // 2, 8 * d), bf16))
        grad = pl.BlockSpec((d // 2, 2 * d), lambda j: (0, j))
        return call(
            functools.partial(feed_backward_kernel, row), 4,
            (x, self.vec, self.order, b, u, dx, self.w, self.w),
            [
                whole(x), whole(self.vec), whole(self.order), whole(b),
                pl.BlockSpec((t, d), lambda j: (0, j)), whole(dx),
                self.weight(lambda j: at + j), self.weight(lambda j: at + 4 + j),
            ],
            outs, [whole(outs[0]), whole(outs[1]), grad, grad],
            scratch=[pltpu.VMEM((d, t), bf16), pltpu.VMEM((t, d), f32)],
            flops=44 * t * d * d,
        )


def spread_matrix():
    k = lax.broadcasted_iota(jnp.int32, (512, 512), 0)
    n = lax.broadcasted_iota(jnp.int32, (512, 512), 1)
    return (k % 4) * 128 + k // 4 == n


def spread(up):
    rows, wide = up.shape
    y = nn(up.reshape(rows * (wide // 512), 512), spread_matrix().astype(bf16)).astype(bf16)
    return y.reshape(rows, wide // 512, 4, 128).transpose(0, 2, 1, 3).reshape(rows, wide)


def unspread(up):
    rows, wide = up.shape
    y = up.reshape(rows, 4, wide // 512, 128).transpose(0, 2, 1, 3)
    y = lax.dot_general(
        y.reshape(rows * (wide // 512), 512), spread_matrix().astype(f32),
        (((1,), (1,)), ((), ())), precision=lax.Precision.HIGHEST,
    )
    return y.reshape(rows, wide)


def local(
    tokens, encoder, patch_count, out_grad,
    u_ag, u_as, u_qkv, u_out, u_mg, u_ms, u_up, u_down,
    m_ag, m_as, m_qkv, m_out, c_g, c_s, c_q, c_pair, c_out, m_mg, m_ms, m_up, m_down,
):
    place = Place()
    captions, length, d = tokens.shape
    rows = u_qkv.shape[0]
    x0 = tokens.reshape(-1, d).astype(f32)
    enc = encoder.reshape(-1, d)
    order = place.order(d)

    vectors = (u_ag, u_as, u_mg, u_ms, m_ag, m_as, c_g, c_s, m_mg, m_ms)
    cols = jnp.pad(jnp.stack(vectors, axis=1), ((0, 0), (0, LANES - len(vectors))))
    shard = jnp.concatenate(
        (
            u_qkv, u_out, spread(u_up), u_down.reshape(rows, -1),
            m_qkv, m_out, spread(m_up), m_down.reshape(rows, -1),
            c_q, c_pair, c_out, cols,
        ),
        axis=1,
    )
    w = lax.all_gather(shard, AXES, axis=0, tiled=True)
    vec = w[:, 28 * d : 28 * d + 16].astype(f32).T
    enc_t = nt(order, enc).astype(bf16)

    net = Layers(captions, captions * length, d, w, vec, order, patch_count)

    w_pair = w[:, 25 * d : 27 * d]
    kv = nn(enc, w_pair).astype(bf16)
    x0a, *k_us = net.self_forward(x0, 0, 0)
    x1, *k_uf = net.feed_forward(x0a, 4, 2)
    x1a, *k_ms = net.self_forward(x1, 12, 4)
    x1b, *k_mc = net.cross_forward(x1a, kv, 24, 6)
    x2, *k_mf = net.feed_forward(x1b, 16, 8)

    def core(x):
        return place.swap(x, BIT_CORE)

    def halves(x):
        at = x.shape[1] // 2
        return x[:, :at], x[:, at:]

    dx = out_grad.reshape(-1, d).astype(f32)
    dx, v_mf, keep, send = net.feed_backward(x1b, k_mf, dx, 16, 8)
    r_mf = scatter_rows(place, halves(keep), halves(core(send)))
    dx, v_mc, keep, send, dkv = net.cross_backward(x1a, k_mc, kv, dx, 24, 6)
    g_pair = nn(enc_t, dkv).astype(bf16)
    denc = nt(dkv, w_pair).astype(bf16)
    r_mc = scatter_rows(
        place, (keep, g_pair[: d // 2]), (core(send), core(g_pair[d // 2 :]))
    )
    dx, v_ms, keep, send = net.self_backward(x1, k_ms, dx, 12, 4)
    r_ms = scatter_rows(place, halves(keep), halves(core(send)))
    dx, v_uf, keep, send = net.feed_backward(x0a, k_uf, dx, 4, 2)
    r_uf = scatter_rows(place, halves(keep), halves(core(send)))
    dx, v_us, keep, send = net.self_backward(x0, k_us, dx, 0, 0)
    v = jnp.concatenate([g[:2] for g in (v_us, v_uf, v_ms, v_mc, v_mf)], axis=0).astype(bf16)
    v = nt(order, jnp.pad(v, ((0, LANES - v.shape[0]), (0, 0)))).astype(bf16)
    got = core(send)
    got_v = core(v[d // 2 :])
    at = 2 * d
    r_us = scatter_rows(
        place,
        (keep[:, :at], jnp.concatenate((keep[:, at:], v[: d // 2]), axis=1)),
        (got[:, :at], jnp.concatenate((got[:, at:], got_v), axis=1)),
    )

    def feed_rows(r):
        up = jnp.concatenate([r[:, (2 * j) * d : (2 * j + 1) * d] for j in range(4)], axis=1)
        down = jnp.concatenate([r[:, (2 * j + 1) * d : (2 * j + 2) * d] for j in range(4)], axis=1)
        return unspread(up), down.reshape(-1, d)

    r_uup, r_udown = feed_rows(r_uf)
    r_mup, r_mdown = feed_rows(r_mf)
    vs = r_us[:, 4 * d :]
    v = [vs[:, i] for i in range(10)]
    return (
        x2.astype(bf16).reshape(tokens.shape),
        dx.astype(bf16).reshape(tokens.shape),
        denc.reshape(encoder.shape),
        v[0], v[1], r_us[:, : 3 * d], r_us[:, 3 * d : 4 * d], v[2], v[3], r_uup, r_udown,
        v[4], v[5], r_ms[:, : 3 * d], r_ms[:, 3 * d :], v[6], v[7],
        r_mc[:, :d], r_mc[:, 2 * d :], r_mc[:, d : 2 * d],
        v[8], v[9], r_mup, r_mdown,
    )


def solution(mesh):
    rows1 = P(AXES)
    rows2 = P(AXES, None)
    rows3 = P(AXES, None, None)
    block = (rows1, rows1, rows2, rows2)
    weights = block * 2 + block + (rows1, rows1, rows2, rows2, rows2) + block
    return jax.shard_map(
        local,
        mesh=mesh,
        in_specs=(rows3, rows3, rows1, rows3) + weights,
        out_specs=(rows3, rows3, rows3) + weights,
        check_vma=False,
    )
```

```python
import functools

import jax
import jax.numpy as jnp
from jax import lax
from jax.experimental import pallas as pl
from jax.experimental.pallas import tpu as pltpu
from jax.sharding import PartitionSpec as P

DH = 64
AXES = ("dp", "hd")
EPS = 1e-05
MASKED = -1e30
LANES = 128
bf16 = jnp.bfloat16
f32 = jnp.float32
sds = jax.ShapeDtypeStruct


BIT_PAIR, BIT_CORE, BIT_NEAR = 1, 2, 4


class Place:
    def __init__(self):
        self.count = lax.axis_size("dp") * lax.axis_size("hd")
        self.outer_size = self.count // 8
        index = lax.axis_index("dp") * lax.axis_size("hd") + lax.axis_index("hd")
        self.pair = index % 2
        self.core = (index // 2) % 2
        self.near = (index // 4) % 2
        self.outer = index // 8

    def swap(self, x, bit):
        return lax.ppermute(x, AXES, [(i, i ^ bit) for i in range(self.count)])

    def shift(self, x, k):
        n = self.count
        return lax.ppermute(x, AXES, [(i, (i + 8 * k) % n) for i in range(n)])

    def order(self, d):
        n, rows = self.outer_size, d // self.count
        k = lax.broadcasted_iota(jnp.int32, (d, 1), 0)
        row = k % rows
        outer = (self.outer + (k // rows) % n) % n
        rest = k // (rows * n)
        pair = (self.pair + rest % 2) % 2
        near = (self.near + (rest // 2) % 2) % 2
        core = (self.core + rest // 4) % 2
        feature = (((outer * 2 + near) * 2 + core) * 2 + pair) * rows + row
        return (feature == lax.broadcasted_iota(jnp.int32, (d, d), 1)).astype(bf16)


def plus(a, b):
    return (a.astype(f32) + b.astype(f32)).astype(bf16)


class Sum:
    def __init__(self, place, kept, send):
        self.place, self.kept, self.send, self.stage = place, kept, send, 0

    def swap(self):
        place = self.place
        if self.stage < 3:
            bits = ((BIT_CORE,) * 2, (BIT_NEAR, BIT_PAIR), (BIT_PAIR, BIT_NEAR))[self.stage]
            self.got = tuple(place.swap(x, bit) for x, bit in zip(self.send, bits))
        else:
            self.got = tuple(place.shift(t, k + 1) for k, t in enumerate(self.send))

    def sums(self):
        (ka, kb), (ga, gb) = self.kept, self.got
        if self.stage == 0:
            rows = ka.shape[0] // 4
            ka, kb, ga, gb = (x.reshape(2, 2, rows, x.shape[1]) for x in (ka, kb, ga, gb))
            self.send = plus(ka[1], ga[1]), plus(kb[:, 1], gb[:, 1])
            self.kept = plus(ka[0], ga[0]), plus(kb[:, 0], gb[:, 0])
        elif self.stage == 1:
            self.send = plus(ka[1], ga[1]), plus(kb[1], gb[1])
            self.kept = plus(ka[0], ga[0]), plus(kb[0], gb[0])
        else:
            n = self.place.outer_size
            t = jnp.concatenate((plus(ka, ga), plus(kb, gb)), axis=1)
            t = t.reshape(n, t.shape[0] // n, t.shape[1])
            self.send = tuple(t[k] for k in range(1, n))
            self.kept = (t[0],)
        self.stage += 1

    def total(self):
        return sum([g.astype(f32) for g in self.got], self.kept[0].astype(f32))


def tie(x, *others):
    out = lax.optimization_barrier((x,) + others)
    return out[0], out[1:]


def hold(x, *groups):
    x, kept = tie(x, *[g.kept for g in groups])
    for g, k in zip(groups, kept):
        g.kept = k
    return x


def need(x, *groups):
    x, send = tie(x, *[g.send for g in groups])
    for g, k in zip(groups, send):
        g.send = k
    return x


def nn(a, b):
    return jnp.dot(a, b, preferred_element_type=f32)


def nt(a, b):
    return lax.dot_general(a, b, (((1,), (1,)), ((), ())), preferred_element_type=f32)


def tn(a, b):
    return lax.dot_general(a, b, (((0,), (0,)), ((), ())), preferred_element_type=f32)


def unit_norm(x):
    centred = x - jnp.mean(x, axis=-1, keepdims=True)
    inv = lax.rsqrt(jnp.mean(centred * centred, axis=-1, keepdims=True) + EPS)
    return centred * inv, inv


def norm_backward(grad, x, gain):
    unit, inv = unit_norm(x)
    du = grad * gain
    dx = inv * (
        du
        - jnp.mean(du, axis=-1, keepdims=True)
        - unit * jnp.mean(du * unit, axis=-1, keepdims=True)
    )
    return dx, jnp.sum(grad * unit, axis=0, keepdims=True), jnp.sum(grad, axis=0, keepdims=True)


GELU_A = 0.7978845608028654
GELU_B = 0.044715


def two_heads(x):
    first = lax.broadcasted_iota(jnp.int32, x.shape, 1) < DH
    zero = jnp.zeros_like(x)
    return jnp.concatenate((jnp.where(first, x, zero), jnp.where(first, zero, x)), axis=0)


def side_by_side(x):
    n = x.shape[0] // 2
    first = lax.broadcasted_iota(jnp.int32, (n, LANES), 1) < DH
    return jnp.where(first, x[:n], x[n:])


def probabilities(qs, k2, allowed):
    s = jnp.where(allowed, nt(qs, k2) * DH ** (-0.5), MASKED)
    e = jnp.exp(s - jnp.max(s, axis=-1, keepdims=True))
    return e / jnp.sum(e, axis=-1, keepdims=True)


def causal_mask(length):
    row = lax.broadcasted_iota(jnp.int32, (2 * length, length), 0)
    col = lax.broadcasted_iota(jnp.int32, (2 * length, length), 1)
    return jnp.where(row >= length, row - length, row) >= col


def attend_back(q2, k2, v2, do2, allowed):
    scale = DH ** (-0.5)
    qs, dos = two_heads(q2), two_heads(do2)
    p = probabilities(qs, k2, allowed)
    dp = nt(dos, v2)
    ds = (p * (dp - jnp.sum(p * dp, axis=-1, keepdims=True))).astype(bf16)
    dq = side_by_side(nn(ds, k2)) * scale
    dk = tn(ds, qs) * scale
    dv = tn(p.astype(bf16), dos)
    return dq.astype(bf16), dk.astype(bf16), dv.astype(bf16)


def self_forward_kernel(captions, row, x_ref, vec_ref, w_ref, y_ref, a_ref, qkv_ref, o_ref):
    j = pl.program_id(0)

    @pl.when(j == 0)
    def _():
        unit, _inv = unit_norm(x_ref[...].astype(f32))
        a_ref[...] = (unit * vec_ref[row : row + 1] + vec_ref[row + 1 : row + 2]).astype(bf16)

    @pl.when(j < 3)
    def _():
        qkv_ref[j] = nn(a_ref[...], w_ref[...]).astype(bf16)

    @pl.when(j == 3)
    def _():
        length = x_ref.shape[0] // captions
        allowed = causal_mask(length)
        for c in range(captions):
            at = slice(c * length, (c + 1) * length)
            for h in range(0, x_ref.shape[1], LANES):
                cols = slice(h, h + LANES)
                p = probabilities(two_heads(qkv_ref[0, at, cols]), qkv_ref[1, at, cols], allowed)
                o_ref[at, cols] = side_by_side(nn(p.astype(bf16), qkv_ref[2, at, cols])).astype(bf16)
        y_ref[...] = x_ref[...].astype(f32) + nn(o_ref[...], w_ref[...])


def emit(g, keep_ref, send_ref):
    half = keep_ref.shape[0]
    keep_ref[...] = g[:half].astype(bf16)
    send_ref[...] = g[half:].astype(bf16)


def self_backward_kernel(
    captions, row, x_ref, vec_ref, order_ref, a_ref, qkv_ref, o_ref, dx_ref, w_ref,
    out_ref, vg_ref, keep_a_ref, keep_b_ref, send_a_ref, send_b_ref, dqkv_ref, at_ref, acc_ref,
):
    j = pl.program_id(0)

    @pl.when(j == 0)
    def _():
        dy = dx_ref[...].astype(bf16)
        emit(nn(nt(order_ref[...], o_ref[...]).astype(bf16), dy), keep_b_ref, send_b_ref)
        do = nt(dy, w_ref[...]).astype(bf16)
        length = x_ref.shape[0] // captions
        allowed = causal_mask(length)
        for c in range(captions):
            at = slice(c * length, (c + 1) * length)
            for h in range(0, x_ref.shape[1], LANES):
                cols = slice(h, h + LANES)
                dq, dk, dv = attend_back(
                    qkv_ref[0, at, cols], qkv_ref[1, at, cols], qkv_ref[2, at, cols],
                    do[at, cols], allowed,
                )
                dqkv_ref[0, at, cols] = dq
                dqkv_ref[1, at, cols] = dk
                dqkv_ref[2, at, cols] = dv
        at_ref[...] = nt(order_ref[...], a_ref[...]).astype(bf16)
        acc_ref[...] = jnp.zeros_like(acc_ref)

    @pl.when(j > 0)
    def _():
        acc_ref[...] += nt(dqkv_ref[j - 1], w_ref[...])

    @pl.when((j == 1) | (j == 2))
    def _():
        emit(nn(at_ref[...], dqkv_ref[j - 1]), keep_a_ref, send_a_ref)

    @pl.when(j == 3)
    def _():
        emit(nn(at_ref[...], dqkv_ref[2]), keep_b_ref, send_b_ref)
        dn, gg, gs = norm_backward(acc_ref[...], x_ref[...].astype(f32), vec_ref[row : row + 1])
        out_ref[...] = dx_ref[...] + dn
        vg_ref[0:1] = gg
        vg_ref[1:2] = gs


def cross_forward_kernel(
    captions, row, count_ref, x_ref, vec_ref, kv_ref, w_ref, y_ref, c_ref, q_ref, o_ref
):
    j = pl.program_id(0)
    d = x_ref.shape[1]

    @pl.when(j == 0)
    def _():
        unit, _inv = unit_norm(x_ref[...])
        c = (unit * vec_ref[row : row + 1] + vec_ref[row + 1 : row + 2]).astype(bf16)
        c_ref[...] = c
        q_ref[...] = nn(c, w_ref[...]).astype(bf16)

    @pl.when(j == 1)
    def _():
        length = x_ref.shape[0] // captions
        patches = kv_ref.shape[0] // captions
        slot = lax.broadcasted_iota(jnp.int32, (2 * length, patches), 1)
        for c in range(captions):
            at = slice(c * length, (c + 1) * length)
            keys = slice(c * patches, (c + 1) * patches)
            allowed = slot < count_ref[c]
            for h in range(0, d, LANES):
                cols = slice(h, h + LANES)
                vcols = slice(d + h, d + h + LANES)
                p = probabilities(two_heads(q_ref[at, cols]), kv_ref[keys, cols], allowed)
                o_ref[at, cols] = side_by_side(nn(p.astype(bf16), kv_ref[keys, vcols])).astype(bf16)
        y_ref[...] = x_ref[...] + nn(o_ref[...], w_ref[...])


def cross_backward_kernel(
    captions, row, count_ref, x_ref, vec_ref, order_ref, c_ref, q_ref, o_ref, kv_ref, dx_ref, w_ref,
    out_ref, vg_ref, keep_ref, send_ref, dkv_ref, dq_ref,
):
    j = pl.program_id(0)
    d = x_ref.shape[1]

    @pl.when(j == 0)
    def _():
        dy = dx_ref[...].astype(bf16)
        emit(nn(nt(order_ref[...], o_ref[...]).astype(bf16), dy), keep_ref, send_ref)
        do = nt(dy, w_ref[...]).astype(bf16)
        length = x_ref.shape[0] // captions
        patches = kv_ref.shape[0] // captions
        slot = lax.broadcasted_iota(jnp.int32, (2 * length, patches), 1)
        for c in range(captions):
            at = slice(c * length, (c + 1) * length)
            keys = slice(c * patches, (c + 1) * patches)
            allowed = slot < count_ref[c]
            for h in range(0, d, LANES):
                cols = slice(h, h + LANES)
                vcols = slice(d + h, d + h + LANES)
                dq, dk, dv = attend_back(
                    q_ref[at, cols], kv_ref[keys, cols], kv_ref[keys, vcols], do[at, cols], allowed
                )
                dq_ref[at, cols] = dq
                dkv_ref[keys, cols] = dk
                dkv_ref[keys, vcols] = dv

    @pl.when(j == 1)
    def _():
        dq = dq_ref[...]
        emit(nn(nt(order_ref[...], c_ref[...]).astype(bf16), dq), keep_ref, send_ref)
        dn, gg, gs = norm_backward(nt(dq, w_ref[...]), x_ref[...], vec_ref[row : row + 1])
        out_ref[...] = dx_ref[...] + dn
        vg_ref[0:1] = gg
        vg_ref[1:2] = gs


def feed_forward_kernel(row, x_ref, vec_ref, up_ref, down_ref, y_ref, b_ref, u_ref):
    @pl.when(pl.program_id(0) == 0)
    def _():
        unit, _inv = unit_norm(x_ref[...])
        b_ref[...] = (unit * vec_ref[row : row + 1] + vec_ref[row + 1 : row + 2]).astype(bf16)
        y_ref[...] = x_ref[...]

    u = nn(b_ref[...], up_ref[...])
    u_ref[...] = u
    g = 0.5 * u * (1.0 + jnp.tanh(GELU_A * (u + GELU_B * u * u * u)))
    y_ref[...] += nn(g.astype(bf16), down_ref[...])


def feed_backward_step(j, order_ref, u, dz, up_ref, down_ref, refs, bt_ref, acc_ref):
    keep_a_ref, keep_b_ref, send_a_ref, send_b_ref = refs
    t = jnp.tanh(GELU_A * (u + GELU_B * u * u * u))
    g = (0.5 * u * (1.0 + t)).astype(bf16)
    slope = 0.5 * (1.0 + t) + 0.5 * u * (1.0 - t * t) * GELU_A * (1.0 + 3.0 * GELU_B * u * u)
    du = (slope * nt(dz, down_ref[...])).astype(bf16)
    acc_ref[...] += nt(du, up_ref[...])
    emit(nn(bt_ref[...], du), keep_a_ref, send_a_ref)
    emit(nn(nt(order_ref[...], g).astype(bf16), dz), keep_b_ref, send_b_ref)
    return g


def feed_backward_kernel(
    row, x_ref, vec_ref, order_ref, b_ref, u_ref, dx_ref, up_ref, down_ref,
    out_ref, vg_ref, keep_a_ref, keep_b_ref, send_a_ref, send_b_ref, bt_ref, acc_ref,
):
    j = pl.program_id(0)

    @pl.when(j == 0)
    def _():
        bt_ref[...] = nt(order_ref[...], b_ref[...]).astype(bf16)
        acc_ref[...] = jnp.zeros_like(acc_ref)

    refs = keep_a_ref, keep_b_ref, send_a_ref, send_b_ref
    dz = dx_ref[...].astype(bf16)
    feed_backward_step(j, order_ref, u_ref[...], dz, up_ref, down_ref, refs, bt_ref, acc_ref)

    @pl.when(j == 3)
    def _():
        dn, gg, gs = norm_backward(acc_ref[...], x_ref[...], vec_ref[row : row + 1])
        out_ref[...] = dx_ref[...] + dn
        vg_ref[0:1] = gg
        vg_ref[1:2] = gs


def feed_both_kernel(
    row, x_ref, vec_ref, order_ref, dx_ref, up_ref, down_ref,
    y_ref, out_ref, vg_ref, keep_a_ref, keep_b_ref, send_a_ref, send_b_ref,
    b_ref, sum_ref, bt_ref, acc_ref,
):
    j = pl.program_id(0)

    @pl.when(j == 0)
    def _():
        unit, _inv = unit_norm(x_ref[...])
        b_ref[...] = (unit * vec_ref[row : row + 1] + vec_ref[row + 1 : row + 2]).astype(bf16)
        bt_ref[...] = nt(order_ref[...], b_ref[...]).astype(bf16)
        acc_ref[...] = jnp.zeros_like(acc_ref)
        sum_ref[...] = x_ref[...]

    refs = keep_a_ref, keep_b_ref, send_a_ref, send_b_ref
    u = nn(b_ref[...], up_ref[...])
    dz = dx_ref[...]
    g = feed_backward_step(j, order_ref, u, dz, up_ref, down_ref, refs, bt_ref, acc_ref)
    sum_ref[...] += nn(g, down_ref[...])

    @pl.when(j == 3)
    def _():
        y_ref[...] = sum_ref[...].astype(bf16)
        dn, gg, gs = norm_backward(acc_ref[...], x_ref[...], vec_ref[row : row + 1])
        out_ref[...] = dx_ref[...].astype(f32) + dn
        vg_ref[0:1] = gg
        vg_ref[1:2] = gs


def pair_backward_kernel(enc_ref, dkv_ref, keep_ref, send_ref):
    emit(nn(enc_ref[...], dkv_ref[...]), keep_ref, send_ref)


def pack_kernel(u_qkv, u_out, u_up, u_down, m_qkv, m_out, m_up, m_down, c_q, c_pair, c_out, vec, out):
    rows, d = u_out.shape
    spread = spread_matrix().astype(bf16)
    i = lax.broadcasted_iota(jnp.int32, (rows, 4 * rows), 0)
    k = lax.broadcasted_iota(jnp.int32, (rows, 4 * rows), 1)

    def layer(at, qkv, w_out, up, down):
        out[:, at : at + 3 * d] = qkv[...]
        out[:, at + 3 * d : at + 4 * d] = w_out[...]
        for b in range(4 * d // 512):
            y = nn(up[:, b * 512 : (b + 1) * 512], spread).astype(bf16)
            for j in range(4):
                to = at + (4 + j) * d + b * LANES
                out[:, to : to + LANES] = y[:, j * LANES : (j + 1) * LANES]
        for j in range(4):
            y = nn((k == 4 * i + j).astype(bf16), down[...])
            out[:, at + (8 + j) * d : at + (9 + j) * d] = y.astype(bf16)

    layer(0, u_qkv, u_out, u_up, u_down)
    layer(12 * d, m_qkv, m_out, m_up, m_down)
    out[:, 24 * d : 25 * d] = c_q[...]
    out[:, 25 * d : 27 * d] = c_pair[...]
    out[:, 27 * d : 28 * d] = c_out[...]
    eye = lax.broadcasted_iota(jnp.int32, (rows, rows), 0) == lax.broadcasted_iota(jnp.int32, (rows, rows), 1)
    out[:, 28 * d :] = nt(eye.astype(bf16), vec[...]).astype(bf16)


def whole(x):
    return pl.BlockSpec(x.shape, lambda *_: (0,) * len(x.shape))


def call(kernel, steps, ins, in_specs, outs, out_specs, scratch=(), scalars=0, flops=0):
    size = sum(x.size * x.dtype.itemsize for x in jax.tree.leaves(outs))
    return pl.pallas_call(
        kernel,
        out_shape=outs,
        grid_spec=pltpu.PrefetchScalarGridSpec(
            num_scalar_prefetch=scalars,
            grid=(steps,),
            in_specs=in_specs,
            out_specs=out_specs,
            scratch_shapes=scratch,
        ),
        compiler_params=pltpu.CompilerParams(
            dimension_semantics=("arbitrary",), vmem_limit_bytes=40 << 20
        ),
        cost_estimate=pl.CostEstimate(flops=flops, bytes_accessed=2 * size, transcendentals=0),
    )(*ins)


class Layers:
    def __init__(self, captions, tokens, d, w, vec, order, count):
        self.captions, self.t, self.d = captions, tokens, d
        self.w, self.vec, self.order, self.count = w, vec, order, count
        self.xs = sds((tokens, d), f32)
        self.hs = sds((tokens, d), bf16)

    def weight(self, index):
        return pl.BlockSpec((self.d, self.d), lambda j, *_: (0, index(j)))

    def self_forward(self, x, at, row):
        outs = (self.xs, self.hs, sds((3, self.t, self.d), bf16), self.hs)
        return call(
            functools.partial(self_forward_kernel, self.captions, row), 4,
            (x, self.vec, self.w),
            [whole(x), whole(self.vec), self.weight(lambda j: at + j)],
            outs, [whole(o) for o in outs], flops=8 * self.t * self.d * self.d,
        )

    def self_backward(self, x, kept, dx, at, row):
        d, t = self.d, self.t
        a, qkv, o = kept
        outs = (self.xs, sds((8, d), f32)) + (sds((d // 2, 2 * d), bf16),) * 4
        grad_a = pl.BlockSpec((d // 2, d), lambda j: (0, j // 2))
        grad_b = pl.BlockSpec((d // 2, d), lambda j: (0, 1 - jnp.minimum(j, 1)))
        ins = (x, self.vec, self.order, a, qkv, o, dx)
        return call(
            functools.partial(self_backward_kernel, self.captions, row), 4,
            ins + (self.w,),
            [whole(i) for i in ins] + [self.weight(lambda j: at + (j + 3) % 4)],
            outs, [whole(outs[0]), whole(outs[1]), grad_a, grad_b, grad_a, grad_b],
            scratch=[pltpu.VMEM((3, t, d), bf16), pltpu.VMEM((d, t), bf16), pltpu.VMEM((t, d), f32)],
            flops=20 * t * d * d,
        )

    def cross_forward(self, x, kv, at, row):
        outs = (self.xs, self.hs, self.hs, self.hs)
        return call(
            functools.partial(cross_forward_kernel, self.captions, row), 2,
            (self.count, x, self.vec, kv, self.w),
            [whole(x), whole(self.vec), whole(kv), self.weight(lambda j: at + 3 * j)],
            outs, [whole(o) for o in outs], scalars=1, flops=10 * self.t * self.d * self.d,
        )

    def cross_backward(self, x, kept, kv, dx, at, row):
        d, t = self.d, self.t
        c, q, o = kept
        outs = (self.xs, sds((8, d), f32)) + (sds((d // 2, 2 * d), bf16),) * 2
        outs = outs + (sds(kv.shape, bf16),)
        grad = pl.BlockSpec((d // 2, d), lambda j, *_: (0, 1 - j))
        ins = (x, self.vec, self.order, c, q, o, kv, dx)
        return call(
            functools.partial(cross_backward_kernel, self.captions, row), 2,
            (self.count,) + ins + (self.w,),
            [whole(i) for i in ins] + [self.weight(lambda j: at + 3 - 3 * j)],
            outs, [whole(outs[0]), whole(outs[1]), grad, grad, whole(outs[4])],
            scratch=[pltpu.VMEM((t, d), bf16)], scalars=1, flops=30 * t * d * d,
        )

    def pair_backward(self, enc_t, dkv):
        d = self.d
        outs = (sds((d // 2, 2 * d), bf16),) * 2
        grad = pl.BlockSpec((d // 2, d), lambda j: (0, j))
        return call(
            pair_backward_kernel, 2, (enc_t, dkv),
            [whole(enc_t), pl.BlockSpec((dkv.shape[0], d), lambda j: (0, j))],
            outs, [grad, grad], flops=4 * enc_t.shape[1] * d * d,
        )

    def feed_forward(self, x, at, row):
        d, t = self.d, self.t
        outs = (self.xs, self.hs, sds((t, 4 * d), f32))
        return call(
            functools.partial(feed_forward_kernel, row), 4,
            (x, self.vec, self.w, self.w),
            [whole(x), whole(self.vec), self.weight(lambda j: at + j), self.weight(lambda j: at + 4 + j)],
            outs, [whole(outs[0]), whole(outs[1]), pl.BlockSpec((t, d), lambda j: (0, j))],
            flops=16 * t * d * d,
        )

    def feed_backward(self, x, kept, dx, at, row):
        d, t = self.d, self.t
        b, u = kept
        outs = (self.xs, sds((8, d), f32)) + (sds((d // 2, 4 * d), bf16),) * 4
        grad = pl.BlockSpec((d // 2, d), lambda j: (0, j))
        return call(
            functools.partial(feed_backward_kernel, row), 4,
            (x, self.vec, self.order, b, u, dx, self.w, self.w),
            [
                whole(x), whole(self.vec), whole(self.order), whole(b),
                pl.BlockSpec((t, d), lambda j: (0, j)), whole(dx),
                self.weight(lambda j: at + j), self.weight(lambda j: at + 4 + j),
            ],
            outs, [whole(outs[0]), whole(outs[1])] + [grad] * 4,
            scratch=[pltpu.VMEM((d, t), bf16), pltpu.VMEM((t, d), f32)],
            flops=44 * t * d * d,
        )

    def feed_both(self, x, dx, at, row):
        d, t = self.d, self.t
        outs = (self.hs, self.xs, sds((8, d), f32)) + (sds((d // 2, 4 * d), bf16),) * 4
        grad = pl.BlockSpec((d // 2, d), lambda j: (0, j))
        ins = (x, self.vec, self.order, dx)
        return call(
            functools.partial(feed_both_kernel, row), 4,
            ins + (self.w, self.w),
            [whole(i) for i in ins] + [self.weight(lambda j: at + j), self.weight(lambda j: at + 4 + j)],
            outs, [whole(o) for o in outs[:3]] + [grad] * 4,
            scratch=[
                pltpu.VMEM((t, d), bf16), pltpu.VMEM((t, d), f32),
                pltpu.VMEM((d, t), bf16), pltpu.VMEM((t, d), f32),
            ],
            flops=60 * t * d * d,
        )


def spread_matrix():
    k = lax.broadcasted_iota(jnp.int32, (512, 512), 0)
    n = lax.broadcasted_iota(jnp.int32, (512, 512), 1)
    return (k % 4) * 128 + k // 4 == n


def unspread(up):
    rows, wide = up.shape
    y = up.reshape(rows, 4, wide // 512, 128).transpose(0, 2, 1, 3)
    y = lax.dot_general(
        y.reshape(rows * (wide // 512), 512), spread_matrix().astype(f32),
        (((1,), (1,)), ((), ())), precision=lax.Precision.HIGHEST,
    )
    return y.reshape(rows, wide)


def local(
    tokens, encoder, patch_count, out_grad,
    u_ag, u_as, u_qkv, u_out, u_mg, u_ms, u_up, u_down,
    m_ag, m_as, m_qkv, m_out, c_g, c_s, c_q, c_pair, c_out, m_mg, m_ms, m_up, m_down,
):
    place = Place()
    captions, length, d = tokens.shape
    rows = u_qkv.shape[0]
    x0 = tokens.reshape(-1, d)
    enc = encoder.reshape(-1, d)
    order = place.order(d)

    vectors = (u_ag, u_as, u_mg, u_ms, m_ag, m_as, c_g, c_s, m_mg, m_ms)
    vectors = jnp.pad(jnp.stack(vectors, axis=0), ((0, LANES - len(vectors)), (0, 0)))
    parts = (u_qkv, u_out, u_up, u_down, m_qkv, m_out, m_up, m_down, c_q, c_pair, c_out, vectors)
    packed = sds((rows, 28 * d + LANES), bf16)
    shard = call(pack_kernel, 1, parts, [whole(p) for p in parts], packed, whole(packed))
    w = lax.all_gather(shard, AXES, axis=0, tiled=True)
    vec = nt(jnp.eye(16, LANES, dtype=bf16), w[:, 28 * d :])
    enc_t = nt(order, enc).astype(bf16)

    net = Layers(captions, captions * length, d, w, vec, order, patch_count)

    w_pair = w[:, 25 * d : 27 * d]
    kv = nn(enc, w_pair).astype(bf16)
    x0a, *k_us = net.self_forward(x0, 0, 0)
    x1, *k_uf = net.feed_forward(x0a, 4, 2)
    x1a, *k_ms = net.self_forward(x1, 12, 4)
    x1b, *k_mc = net.cross_forward(x1a, kv, 24, 6)

    x2, dx, v_mf, *g = net.feed_both(x1b, out_grad.reshape(-1, d), 16, 8)
    s_mf = Sum(place, g[:2], g[2:])
    s_mf.swap()
    dx, v_mc, keep, send, dkv = net.cross_backward(x1a, k_mc, kv, dx, 24, 6)
    keep_p, send_p = net.pair_backward(enc_t, dkv)
    s_mc = Sum(place, (keep, keep_p), (send, send_p))
    dx = hold(dx, s_mf)
    s_mf.sums()
    dx = need(dx, s_mf, s_mc)
    s_mf.swap()
    s_mc.swap()
    dx, v_ms, *g = net.self_backward(x1, k_ms, dx, 12, 4)
    s_ms = Sum(place, g[:2], g[2:])
    dx = hold(dx, s_mc)
    s_mc.sums()
    dx = need(dx, s_mc, s_ms)
    s_mc.swap()
    s_ms.swap()
    dx, v_uf, *g = net.feed_backward(x0a, k_uf, dx, 4, 2)
    s_uf = Sum(place, g[:2], g[2:])
    dx = hold(dx, s_mf, s_ms)
    s_mf.sums()
    s_ms.sums()
    dx = need(dx, s_mf, s_ms, s_uf)
    s_mf.swap()
    s_ms.swap()
    s_uf.swap()
    dx, v_us, *g = net.self_backward(x0, k_us, dx, 0, 0)
    v = jnp.concatenate([g[:2] for g in (v_us, v_uf, v_ms, v_mc, v_mf)], axis=0).astype(bf16)
    v = nt(order, jnp.pad(v, ((0, LANES - v.shape[0]), (0, 0)))).astype(bf16)
    s_us = Sum(place, g[:2], g[2:])
    s_us.kept = s_us.kept[0], jnp.concatenate((s_us.kept[1], v[: d // 2]), axis=1)
    dx = hold(dx, s_uf, s_mc)
    s_uf.sums()
    s_mc.sums()
    dx = need(dx, s_uf, s_mc, s_us)
    s_us.send = s_us.send[0], jnp.concatenate((s_us.send[1], v[d // 2 :]), axis=1)
    s_us.swap()
    s_uf.swap()
    s_mc.swap()
    dx, (dkv,) = tie(dx, dkv)
    denc = nt(dkv, w_pair).astype(bf16)
    dx, (denc,) = tie(dx, denc)
    for group in (s_us, s_mf, s_ms, s_uf, s_mc, s_us, s_ms, s_uf, s_us):
        dx = hold(dx, group)
        group.sums()
        dx = need(dx, group)
        group.swap()
    r_mf, r_mc, r_ms, r_uf, r_us = (x.total() for x in (s_mf, s_mc, s_ms, s_uf, s_us))

    def feed_rows(r):
        return unspread(r[:, : 4 * d]), r[:, 4 * d :].reshape(-1, d)

    r_uup, r_udown = feed_rows(r_uf)
    r_mup, r_mdown = feed_rows(r_mf)
    vs = r_us[:, 4 * d :]
    v = [vs[:, i] for i in range(10)]
    return (
        x2.reshape(tokens.shape),
        dx.astype(bf16).reshape(tokens.shape),
        denc.reshape(encoder.shape),
        v[0], v[1], r_us[:, : 3 * d], r_us[:, 3 * d : 4 * d], v[2], v[3], r_uup, r_udown,
        v[4], v[5], r_ms[:, : 3 * d], r_ms[:, 3 * d :], v[6], v[7],
        r_mc[:, :d], r_mc[:, 2 * d :], r_mc[:, d : 2 * d],
        v[8], v[9], r_mup, r_mdown,
    )


def solution(mesh):
    rows1 = P(AXES)
    rows2 = P(AXES, None)
    rows3 = P(AXES, None, None)
    block = (rows1, rows1, rows2, rows2)
    weights = block * 2 + block + (rows1, rows1, rows2, rows2, rows2) + block
    return jax.shard_map(
        local,
        mesh=mesh,
        in_specs=(rows3, rows3, rows1, rows3) + weights,
        out_specs=(rows3, rows3, rows3) + weights,
        check_vma=False,
    )
```

```python
import functools

import jax
import jax.numpy as jnp
from jax import lax
from jax.experimental import pallas as pl
from jax.experimental.pallas import tpu as pltpu
from jax.sharding import PartitionSpec as P

DH = 64
AXES = ("dp", "hd")
EPS = 1e-05
MASKED = -1e30
LANES = 128
bf16 = jnp.bfloat16
f32 = jnp.float32
sds = jax.ShapeDtypeStruct


BIT_PAIR, BIT_CORE, BIT_NEAR = 1, 2, 4


class Place:
    def __init__(self):
        self.count = lax.axis_size("dp") * lax.axis_size("hd")
        self.outer_size = self.count // 8
        index = lax.axis_index("dp") * lax.axis_size("hd") + lax.axis_index("hd")
        self.pair = index % 2
        self.core = (index // 2) % 2
        self.near = (index // 4) % 2
        self.outer = index // 8
        self.outer_bits = self.outer_size.bit_length() - 1

    def swap(self, x, bit):
        return lax.ppermute(x, AXES, [(i, i ^ bit) for i in range(self.count)])

    def order(self, d, near_first):
        n, rows = self.outer_size, d // self.count
        k = lax.broadcasted_iota(jnp.int32, (d, 1), 0)
        row, place = k % rows, (k // rows) % n
        outer = jnp.zeros_like(k)
        for b in range(self.outer_bits):
            outer = outer + ((place >> (self.outer_bits - 1 - b)) & 1) * (1 << b)
        outer = outer ^ self.outer
        rest = k // (rows * n)
        low, high = rest % 2, (rest // 2) % 2
        near, pair = (high, low) if near_first else (low, high)
        feature = outer * 2 + (near ^ self.near)
        feature = (feature * 2 + ((rest // 4) ^ self.core)) * 2 + (pair ^ self.pair)
        feature = feature * rows + row
        return (feature == lax.broadcasted_iota(jnp.int32, (d, d), 1)).astype(bf16)


def plus(a, b):
    return (a.astype(f32) + b.astype(f32)).astype(bf16)


class Sum:
    def __init__(self, place, grads):
        self.place, self.stage = place, 0
        send_a, keep_a, send_b, keep_b = grads
        self.send, self.kept = (send_a, send_b), (keep_a, keep_b)

    def swap(self):
        if self.stage < 2:
            bits = ((BIT_NEAR, BIT_PAIR), (BIT_PAIR, BIT_NEAR))[self.stage]
        else:
            bits = (8 << (self.stage - 2),)
        self.got = tuple(self.place.swap(x, bit) for x, bit in zip(self.send, bits))

    def sums(self):
        def part(at):
            return tuple(plus(k[at], g[at]) for k, g in zip(self.kept, self.got))

        if self.stage == 1:
            t = jnp.concatenate(part(slice(None)), axis=1)
            half = t.shape[0] // 2
            self.kept, self.send = (t[:half],), (t[half:],)
        else:
            half = self.kept[0].shape[0] // 2
            self.kept, self.send = part(slice(half)), part(slice(half, None))
        self.stage += 1

    def total(self):
        return self.kept[0].astype(f32) + self.got[0].astype(f32)


def tie(x, *others):
    out = lax.optimization_barrier((x,) + others)
    return out[0], out[1:]


def hold(x, *groups):
    x, kept = tie(x, *[g.kept for g in groups])
    for g, k in zip(groups, kept):
        g.kept = k
    return x


def need(x, *groups):
    x, send = tie(x, *[g.send for g in groups])
    for g, k in zip(groups, send):
        g.send = k
    return x


def nn(a, b):
    return jnp.dot(a, b, preferred_element_type=f32)


def nt(a, b):
    return lax.dot_general(a, b, (((1,), (1,)), ((), ())), preferred_element_type=f32)


def tn(a, b):
    return lax.dot_general(a, b, (((0,), (0,)), ((), ())), preferred_element_type=f32)


def unit_norm(x):
    centred = x - jnp.mean(x, axis=-1, keepdims=True)
    inv = lax.rsqrt(jnp.mean(centred * centred, axis=-1, keepdims=True) + EPS)
    return centred * inv, inv


def norm_backward(grad, x, gain):
    unit, inv = unit_norm(x)
    du = grad * gain
    dx = inv * (
        du
        - jnp.mean(du, axis=-1, keepdims=True)
        - unit * jnp.mean(du * unit, axis=-1, keepdims=True)
    )
    return dx, jnp.sum(grad * unit, axis=0, keepdims=True), jnp.sum(grad, axis=0, keepdims=True)


GELU_A = 0.7978845608028654
GELU_B = 0.044715


def two_heads(x):
    first = lax.broadcasted_iota(jnp.int32, x.shape, 1) < DH
    zero = jnp.zeros_like(x)
    return jnp.concatenate((jnp.where(first, x, zero), jnp.where(first, zero, x)), axis=0)


def side_by_side(x):
    n = x.shape[0] // 2
    first = lax.broadcasted_iota(jnp.int32, (n, LANES), 1) < DH
    return jnp.where(first, x[:n], x[n:])


def probabilities(qs, k2, allowed):
    s = jnp.where(allowed, nt(qs, k2) * DH ** (-0.5), MASKED)
    e = jnp.exp(s - jnp.max(s, axis=-1, keepdims=True))
    return e / jnp.sum(e, axis=-1, keepdims=True)


def causal_mask(length):
    row = lax.broadcasted_iota(jnp.int32, (2 * length, length), 0)
    col = lax.broadcasted_iota(jnp.int32, (2 * length, length), 1)
    return jnp.where(row >= length, row - length, row) >= col


def attend_back(q2, k2, v2, do2, allowed):
    scale = DH ** (-0.5)
    qs, dos = two_heads(q2), two_heads(do2)
    p = probabilities(qs, k2, allowed)
    dp = nt(dos, v2)
    ds = (p * (dp - jnp.sum(p * dp, axis=-1, keepdims=True))).astype(bf16)
    dq = side_by_side(nn(ds, k2)) * scale
    dk = tn(ds, qs) * scale
    dv = tn(p.astype(bf16), dos)
    return dq.astype(bf16), dk.astype(bf16), dv.astype(bf16)


def self_forward_kernel(captions, row, x_ref, vec_ref, w_ref, y_ref, a_ref, qkv_ref, o_ref):
    j = pl.program_id(0)

    @pl.when(j == 0)
    def _():
        unit, _inv = unit_norm(x_ref[...].astype(f32))
        a_ref[...] = (unit * vec_ref[row : row + 1] + vec_ref[row + 1 : row + 2]).astype(bf16)

    @pl.when(j < 3)
    def _():
        qkv_ref[j] = nn(a_ref[...], w_ref[...]).astype(bf16)

    @pl.when(j == 3)
    def _():
        length = x_ref.shape[0] // captions
        allowed = causal_mask(length)
        for c in range(captions):
            at = slice(c * length, (c + 1) * length)
            for h in range(0, x_ref.shape[1], LANES):
                cols = slice(h, h + LANES)
                p = probabilities(two_heads(qkv_ref[0, at, cols]), qkv_ref[1, at, cols], allowed)
                o_ref[at, cols] = side_by_side(nn(p.astype(bf16), qkv_ref[2, at, cols])).astype(bf16)
        y_ref[...] = x_ref[...].astype(f32) + nn(o_ref[...], w_ref[...])


def self_backward_kernel(
    captions, row, x_ref, vec_ref, a_ref, qkv_ref, o_ref, dx_ref, w_ref, *refs
):
    out_ref, vg_ref, p_ref, acc_ref = refs[-4:]
    j = pl.program_id(0)

    @pl.when(j == 0)
    def _():
        dy = dx_ref[...].astype(bf16)
        p_ref[0] = a_ref[...]
        p_ref[1] = o_ref[...]
        p_ref[5] = dy
        do = nt(dy, w_ref[...]).astype(bf16)
        length = x_ref.shape[0] // captions
        allowed = causal_mask(length)
        for c in range(captions):
            at = slice(c * length, (c + 1) * length)
            for h in range(0, x_ref.shape[1], LANES):
                cols = slice(h, h + LANES)
                dq, dk, dv = attend_back(
                    qkv_ref[0, at, cols], qkv_ref[1, at, cols], qkv_ref[2, at, cols],
                    do[at, cols], allowed,
                )
                p_ref[2, at, cols] = dq
                p_ref[3, at, cols] = dk
                p_ref[4, at, cols] = dv
        acc_ref[...] = jnp.zeros_like(acc_ref)

    @pl.when(j > 0)
    def _():
        acc_ref[...] += nt(p_ref[1 + j], w_ref[...])

    @pl.when(j == 3)
    def _():
        dn, gg, gs = norm_backward(acc_ref[...], x_ref[...].astype(f32), vec_ref[row : row + 1])
        out_ref[...] = dx_ref[...] + dn
        vg_ref[0:1] = gg
        vg_ref[1:2] = gs
        if len(refs) > 4:
            at = lax.broadcasted_iota(jnp.int32, refs[0].shape, 0)
            rows = jnp.where(at == 0, gg, jnp.where(at == 1, gs, refs[0][...]))
            p_ref[6] = jnp.zeros_like(p_ref[6])
            p_ref[6, 0 : refs[0].shape[0]] = rows.astype(bf16)


def cross_forward_kernel(
    captions, row, count_ref, x_ref, vec_ref, kv_ref, w_ref, y_ref, c_ref, q_ref, o_ref
):
    j = pl.program_id(0)
    d = x_ref.shape[1]

    @pl.when(j == 0)
    def _():
        unit, _inv = unit_norm(x_ref[...])
        c = (unit * vec_ref[row : row + 1] + vec_ref[row + 1 : row + 2]).astype(bf16)
        c_ref[...] = c
        q_ref[...] = nn(c, w_ref[...]).astype(bf16)

    @pl.when(j == 1)
    def _():
        length = x_ref.shape[0] // captions
        patches = kv_ref.shape[0] // captions
        slot = lax.broadcasted_iota(jnp.int32, (2 * length, patches), 1)
        for c in range(captions):
            at = slice(c * length, (c + 1) * length)
            keys = slice(c * patches, (c + 1) * patches)
            allowed = slot < count_ref[c]
            for h in range(0, d, LANES):
                cols = slice(h, h + LANES)
                vcols = slice(d + h, d + h + LANES)
                p = probabilities(two_heads(q_ref[at, cols]), kv_ref[keys, cols], allowed)
                o_ref[at, cols] = side_by_side(nn(p.astype(bf16), kv_ref[keys, vcols])).astype(bf16)
        y_ref[...] = x_ref[...] + nn(o_ref[...], w_ref[...])


def cross_backward_kernel(
    captions, row, count_ref, x_ref, vec_ref, c_ref, q_ref, o_ref, kv_ref, dx_ref, w_ref,
    out_ref, vg_ref, p_ref, dkv_ref,
):
    j = pl.program_id(0)
    d = x_ref.shape[1]

    @pl.when(j == 0)
    def _():
        dy = dx_ref[...].astype(bf16)
        p_ref[0] = c_ref[...]
        p_ref[1] = o_ref[...]
        p_ref[3] = dy
        do = nt(dy, w_ref[...]).astype(bf16)
        length = x_ref.shape[0] // captions
        patches = kv_ref.shape[0] // captions
        slot = lax.broadcasted_iota(jnp.int32, (2 * length, patches), 1)
        for c in range(captions):
            at = slice(c * length, (c + 1) * length)
            keys = slice(c * patches, (c + 1) * patches)
            allowed = slot < count_ref[c]
            for h in range(0, d, LANES):
                cols = slice(h, h + LANES)
                vcols = slice(d + h, d + h + LANES)
                dq, dk, dv = attend_back(
                    q_ref[at, cols], kv_ref[keys, cols], kv_ref[keys, vcols], do[at, cols], allowed
                )
                p_ref[2, at, cols] = dq
                dkv_ref[keys, cols] = dk
                dkv_ref[keys, vcols] = dv

    @pl.when(j == 1)
    def _():
        dn, gg, gs = norm_backward(nt(p_ref[2], w_ref[...]), x_ref[...], vec_ref[row : row + 1])
        out_ref[...] = dx_ref[...] + dn
        vg_ref[0:1] = gg
        vg_ref[1:2] = gs


def feed_forward_kernel(row, x_ref, vec_ref, up_ref, down_ref, y_ref, b_ref, u_ref):
    @pl.when(pl.program_id(0) == 0)
    def _():
        unit, _inv = unit_norm(x_ref[...])
        b_ref[...] = (unit * vec_ref[row : row + 1] + vec_ref[row + 1 : row + 2]).astype(bf16)
        y_ref[...] = x_ref[...]

    u = nn(b_ref[...], up_ref[...])
    u_ref[...] = u
    g = 0.5 * u * (1.0 + jnp.tanh(GELU_A * (u + GELU_B * u * u * u)))
    y_ref[...] += nn(g.astype(bf16), down_ref[...])


def feed_backward_kernel(
    row, x_ref, vec_ref, dx_ref, up_ref, down_ref, *refs
):
    out_ref, vg_ref, p_ref, acc_ref = refs[-4:]
    j = pl.program_id(0)

    @pl.when(j == 0)
    def _():
        if len(refs) > 4:
            p_ref[0] = refs[0][...]
        else:
            unit, _inv = unit_norm(x_ref[...])
            p_ref[0] = (unit * vec_ref[row : row + 1] + vec_ref[row + 1 : row + 2]).astype(bf16)
        p_ref[1] = dx_ref[...].astype(bf16)
        acc_ref[...] = jnp.zeros_like(acc_ref)

    u = refs[1][...] if len(refs) > 4 else nn(p_ref[0], up_ref[...])
    t = jnp.tanh(GELU_A * (u + GELU_B * u * u * u))
    p_ref[2 + j] = (0.5 * u * (1.0 + t)).astype(bf16)
    slope = 0.5 * (1.0 + t) + 0.5 * u * (1.0 - t * t) * GELU_A * (1.0 + 3.0 * GELU_B * u * u)
    du = (slope * nt(p_ref[1], down_ref[...])).astype(bf16)
    p_ref[6 + j] = du
    acc_ref[...] += nt(du, up_ref[...])

    @pl.when(j == 3)
    def _():
        dn, gg, gs = norm_backward(acc_ref[...], x_ref[...], vec_ref[row : row + 1])
        out_ref[...] = dx_ref[...].astype(f32) + dn
        vg_ref[0:1] = gg
        vg_ref[1:2] = gs


def feed_out_kernel(x_ref, g_ref, down_ref, y_ref, acc_ref):
    j = pl.program_id(0)

    @pl.when(j == 0)
    def _():
        acc_ref[...] = x_ref[...]

    acc_ref[...] += nn(g_ref[0], down_ref[...])

    @pl.when(j == 3)
    def _():
        y_ref[...] = acc_ref[...].astype(bf16)


def both(own_ref, got_ref):
    return jnp.concatenate((own_ref[0], got_ref[0]), axis=0)


def emit(g, send_ref, keep_ref):
    half = keep_ref.shape[0]
    keep_ref[...] = g[:half].astype(bf16)
    send_ref[...] = g[half:].astype(bf16)


def feed_grads_kernel(
    order_ref, b_ref, b2_ref, z_ref, z2_ref, g_ref, g2_ref, u_ref, u2_ref,
    send_a_ref, keep_a_ref, send_b_ref, keep_b_ref, bt_ref,
):
    @pl.when(pl.program_id(0) == 0)
    def _():
        bt_ref[...] = nt(order_ref[0], both(b_ref, b2_ref)).astype(bf16)

    emit(nn(bt_ref[...], both(u_ref, u2_ref)), send_a_ref, keep_a_ref)
    gt = nt(order_ref[1], both(g_ref, g2_ref)).astype(bf16)
    emit(nn(gt, both(z_ref, z2_ref)), send_b_ref, keep_b_ref)


def attend_grads_kernel(
    order_ref, s_ref, s2_ref, sd_ref, sd2_ref, *refs
):
    send_a_ref, keep_a_ref, send_b_ref, keep_b_ref = refs[-4:]
    j = pl.program_id(0)

    def product(a_ref, a2_ref, d_ref, d2_ref):
        at = nt(order_ref[0], both(a_ref, a2_ref)).astype(bf16)
        return nn(at, both(d_ref, d2_ref))

    @pl.when(j < 2)
    def _():
        emit(product(s_ref, s2_ref, sd_ref, sd2_ref), send_a_ref, keep_a_ref)

    @pl.when((j == 2) | (j == 3))
    def _():
        emit(product(s_ref, s2_ref, sd_ref, sd2_ref), send_b_ref, keep_b_ref)

    if len(refs) > 4:
        c_ref, c2_ref, cd_ref, cd2_ref, pair_ref, pair2_ref = refs[:6]

        @pl.when((j == 4) | (j == 5))
        def _():
            emit(product(c_ref, c2_ref, cd_ref, cd2_ref), send_a_ref, keep_a_ref)

        @pl.when(j > 5)
        def _():
            emit(pair_ref[...].astype(f32) + pair2_ref[...].astype(f32), send_b_ref, keep_b_ref)


def pair_grads_kernel(enc_ref, dkv_ref, keep_ref, send_ref):
    emit(nn(enc_ref[...], dkv_ref[...]), send_ref, keep_ref)


def pack_kernel(u_qkv, u_out, u_up, u_down, m_qkv, m_out, m_up, m_down, c_q, c_pair, c_out, vec, out):
    rows, d = u_out.shape
    spread = spread_matrix().astype(bf16)
    i = lax.broadcasted_iota(jnp.int32, (rows, 4 * rows), 0)
    k = lax.broadcasted_iota(jnp.int32, (rows, 4 * rows), 1)

    def layer(at, qkv, w_out, up, down):
        out[:, at : at + 3 * d] = qkv[...]
        out[:, at + 3 * d : at + 4 * d] = w_out[...]
        for b in range(4 * d // 512):
            y = nn(up[:, b * 512 : (b + 1) * 512], spread).astype(bf16)
            for j in range(4):
                to = at + (4 + j) * d + b * LANES
                out[:, to : to + LANES] = y[:, j * LANES : (j + 1) * LANES]
        for j in range(4):
            y = nn((k == 4 * i + j).astype(bf16), down[...])
            out[:, at + (8 + j) * d : at + (9 + j) * d] = y.astype(bf16)

    layer(0, u_qkv, u_out, u_up, u_down)
    layer(12 * d, m_qkv, m_out, m_up, m_down)
    out[:, 24 * d : 25 * d] = c_q[...]
    out[:, 25 * d : 27 * d] = c_pair[...]
    out[:, 27 * d : 28 * d] = c_out[...]
    eye = lax.broadcasted_iota(jnp.int32, (rows, rows), 0) == lax.broadcasted_iota(jnp.int32, (rows, rows), 1)
    out[:, 28 * d :] = nt(eye.astype(bf16), vec[...]).astype(bf16)


def whole(x):
    return pl.BlockSpec(x.shape, lambda *_: (0,) * len(x.shape))


def call(kernel, steps, ins, in_specs, outs, out_specs, scratch=(), scalars=0):
    return pl.pallas_call(
        kernel,
        out_shape=outs,
        grid_spec=pltpu.PrefetchScalarGridSpec(
            num_scalar_prefetch=scalars,
            grid=(steps,),
            in_specs=in_specs,
            out_specs=out_specs,
            scratch_shapes=scratch,
        ),
        compiler_params=pltpu.CompilerParams(
            dimension_semantics=("arbitrary",), vmem_limit_bytes=40 << 20
        ),
        cost_estimate=pl.CostEstimate(flops=1000, bytes_accessed=1000, transcendentals=0),
    )(*ins)


class Layers:
    def __init__(self, captions, tokens, d, w, vec, order, count):
        self.captions, self.t, self.d = captions, tokens, d
        self.w, self.vec, self.order, self.count = w, vec, order, count
        self.xs = sds((tokens, d), f32)
        self.hs = sds((tokens, d), bf16)

    def weight(self, index):
        return pl.BlockSpec((self.d, self.d), lambda j, *_: (0, index(j)))

    def self_forward(self, x, at, row):
        outs = (self.xs, self.hs, sds((3, self.t, self.d), bf16), self.hs)
        return call(
            functools.partial(self_forward_kernel, self.captions, row), 4,
            (x, self.vec, self.w),
            [whole(x), whole(self.vec), self.weight(lambda j: at + j)],
            outs, [whole(o) for o in outs],
        )

    def self_backward(self, x, kept, dx, at, row, vectors=()):
        d, t = self.d, self.t
        a, qkv, o = kept
        outs = (self.xs, sds((8, d), f32), sds((6 + len(vectors), t, d), bf16))
        ins = (x, self.vec, a, qkv, o, dx)
        return call(
            functools.partial(self_backward_kernel, self.captions, row), 4,
            ins + (self.w,) + vectors,
            [whole(i) for i in ins] + [self.weight(lambda j: at + (j + 3) % 4)]
            + [whole(v) for v in vectors],
            outs, [whole(i) for i in outs],
            scratch=[pltpu.VMEM((t, d), f32)],
        )

    def cross_forward(self, x, kv, at, row):
        outs = (self.xs, self.hs, self.hs, self.hs)
        return call(
            functools.partial(cross_forward_kernel, self.captions, row), 2,
            (self.count, x, self.vec, kv, self.w),
            [whole(x), whole(self.vec), whole(kv), self.weight(lambda j: at + 3 * j)],
            outs, [whole(o) for o in outs], scalars=1,
        )

    def cross_backward(self, x, kept, kv, dx, at, row):
        d, t = self.d, self.t
        c, q, o = kept
        outs = (self.xs, sds((8, d), f32), sds((4, t, d), bf16), sds(kv.shape, bf16))
        ins = (x, self.vec, c, q, o, kv, dx)
        return call(
            functools.partial(cross_backward_kernel, self.captions, row), 2,
            (self.count,) + ins + (self.w,),
            [whole(i) for i in ins] + [self.weight(lambda j: at + 3 - 3 * j)],
            outs, [whole(i) for i in outs], scalars=1,
        )

    def pair_grads(self, enc_t, dkv):
        d = self.d
        outs = (sds((d // 2, 2 * d), bf16),) * 2
        grad = pl.BlockSpec((d // 2, d), lambda j: (0, j))
        return call(
            pair_grads_kernel, 2, (enc_t, dkv),
            [whole(enc_t), pl.BlockSpec((dkv.shape[0], d), lambda j: (0, j))],
            outs, [grad, grad],
        )

    def block(self, index):
        return pl.BlockSpec((1, self.t, self.d), lambda j: (index(j), 0, 0))

    def feed_grads(self, own, got):
        d, t = self.d, self.t
        outs = (sds((d // 4, 4 * d), bf16),) * 4
        at = [self.block(i) for i in (lambda j: 0, lambda j: 1, lambda j: 2 + j, lambda j: 6 + j)]
        return call(
            feed_grads_kernel, 4, (self.order,) + (own, got) * 4,
            [whole(self.order)] + [at[i // 2] for i in range(8)],
            outs, [pl.BlockSpec((d // 4, d), lambda j: (0, j))] * 4,
            scratch=[pltpu.VMEM((d // 2, 2 * t), bf16)],
        )

    def attend_grads(self, own, got, cross=()):
        d, t = self.d, self.t
        steps = 8 if cross else 4
        outs = (sds((d // 4, steps // 2 * d), bf16),) * 4

        def first(j):
            return jnp.where(j < 4, jnp.minimum(j, 1), jnp.minimum(j - 2, 3))

        def second(j):
            return jnp.where(j < 6, jnp.clip(j - 2, 0, 1), j - 4)

        grad_a = pl.BlockSpec((d // 4, d), lambda j: (0, first(j)))
        grad_b = pl.BlockSpec((d // 4, d), lambda j: (0, second(j)))
        order = pl.BlockSpec(
            (1, d // 2, d), lambda j: (jnp.where((j == 2) | (j == 3), 1, 0), 0, 0)
        )
        lhs = self.block(lambda j: jnp.minimum(j // 3, 1))
        rhs = self.block(lambda j: 2 + jnp.minimum(j, 3))
        ins, specs = (self.order, own, got, own, got), [order, lhs, lhs, rhs, rhs]
        if cross:
            own_c, got_c, pair, pair2 = cross
            lhs = self.block(lambda j: jnp.clip(j - 4, 0, 1))
            rhs = self.block(lambda j: 2 + jnp.clip(j - 4, 0, 1))
            half = pl.BlockSpec((d // 2, d), lambda j: (0, jnp.clip(j - 6, 0, 1)))
            ins = ins + (own_c, got_c, own_c, got_c, pair, pair2)
            specs = specs + [lhs, lhs, rhs, rhs, half, half]
        return call(
            attend_grads_kernel, steps, ins, specs, outs, [grad_a, grad_a, grad_b, grad_b]
        )

    def feed_forward(self, x, at, row):
        d, t = self.d, self.t
        outs = (self.xs, self.hs, sds((t, 4 * d), f32))
        return call(
            functools.partial(feed_forward_kernel, row), 4,
            (x, self.vec, self.w, self.w),
            [whole(x), whole(self.vec), self.weight(lambda j: at + j), self.weight(lambda j: at + 4 + j)],
            outs, [whole(outs[0]), whole(outs[1]), pl.BlockSpec((t, d), lambda j: (0, j))],
        )

    def feed_backward(self, x, kept, dx, at, row):
        d, t = self.d, self.t
        outs = (self.xs, sds((8, d), f32), sds((10, t, d), bf16))
        specs = [whole(kept[0]), pl.BlockSpec((t, d), lambda j: (0, j))] if kept else []
        return call(
            functools.partial(feed_backward_kernel, row), 4,
            (x, self.vec, dx, self.w, self.w) + tuple(kept),
            [
                whole(x), whole(self.vec), whole(dx),
                self.weight(lambda j: at + j), self.weight(lambda j: at + 4 + j),
            ] + specs,
            outs, [whole(i) for i in outs],
            scratch=[pltpu.VMEM((t, d), f32)],
        )

    def feed_out(self, x, p, at):
        return call(
            feed_out_kernel, 4, (x, p, self.w),
            [whole(x), self.block(lambda j: 2 + j), self.weight(lambda j: at + 4 + j)],
            self.hs, whole(self.hs), scratch=[pltpu.VMEM((self.t, self.d), f32)],
        )


def spread_matrix():
    k = lax.broadcasted_iota(jnp.int32, (512, 512), 0)
    n = lax.broadcasted_iota(jnp.int32, (512, 512), 1)
    return (k % 4) * 128 + k // 4 == n


def unspread(up):
    rows, wide = up.shape
    y = up.reshape(rows, 4, wide // 512, 128).transpose(0, 2, 1, 3)
    y = lax.dot_general(
        y.reshape(rows * (wide // 512), 512), spread_matrix().astype(f32),
        (((1,), (1,)), ((), ())), precision=lax.Precision.HIGHEST,
    )
    return y.reshape(rows, wide)


def local(
    tokens, encoder, patch_count, out_grad,
    u_ag, u_as, u_qkv, u_out, u_mg, u_ms, u_up, u_down,
    m_ag, m_as, m_qkv, m_out, c_g, c_s, c_q, c_pair, c_out, m_mg, m_ms, m_up, m_down,
):
    place = Place()
    captions, length, d = tokens.shape
    rows = u_qkv.shape[0]
    x0 = tokens.reshape(-1, d)
    enc = encoder.reshape(-1, d)
    order = jnp.stack((place.order(d, True), place.order(d, False)))
    order_pair = order[1]
    order = order[:, : d // 2]

    vectors = (u_ag, u_as, u_mg, u_ms, m_ag, m_as, c_g, c_s, m_mg, m_ms)
    vectors = jnp.pad(jnp.stack(vectors, axis=0), ((0, LANES - len(vectors)), (0, 0)))
    parts = (u_qkv, u_out, u_up, u_down, m_qkv, m_out, m_up, m_down, c_q, c_pair, c_out, vectors)
    packed = sds((rows, 28 * d + LANES), bf16)
    shard = call(pack_kernel, 1, parts, [whole(p) for p in parts], packed, whole(packed))
    enc_t = nt(order_pair, enc).astype(bf16)
    w = lax.all_gather(shard, AXES, axis=0, tiled=True)
    w, (order, enc_t) = tie(w, order, enc_t)
    vec = nt(jnp.eye(16, LANES, dtype=bf16), w[:, 28 * d :])

    net = Layers(captions, captions * length, d, w, vec, order, patch_count)

    w_pair = w[:, 25 * d : 27 * d]
    kv = nn(enc, w_pair).astype(bf16)
    x0a, *k_us = net.self_forward(x0, 0, 0)
    x1, *k_uf = net.feed_forward(x0a, 4, 2)
    x1a, *k_ms = net.self_forward(x1, 12, 4)
    x1b, *k_mc = net.cross_forward(x1a, kv, 24, 6)

    def core(x):
        return place.swap(x, BIT_CORE)

    def go_on(x, sums=(), start=()):
        x = hold(x, *sums)
        for g in sums:
            g.sums()
        x = need(x, *(tuple(sums) + tuple(g for g in start if g not in sums)))
        for g in start:
            g.swap()
        return x

    def rest(x, *groups):
        for _ in range(place.outer_bits - 1):
            for g in groups:
                x = go_on(x, [g], [g])
        return x

    dx, v_mf, p = net.feed_backward(x1b, (), out_grad.reshape(-1, d), 16, 8)
    q = core(p)
    x2 = net.feed_out(x1b, p, 16)
    p, (x2,) = tie(p, x2)
    s_mf = Sum(place, net.feed_grads(p, q))
    dx = go_on(dx, start=[s_mf])
    dx, v_mc, p_c, dkv = net.cross_backward(x1a, k_mc, kv, dx, 24, 6)
    q_c = core(p_c)
    keep, send = net.pair_grads(enc_t, dkv)
    dx, (send,) = tie(dx, send)
    got = core(send)
    dx, v_ms, p = net.self_backward(x1, k_ms, dx, 12, 4)
    q = core(p)
    dx = go_on(dx, [s_mf], [s_mf])
    dx, (p, p_c, keep) = tie(dx, p, p_c, keep)
    s_ma = Sum(place, net.attend_grads(p, q, (p_c, q_c, keep, got)))
    dx = go_on(dx, start=[s_ma])
    dx, v_uf, p = net.feed_backward(x0a, k_uf, dx, 4, 2)
    s_uf = Sum(place, net.feed_grads(p, core(p)))
    dx = need(dx, s_uf)
    dx = go_on(dx, [s_mf], [s_uf])
    v = [g[:2] for g in (v_uf, v_ms, v_mc, v_mf)]
    v = jnp.pad(jnp.concatenate(v, axis=0), ((2, 6), (0, 0)))
    dx, _v, p = net.self_backward(x0, k_us, dx, 0, 0, (v,))
    q = core(p)
    dx, (dkv,) = tie(dx, dkv)
    denc = nt(dkv, w_pair).astype(bf16)
    p, (denc,) = tie(p, denc)
    send_a, keep_a, send_b, keep_b = net.attend_grads(p, q)
    v = nt(order[1], plus(p[6], q[6])[:LANES]).astype(bf16)
    send_b = jnp.concatenate((send_b, v[d // 4 :]), axis=1)
    keep_b = jnp.concatenate((keep_b, v[: d // 4]), axis=1)
    s_us = Sum(place, (send_a, keep_a, send_b, keep_b))
    dx = need(dx, s_us)
    dx = go_on(dx, start=[s_mf])
    dx = go_on(dx, [s_ma], [s_ma])
    dx = rest(dx, s_mf)
    dx = go_on(dx, [s_uf], [s_us])
    dx, (r_mf,) = tie(dx, s_mf.total())
    dx = go_on(dx, [s_ma], [s_ma, s_uf])
    dx = go_on(dx, [s_us], [s_us])
    dx = rest(dx, s_ma)
    dx = go_on(dx, [s_uf], [s_uf])
    dx, (r_ma,) = tie(dx, s_ma.total())
    dx = go_on(dx, [s_us], [s_us])
    dx = rest(dx, s_uf, s_us)
    r_uf, r_us = s_uf.total(), s_us.total()

    def feed_rows(r):
        return unspread(r[:, : 4 * d]), r[:, 4 * d :].reshape(-1, d)

    def columns(r, *blocks):
        parts = [r[:, b * d : (b + 1) * d] for b in blocks]
        return jnp.concatenate(parts, axis=1) if len(parts) > 1 else parts[0]

    r_uup, r_udown = feed_rows(r_uf)
    r_mup, r_mdown = feed_rows(r_mf)
    vs = r_us[:, 4 * d :]
    v = [vs[:, i] for i in range(10)]
    return (
        x2.reshape(tokens.shape),
        dx.astype(bf16).reshape(tokens.shape),
        denc.reshape(encoder.shape),
        v[0], v[1], r_us[:, : 3 * d], r_us[:, 3 * d : 4 * d], v[2], v[3], r_uup, r_udown,
        v[4], v[5], columns(r_ma, 0, 1, 4), columns(r_ma, 5), v[6], v[7],
        columns(r_ma, 2), columns(r_ma, 6, 7), columns(r_ma, 3),
        v[8], v[9], r_mup, r_mdown,
    )


def solution(mesh):
    rows1 = P(AXES)
    rows2 = P(AXES, None)
    rows3 = P(AXES, None, None)
    block = (rows1, rows1, rows2, rows2)
    weights = block * 2 + block + (rows1, rows1, rows2, rows2, rows2) + block
    return jax.shard_map(
        local,
        mesh=mesh,
        in_specs=(rows3, rows3, rows1, rows3) + weights,
        out_specs=(rows3, rows3, rows3) + weights,
        check_vma=False,
    )
```

```python
import functools

import jax
import jax.numpy as jnp
from jax import lax
from jax.experimental import pallas as pl
from jax.experimental.pallas import tpu as pltpu
from jax.sharding import PartitionSpec as P

DH = 64
AXES = ("dp", "hd")
EPS = 1e-05
MASKED = -1e30
LANES = 128
bf16 = jnp.bfloat16
f32 = jnp.float32
sds = jax.ShapeDtypeStruct


BIT_PAIR, BIT_CORE, BIT_NEAR = 1, 2, 4


class Place:
    def __init__(self):
        self.count = lax.axis_size("dp") * lax.axis_size("hd")
        self.outer_size = self.count // 8
        index = lax.axis_index("dp") * lax.axis_size("hd") + lax.axis_index("hd")
        self.pair = index % 2
        self.core = (index // 2) % 2
        self.near = (index // 4) % 2
        self.outer = index // 8
        self.outer_bits = self.outer_size.bit_length() - 1

    def swap(self, x, bit):
        return lax.ppermute(x, AXES, [(i, i ^ bit) for i in range(self.count)])

    def order(self, d, near_first):
        n, rows = self.outer_size, d // self.count
        k = lax.broadcasted_iota(jnp.int32, (d, 1), 0)
        row, place = k % rows, (k // rows) % n
        outer = jnp.zeros_like(k)
        for b in range(self.outer_bits):
            outer = outer + ((place >> (self.outer_bits - 1 - b)) & 1) * (1 << b)
        outer = outer ^ self.outer
        rest = k // (rows * n)
        low, high = rest % 2, (rest // 2) % 2
        near, pair = (high, low) if near_first else (low, high)
        feature = outer * 2 + (near ^ self.near)
        feature = (feature * 2 + ((rest // 4) ^ self.core)) * 2 + (pair ^ self.pair)
        feature = feature * rows + row
        return (feature == lax.broadcasted_iota(jnp.int32, (d, d), 1)).astype(bf16)


def plus(a, b):
    return (a.astype(f32) + b.astype(f32)).astype(bf16)


class Sum:
    def __init__(self, place, grads):
        self.place, self.stage = place, 0
        send_a, keep_a, send_b, keep_b = grads
        self.send, self.kept = (send_a, send_b), (keep_a, keep_b)

    def swap(self):
        if self.stage < 2:
            bits = ((BIT_NEAR, BIT_PAIR), (BIT_PAIR, BIT_NEAR))[self.stage]
        else:
            bits = (8 << (self.stage - 2),)
        self.got = tuple(self.place.swap(x, bit) for x, bit in zip(self.send, bits))

    def sums(self):
        def part(at):
            return tuple(plus(k[at], g[at]) for k, g in zip(self.kept, self.got))

        if self.stage == 1:
            t = jnp.concatenate(part(slice(None)), axis=1)
            half = t.shape[0] // 2
            self.kept, self.send = (t[:half],), (t[half:],)
        else:
            half = self.kept[0].shape[0] // 2
            self.kept, self.send = part(slice(half)), part(slice(half, None))
        self.stage += 1

    def total(self):
        return self.kept[0].astype(f32) + self.got[0].astype(f32)


def tie(x, *others):
    out = lax.optimization_barrier((x,) + others)
    return out[0], out[1:]


def hold(x, *groups):
    x, terms = tie(x, *[(g.kept, g.got) for g in groups])
    for g, t in zip(groups, terms):
        g.kept, g.got = t
    return x


def need(x, *groups):
    x, send = tie(x, *[g.send for g in groups])
    for g, k in zip(groups, send):
        g.send = k
    return x


def nn(a, b):
    return jnp.dot(a, b, preferred_element_type=f32)


def nt(a, b):
    return lax.dot_general(a, b, (((1,), (1,)), ((), ())), preferred_element_type=f32)


def tn(a, b):
    return lax.dot_general(a, b, (((0,), (0,)), ((), ())), preferred_element_type=f32)


def unit_norm(x):
    centred = x - jnp.mean(x, axis=-1, keepdims=True)
    inv = lax.rsqrt(jnp.mean(centred * centred, axis=-1, keepdims=True) + EPS)
    return centred * inv, inv


def norm_backward(grad, x, gain):
    unit, inv = unit_norm(x)
    du = grad * gain
    dx = inv * (
        du
        - jnp.mean(du, axis=-1, keepdims=True)
        - unit * jnp.mean(du * unit, axis=-1, keepdims=True)
    )
    return dx, jnp.sum(grad * unit, axis=0, keepdims=True), jnp.sum(grad, axis=0, keepdims=True)


GELU_A = 0.7978845608028654
GELU_B = 0.044715


def two_heads(x):
    first = lax.broadcasted_iota(jnp.int32, x.shape, 1) < DH
    zero = jnp.zeros_like(x)
    return jnp.concatenate((jnp.where(first, x, zero), jnp.where(first, zero, x)), axis=0)


def side_by_side(x):
    n = x.shape[0] // 2
    first = lax.broadcasted_iota(jnp.int32, (n, LANES), 1) < DH
    return jnp.where(first, x[:n], x[n:])


def probabilities(qs, k2, allowed):
    s = jnp.where(allowed, nt(qs, k2) * DH ** (-0.5), MASKED)
    e = jnp.exp(s - jnp.max(s, axis=-1, keepdims=True))
    return e / jnp.sum(e, axis=-1, keepdims=True)


def causal_mask(length):
    row = lax.broadcasted_iota(jnp.int32, (2 * length, length), 0)
    col = lax.broadcasted_iota(jnp.int32, (2 * length, length), 1)
    return jnp.where(row >= length, row - length, row) >= col


def attend_back(q2, k2, v2, do2, allowed):
    scale = DH ** (-0.5)
    qs, dos = two_heads(q2), two_heads(do2)
    p = probabilities(qs, k2, allowed)
    dp = nt(dos, v2)
    ds = (p * (dp - jnp.sum(p * dp, axis=-1, keepdims=True))).astype(bf16)
    dq = side_by_side(nn(ds, k2)) * scale
    dk = tn(ds, qs) * scale
    dv = tn(p.astype(bf16), dos)
    return dq.astype(bf16), dk.astype(bf16), dv.astype(bf16)


def self_forward_kernel(captions, row, x_ref, vec_ref, w_ref, y_ref, f_ref, qkv_ref):
    j = pl.program_id(0)

    @pl.when(j == 0)
    def _():
        unit, _inv = unit_norm(x_ref[...].astype(f32))
        f_ref[0] = (unit * vec_ref[row : row + 1] + vec_ref[row + 1 : row + 2]).astype(bf16)

    @pl.when(j < 3)
    def _():
        qkv_ref[j] = nn(f_ref[0], w_ref[...]).astype(bf16)

    @pl.when(j == 3)
    def _():
        length = x_ref.shape[0] // captions
        allowed = causal_mask(length)
        for c in range(captions):
            at = slice(c * length, (c + 1) * length)
            for h in range(0, x_ref.shape[1], LANES):
                cols = slice(h, h + LANES)
                p = probabilities(two_heads(qkv_ref[0, at, cols]), qkv_ref[1, at, cols], allowed)
                o = side_by_side(nn(p.astype(bf16), qkv_ref[2, at, cols]))
                f_ref[1, at, cols] = o.astype(bf16)
        y_ref[...] = x_ref[...].astype(f32) + nn(f_ref[1], w_ref[...])


def self_backward_kernel(
    captions, row, x_ref, vec_ref, qkv_ref, dx_ref, w_ref, *refs
):
    out_ref, vg_ref, p_ref, acc_ref = refs[-4:]
    j = pl.program_id(0)

    @pl.when(j == 0)
    def _():
        dy = dx_ref[...].astype(bf16)
        p_ref[3] = dy
        do = nt(dy, w_ref[...]).astype(bf16)
        length = x_ref.shape[0] // captions
        allowed = causal_mask(length)
        for c in range(captions):
            at = slice(c * length, (c + 1) * length)
            for h in range(0, x_ref.shape[1], LANES):
                cols = slice(h, h + LANES)
                dq, dk, dv = attend_back(
                    qkv_ref[0, at, cols], qkv_ref[1, at, cols], qkv_ref[2, at, cols],
                    do[at, cols], allowed,
                )
                p_ref[0, at, cols] = dq
                p_ref[1, at, cols] = dk
                p_ref[2, at, cols] = dv
        acc_ref[...] = jnp.zeros_like(acc_ref)

    @pl.when(j > 0)
    def _():
        acc_ref[...] += nt(p_ref[j - 1], w_ref[...])

    @pl.when(j == 3)
    def _():
        dn, gg, gs = norm_backward(acc_ref[...], x_ref[...].astype(f32), vec_ref[row : row + 1])
        out_ref[...] = dx_ref[...] + dn
        vg_ref[0:1] = gg
        vg_ref[1:2] = gs
        if len(refs) > 4:
            at = lax.broadcasted_iota(jnp.int32, refs[0].shape, 0)
            rows = jnp.where(at == 0, gg, jnp.where(at == 1, gs, refs[0][...]))
            p_ref[4] = jnp.zeros_like(p_ref[4])
            p_ref[4, 0 : refs[0].shape[0]] = rows.astype(bf16)


def cross_forward_kernel(
    captions, row, count_ref, x_ref, vec_ref, kv_ref, w_ref, y_ref, f_ref, q_ref
):
    j = pl.program_id(0)
    d = x_ref.shape[1]

    @pl.when(j == 0)
    def _():
        unit, _inv = unit_norm(x_ref[...])
        c = (unit * vec_ref[row : row + 1] + vec_ref[row + 1 : row + 2]).astype(bf16)
        f_ref[0] = c
        q_ref[...] = nn(c, w_ref[...]).astype(bf16)

    @pl.when(j == 1)
    def _():
        length = x_ref.shape[0] // captions
        patches = kv_ref.shape[0] // captions
        slot = lax.broadcasted_iota(jnp.int32, (2 * length, patches), 1)
        for c in range(captions):
            at = slice(c * length, (c + 1) * length)
            keys = slice(c * patches, (c + 1) * patches)
            allowed = slot < count_ref[c]
            for h in range(0, d, LANES):
                cols = slice(h, h + LANES)
                vcols = slice(d + h, d + h + LANES)
                p = probabilities(two_heads(q_ref[at, cols]), kv_ref[keys, cols], allowed)
                o = side_by_side(nn(p.astype(bf16), kv_ref[keys, vcols]))
                f_ref[1, at, cols] = o.astype(bf16)
        y_ref[...] = x_ref[...] + nn(f_ref[1], w_ref[...])


def cross_backward_kernel(
    captions, row, count_ref, x_ref, vec_ref, q_ref, kv_ref, dx_ref, w_ref,
    out_ref, vg_ref, p_ref, dkv_ref,
):
    j = pl.program_id(0)
    d = x_ref.shape[1]

    @pl.when(j == 0)
    def _():
        dy = dx_ref[...].astype(bf16)
        p_ref[1] = dy
        do = nt(dy, w_ref[...]).astype(bf16)
        length = x_ref.shape[0] // captions
        patches = kv_ref.shape[0] // captions
        slot = lax.broadcasted_iota(jnp.int32, (2 * length, patches), 1)
        for c in range(captions):
            at = slice(c * length, (c + 1) * length)
            keys = slice(c * patches, (c + 1) * patches)
            allowed = slot < count_ref[c]
            for h in range(0, d, LANES):
                cols = slice(h, h + LANES)
                vcols = slice(d + h, d + h + LANES)
                dq, dk, dv = attend_back(
                    q_ref[at, cols], kv_ref[keys, cols], kv_ref[keys, vcols], do[at, cols], allowed
                )
                p_ref[0, at, cols] = dq
                dkv_ref[keys, cols] = dk
                dkv_ref[keys, vcols] = dv

    @pl.when(j == 1)
    def _():
        dn, gg, gs = norm_backward(nt(p_ref[0], w_ref[...]), x_ref[...], vec_ref[row : row + 1])
        out_ref[...] = dx_ref[...] + dn
        vg_ref[0:1] = gg
        vg_ref[1:2] = gs


def feed_forward_kernel(row, x_ref, vec_ref, up_ref, down_ref, y_ref, f_ref, u_ref):
    j = pl.program_id(0)

    @pl.when(j == 0)
    def _():
        unit, _inv = unit_norm(x_ref[...])
        f_ref[0] = (unit * vec_ref[row : row + 1] + vec_ref[row + 1 : row + 2]).astype(bf16)
        y_ref[...] = x_ref[...]

    u = nn(f_ref[0], up_ref[...])
    u_ref[...] = u
    g = (0.5 * u * (1.0 + jnp.tanh(GELU_A * (u + GELU_B * u * u * u)))).astype(bf16)
    f_ref[1 + j] = g
    y_ref[...] += nn(g, down_ref[...])


def feed_backward_kernel(row, kept, x_ref, vec_ref, dx_ref, up_ref, down_ref, *refs):
    out_ref, vg_ref, p_ref = refs[1:4] if kept else refs[:3]
    acc_ref = refs[-1]
    j = pl.program_id(0)

    @pl.when(j == 0)
    def _():
        if not kept:
            unit, _inv = unit_norm(x_ref[...])
            refs[3][0] = (unit * vec_ref[row : row + 1] + vec_ref[row + 1 : row + 2]).astype(bf16)
        p_ref[0] = dx_ref[...].astype(bf16)
        acc_ref[...] = jnp.zeros_like(acc_ref)

    u = refs[0][...] if kept else nn(refs[3][0], up_ref[...])
    t = jnp.tanh(GELU_A * (u + GELU_B * u * u * u))
    if not kept:
        refs[3][1 + j] = (0.5 * u * (1.0 + t)).astype(bf16)
    slope = 0.5 * (1.0 + t) + 0.5 * u * (1.0 - t * t) * GELU_A * (1.0 + 3.0 * GELU_B * u * u)
    du = (slope * nt(p_ref[0], down_ref[...])).astype(bf16)
    p_ref[1 + j] = du
    acc_ref[...] += nt(du, up_ref[...])

    @pl.when(j == 3)
    def _():
        dn, gg, gs = norm_backward(acc_ref[...], x_ref[...], vec_ref[row : row + 1])
        out_ref[...] = dx_ref[...].astype(f32) + dn
        vg_ref[0:1] = gg
        vg_ref[1:2] = gs


def feed_out_kernel(x_ref, g_ref, down_ref, y_ref, acc_ref):
    j = pl.program_id(0)

    @pl.when(j == 0)
    def _():
        acc_ref[...] = x_ref[...]

    acc_ref[...] += nn(g_ref[0], down_ref[...])

    @pl.when(j == 3)
    def _():
        y_ref[...] = acc_ref[...].astype(bf16)


def both(own_ref, got_ref):
    return jnp.concatenate((own_ref[0], got_ref[0]), axis=0)


def emit(g, send_ref, keep_ref):
    half = keep_ref.shape[0]
    keep_ref[...] = g[:half].astype(bf16)
    send_ref[...] = g[half:].astype(bf16)


def feed_grads_kernel(
    order_ref, b_ref, b2_ref, z_ref, z2_ref, g_ref, g2_ref, u_ref, u2_ref,
    send_a_ref, keep_a_ref, send_b_ref, keep_b_ref, bt_ref,
):
    @pl.when(pl.program_id(0) == 0)
    def _():
        bt_ref[...] = nt(order_ref[0], both(b_ref, b2_ref)).astype(bf16)

    emit(nn(bt_ref[...], both(u_ref, u2_ref)), send_a_ref, keep_a_ref)
    gt = nt(order_ref[1], both(g_ref, g2_ref)).astype(bf16)
    emit(nn(gt, both(z_ref, z2_ref)), send_b_ref, keep_b_ref)


def attend_grads_kernel(
    order_ref, s_ref, s2_ref, sd_ref, sd2_ref, *refs
):
    send_a_ref, keep_a_ref, send_b_ref, keep_b_ref = refs[-4:]
    j = pl.program_id(0)

    def product(a_ref, a2_ref, d_ref, d2_ref):
        at = nt(order_ref[0], both(a_ref, a2_ref)).astype(bf16)
        return nn(at, both(d_ref, d2_ref))

    @pl.when(j < 2)
    def _():
        emit(product(s_ref, s2_ref, sd_ref, sd2_ref), send_a_ref, keep_a_ref)

    @pl.when((j == 2) | (j == 3))
    def _():
        emit(product(s_ref, s2_ref, sd_ref, sd2_ref), send_b_ref, keep_b_ref)

    if len(refs) > 4:
        c_ref, c2_ref, cd_ref, cd2_ref, pair_ref, pair2_ref = refs[:6]

        @pl.when((j == 4) | (j == 5))
        def _():
            emit(product(c_ref, c2_ref, cd_ref, cd2_ref), send_a_ref, keep_a_ref)

        @pl.when(j > 5)
        def _():
            emit(pair_ref[...].astype(f32) + pair2_ref[...].astype(f32), send_b_ref, keep_b_ref)


def pair_grads_kernel(enc_ref, dkv_ref, keep_ref, send_ref):
    emit(nn(enc_ref[...], dkv_ref[...]), send_ref, keep_ref)


def pack_kernel(u_qkv, u_out, u_up, u_down, m_qkv, m_out, m_up, m_down, c_q, c_pair, c_out, vec, out):
    rows, d = u_out.shape
    spread = spread_matrix().astype(bf16)
    i = lax.broadcasted_iota(jnp.int32, (rows, 4 * rows), 0)
    k = lax.broadcasted_iota(jnp.int32, (rows, 4 * rows), 1)

    def layer(at, qkv, w_out, up, down):
        out[:, at : at + 3 * d] = qkv[...]
        out[:, at + 3 * d : at + 4 * d] = w_out[...]
        for b in range(4 * d // 512):
            y = nn(up[:, b * 512 : (b + 1) * 512], spread).astype(bf16)
            for j in range(4):
                to = at + (4 + j) * d + b * LANES
                out[:, to : to + LANES] = y[:, j * LANES : (j + 1) * LANES]
        for j in range(4):
            y = nn((k == 4 * i + j).astype(bf16), down[...])
            out[:, at + (8 + j) * d : at + (9 + j) * d] = y.astype(bf16)

    layer(0, u_qkv, u_out, u_up, u_down)
    layer(12 * d, m_qkv, m_out, m_up, m_down)
    out[:, 24 * d : 25 * d] = c_q[...]
    out[:, 25 * d : 27 * d] = c_pair[...]
    out[:, 27 * d : 28 * d] = c_out[...]
    eye = lax.broadcasted_iota(jnp.int32, (rows, rows), 0) == lax.broadcasted_iota(jnp.int32, (rows, rows), 1)
    out[:, 28 * d :] = nt(eye.astype(bf16), vec[...]).astype(bf16)


def whole(x):
    return pl.BlockSpec(x.shape, lambda *_: (0,) * len(x.shape))


def call(kernel, steps, ins, in_specs, outs, out_specs, scratch=(), scalars=0, vmem=40):
    return pl.pallas_call(
        kernel,
        out_shape=outs,
        grid_spec=pltpu.PrefetchScalarGridSpec(
            num_scalar_prefetch=scalars,
            grid=(steps,),
            in_specs=in_specs,
            out_specs=out_specs,
            scratch_shapes=scratch,
        ),
        compiler_params=pltpu.CompilerParams(
            dimension_semantics=("arbitrary",), vmem_limit_bytes=vmem << 20
        ),
        cost_estimate=pl.CostEstimate(flops=1000, bytes_accessed=1000, transcendentals=0),
    )(*ins)


class Layers:
    def __init__(self, captions, tokens, d, w, vec, order, count):
        self.captions, self.t, self.d = captions, tokens, d
        self.w, self.vec, self.order, self.count = w, vec, order, count
        self.xs = sds((tokens, d), f32)
        self.hs = sds((tokens, d), bf16)

    def weight(self, index):
        return pl.BlockSpec((self.d, self.d), lambda j, *_: (0, index(j)))

    def self_forward(self, x, at, row):
        outs = (self.xs, sds((2, self.t, self.d), bf16), sds((3, self.t, self.d), bf16))
        return call(
            functools.partial(self_forward_kernel, self.captions, row), 4,
            (x, self.vec, self.w),
            [whole(x), whole(self.vec), self.weight(lambda j: at + j)],
            outs, [whole(o) for o in outs],
        )

    def self_backward(self, x, kept, dx, at, row, vectors=()):
        d, t = self.d, self.t
        outs = (self.xs, sds((8, d), f32), sds((4 + len(vectors), t, d), bf16))
        ins = (x, self.vec, kept, dx)
        return call(
            functools.partial(self_backward_kernel, self.captions, row), 4,
            ins + (self.w,) + vectors,
            [whole(i) for i in ins] + [self.weight(lambda j: at + (j + 3) % 4)]
            + [whole(v) for v in vectors],
            outs, [whole(i) for i in outs],
            scratch=[pltpu.VMEM((t, d), f32)],
        )

    def cross_forward(self, x, kv, at, row):
        outs = (self.xs, sds((2, self.t, self.d), bf16), self.hs)
        return call(
            functools.partial(cross_forward_kernel, self.captions, row), 2,
            (self.count, x, self.vec, kv, self.w),
            [whole(x), whole(self.vec), whole(kv), self.weight(lambda j: at + 3 * j)],
            outs, [whole(o) for o in outs], scalars=1,
        )

    def cross_backward(self, x, kept, kv, dx, at, row):
        d, t = self.d, self.t
        outs = (self.xs, sds((8, d), f32), sds((2, t, d), bf16), sds(kv.shape, bf16))
        ins = (x, self.vec, kept, kv, dx)
        return call(
            functools.partial(cross_backward_kernel, self.captions, row), 2,
            (self.count,) + ins + (self.w,),
            [whole(i) for i in ins] + [self.weight(lambda j: at + 3 - 3 * j)],
            outs, [whole(i) for i in outs], scalars=1,
        )

    def pair_grads(self, enc_t, dkv):
        d = self.d
        outs = (sds((d // 2, 2 * d), bf16),) * 2
        grad = pl.BlockSpec((d // 2, d), lambda j: (0, j))
        return call(
            pair_grads_kernel, 2, (enc_t, dkv),
            [whole(enc_t), pl.BlockSpec((dkv.shape[0], d), lambda j: (0, j))],
            outs, [grad, grad],
        )

    def block(self, index):
        return pl.BlockSpec((1, self.t, self.d), lambda j: (index(j), 0, 0))

    def feed_grads(self, f, p):
        d, t = self.d, self.t
        outs = (sds((d // 4, 4 * d), bf16),) * 4
        first, later = self.block(lambda j: 0), self.block(lambda j: 1 + j)
        return call(
            feed_grads_kernel, 4, (self.order,) + f + p + f + p,
            [whole(self.order)] + [first] * 4 + [later] * 4,
            outs, [pl.BlockSpec((d // 4, d), lambda j: (0, j))] * 4,
            scratch=[pltpu.VMEM((d // 2, 2 * t), bf16)],
        )

    def attend_grads(self, f, p, cross=()):
        d, t = self.d, self.t
        steps = 8 if cross else 4
        outs = (sds((d // 4, steps // 2 * d), bf16),) * 4

        def first(j):
            return jnp.where(j < 4, jnp.minimum(j, 1), jnp.minimum(j - 2, 3))

        def second(j):
            return jnp.where(j < 6, jnp.clip(j - 2, 0, 1), j - 4)

        grad_a = pl.BlockSpec((d // 4, d), lambda j: (0, first(j)))
        grad_b = pl.BlockSpec((d // 4, d), lambda j: (0, second(j)))
        order = pl.BlockSpec(
            (1, d // 2, d), lambda j: (jnp.where((j == 2) | (j == 3), 1, 0), 0, 0)
        )
        lhs = self.block(lambda j: jnp.minimum(j // 3, 1))
        rhs = self.block(lambda j: jnp.minimum(j, 3))
        ins, specs = (self.order,) + f + p, [order, lhs, lhs, rhs, rhs]
        if cross:
            f, p, pair = cross
            lhs = self.block(lambda j: jnp.clip(j - 4, 0, 1))
            rhs = lhs
            half = pl.BlockSpec((d // 2, d), lambda j: (0, jnp.clip(j - 6, 0, 1)))
            ins = ins + f + p + pair
            specs = specs + [lhs, lhs, rhs, rhs, half, half]
        return call(
            attend_grads_kernel, steps, ins, specs, outs, [grad_a, grad_a, grad_b, grad_b]
        )

    def feed_forward(self, x, at, row):
        d, t = self.d, self.t
        outs = (self.xs, sds((5, t, d), bf16), sds((t, 4 * d), f32))
        return call(
            functools.partial(feed_forward_kernel, row), 4,
            (x, self.vec, self.w, self.w),
            [whole(x), whole(self.vec), self.weight(lambda j: at + j), self.weight(lambda j: at + 4 + j)],
            outs, [whole(outs[0]), whole(outs[1]), pl.BlockSpec((t, d), lambda j: (0, j))],
        )

    def feed_backward(self, x, kept, dx, at, row):
        d, t = self.d, self.t
        outs = (self.xs, sds((8, d), f32), sds((5, t, d), bf16))
        if not kept:
            outs = outs + (sds((5, t, d), bf16),)
        return call(
            functools.partial(feed_backward_kernel, row, bool(kept)), 4,
            (x, self.vec, dx, self.w, self.w) + kept,
            [
                whole(x), whole(self.vec), whole(dx),
                self.weight(lambda j: at + j), self.weight(lambda j: at + 4 + j),
            ] + [pl.BlockSpec((t, d), lambda j: (0, j)) for _ in kept],
            outs, [whole(i) for i in outs],
            scratch=[pltpu.VMEM((t, d), f32)],
        )

    def feed_out(self, x, p, at):
        return call(
            feed_out_kernel, 4, (x, p, self.w),
            [whole(x), self.block(lambda j: 1 + j), self.weight(lambda j: at + 4 + j)],
            self.hs, whole(self.hs), scratch=[pltpu.VMEM((self.t, self.d), f32)],
        )


def spread_matrix():
    k = lax.broadcasted_iota(jnp.int32, (512, 512), 0)
    n = lax.broadcasted_iota(jnp.int32, (512, 512), 1)
    return (k % 4) * 128 + k // 4 == n


def unspread(up):
    rows, wide = up.shape
    y = up.reshape(rows, 4, wide // 512, 128).transpose(0, 2, 1, 3)
    y = lax.dot_general(
        y.reshape(rows * (wide // 512), 512), spread_matrix().astype(f32),
        (((1,), (1,)), ((), ())), precision=lax.Precision.HIGHEST,
    )
    return y.reshape(rows, wide)


def local(
    tokens, encoder, patch_count, out_grad,
    u_ag, u_as, u_qkv, u_out, u_mg, u_ms, u_up, u_down,
    m_ag, m_as, m_qkv, m_out, c_g, c_s, c_q, c_pair, c_out, m_mg, m_ms, m_up, m_down,
):
    place = Place()
    captions, length, d = tokens.shape
    rows = u_qkv.shape[0]
    x0 = tokens.reshape(-1, d)
    enc = encoder.reshape(-1, d)
    order = jnp.stack((place.order(d, True), place.order(d, False)))
    order_pair = order[1]
    order = order[:, : d // 2]

    vectors = (u_ag, u_as, u_mg, u_ms, m_ag, m_as, c_g, c_s, m_mg, m_ms)
    vectors = jnp.pad(jnp.stack(vectors, axis=0), ((0, LANES - len(vectors)), (0, 0)))
    parts = (u_qkv, u_out, u_up, u_down, m_qkv, m_out, m_up, m_down, c_q, c_pair, c_out, vectors)
    packed = sds((rows, 28 * d + LANES), bf16)
    shard = call(pack_kernel, 1, parts, [whole(p) for p in parts], packed, whole(packed), vmem=60)
    enc_t = nt(order_pair, enc).astype(bf16)
    w = lax.all_gather(shard, AXES, axis=0, tiled=True)
    w, (order, enc_t) = tie(w, order, enc_t)
    vec = nt(jnp.eye(16, LANES, dtype=bf16), w[:, 28 * d :])

    net = Layers(captions, captions * length, d, w, vec, order, patch_count)

    w_pair = w[:, 25 * d : 27 * d]
    kv = nn(enc, w_pair).astype(bf16)
    x0a, f_us, k_us = net.self_forward(x0, 0, 0)
    x1, f_uf, k_uf = net.feed_forward(x0a, 4, 2)
    x1a, f_ms, k_ms = net.self_forward(x1, 12, 4)
    x1b, f_mc, k_mc = net.cross_forward(x1a, kv, 24, 6)

    def core(x):
        return place.swap(x, BIT_CORE)

    def go_on(x, sums=(), start=()):
        x = hold(x, *sums)
        for g in sums:
            g.sums()
        x = need(x, *(tuple(sums) + tuple(g for g in start if g not in sums)))
        for g in start:
            g.swap()
        return x

    def rest(x, *groups):
        for _ in range(place.outer_bits - 1):
            for g in groups:
                x = go_on(x, [g], [g])
        return x

    def pairs(x):
        return x, core(x)

    f_us, f_uf, f_ms = pairs(f_us), pairs(f_uf), pairs(f_ms)
    x1b, (f_us, f_uf, f_ms) = tie(x1b, f_us, f_uf, f_ms)
    f_mc = pairs(f_mc)
    dx, v_mf, p, f = net.feed_backward(x1b, (), out_grad.reshape(-1, d), 16, 8)
    p, f = pairs(p), pairs(f)
    x2 = net.feed_out(x1b, f[0], 16)
    p, (x2,) = tie(p, x2)
    s_mf = Sum(place, net.feed_grads(f, p))
    dx, (f_mc,) = tie(dx, f_mc)
    dx = go_on(dx, start=[s_mf])
    dx, v_mc, p_c, dkv = net.cross_backward(x1a, k_mc, kv, dx, 24, 6)
    p_c = pairs(p_c)
    pair, send = net.pair_grads(enc_t, dkv)
    dx, (send,) = tie(dx, send)
    pair = pair, core(send)
    dx, v_ms, p = net.self_backward(x1, k_ms, dx, 12, 4)
    p = pairs(p)
    dx = go_on(dx, [s_mf], [s_mf])
    dx, (p, p_c, pair) = tie(dx, p, p_c, pair)
    s_ma = Sum(place, net.attend_grads(f_ms, p, (f_mc, p_c, pair)))
    dx = go_on(dx, start=[s_ma])
    dx, v_uf, p = net.feed_backward(x0a, (k_uf,), dx, 4, 2)
    p = pairs(p)
    dx = go_on(dx, [s_ma, s_mf])
    dx, (p,) = tie(dx, p)
    s_uf = Sum(place, net.feed_grads(f_uf, p))
    dx = go_on(dx, start=[s_uf, s_ma])
    v = [g[:2] for g in (v_uf, v_ms, v_mc, v_mf)]
    v = jnp.pad(jnp.concatenate(v, axis=0), ((2, 6), (0, 0)))
    dx, _v, p = net.self_backward(x0, k_us, dx, 0, 0, (v,))
    p = pairs(p)
    dx = go_on(dx, [s_ma, s_uf])
    dx, (dkv,) = tie(dx, dkv)
    denc = nt(dkv, w_pair).astype(bf16)
    dx, (denc,) = tie(dx, denc)
    dx, (p,) = tie(dx, p)
    dx = go_on(dx, start=[s_mf, s_uf])
    dx, (p,) = tie(dx, p)
    send_a, keep_a, send_b, keep_b = net.attend_grads(f_us, p)
    v = nt(order[1], plus(p[0][4], p[1][4])[:LANES]).astype(bf16)
    send_b = jnp.concatenate((send_b, v[d // 4 :]), axis=1)
    keep_b = jnp.concatenate((keep_b, v[: d // 4]), axis=1)
    s_us = Sum(place, (send_a, keep_a, send_b, keep_b))
    dx = go_on(dx, start=[s_us])
    dx = rest(dx, s_mf)
    dx, (r_mf,) = tie(dx, s_mf.total())
    dx = go_on(dx, start=[s_ma])
    dx = rest(dx, s_ma)
    dx = go_on(dx, [s_us], [s_us])
    dx, (r_ma,) = tie(dx, s_ma.total())
    dx = go_on(dx, [s_uf], [s_uf])
    dx = go_on(dx, [s_us], [s_us])
    dx = rest(dx, s_uf, s_us)
    r_uf, r_us = s_uf.total(), s_us.total()

    def feed_rows(r):
        return unspread(r[:, : 4 * d]), r[:, 4 * d :].reshape(-1, d)

    def columns(r, *blocks):
        parts = [r[:, b * d : (b + 1) * d] for b in blocks]
        return jnp.concatenate(parts, axis=1) if len(parts) > 1 else parts[0]

    r_uup, r_udown = feed_rows(r_uf)
    r_mup, r_mdown = feed_rows(r_mf)
    vs = r_us[:, 4 * d :]
    v = [vs[:, i] for i in range(10)]
    return (
        x2.reshape(tokens.shape),
        dx.astype(bf16).reshape(tokens.shape),
        denc.reshape(encoder.shape),
        v[0], v[1], r_us[:, : 3 * d], r_us[:, 3 * d : 4 * d], v[2], v[3], r_uup, r_udown,
        v[4], v[5], columns(r_ma, 0, 1, 4), columns(r_ma, 5), v[6], v[7],
        columns(r_ma, 2), columns(r_ma, 6, 7), columns(r_ma, 3),
        v[8], v[9], r_mup, r_mdown,
    )


def solution(mesh):
    rows1 = P(AXES)
    rows2 = P(AXES, None)
    rows3 = P(AXES, None, None)
    block = (rows1, rows1, rows2, rows2)
    weights = block * 2 + block + (rows1, rows1, rows2, rows2, rows2) + block
    return jax.shard_map(
        local,
        mesh=mesh,
        in_specs=(rows3, rows3, rows1, rows3) + weights,
        out_specs=(rows3, rows3, rows3) + weights,
        check_vma=False,
    )
```

```python
import functools

import jax
import jax.numpy as jnp
from jax import lax
from jax.experimental import pallas as pl
from jax.experimental.pallas import tpu as pltpu
from jax.sharding import PartitionSpec as P

DH = 64
AXES = ("dp", "hd")
EPS = 1e-05
MASKED = -1e30
LANES = 128
bf16 = jnp.bfloat16
f32 = jnp.float32
sds = jax.ShapeDtypeStruct


BIT_PAIR, BIT_CORE, BIT_NEAR = 1, 2, 4


class Place:
    def __init__(self):
        self.count = lax.axis_size("dp") * lax.axis_size("hd")
        self.outer_size = self.count // 8
        index = lax.axis_index("dp") * lax.axis_size("hd") + lax.axis_index("hd")
        self.pair = index % 2
        self.core = (index // 2) % 2
        self.near = (index // 4) % 2
        self.outer = index // 8
        self.outer_bits = self.outer_size.bit_length() - 1

    def swap(self, x, bit):
        return lax.ppermute(x, AXES, [(i, i ^ bit) for i in range(self.count)])

    def order(self, d, near_first):
        n, rows = self.outer_size, d // self.count
        k = lax.broadcasted_iota(jnp.int32, (d, 1), 0)
        row, place = k % rows, (k // rows) % n
        outer = jnp.zeros_like(k)
        for b in range(self.outer_bits):
            outer = outer + ((place >> (self.outer_bits - 1 - b)) & 1) * (1 << b)
        outer = outer ^ self.outer
        rest = k // (rows * n)
        low, high = rest % 2, (rest // 2) % 2
        near, pair = (high, low) if near_first else (low, high)
        feature = outer * 2 + (near ^ self.near)
        feature = (feature * 2 + ((rest // 4) ^ self.core)) * 2 + (pair ^ self.pair)
        feature = feature * rows + row
        return (feature == lax.broadcasted_iota(jnp.int32, (d, d), 1)).astype(bf16)


def plus(a, b):
    return (a.astype(f32) + b.astype(f32)).astype(bf16)


class Sum:
    def __init__(self, place, grads):
        self.place, self.stage = place, 0
        send_a, keep_a, send_b, keep_b = grads
        self.send, self.kept = (send_a, send_b), (keep_a, keep_b)

    def swap(self):
        if self.stage < 2:
            bits = ((BIT_NEAR, BIT_PAIR), (BIT_PAIR, BIT_NEAR))[self.stage]
        else:
            bits = (8 << (self.stage - 2),)
        self.got = tuple(self.place.swap(x, bit) for x, bit in zip(self.send, bits))

    def sums(self):
        def part(at):
            return tuple(plus(k[at], g[at]) for k, g in zip(self.kept, self.got))

        if self.stage == 1:
            t = jnp.concatenate(part(slice(None)), axis=1)
            half = t.shape[0] // 2
            self.kept, self.send = (t[:half],), (t[half:],)
        else:
            half = self.kept[0].shape[0] // 2
            self.kept, self.send = part(slice(half)), part(slice(half, None))
        self.stage += 1

    def total(self):
        return self.kept[0].astype(f32) + self.got[0].astype(f32)


def tie(x, *others):
    out = lax.optimization_barrier((x,) + others)
    return out[0], out[1:]


def hold(x, *groups):
    x, terms = tie(x, *[(g.kept, g.got) for g in groups])
    for g, t in zip(groups, terms):
        g.kept, g.got = t
    return x


def need(x, *groups):
    x, send = tie(x, *[g.send for g in groups])
    for g, k in zip(groups, send):
        g.send = k
    return x


def nn(a, b):
    return jnp.dot(a, b, preferred_element_type=f32)


def nt(a, b):
    return lax.dot_general(a, b, (((1,), (1,)), ((), ())), preferred_element_type=f32)


def tn(a, b):
    return lax.dot_general(a, b, (((0,), (0,)), ((), ())), preferred_element_type=f32)


def unit_norm(x):
    centred = x - jnp.mean(x, axis=-1, keepdims=True)
    inv = lax.rsqrt(jnp.mean(centred * centred, axis=-1, keepdims=True) + EPS)
    return centred * inv, inv


def norm_backward(grad, x, gain):
    unit, inv = unit_norm(x)
    du = grad * gain
    dx = inv * (
        du
        - jnp.mean(du, axis=-1, keepdims=True)
        - unit * jnp.mean(du * unit, axis=-1, keepdims=True)
    )
    return dx, jnp.sum(grad * unit, axis=0, keepdims=True), jnp.sum(grad, axis=0, keepdims=True)


GELU_A = 0.7978845608028654
GELU_B = 0.044715


def two_heads(x):
    first = lax.broadcasted_iota(jnp.int32, x.shape, 1) < DH
    zero = jnp.zeros_like(x)
    return jnp.concatenate((jnp.where(first, x, zero), jnp.where(first, zero, x)), axis=0)


def side_by_side(x):
    n = x.shape[0] // 2
    first = lax.broadcasted_iota(jnp.int32, (n, LANES), 1) < DH
    return jnp.where(first, x[:n], x[n:])


def probabilities(qs, k2, allowed):
    s = jnp.where(allowed, nt(qs, k2) * DH ** (-0.5), MASKED)
    e = jnp.exp(s - jnp.max(s, axis=-1, keepdims=True))
    return e / jnp.sum(e, axis=-1, keepdims=True)


def causal_mask(length):
    row = lax.broadcasted_iota(jnp.int32, (2 * length, length), 0)
    col = lax.broadcasted_iota(jnp.int32, (2 * length, length), 1)
    return jnp.where(row >= length, row - length, row) >= col


def attend_back(q2, k2, v2, do2, allowed):
    scale = DH ** (-0.5)
    qs, dos = two_heads(q2), two_heads(do2)
    p = probabilities(qs, k2, allowed)
    dp = nt(dos, v2)
    ds = (p * (dp - jnp.sum(p * dp, axis=-1, keepdims=True))).astype(bf16)
    dq = side_by_side(nn(ds, k2)) * scale
    dk = tn(ds, qs) * scale
    dv = tn(p.astype(bf16), dos)
    return dq.astype(bf16), dk.astype(bf16), dv.astype(bf16)


def self_forward_kernel(captions, row, x_ref, vec_ref, w_ref, y_ref, f_ref, qkv_ref):
    j = pl.program_id(0)

    @pl.when(j == 0)
    def _():
        unit, _inv = unit_norm(x_ref[...].astype(f32))
        f_ref[0] = (unit * vec_ref[row : row + 1] + vec_ref[row + 1 : row + 2]).astype(bf16)

    @pl.when(j < 3)
    def _():
        qkv_ref[j] = nn(f_ref[0], w_ref[...]).astype(bf16)

    @pl.when(j == 3)
    def _():
        length = x_ref.shape[0] // captions
        allowed = causal_mask(length)
        for c in range(captions):
            at = slice(c * length, (c + 1) * length)
            for h in range(0, x_ref.shape[1], LANES):
                cols = slice(h, h + LANES)
                p = probabilities(two_heads(qkv_ref[0, at, cols]), qkv_ref[1, at, cols], allowed)
                o = side_by_side(nn(p.astype(bf16), qkv_ref[2, at, cols]))
                f_ref[1, at, cols] = o.astype(bf16)
        y_ref[...] = x_ref[...].astype(f32) + nn(f_ref[1], w_ref[...])


def self_backward_kernel(
    captions, row, x_ref, vec_ref, qkv_ref, dx_ref, w_ref, *refs
):
    out_ref, vg_ref, p_ref, acc_ref = refs[-4:]
    j = pl.program_id(0)

    @pl.when(j == 0)
    def _():
        dy = dx_ref[...].astype(bf16)
        p_ref[3] = dy
        do = nt(dy, w_ref[...]).astype(bf16)
        length = x_ref.shape[0] // captions
        allowed = causal_mask(length)
        for c in range(captions):
            at = slice(c * length, (c + 1) * length)
            for h in range(0, x_ref.shape[1], LANES):
                cols = slice(h, h + LANES)
                dq, dk, dv = attend_back(
                    qkv_ref[0, at, cols], qkv_ref[1, at, cols], qkv_ref[2, at, cols],
                    do[at, cols], allowed,
                )
                p_ref[0, at, cols] = dq
                p_ref[1, at, cols] = dk
                p_ref[2, at, cols] = dv
        acc_ref[...] = jnp.zeros_like(acc_ref)

    @pl.when(j > 0)
    def _():
        acc_ref[...] += nt(p_ref[j - 1], w_ref[...])

    @pl.when(j == 3)
    def _():
        dn, gg, gs = norm_backward(acc_ref[...], x_ref[...].astype(f32), vec_ref[row : row + 1])
        out_ref[...] = dx_ref[...] + dn
        vg_ref[0:1] = gg
        vg_ref[1:2] = gs
        if len(refs) > 4:
            at = lax.broadcasted_iota(jnp.int32, refs[0].shape, 0)
            rows = jnp.where(at == 0, gg, jnp.where(at == 1, gs, refs[0][...]))
            p_ref[4] = jnp.zeros_like(p_ref[4])
            p_ref[4, 0 : refs[0].shape[0]] = rows.astype(bf16)


def cross_forward_kernel(
    captions, row, count_ref, x_ref, vec_ref, kv_ref, w_ref, y_ref, f_ref, q_ref
):
    j = pl.program_id(0)
    d = x_ref.shape[1]

    @pl.when(j == 0)
    def _():
        unit, _inv = unit_norm(x_ref[...])
        c = (unit * vec_ref[row : row + 1] + vec_ref[row + 1 : row + 2]).astype(bf16)
        f_ref[0] = c
        q_ref[...] = nn(c, w_ref[...]).astype(bf16)

    @pl.when(j == 1)
    def _():
        length = x_ref.shape[0] // captions
        patches = kv_ref.shape[0] // captions
        slot = lax.broadcasted_iota(jnp.int32, (2 * length, patches), 1)
        for c in range(captions):
            at = slice(c * length, (c + 1) * length)
            keys = slice(c * patches, (c + 1) * patches)
            allowed = slot < count_ref[c]
            for h in range(0, d, LANES):
                cols = slice(h, h + LANES)
                vcols = slice(d + h, d + h + LANES)
                p = probabilities(two_heads(q_ref[at, cols]), kv_ref[keys, cols], allowed)
                o = side_by_side(nn(p.astype(bf16), kv_ref[keys, vcols]))
                f_ref[1, at, cols] = o.astype(bf16)
        y_ref[...] = x_ref[...] + nn(f_ref[1], w_ref[...])


def cross_backward_kernel(
    captions, row, count_ref, x_ref, vec_ref, q_ref, kv_ref, dx_ref, w_ref,
    out_ref, vg_ref, p_ref, dkv_ref,
):
    j = pl.program_id(0)
    d = x_ref.shape[1]

    @pl.when(j == 0)
    def _():
        dy = dx_ref[...].astype(bf16)
        p_ref[1] = dy
        do = nt(dy, w_ref[...]).astype(bf16)
        length = x_ref.shape[0] // captions
        patches = kv_ref.shape[0] // captions
        slot = lax.broadcasted_iota(jnp.int32, (2 * length, patches), 1)
        for c in range(captions):
            at = slice(c * length, (c + 1) * length)
            keys = slice(c * patches, (c + 1) * patches)
            allowed = slot < count_ref[c]
            for h in range(0, d, LANES):
                cols = slice(h, h + LANES)
                vcols = slice(d + h, d + h + LANES)
                dq, dk, dv = attend_back(
                    q_ref[at, cols], kv_ref[keys, cols], kv_ref[keys, vcols], do[at, cols], allowed
                )
                p_ref[0, at, cols] = dq
                dkv_ref[keys, cols] = dk
                dkv_ref[keys, vcols] = dv

    @pl.when(j == 1)
    def _():
        dn, gg, gs = norm_backward(nt(p_ref[0], w_ref[...]), x_ref[...], vec_ref[row : row + 1])
        out_ref[...] = dx_ref[...] + dn
        vg_ref[0:1] = gg
        vg_ref[1:2] = gs


def feed_forward_kernel(row, x_ref, vec_ref, up_ref, down_ref, y_ref, f_ref, u_ref):
    j = pl.program_id(0)

    @pl.when(j == 0)
    def _():
        unit, _inv = unit_norm(x_ref[...])
        f_ref[0] = (unit * vec_ref[row : row + 1] + vec_ref[row + 1 : row + 2]).astype(bf16)
        y_ref[...] = x_ref[...]

    u = nn(f_ref[0], up_ref[...])
    u_ref[...] = u
    g = (0.5 * u * (1.0 + jnp.tanh(GELU_A * (u + GELU_B * u * u * u)))).astype(bf16)
    f_ref[1 + j] = g
    y_ref[...] += nn(g, down_ref[...])


def feed_backward_kernel(row, kept, x_ref, vec_ref, dx_ref, up_ref, down_ref, *refs):
    out_ref, vg_ref, p_ref = refs[1:4] if kept else refs[:3]
    acc_ref = refs[-1]
    j = pl.program_id(0)

    @pl.when(j == 0)
    def _():
        if not kept:
            unit, _inv = unit_norm(x_ref[...])
            refs[3][0] = (unit * vec_ref[row : row + 1] + vec_ref[row + 1 : row + 2]).astype(bf16)
        p_ref[0] = dx_ref[...].astype(bf16)
        acc_ref[...] = jnp.zeros_like(acc_ref)

    u = refs[0][...] if kept else nn(refs[3][0], up_ref[...])
    t = jnp.tanh(GELU_A * (u + GELU_B * u * u * u))
    if not kept:
        refs[3][1 + j] = (0.5 * u * (1.0 + t)).astype(bf16)
    slope = 0.5 * (1.0 + t) + 0.5 * u * (1.0 - t * t) * GELU_A * (1.0 + 3.0 * GELU_B * u * u)
    du = (slope * nt(p_ref[0], down_ref[...])).astype(bf16)
    p_ref[1 + j] = du
    acc_ref[...] += nt(du, up_ref[...])

    @pl.when(j == 3)
    def _():
        dn, gg, gs = norm_backward(acc_ref[...], x_ref[...], vec_ref[row : row + 1])
        out_ref[...] = dx_ref[...].astype(f32) + dn
        vg_ref[0:1] = gg
        vg_ref[1:2] = gs


def feed_out_kernel(x_ref, g_ref, down_ref, y_ref, acc_ref):
    j = pl.program_id(0)

    @pl.when(j == 0)
    def _():
        acc_ref[...] = x_ref[...]

    acc_ref[...] += nn(g_ref[0], down_ref[...])

    @pl.when(j == 3)
    def _():
        y_ref[...] = acc_ref[...].astype(bf16)


def both(own_ref, got_ref):
    return jnp.concatenate((own_ref[0], got_ref[0]), axis=0)


def emit(g, send_ref, keep_ref):
    half = keep_ref.shape[0]
    keep_ref[...] = g[:half].astype(bf16)
    send_ref[...] = g[half:].astype(bf16)


def feed_grads_kernel(
    order_ref, b_ref, b2_ref, z_ref, z2_ref, g_ref, g2_ref, u_ref, u2_ref,
    send_a_ref, keep_a_ref, send_b_ref, keep_b_ref, bt_ref,
):
    @pl.when(pl.program_id(0) == 0)
    def _():
        bt_ref[...] = nt(order_ref[0], both(b_ref, b2_ref)).astype(bf16)

    emit(nn(bt_ref[...], both(u_ref, u2_ref)), send_a_ref, keep_a_ref)
    gt = nt(order_ref[1], both(g_ref, g2_ref)).astype(bf16)
    emit(nn(gt, both(z_ref, z2_ref)), send_b_ref, keep_b_ref)


def attend_grads_kernel(
    order_ref, s_ref, s2_ref, sd_ref, sd2_ref, *refs
):
    send_a_ref, keep_a_ref, send_b_ref, keep_b_ref = refs[-4:]
    j = pl.program_id(0)

    def product(a_ref, a2_ref, d_ref, d2_ref):
        at = nt(order_ref[0], both(a_ref, a2_ref)).astype(bf16)
        return nn(at, both(d_ref, d2_ref))

    @pl.when(j < 2)
    def _():
        emit(product(s_ref, s2_ref, sd_ref, sd2_ref), send_a_ref, keep_a_ref)

    @pl.when((j == 2) | (j == 3))
    def _():
        emit(product(s_ref, s2_ref, sd_ref, sd2_ref), send_b_ref, keep_b_ref)

    if len(refs) > 4:
        c_ref, c2_ref, cd_ref, cd2_ref, pair_ref, pair2_ref = refs[:6]

        @pl.when((j == 4) | (j == 5))
        def _():
            emit(product(c_ref, c2_ref, cd_ref, cd2_ref), send_a_ref, keep_a_ref)

        @pl.when(j > 5)
        def _():
            emit(pair_ref[...].astype(f32) + pair2_ref[...].astype(f32), send_b_ref, keep_b_ref)


def pair_grads_kernel(enc_ref, dkv_ref, keep_ref, send_ref):
    emit(nn(enc_ref[...], dkv_ref[...]), send_ref, keep_ref)


def pack_kernel(u_qkv, u_out, u_up, u_down, m_qkv, m_out, m_up, m_down, c_q, c_pair, c_out, vec, out):
    rows, d = u_out.shape
    spread = spread_matrix().astype(bf16)
    i = lax.broadcasted_iota(jnp.int32, (rows, 4 * rows), 0)
    k = lax.broadcasted_iota(jnp.int32, (rows, 4 * rows), 1)

    def layer(at, qkv, w_out, up, down):
        out[:, at : at + 3 * d] = qkv[...]
        out[:, at + 3 * d : at + 4 * d] = w_out[...]
        for b in range(4 * d // 512):
            y = nn(up[:, b * 512 : (b + 1) * 512], spread).astype(bf16)
            for j in range(4):
                to = at + (4 + j) * d + b * LANES
                out[:, to : to + LANES] = y[:, j * LANES : (j + 1) * LANES]
        for j in range(4):
            y = nn((k == 4 * i + j).astype(bf16), down[...])
            out[:, at + (8 + j) * d : at + (9 + j) * d] = y.astype(bf16)

    layer(0, u_qkv, u_out, u_up, u_down)
    layer(12 * d, m_qkv, m_out, m_up, m_down)
    out[:, 24 * d : 25 * d] = c_q[...]
    out[:, 25 * d : 27 * d] = c_pair[...]
    out[:, 27 * d : 28 * d] = c_out[...]
    eye = lax.broadcasted_iota(jnp.int32, (rows, rows), 0) == lax.broadcasted_iota(jnp.int32, (rows, rows), 1)
    out[:, 28 * d :] = nt(eye.astype(bf16), vec[...]).astype(bf16)


def whole(x):
    return pl.BlockSpec(x.shape, lambda *_: (0,) * len(x.shape))


def call(kernel, steps, ins, in_specs, outs, out_specs, scratch=(), scalars=0, vmem=40):
    return pl.pallas_call(
        kernel,
        out_shape=outs,
        grid_spec=pltpu.PrefetchScalarGridSpec(
            num_scalar_prefetch=scalars,
            grid=(steps,),
            in_specs=in_specs,
            out_specs=out_specs,
            scratch_shapes=scratch,
        ),
        compiler_params=pltpu.CompilerParams(
            dimension_semantics=("arbitrary",), vmem_limit_bytes=vmem << 20
        ),
        cost_estimate=pl.CostEstimate(flops=1000, bytes_accessed=1000, transcendentals=0),
    )(*ins)


class Layers:
    def __init__(self, captions, tokens, d, w, vec, order, count):
        self.captions, self.t, self.d = captions, tokens, d
        self.w, self.vec, self.order, self.count = w, vec, order, count
        self.xs = sds((tokens, d), f32)
        self.hs = sds((tokens, d), bf16)

    def weight(self, index):
        return pl.BlockSpec((self.d, self.d), lambda j, *_: (0, index(j)))

    def self_forward(self, x, at, row):
        outs = (self.xs, sds((2, self.t, self.d), bf16), sds((3, self.t, self.d), bf16))
        return call(
            functools.partial(self_forward_kernel, self.captions, row), 4,
            (x, self.vec, self.w),
            [whole(x), whole(self.vec), self.weight(lambda j: at + j)],
            outs, [whole(o) for o in outs],
        )

    def self_backward(self, x, kept, dx, at, row, vectors=()):
        d, t = self.d, self.t
        outs = (self.xs, sds((8, d), f32), sds((4 + len(vectors), t, d), bf16))
        ins = (x, self.vec, kept, dx)
        return call(
            functools.partial(self_backward_kernel, self.captions, row), 4,
            ins + (self.w,) + vectors,
            [whole(i) for i in ins] + [self.weight(lambda j: at + (j + 3) % 4)]
            + [whole(v) for v in vectors],
            outs, [whole(i) for i in outs],
            scratch=[pltpu.VMEM((t, d), f32)],
        )

    def cross_forward(self, x, kv, at, row):
        outs = (self.xs, sds((2, self.t, self.d), bf16), self.hs)
        return call(
            functools.partial(cross_forward_kernel, self.captions, row), 2,
            (self.count, x, self.vec, kv, self.w),
            [whole(x), whole(self.vec), whole(kv), self.weight(lambda j: at + 3 * j)],
            outs, [whole(o) for o in outs], scalars=1,
        )

    def cross_backward(self, x, kept, kv, dx, at, row):
        d, t = self.d, self.t
        outs = (self.xs, sds((8, d), f32), sds((2, t, d), bf16), sds(kv.shape, bf16))
        ins = (x, self.vec, kept, kv, dx)
        return call(
            functools.partial(cross_backward_kernel, self.captions, row), 2,
            (self.count,) + ins + (self.w,),
            [whole(i) for i in ins] + [self.weight(lambda j: at + 3 - 3 * j)],
            outs, [whole(i) for i in outs], scalars=1,
        )

    def pair_grads(self, enc_t, dkv):
        d = self.d
        outs = (sds((d // 2, 2 * d), bf16),) * 2
        grad = pl.BlockSpec((d // 2, d), lambda j: (0, j))
        return call(
            pair_grads_kernel, 2, (enc_t, dkv),
            [whole(enc_t), pl.BlockSpec((dkv.shape[0], d), lambda j: (0, j))],
            outs, [grad, grad],
        )

    def block(self, index):
        return pl.BlockSpec((1, self.t, self.d), lambda j: (index(j), 0, 0))

    def feed_grads(self, f, p):
        d, t = self.d, self.t
        outs = (sds((d // 4, 4 * d), bf16),) * 4
        first, later = self.block(lambda j: 0), self.block(lambda j: 1 + j)
        return call(
            feed_grads_kernel, 4, (self.order,) + f + p + f + p,
            [whole(self.order)] + [first] * 4 + [later] * 4,
            outs, [pl.BlockSpec((d // 4, d), lambda j: (0, j))] * 4,
            scratch=[pltpu.VMEM((d // 2, 2 * t), bf16)],
        )

    def attend_grads(self, f, p, cross=()):
        d, t = self.d, self.t
        steps = 8 if cross else 4
        outs = (sds((d // 4, steps // 2 * d), bf16),) * 4

        def first(j):
            return jnp.where(j < 4, jnp.minimum(j, 1), jnp.minimum(j - 2, 3))

        def second(j):
            return jnp.where(j < 6, jnp.clip(j - 2, 0, 1), j - 4)

        grad_a = pl.BlockSpec((d // 4, d), lambda j: (0, first(j)))
        grad_b = pl.BlockSpec((d // 4, d), lambda j: (0, second(j)))
        order = pl.BlockSpec(
            (1, d // 2, d), lambda j: (jnp.where((j == 2) | (j == 3), 1, 0), 0, 0)
        )
        lhs = self.block(lambda j: jnp.minimum(j // 3, 1))
        rhs = self.block(lambda j: jnp.minimum(j, 3))
        ins, specs = (self.order,) + f + p, [order, lhs, lhs, rhs, rhs]
        if cross:
            f, p, pair = cross
            lhs = self.block(lambda j: jnp.clip(j - 4, 0, 1))
            rhs = lhs
            half = pl.BlockSpec((d // 2, d), lambda j: (0, jnp.clip(j - 6, 0, 1)))
            ins = ins + f + p + pair
            specs = specs + [lhs, lhs, rhs, rhs, half, half]
        return call(
            attend_grads_kernel, steps, ins, specs, outs, [grad_a, grad_a, grad_b, grad_b]
        )

    def feed_forward(self, x, at, row):
        d, t = self.d, self.t
        outs = (self.xs, sds((5, t, d), bf16), sds((t, 4 * d), f32))
        return call(
            functools.partial(feed_forward_kernel, row), 4,
            (x, self.vec, self.w, self.w),
            [whole(x), whole(self.vec), self.weight(lambda j: at + j), self.weight(lambda j: at + 4 + j)],
            outs, [whole(outs[0]), whole(outs[1]), pl.BlockSpec((t, d), lambda j: (0, j))],
        )

    def feed_backward(self, x, kept, dx, at, row):
        d, t = self.d, self.t
        outs = (self.xs, sds((8, d), f32), sds((5, t, d), bf16))
        if not kept:
            outs = outs + (sds((5, t, d), bf16),)
        return call(
            functools.partial(feed_backward_kernel, row, bool(kept)), 4,
            (x, self.vec, dx, self.w, self.w) + kept,
            [
                whole(x), whole(self.vec), whole(dx),
                self.weight(lambda j: at + j), self.weight(lambda j: at + 4 + j),
            ] + [pl.BlockSpec((t, d), lambda j: (0, j)) for _ in kept],
            outs, [whole(i) for i in outs],
            scratch=[pltpu.VMEM((t, d), f32)],
        )

    def feed_out(self, x, p, at):
        return call(
            feed_out_kernel, 4, (x, p, self.w),
            [whole(x), self.block(lambda j: 1 + j), self.weight(lambda j: at + 4 + j)],
            self.hs, whole(self.hs), scratch=[pltpu.VMEM((self.t, self.d), f32)],
        )


def spread_matrix():
    k = lax.broadcasted_iota(jnp.int32, (512, 512), 0)
    n = lax.broadcasted_iota(jnp.int32, (512, 512), 1)
    return (k % 4) * 128 + k // 4 == n


def unspread(up):
    rows, wide = up.shape
    y = up.reshape(rows, 4, wide // 512, 128).transpose(0, 2, 1, 3)
    y = lax.dot_general(
        y.reshape(rows * (wide // 512), 512), spread_matrix().astype(f32),
        (((1,), (1,)), ((), ())), precision=lax.Precision.HIGHEST,
    )
    return y.reshape(rows, wide)


def local(
    tokens, encoder, patch_count, out_grad,
    u_ag, u_as, u_qkv, u_out, u_mg, u_ms, u_up, u_down,
    m_ag, m_as, m_qkv, m_out, c_g, c_s, c_q, c_pair, c_out, m_mg, m_ms, m_up, m_down,
):
    place = Place()
    captions, length, d = tokens.shape
    rows = u_qkv.shape[0]
    x0 = tokens.reshape(-1, d)
    enc = encoder.reshape(-1, d)
    order = jnp.stack((place.order(d, True), place.order(d, False)))
    order_pair = order[1]
    order = order[:, : d // 2]

    vectors = (u_ag, u_as, u_mg, u_ms, m_ag, m_as, c_g, c_s, m_mg, m_ms)
    vectors = jnp.pad(jnp.stack(vectors, axis=0), ((0, LANES - len(vectors)), (0, 0)))
    parts = (u_qkv, u_out, u_up, u_down, m_qkv, m_out, m_up, m_down, c_q, c_pair, c_out, vectors)
    packed = sds((rows, 28 * d + LANES), bf16)
    shard = call(pack_kernel, 1, parts, [whole(p) for p in parts], packed, whole(packed), vmem=60)
    enc_t = nt(order_pair, enc).astype(bf16)
    w = lax.all_gather(shard, AXES, axis=0, tiled=True)
    w, (order, enc_t) = tie(w, order, enc_t)
    vec = nt(jnp.eye(16, LANES, dtype=bf16), w[:, 28 * d :])

    net = Layers(captions, captions * length, d, w, vec, order, patch_count)

    w_pair = w[:, 25 * d : 27 * d]
    kv = nn(enc, w_pair).astype(bf16)
    x0a, f_us, k_us = net.self_forward(x0, 0, 0)
    x1, f_uf, k_uf = net.feed_forward(x0a, 4, 2)
    x1a, f_ms, k_ms = net.self_forward(x1, 12, 4)
    x1b, f_mc, k_mc = net.cross_forward(x1a, kv, 24, 6)

    def core(x):
        return place.swap(x, BIT_CORE)

    def go_on(x, sums=(), start=()):
        x = hold(x, *sums)
        for g in sums:
            g.sums()
        x = need(x, *(tuple(sums) + tuple(g for g in start if g not in sums)))
        for g in start:
            g.swap()
        return x

    def rest(x, *groups):
        for _ in range(place.outer_bits - 1):
            for g in groups:
                x = go_on(x, [g], [g])
        return x

    def pairs(x):
        return x, core(x)

    f_us, f_uf, f_ms = pairs(f_us), pairs(f_uf), pairs(f_ms)
    x1b, (f_us, f_uf, f_ms) = tie(x1b, f_us, f_uf, f_ms)
    f_mc = pairs(f_mc)
    dx, v_mf, p, f = net.feed_backward(x1b, (), out_grad.reshape(-1, d), 16, 8)
    p, f = pairs(p), pairs(f)
    x2 = net.feed_out(x1b, f[0], 16)
    p, (x2,) = tie(p, x2)
    s_mf = Sum(place, net.feed_grads(f, p))
    dx, (f_mc,) = tie(dx, f_mc)
    dx = go_on(dx, start=[s_mf])
    dx, v_mc, p_c, dkv = net.cross_backward(x1a, k_mc, kv, dx, 24, 6)
    p_c = pairs(p_c)
    pair, send = net.pair_grads(enc_t, dkv)
    dx, (send,) = tie(dx, send)
    pair = pair, core(send)
    dx, v_ms, p = net.self_backward(x1, k_ms, dx, 12, 4)
    p = pairs(p)
    dx = go_on(dx, [s_mf], [s_mf])
    dx, (p, p_c, pair) = tie(dx, p, p_c, pair)
    s_ma = Sum(place, net.attend_grads(f_ms, p, (f_mc, p_c, pair)))
    dx = go_on(dx, start=[s_ma])
    dx, v_uf, p = net.feed_backward(x0a, (k_uf,), dx, 4, 2)
    p = pairs(p)
    dx = go_on(dx, [s_ma], [s_ma])
    dx, (p,) = tie(dx, p)
    s_uf = Sum(place, net.feed_grads(f_uf, p))
    dx = need(dx, s_uf)
    dx = go_on(dx, [s_mf], [s_uf])
    v = [g[:2] for g in (v_uf, v_ms, v_mc, v_mf)]
    v = jnp.pad(jnp.concatenate(v, axis=0), ((2, 6), (0, 0)))
    dx, _v, p = net.self_backward(x0, k_us, dx, 0, 0, (v,))
    p = pairs(p)
    dx = go_on(dx, [s_ma], [s_mf])
    dx, (dkv,) = tie(dx, dkv)
    denc = nt(dkv, w_pair).astype(bf16)
    dx, (p, denc) = tie(dx, p, denc)
    send_a, keep_a, send_b, keep_b = net.attend_grads(f_us, p)
    v = nt(order[1], plus(p[0][4], p[1][4])[:LANES]).astype(bf16)
    send_b = jnp.concatenate((send_b, v[d // 4 :]), axis=1)
    keep_b = jnp.concatenate((keep_b, v[: d // 4]), axis=1)
    s_us = Sum(place, (send_a, keep_a, send_b, keep_b))
    dx = go_on(dx, start=[s_us])
    dx = rest(dx, s_mf)
    dx = go_on(dx, [s_uf], [s_uf])
    dx, (r_mf,) = tie(dx, s_mf.total())
    dx = go_on(dx, start=[s_ma])
    dx = go_on(dx, [s_us], [s_us])
    dx = rest(dx, s_ma)
    dx = go_on(dx, [s_uf], [s_uf])
    dx, (r_ma,) = tie(dx, s_ma.total())
    dx = go_on(dx, [s_us], [s_us])
    dx = rest(dx, s_uf, s_us)
    r_uf, r_us = s_uf.total(), s_us.total()

    def feed_rows(r):
        return unspread(r[:, : 4 * d]), r[:, 4 * d :].reshape(-1, d)

    def columns(r, *blocks):
        parts = [r[:, b * d : (b + 1) * d] for b in blocks]
        return jnp.concatenate(parts, axis=1) if len(parts) > 1 else parts[0]

    r_uup, r_udown = feed_rows(r_uf)
    r_mup, r_mdown = feed_rows(r_mf)
    vs = r_us[:, 4 * d :]
    v = [vs[:, i] for i in range(10)]
    return (
        x2.reshape(tokens.shape),
        dx.astype(bf16).reshape(tokens.shape),
        denc.reshape(encoder.shape),
        v[0], v[1], r_us[:, : 3 * d], r_us[:, 3 * d : 4 * d], v[2], v[3], r_uup, r_udown,
        v[4], v[5], columns(r_ma, 0, 1, 4), columns(r_ma, 5), v[6], v[7],
        columns(r_ma, 2), columns(r_ma, 6, 7), columns(r_ma, 3),
        v[8], v[9], r_mup, r_mdown,
    )


def solution(mesh):
    rows1 = P(AXES)
    rows2 = P(AXES, None)
    rows3 = P(AXES, None, None)
    block = (rows1, rows1, rows2, rows2)
    weights = block * 2 + block + (rows1, rows1, rows2, rows2, rows2) + block
    return jax.shard_map(
        local,
        mesh=mesh,
        in_specs=(rows3, rows3, rows1, rows3) + weights,
        out_specs=(rows3, rows3, rows3) + weights,
        check_vma=False,
    )
```

```python
import functools

import jax
import jax.numpy as jnp
from jax import lax
from jax.experimental import pallas as pl
from jax.experimental.pallas import tpu as pltpu
from jax.sharding import PartitionSpec as P

DH = 64
AXES = ("dp", "hd")
EPS = 1e-05
MASKED = -1e30
LANES = 128
bf16 = jnp.bfloat16
f32 = jnp.float32
sds = jax.ShapeDtypeStruct


BIT_PAIR, BIT_CORE, BIT_NEAR = 1, 2, 4


class Place:
    def __init__(self):
        self.count = lax.axis_size("dp") * lax.axis_size("hd")
        self.outer_size = self.count // 8
        index = lax.axis_index("dp") * lax.axis_size("hd") + lax.axis_index("hd")
        self.pair = index % 2
        self.core = (index // 2) % 2
        self.near = (index // 4) % 2
        self.outer = index // 8
        self.outer_bits = self.outer_size.bit_length() - 1

    def swap(self, x, bit):
        return lax.ppermute(x, AXES, [(i, i ^ bit) for i in range(self.count)])

    def order(self, d, near_first):
        n, rows = self.outer_size, d // self.count
        k = lax.broadcasted_iota(jnp.int32, (d, 1), 0)
        row, place = k % rows, (k // rows) % n
        outer = jnp.zeros_like(k)
        for b in range(self.outer_bits):
            outer = outer + ((place >> (self.outer_bits - 1 - b)) & 1) * (1 << b)
        outer = outer ^ self.outer
        rest = k // (rows * n)
        low, high = rest % 2, (rest // 2) % 2
        near, pair = (high, low) if near_first else (low, high)
        feature = outer * 2 + (near ^ self.near)
        feature = (feature * 2 + ((rest // 4) ^ self.core)) * 2 + (pair ^ self.pair)
        feature = feature * rows + row
        return (feature == lax.broadcasted_iota(jnp.int32, (d, d), 1)).astype(bf16)


def plus(a, b):
    return (a.astype(f32) + b.astype(f32)).astype(bf16)


class Sum:
    def __init__(self, place, grads):
        self.place, self.stage = place, 0
        send_a, keep_a, send_b, keep_b = grads
        self.send, self.kept = (send_a, send_b), (keep_a, keep_b)

    def swap(self):
        if self.stage < 2:
            bits = ((BIT_NEAR, BIT_PAIR), (BIT_PAIR, BIT_NEAR))[self.stage]
        else:
            bits = (8 << (self.stage - 2),)
        self.got = tuple(self.place.swap(x, bit) for x, bit in zip(self.send, bits))

    def sums(self):
        def part(at):
            return tuple(plus(k[at], g[at]) for k, g in zip(self.kept, self.got))

        if self.stage == 1:
            t = jnp.concatenate(part(slice(None)), axis=1)
            half = t.shape[0] // 2
            self.kept, self.send = (t[:half],), (t[half:],)
        else:
            half = self.kept[0].shape[0] // 2
            self.kept, self.send = part(slice(half)), part(slice(half, None))
        self.stage += 1

    def total(self):
        return self.kept[0].astype(f32) + self.got[0].astype(f32)


class Gather:
    def __init__(self, place, shard):
        self.place, self.x, self.stage = place, (shard,), 0

    def swap(self):
        outer = self.place.outer_bits
        at = self.stage - outer
        if at < 0:
            bits = (8 << (outer - 1 - self.stage),)
        else:
            bits = ((BIT_PAIR, BIT_NEAR), (BIT_NEAR, BIT_PAIR), (BIT_CORE,) * 2)[at]
        self.got = tuple(self.place.swap(x, bit) for x, bit in zip(self.x, bits))

    def join(self):
        self.stage += 1
        terms = list(zip(self.x, self.got))
        if self.stage == self.place.outer_bits:
            (x, got), half = terms[0], self.x[0].shape[1] // 2
            terms = [(x[:, :half], got[:, :half]), (x[:, half:], got[:, half:])]
        self.x = tuple(jnp.concatenate(t, axis=0) for t in terms)

    def halves(self):
        return self.x[0], self.got[0], self.x[1], self.got[1]


def tie(x, *others):
    out = lax.optimization_barrier((x,) + others)
    return out[0], out[1:]


def hold(x, *groups):
    x, terms = tie(x, *[(g.kept, g.got) for g in groups])
    for g, t in zip(groups, terms):
        g.kept, g.got = t
    return x


def need(x, *groups):
    x, send = tie(x, *[g.send for g in groups])
    for g, k in zip(groups, send):
        g.send = k
    return x


def nn(a, b):
    return jnp.dot(a, b, preferred_element_type=f32)


def nt(a, b):
    return lax.dot_general(a, b, (((1,), (1,)), ((), ())), preferred_element_type=f32)


def tn(a, b):
    return lax.dot_general(a, b, (((0,), (0,)), ((), ())), preferred_element_type=f32)


def unit_norm(x):
    centred = x - jnp.mean(x, axis=-1, keepdims=True)
    inv = lax.rsqrt(jnp.mean(centred * centred, axis=-1, keepdims=True) + EPS)
    return centred * inv, inv


def norm_backward(grad, x, gain):
    unit, inv = unit_norm(x)
    du = grad * gain
    dx = inv * (
        du
        - jnp.mean(du, axis=-1, keepdims=True)
        - unit * jnp.mean(du * unit, axis=-1, keepdims=True)
    )
    return dx, jnp.sum(grad * unit, axis=0, keepdims=True), jnp.sum(grad, axis=0, keepdims=True)


GELU_A = 0.7978845608028654
GELU_B = 0.044715


def two_heads(x):
    first = lax.broadcasted_iota(jnp.int32, x.shape, 1) < DH
    zero = jnp.zeros_like(x)
    return jnp.concatenate((jnp.where(first, x, zero), jnp.where(first, zero, x)), axis=0)


def side_by_side(x):
    n = x.shape[0] // 2
    first = lax.broadcasted_iota(jnp.int32, (n, LANES), 1) < DH
    return jnp.where(first, x[:n], x[n:])


def probabilities(qs, k2, allowed):
    s = jnp.where(allowed, nt(qs, k2) * DH ** (-0.5), MASKED)
    e = jnp.exp(s - jnp.max(s, axis=-1, keepdims=True))
    return e / jnp.sum(e, axis=-1, keepdims=True)


def causal_mask(length):
    row = lax.broadcasted_iota(jnp.int32, (2 * length, length), 0)
    col = lax.broadcasted_iota(jnp.int32, (2 * length, length), 1)
    return jnp.where(row >= length, row - length, row) >= col


def attend_back(q2, k2, v2, do2, allowed):
    scale = DH ** (-0.5)
    qs, dos = two_heads(q2), two_heads(do2)
    p = probabilities(qs, k2, allowed)
    dp = nt(dos, v2)
    ds = (p * (dp - jnp.sum(p * dp, axis=-1, keepdims=True))).astype(bf16)
    dq = side_by_side(nn(ds, k2)) * scale
    dk = tn(ds, qs) * scale
    dv = tn(p.astype(bf16), dos)
    return dq.astype(bf16), dk.astype(bf16), dv.astype(bf16)


def self_forward_kernel(captions, row, x_ref, vec_ref, w_ref, y_ref, f_ref, qkv_ref):
    j = pl.program_id(0)

    @pl.when(j == 0)
    def _():
        unit, _inv = unit_norm(x_ref[...].astype(f32))
        f_ref[0] = (unit * vec_ref[row : row + 1] + vec_ref[row + 1 : row + 2]).astype(bf16)

    @pl.when(j < 3)
    def _():
        qkv_ref[j] = nn(f_ref[0], w_ref[...]).astype(bf16)

    @pl.when(j == 3)
    def _():
        length = x_ref.shape[0] // captions
        allowed = causal_mask(length)
        for c in range(captions):
            at = slice(c * length, (c + 1) * length)
            for h in range(0, x_ref.shape[1], LANES):
                cols = slice(h, h + LANES)
                p = probabilities(two_heads(qkv_ref[0, at, cols]), qkv_ref[1, at, cols], allowed)
                o = side_by_side(nn(p.astype(bf16), qkv_ref[2, at, cols]))
                f_ref[1, at, cols] = o.astype(bf16)
        y_ref[...] = x_ref[...].astype(f32) + nn(f_ref[1], w_ref[...])


def self_backward_kernel(
    captions, row, x_ref, vec_ref, qkv_ref, dx_ref, w_ref, *refs
):
    out_ref, vg_ref, p_ref, acc_ref = refs[-4:]
    j = pl.program_id(0)

    @pl.when(j == 0)
    def _():
        dy = dx_ref[...].astype(bf16)
        p_ref[3] = dy
        do = nt(dy, w_ref[...]).astype(bf16)
        length = x_ref.shape[0] // captions
        allowed = causal_mask(length)
        for c in range(captions):
            at = slice(c * length, (c + 1) * length)
            for h in range(0, x_ref.shape[1], LANES):
                cols = slice(h, h + LANES)
                dq, dk, dv = attend_back(
                    qkv_ref[0, at, cols], qkv_ref[1, at, cols], qkv_ref[2, at, cols],
                    do[at, cols], allowed,
                )
                p_ref[0, at, cols] = dq
                p_ref[1, at, cols] = dk
                p_ref[2, at, cols] = dv
        acc_ref[...] = jnp.zeros_like(acc_ref)

    @pl.when(j > 0)
    def _():
        acc_ref[...] += nt(p_ref[j - 1], w_ref[...])

    @pl.when(j == 3)
    def _():
        dn, gg, gs = norm_backward(acc_ref[...], x_ref[...].astype(f32), vec_ref[row : row + 1])
        out_ref[...] = dx_ref[...] + dn
        vg_ref[0:1] = gg
        vg_ref[1:2] = gs
        if len(refs) > 4:
            at = lax.broadcasted_iota(jnp.int32, refs[0].shape, 0)
            rows = jnp.where(at == 0, gg, jnp.where(at == 1, gs, refs[0][...]))
            p_ref[4] = jnp.zeros_like(p_ref[4])
            p_ref[4, 0 : refs[0].shape[0]] = rows.astype(bf16)


def cross_forward_kernel(
    captions, row, count_ref, x_ref, vec_ref, kv_ref, w_ref, y_ref, f_ref, q_ref
):
    j = pl.program_id(0)
    d = x_ref.shape[1]

    @pl.when(j == 0)
    def _():
        unit, _inv = unit_norm(x_ref[...])
        c = (unit * vec_ref[row : row + 1] + vec_ref[row + 1 : row + 2]).astype(bf16)
        f_ref[0] = c
        q_ref[...] = nn(c, w_ref[...]).astype(bf16)

    @pl.when(j == 1)
    def _():
        length = x_ref.shape[0] // captions
        patches = kv_ref.shape[0] // captions
        slot = lax.broadcasted_iota(jnp.int32, (2 * length, patches), 1)
        for c in range(captions):
            at = slice(c * length, (c + 1) * length)
            keys = slice(c * patches, (c + 1) * patches)
            allowed = slot < count_ref[c]
            for h in range(0, d, LANES):
                cols = slice(h, h + LANES)
                vcols = slice(d + h, d + h + LANES)
                p = probabilities(two_heads(q_ref[at, cols]), kv_ref[keys, cols], allowed)
                o = side_by_side(nn(p.astype(bf16), kv_ref[keys, vcols]))
                f_ref[1, at, cols] = o.astype(bf16)
        y_ref[...] = x_ref[...] + nn(f_ref[1], w_ref[...])


def cross_backward_kernel(
    captions, row, count_ref, x_ref, vec_ref, q_ref, kv_ref, dx_ref, w_ref,
    out_ref, vg_ref, p_ref, dkv_ref,
):
    j = pl.program_id(0)
    d = x_ref.shape[1]

    @pl.when(j == 0)
    def _():
        dy = dx_ref[...].astype(bf16)
        p_ref[1] = dy
        do = nt(dy, w_ref[...]).astype(bf16)
        length = x_ref.shape[0] // captions
        patches = kv_ref.shape[0] // captions
        slot = lax.broadcasted_iota(jnp.int32, (2 * length, patches), 1)
        for c in range(captions):
            at = slice(c * length, (c + 1) * length)
            keys = slice(c * patches, (c + 1) * patches)
            allowed = slot < count_ref[c]
            for h in range(0, d, LANES):
                cols = slice(h, h + LANES)
                vcols = slice(d + h, d + h + LANES)
                dq, dk, dv = attend_back(
                    q_ref[at, cols], kv_ref[keys, cols], kv_ref[keys, vcols], do[at, cols], allowed
                )
                p_ref[0, at, cols] = dq
                dkv_ref[keys, cols] = dk
                dkv_ref[keys, vcols] = dv

    @pl.when(j == 1)
    def _():
        dn, gg, gs = norm_backward(nt(p_ref[0], w_ref[...]), x_ref[...], vec_ref[row : row + 1])
        out_ref[...] = dx_ref[...] + dn
        vg_ref[0:1] = gg
        vg_ref[1:2] = gs


def by_rows(x, order, top_ref, low_ref):
    half = top_ref.shape[0]
    x = nt(x, order).astype(bf16)
    return nn(x[:, :half], top_ref[...]) + nn(x[:, half:], low_ref[...])


def feed_forward_kernel(
    row, x_ref, vec_ref, order_ref, up_ref, up2_ref, down_ref, down2_ref, y_ref, f_ref, u_ref
):
    j = pl.program_id(0)

    @pl.when(j == 0)
    def _():
        unit, _inv = unit_norm(x_ref[...])
        f_ref[0] = (unit * vec_ref[row : row + 1] + vec_ref[row + 1 : row + 2]).astype(bf16)
        y_ref[...] = x_ref[...]

    u = by_rows(f_ref[0], order_ref[0], up_ref, up2_ref)
    u_ref[...] = u
    g = (0.5 * u * (1.0 + jnp.tanh(GELU_A * (u + GELU_B * u * u * u)))).astype(bf16)
    f_ref[1 + j] = g
    y_ref[...] += by_rows(g, order_ref[1], down_ref, down2_ref)


def feed_backward_kernel(
    row, kept, x_ref, vec_ref, order_ref, dx_ref, up_ref, up2_ref, down_ref, down2_ref, *refs
):
    out_ref, vg_ref, p_ref = refs[1:4] if kept else refs[:3]
    acc_ref = refs[-1]
    j = pl.program_id(0)
    half = up_ref.shape[0]

    @pl.when(j == 0)
    def _():
        if not kept:
            unit, _inv = unit_norm(x_ref[...])
            refs[3][0] = (unit * vec_ref[row : row + 1] + vec_ref[row + 1 : row + 2]).astype(bf16)
        p_ref[0] = dx_ref[...].astype(bf16)
        acc_ref[...] = jnp.zeros_like(acc_ref)

    u = refs[0][...] if kept else by_rows(refs[3][0], order_ref[0], up_ref, up2_ref)
    t = jnp.tanh(GELU_A * (u + GELU_B * u * u * u))
    if not kept:
        refs[3][1 + j] = (0.5 * u * (1.0 + t)).astype(bf16)
    slope = 0.5 * (1.0 + t) + 0.5 * u * (1.0 - t * t) * GELU_A * (1.0 + 3.0 * GELU_B * u * u)
    dz = p_ref[0]
    dg = jnp.concatenate((nt(dz, down_ref[...]), nt(dz, down2_ref[...])), axis=1)
    du = (slope * nn(dg.astype(bf16), order_ref[1])).astype(bf16)
    p_ref[1 + j] = du
    acc_ref[:, :half] += nt(du, up_ref[...])
    acc_ref[:, half:] += nt(du, up2_ref[...])

    @pl.when(j == 3)
    def _():
        db = acc_ref[...]
        high = db.astype(bf16)
        low = (db - high.astype(f32)).astype(bf16)
        db = nn(high, order_ref[0]) + nn(low, order_ref[0])
        dn, gg, gs = norm_backward(db, x_ref[...], vec_ref[row : row + 1])
        out_ref[...] = dx_ref[...].astype(f32) + dn
        vg_ref[0:1] = gg
        vg_ref[1:2] = gs


def feed_out_kernel(x_ref, order_ref, g_ref, down_ref, down2_ref, y_ref, acc_ref):
    j = pl.program_id(0)

    @pl.when(j == 0)
    def _():
        acc_ref[...] = x_ref[...]

    acc_ref[...] += by_rows(g_ref[0], order_ref[1], down_ref, down2_ref)

    @pl.when(j == 3)
    def _():
        y_ref[...] = acc_ref[...].astype(bf16)


def both(own_ref, got_ref):
    return jnp.concatenate((own_ref[0], got_ref[0]), axis=0)


def emit(g, send_ref, keep_ref):
    half = keep_ref.shape[0]
    keep_ref[...] = g[:half].astype(bf16)
    send_ref[...] = g[half:].astype(bf16)


def feed_grads_kernel(
    order_ref, b_ref, b2_ref, z_ref, z2_ref, g_ref, g2_ref, u_ref, u2_ref,
    send_a_ref, keep_a_ref, send_b_ref, keep_b_ref, bt_ref,
):
    @pl.when(pl.program_id(0) == 0)
    def _():
        bt_ref[...] = nt(order_ref[0], both(b_ref, b2_ref)).astype(bf16)

    emit(nn(bt_ref[...], both(u_ref, u2_ref)), send_a_ref, keep_a_ref)
    gt = nt(order_ref[1], both(g_ref, g2_ref)).astype(bf16)
    emit(nn(gt, both(z_ref, z2_ref)), send_b_ref, keep_b_ref)


def attend_grads_kernel(
    order_ref, s_ref, s2_ref, sd_ref, sd2_ref, *refs
):
    send_a_ref, keep_a_ref, send_b_ref, keep_b_ref = refs[-4:]
    j = pl.program_id(0)

    def product(a_ref, a2_ref, d_ref, d2_ref):
        at = nt(order_ref[0], both(a_ref, a2_ref)).astype(bf16)
        return nn(at, both(d_ref, d2_ref))

    @pl.when(j < 2)
    def _():
        emit(product(s_ref, s2_ref, sd_ref, sd2_ref), send_a_ref, keep_a_ref)

    @pl.when((j == 2) | (j == 3))
    def _():
        emit(product(s_ref, s2_ref, sd_ref, sd2_ref), send_b_ref, keep_b_ref)

    if len(refs) > 4:
        c_ref, c2_ref, cd_ref, cd2_ref, pair_ref, pair2_ref = refs[:6]

        @pl.when((j == 4) | (j == 5))
        def _():
            emit(product(c_ref, c2_ref, cd_ref, cd2_ref), send_a_ref, keep_a_ref)

        @pl.when(j > 5)
        def _():
            emit(pair_ref[...].astype(f32) + pair2_ref[...].astype(f32), send_b_ref, keep_b_ref)


def pair_grads_kernel(enc_ref, dkv_ref, keep_ref, send_ref):
    emit(nn(enc_ref[...], dkv_ref[...]), send_ref, keep_ref)


def pack_kernel(u_qkv, u_out, u_up, u_down, m_qkv, m_out, m_up, m_down, c_q, c_pair, c_out, vec, out, u_feed, m_feed):
    rows, d = u_out.shape
    spread = spread_matrix().astype(bf16)
    i = lax.broadcasted_iota(jnp.int32, (rows, 4 * rows), 0)
    k = lax.broadcasted_iota(jnp.int32, (rows, 4 * rows), 1)

    def feed(out, up, down):
        for b in range(4 * d // 512):
            y = nn(up[:, b * 512 : (b + 1) * 512], spread).astype(bf16)
            for j in range(4):
                to = j * d + b * LANES
                out[:, to : to + LANES] = y[:, j * LANES : (j + 1) * LANES]
        for j in range(4):
            y = nn((k == 4 * i + j).astype(bf16), down[...])
            out[:, (4 + j) * d : (5 + j) * d] = y.astype(bf16)

    feed(u_feed, u_up, u_down)
    feed(m_feed, m_up, m_down)
    out[:, : 3 * d] = u_qkv[...]
    out[:, 3 * d : 4 * d] = u_out[...]
    out[:, 4 * d : 7 * d] = m_qkv[...]
    out[:, 7 * d : 8 * d] = m_out[...]
    out[:, 8 * d : 9 * d] = c_q[...]
    out[:, 9 * d : 11 * d] = c_pair[...]
    out[:, 11 * d : 12 * d] = c_out[...]
    eye = lax.broadcasted_iota(jnp.int32, (rows, rows), 0) == lax.broadcasted_iota(jnp.int32, (rows, rows), 1)
    out[:, 12 * d :] = nt(eye.astype(bf16), vec[...]).astype(bf16)


def whole(x):
    return pl.BlockSpec(x.shape, lambda *_: (0,) * len(x.shape))


def call(kernel, steps, ins, in_specs, outs, out_specs, scratch=(), scalars=0, vmem=40):
    return pl.pallas_call(
        kernel,
        out_shape=outs,
        grid_spec=pltpu.PrefetchScalarGridSpec(
            num_scalar_prefetch=scalars,
            grid=(steps,),
            in_specs=in_specs,
            out_specs=out_specs,
            scratch_shapes=scratch,
        ),
        compiler_params=pltpu.CompilerParams(
            dimension_semantics=("arbitrary",), vmem_limit_bytes=vmem << 20
        ),
        cost_estimate=pl.CostEstimate(flops=1000, bytes_accessed=1000, transcendentals=0),
    )(*ins)


class Layers:
    def __init__(self, captions, tokens, d, w, vec, order, count):
        self.captions, self.t, self.d = captions, tokens, d
        self.w, self.vec, self.order, self.count = w, vec, order, count
        self.xs = sds((tokens, d), f32)
        self.hs = sds((tokens, d), bf16)

    def weight(self, index):
        return pl.BlockSpec((self.d, self.d), lambda j, *_: (0, index(j)))

    def self_forward(self, x, at, row):
        outs = (self.xs, sds((2, self.t, self.d), bf16), sds((3, self.t, self.d), bf16))
        return call(
            functools.partial(self_forward_kernel, self.captions, row), 4,
            (x, self.vec, self.w),
            [whole(x), whole(self.vec), self.weight(lambda j: at + j)],
            outs, [whole(o) for o in outs],
        )

    def self_backward(self, x, kept, dx, at, row, vectors=()):
        d, t = self.d, self.t
        outs = (self.xs, sds((8, d), f32), sds((4 + len(vectors), t, d), bf16))
        ins = (x, self.vec, kept, dx)
        return call(
            functools.partial(self_backward_kernel, self.captions, row), 4,
            ins + (self.w,) + vectors,
            [whole(i) for i in ins] + [self.weight(lambda j: at + (j + 3) % 4)]
            + [whole(v) for v in vectors],
            outs, [whole(i) for i in outs],
            scratch=[pltpu.VMEM((t, d), f32)],
        )

    def cross_forward(self, x, kv, at, row):
        outs = (self.xs, sds((2, self.t, self.d), bf16), self.hs)
        return call(
            functools.partial(cross_forward_kernel, self.captions, row), 2,
            (self.count, x, self.vec, kv, self.w),
            [whole(x), whole(self.vec), whole(kv), self.weight(lambda j: at + 3 * j)],
            outs, [whole(o) for o in outs], scalars=1,
        )

    def cross_backward(self, x, kept, kv, dx, at, row):
        d, t = self.d, self.t
        outs = (self.xs, sds((8, d), f32), sds((2, t, d), bf16), sds(kv.shape, bf16))
        ins = (x, self.vec, kept, kv, dx)
        return call(
            functools.partial(cross_backward_kernel, self.captions, row), 2,
            (self.count,) + ins + (self.w,),
            [whole(i) for i in ins] + [self.weight(lambda j: at + 3 - 3 * j)],
            outs, [whole(i) for i in outs], scalars=1,
        )

    def pair_grads(self, enc_t, dkv):
        d = self.d
        outs = (sds((d // 2, 2 * d), bf16),) * 2
        grad = pl.BlockSpec((d // 2, d), lambda j: (0, j))
        return call(
            pair_grads_kernel, 2, (enc_t, dkv),
            [whole(enc_t), pl.BlockSpec((dkv.shape[0], d), lambda j: (0, j))],
            outs, [grad, grad],
        )

    def block(self, index):
        return pl.BlockSpec((1, self.t, self.d), lambda j: (index(j), 0, 0))

    def feed_grads(self, f, p):
        d, t = self.d, self.t
        outs = (sds((d // 4, 4 * d), bf16),) * 4
        first, later = self.block(lambda j: 0), self.block(lambda j: 1 + j)
        return call(
            feed_grads_kernel, 4, (self.order,) + f + p + f + p,
            [pl.BlockSpec((2, d // 2, d), lambda j: (0, 0, 0))] + [first] * 4 + [later] * 4,
            outs, [pl.BlockSpec((d // 4, d), lambda j: (0, j))] * 4,
            scratch=[pltpu.VMEM((d // 2, 2 * t), bf16)],
        )

    def attend_grads(self, f, p, cross=()):
        d, t = self.d, self.t
        steps = 8 if cross else 4
        outs = (sds((d // 4, steps // 2 * d), bf16),) * 4

        def first(j):
            return jnp.where(j < 4, jnp.minimum(j, 1), jnp.minimum(j - 2, 3))

        def second(j):
            return jnp.where(j < 6, jnp.clip(j - 2, 0, 1), j - 4)

        grad_a = pl.BlockSpec((d // 4, d), lambda j: (0, first(j)))
        grad_b = pl.BlockSpec((d // 4, d), lambda j: (0, second(j)))
        order = pl.BlockSpec(
            (1, d // 2, d), lambda j: (jnp.where((j == 2) | (j == 3), 1, 0), 0, 0)
        )
        lhs = self.block(lambda j: jnp.minimum(j // 3, 1))
        rhs = self.block(lambda j: jnp.minimum(j, 3))
        ins, specs = (self.order,) + f + p, [order, lhs, lhs, rhs, rhs]
        if cross:
            f, p, pair = cross
            lhs = self.block(lambda j: jnp.clip(j - 4, 0, 1))
            rhs = lhs
            half = pl.BlockSpec((d // 2, d), lambda j: (0, jnp.clip(j - 6, 0, 1)))
            ins = ins + f + p + pair
            specs = specs + [lhs, lhs, rhs, rhs, half, half]
        return call(
            attend_grads_kernel, steps, ins, specs, outs, [grad_a, grad_a, grad_b, grad_b]
        )

    def feed_forward(self, x, w, row):
        d, t = self.d, self.t
        outs = (self.xs, sds((5, t, d), bf16), sds((t, 4 * d), f32))
        ins = (x, self.vec, self.order)
        half = pl.BlockSpec((d // 2, d), lambda j: (0, j))
        return call(
            functools.partial(feed_forward_kernel, row), 4,
            ins + w, [whole(i) for i in ins] + [half] * 4,
            outs, [whole(outs[0]), whole(outs[1]), pl.BlockSpec((t, d), lambda j: (0, j))],
        )

    def feed_backward(self, x, kept, dx, w, row):
        d, t = self.d, self.t
        outs = (self.xs, sds((8, d), f32), sds((5, t, d), bf16))
        if not kept:
            outs = outs + (sds((5, t, d), bf16),)
        ins = (x, self.vec, self.order, dx)
        half = pl.BlockSpec((d // 2, d), lambda j: (0, j))
        return call(
            functools.partial(feed_backward_kernel, row, bool(kept)), 4,
            ins + w + kept,
            [whole(i) for i in ins] + [half] * 4
            + [pl.BlockSpec((t, d), lambda j: (0, j)) for _ in kept],
            outs, [whole(i) for i in outs],
            scratch=[pltpu.VMEM((t, d), f32)],
        )

    def feed_out(self, x, p, w):
        half = pl.BlockSpec((self.d // 2, self.d), lambda j: (0, j))
        return call(
            feed_out_kernel, 4, (x, self.order, p) + w[2:],
            [whole(x), whole(self.order), self.block(lambda j: 1 + j), half, half],
            self.hs, whole(self.hs), scratch=[pltpu.VMEM((self.t, self.d), f32)],
        )


def spread_matrix():
    k = lax.broadcasted_iota(jnp.int32, (512, 512), 0)
    n = lax.broadcasted_iota(jnp.int32, (512, 512), 1)
    return (k % 4) * 128 + k // 4 == n


def unspread(up):
    rows, wide = up.shape
    y = up.reshape(rows, 4, wide // 512, 128).transpose(0, 2, 1, 3)
    y = lax.dot_general(
        y.reshape(rows * (wide // 512), 512), spread_matrix().astype(f32),
        (((1,), (1,)), ((), ())), precision=lax.Precision.HIGHEST,
    )
    return y.reshape(rows, wide)


def local(
    tokens, encoder, patch_count, out_grad,
    u_ag, u_as, u_qkv, u_out, u_mg, u_ms, u_up, u_down,
    m_ag, m_as, m_qkv, m_out, c_g, c_s, c_q, c_pair, c_out, m_mg, m_ms, m_up, m_down,
):
    place = Place()
    captions, length, d = tokens.shape
    rows = u_qkv.shape[0]
    x0 = tokens.reshape(-1, d)
    enc = encoder.reshape(-1, d)
    order = jnp.stack((place.order(d, True), place.order(d, False)))

    vectors = (u_ag, u_as, u_mg, u_ms, m_ag, m_as, c_g, c_s, m_mg, m_ms)
    vectors = jnp.pad(jnp.stack(vectors, axis=0), ((0, LANES - len(vectors)), (0, 0)))
    parts = (u_qkv, u_out, u_up, u_down, m_qkv, m_out, m_up, m_down, c_q, c_pair, c_out, vectors)
    packed = sds((rows, 12 * d + LANES), bf16), sds((rows, 8 * d), bf16), sds((rows, 8 * d), bf16)
    shard, u_feed, m_feed = call(
        pack_kernel, 1, parts, [whole(p) for p in parts], packed, [whole(p) for p in packed], vmem=60
    )
    enc_t = nt(order[1], enc).astype(bf16)
    w = lax.all_gather(shard, AXES, axis=0, tiled=True)

    u_feed, m_feed = Gather(place, u_feed), Gather(place, m_feed)
    feeds = (u_feed, m_feed)
    for _ in range(place.outer_bits):
        for g in feeds:
            g.swap()
            g.join()
    u_feed.swap()
    u_feed.join()
    u_feed.swap()
    m_feed.swap()
    u_feed.join()
    u_feed.swap()
    m_feed.join()
    w, (order, enc_t, m_feed.x, u_feed.x, u_feed.got) = tie(
        w, order, enc_t, m_feed.x, u_feed.x, u_feed.got
    )
    m_feed.swap()
    vec = nt(jnp.eye(16, LANES, dtype=bf16), w[:, 12 * d :])

    net = Layers(captions, captions * length, d, w, vec, order, patch_count)

    w_pair = w[:, 9 * d : 11 * d]
    kv = nn(enc, w_pair).astype(bf16)
    x0a, f_us, k_us = net.self_forward(x0, 0, 0)
    x1, f_uf, k_uf = net.feed_forward(x0a, u_feed.halves(), 2)
    x1, (m_feed.x, m_feed.got) = tie(x1, m_feed.x, m_feed.got)
    m_feed.join()
    x1, (m_feed.x,) = tie(x1, m_feed.x)
    m_feed.swap()
    x1a, f_ms, k_ms = net.self_forward(x1, 4, 4)
    x1b, f_mc, k_mc = net.cross_forward(x1a, kv, 8, 6)

    def core(x):
        return place.swap(x, BIT_CORE)

    def go_on(x, sums=(), start=()):
        x = hold(x, *sums)
        for g in sums:
            g.sums()
        x = need(x, *(tuple(sums) + tuple(g for g in start if g not in sums)))
        for g in start:
            g.swap()
        return x

    def rest(x, *groups):
        for _ in range(place.outer_bits - 1):
            for g in groups:
                x = go_on(x, [g], [g])
        return x

    def pairs(x):
        return x, core(x)

    f_us, f_uf, f_ms = pairs(f_us), pairs(f_uf), pairs(f_ms)
    x1b, (f_us, f_uf, f_ms) = tie(x1b, f_us, f_uf, f_ms)
    f_mc = pairs(f_mc)
    dx, v_mf, p, f = net.feed_backward(x1b, (), out_grad.reshape(-1, d), m_feed.halves(), 8)
    p, f = pairs(p), pairs(f)
    x2 = net.feed_out(x1b, f[0], m_feed.halves())
    p, (x2,) = tie(p, x2)
    s_mf = Sum(place, net.feed_grads(f, p))
    dx, (f_mc,) = tie(dx, f_mc)
    dx = go_on(dx, start=[s_mf])
    dx, v_mc, p_c, dkv = net.cross_backward(x1a, k_mc, kv, dx, 8, 6)
    p_c = pairs(p_c)
    pair, send = net.pair_grads(enc_t, dkv)
    dx, (send,) = tie(dx, send)
    pair = pair, core(send)
    dx, v_ms, p = net.self_backward(x1, k_ms, dx, 4, 4)
    p = pairs(p)
    dx = go_on(dx, [s_mf], [s_mf])
    dx, (p, p_c, pair) = tie(dx, p, p_c, pair)
    s_ma = Sum(place, net.attend_grads(f_ms, p, (f_mc, p_c, pair)))
    dx = go_on(dx, start=[s_ma])
    dx, v_uf, p = net.feed_backward(x0a, (k_uf,), dx, u_feed.halves(), 2)
    p = pairs(p)
    dx = go_on(dx, [s_ma], [s_ma])
    dx, (p,) = tie(dx, p)
    s_uf = Sum(place, net.feed_grads(f_uf, p))
    dx = need(dx, s_uf)
    dx = go_on(dx, [s_mf], [s_uf])
    v = [g[:2] for g in (v_uf, v_ms, v_mc, v_mf)]
    v = jnp.pad(jnp.concatenate(v, axis=0), ((2, 6), (0, 0)))
    dx, _v, p = net.self_backward(x0, k_us, dx, 0, 0, (v,))
    p = pairs(p)
    dx = go_on(dx, [s_ma], [s_mf])
    dx, (dkv,) = tie(dx, dkv)
    denc = nt(dkv, w_pair).astype(bf16)
    dx, (p, denc) = tie(dx, p, denc)
    send_a, keep_a, send_b, keep_b = net.attend_grads(f_us, p)
    v = nt(order[1, : d // 2], plus(p[0][4], p[1][4])[:LANES]).astype(bf16)
    send_b = jnp.concatenate((send_b, v[d // 4 :]), axis=1)
    keep_b = jnp.concatenate((keep_b, v[: d // 4]), axis=1)
    s_us = Sum(place, (send_a, keep_a, send_b, keep_b))
    dx = go_on(dx, start=[s_us])
    dx = rest(dx, s_mf)
    dx = go_on(dx, [s_uf], [s_uf])
    dx, (r_mf,) = tie(dx, s_mf.total())
    dx = go_on(dx, start=[s_ma])
    dx = go_on(dx, [s_us], [s_us])
    dx = rest(dx, s_ma)
    dx = go_on(dx, [s_uf], [s_uf])
    dx, (r_ma,) = tie(dx, s_ma.total())
    dx = go_on(dx, [s_us], [s_us])
    dx = rest(dx, s_uf, s_us)
    r_uf, r_us = s_uf.total(), s_us.total()

    def feed_rows(r):
        return unspread(r[:, : 4 * d]), r[:, 4 * d :].reshape(-1, d)

    def columns(r, *blocks):
        parts = [r[:, b * d : (b + 1) * d] for b in blocks]
        return jnp.concatenate(parts, axis=1) if len(parts) > 1 else parts[0]

    r_uup, r_udown = feed_rows(r_uf)
    r_mup, r_mdown = feed_rows(r_mf)
    vs = r_us[:, 4 * d :]
    v = [vs[:, i] for i in range(10)]
    return (
        x2.reshape(tokens.shape),
        dx.astype(bf16).reshape(tokens.shape),
        denc.reshape(encoder.shape),
        v[0], v[1], r_us[:, : 3 * d], r_us[:, 3 * d : 4 * d], v[2], v[3], r_uup, r_udown,
        v[4], v[5], columns(r_ma, 0, 1, 4), columns(r_ma, 5), v[6], v[7],
        columns(r_ma, 2), columns(r_ma, 6, 7), columns(r_ma, 3),
        v[8], v[9], r_mup, r_mdown,
    )


def solution(mesh):
    rows1 = P(AXES)
    rows2 = P(AXES, None)
    rows3 = P(AXES, None, None)
    block = (rows1, rows1, rows2, rows2)
    weights = block * 2 + block + (rows1, rows1, rows2, rows2, rows2) + block
    return jax.shard_map(
        local,
        mesh=mesh,
        in_specs=(rows3, rows3, rows1, rows3) + weights,
        out_specs=(rows3, rows3, rows3) + weights,
        check_vma=False,
    )
```

```python
import functools

import jax
import jax.numpy as jnp
from jax import lax
from jax.experimental import pallas as pl
from jax.experimental.pallas import tpu as pltpu
from jax.sharding import PartitionSpec as P

DH = 64
AXES = ("dp", "hd")
EPS = 1e-05
MASKED = -1e30
LANES = 128
bf16 = jnp.bfloat16
f32 = jnp.float32
sds = jax.ShapeDtypeStruct


BIT_PAIR, BIT_CORE, BIT_NEAR = 1, 2, 4


class Place:
    def __init__(self):
        self.count = lax.axis_size("dp") * lax.axis_size("hd")
        self.outer_size = self.count // 8
        index = lax.axis_index("dp") * lax.axis_size("hd") + lax.axis_index("hd")
        self.pair = index % 2
        self.core = (index // 2) % 2
        self.near = (index // 4) % 2
        self.outer = index // 8
        self.outer_bits = self.outer_size.bit_length() - 1

    def swap(self, x, bit):
        return lax.ppermute(x, AXES, [(i, i ^ bit) for i in range(self.count)])

    def swap_by_core(self, x, bits):
        pairs = [(i, i ^ bits[(i // BIT_CORE) % 2]) for i in range(self.count)]
        return lax.ppermute(x, AXES, pairs)

    def order(self, d):
        n, rows = self.outer_size, d // self.count
        k = lax.broadcasted_iota(jnp.int32, (d, 1), 0)
        row, place = k % rows, (k // rows) % n
        outer = jnp.zeros_like(k)
        for b in range(self.outer_bits):
            outer = outer + ((place >> (self.outer_bits - 1 - b)) & 1) * (1 << b)
        outer = outer ^ self.outer
        rest = k // (rows * n)
        low, high = rest % 2, (rest // 2) % 2
        near = jnp.where((rest // 4) ^ self.core == 0, high, low)
        pair = high + low - near
        feature = outer * 2 + (near ^ self.near)
        feature = (feature * 2 + ((rest // 4) ^ self.core)) * 2 + (pair ^ self.pair)
        feature = feature * rows + row
        return (feature == lax.broadcasted_iota(jnp.int32, (d, d), 1)).astype(bf16)


def plus(a, b):
    return (a.astype(f32) + b.astype(f32)).astype(bf16)


class Sum:
    def __init__(self, place, grads):
        self.place, self.stage = place, 0
        self.send, self.kept = grads

    def swap(self):
        if self.stage < 2:
            bits = ((BIT_NEAR, BIT_PAIR), (BIT_PAIR, BIT_NEAR))[self.stage]
            self.got = self.place.swap_by_core(self.send, bits)
        else:
            self.got = self.place.swap(self.send, 8 << (self.stage - 2))

    def sums(self):
        if self.stage < 2:
            self.send, self.kept = half_sums(self.kept, self.got)
        else:
            half = self.kept.shape[0] // 2
            self.send = plus(self.kept[half:], self.got[half:])
            self.kept = plus(self.kept[:half], self.got[:half])
        self.stage += 1

    def total(self):
        return self.kept.astype(f32) + self.got.astype(f32)


def tie(x, *others):
    out = lax.optimization_barrier((x,) + others)
    return out[0], out[1:]


def hold(x, *groups):
    x, terms = tie(x, *[(g.kept, g.got) for g in groups])
    for g, t in zip(groups, terms):
        g.kept, g.got = t
    return x


def need(x, *groups):
    x, send = tie(x, *[g.send for g in groups])
    for g, k in zip(groups, send):
        g.send = k
    return x


def nn(a, b):
    return jnp.dot(a, b, preferred_element_type=f32)


def nt(a, b):
    return lax.dot_general(a, b, (((1,), (1,)), ((), ())), preferred_element_type=f32)


def tn(a, b):
    return lax.dot_general(a, b, (((0,), (0,)), ((), ())), preferred_element_type=f32)


def unit_norm(x):
    centred = x - jnp.mean(x, axis=-1, keepdims=True)
    inv = lax.rsqrt(jnp.mean(centred * centred, axis=-1, keepdims=True) + EPS)
    return centred * inv, inv


def norm_backward(grad, x, gain):
    unit, inv = unit_norm(x)
    du = grad * gain
    dx = inv * (
        du
        - jnp.mean(du, axis=-1, keepdims=True)
        - unit * jnp.mean(du * unit, axis=-1, keepdims=True)
    )
    return dx, jnp.sum(grad * unit, axis=0, keepdims=True), jnp.sum(grad, axis=0, keepdims=True)


GELU_A = 0.7978845608028654
GELU_B = 0.044715


def two_heads(x):
    first = lax.broadcasted_iota(jnp.int32, x.shape, 1) < DH
    zero = jnp.zeros_like(x)
    return jnp.concatenate((jnp.where(first, x, zero), jnp.where(first, zero, x)), axis=0)


def side_by_side(x):
    n = x.shape[0] // 2
    first = lax.broadcasted_iota(jnp.int32, (n, LANES), 1) < DH
    return jnp.where(first, x[:n], x[n:])


def probabilities(qs, k2, allowed):
    s = jnp.where(allowed, nt(qs, k2) * DH ** (-0.5), MASKED)
    e = jnp.exp(s - jnp.max(s, axis=-1, keepdims=True))
    return e / jnp.sum(e, axis=-1, keepdims=True)


def causal_mask(length):
    row = lax.broadcasted_iota(jnp.int32, (2 * length, length), 0)
    col = lax.broadcasted_iota(jnp.int32, (2 * length, length), 1)
    return jnp.where(row >= length, row - length, row) >= col


def attend_back(q2, k2, v2, do2, allowed):
    scale = DH ** (-0.5)
    qs, dos = two_heads(q2), two_heads(do2)
    p = probabilities(qs, k2, allowed)
    dp = nt(dos, v2)
    ds = (p * (dp - jnp.sum(p * dp, axis=-1, keepdims=True))).astype(bf16)
    dq = side_by_side(nn(ds, k2)) * scale
    dk = tn(ds, qs) * scale
    dv = tn(p.astype(bf16), dos)
    return dq.astype(bf16), dk.astype(bf16), dv.astype(bf16)


def self_forward_kernel(captions, row, x_ref, vec_ref, w_ref, y_ref, f_ref, qkv_ref):
    j = pl.program_id(0)

    @pl.when(j == 0)
    def _():
        unit, _inv = unit_norm(x_ref[...].astype(f32))
        f_ref[0] = (unit * vec_ref[row : row + 1] + vec_ref[row + 1 : row + 2]).astype(bf16)

    @pl.when(j < 3)
    def _():
        qkv_ref[j] = nn(f_ref[0], w_ref[...]).astype(bf16)

    @pl.when(j == 3)
    def _():
        length = x_ref.shape[0] // captions
        allowed = causal_mask(length)
        for c in range(captions):
            at = slice(c * length, (c + 1) * length)
            for h in range(0, x_ref.shape[1], LANES):
                cols = slice(h, h + LANES)
                p = probabilities(two_heads(qkv_ref[0, at, cols]), qkv_ref[1, at, cols], allowed)
                o = side_by_side(nn(p.astype(bf16), qkv_ref[2, at, cols]))
                f_ref[1, at, cols] = o.astype(bf16)
        y_ref[...] = x_ref[...].astype(f32) + nn(f_ref[1], w_ref[...])


def self_backward_kernel(
    captions, row, x_ref, vec_ref, qkv_ref, dx_ref, w_ref, *refs
):
    out_ref, vg_ref, p_ref, acc_ref = refs[-4:]
    j = pl.program_id(0)

    @pl.when(j == 0)
    def _():
        dy = dx_ref[...].astype(bf16)
        p_ref[3] = dy
        do = nt(dy, w_ref[...]).astype(bf16)
        length = x_ref.shape[0] // captions
        allowed = causal_mask(length)
        for c in range(captions):
            at = slice(c * length, (c + 1) * length)
            for h in range(0, x_ref.shape[1], LANES):
                cols = slice(h, h + LANES)
                dq, dk, dv = attend_back(
                    qkv_ref[0, at, cols], qkv_ref[1, at, cols], qkv_ref[2, at, cols],
                    do[at, cols], allowed,
                )
                p_ref[0, at, cols] = dq
                p_ref[1, at, cols] = dk
                p_ref[2, at, cols] = dv
        acc_ref[...] = jnp.zeros_like(acc_ref)

    @pl.when(j > 0)
    def _():
        acc_ref[...] += nt(p_ref[j - 1], w_ref[...])

    @pl.when(j == 3)
    def _():
        dn, gg, gs = norm_backward(acc_ref[...], x_ref[...].astype(f32), vec_ref[row : row + 1])
        out_ref[...] = dx_ref[...] + dn
        vg_ref[0:1] = gg
        vg_ref[1:2] = gs
        if len(refs) > 4:
            at = lax.broadcasted_iota(jnp.int32, refs[0].shape, 0)
            rows = jnp.where(at == 0, gg, jnp.where(at == 1, gs, refs[0][...]))
            p_ref[4] = jnp.zeros_like(p_ref[4])
            p_ref[4, 0 : refs[0].shape[0]] = rows.astype(bf16)


def cross_forward_kernel(
    captions, row, count_ref, x_ref, vec_ref, kv_ref, w_ref, y_ref, f_ref, q_ref
):
    j = pl.program_id(0)
    d = x_ref.shape[1]

    @pl.when(j == 0)
    def _():
        unit, _inv = unit_norm(x_ref[...])
        c = (unit * vec_ref[row : row + 1] + vec_ref[row + 1 : row + 2]).astype(bf16)
        f_ref[0] = c
        q_ref[...] = nn(c, w_ref[...]).astype(bf16)

    @pl.when(j == 1)
    def _():
        length = x_ref.shape[0] // captions
        patches = kv_ref.shape[0] // captions
        slot = lax.broadcasted_iota(jnp.int32, (2 * length, patches), 1)
        for c in range(captions):
            at = slice(c * length, (c + 1) * length)
            keys = slice(c * patches, (c + 1) * patches)
            allowed = slot < count_ref[c]
            for h in range(0, d, LANES):
                cols = slice(h, h + LANES)
                vcols = slice(d + h, d + h + LANES)
                p = probabilities(two_heads(q_ref[at, cols]), kv_ref[keys, cols], allowed)
                o = side_by_side(nn(p.astype(bf16), kv_ref[keys, vcols]))
                f_ref[1, at, cols] = o.astype(bf16)
        y_ref[...] = x_ref[...] + nn(f_ref[1], w_ref[...])


def cross_backward_kernel(
    captions, row, count_ref, x_ref, vec_ref, q_ref, kv_ref, dx_ref, w_ref,
    out_ref, vg_ref, p_ref, dkv_ref,
):
    j = pl.program_id(0)
    d = x_ref.shape[1]

    @pl.when(j == 0)
    def _():
        dy = dx_ref[...].astype(bf16)
        p_ref[1] = dy
        do = nt(dy, w_ref[...]).astype(bf16)
        length = x_ref.shape[0] // captions
        patches = kv_ref.shape[0] // captions
        slot = lax.broadcasted_iota(jnp.int32, (2 * length, patches), 1)
        for c in range(captions):
            at = slice(c * length, (c + 1) * length)
            keys = slice(c * patches, (c + 1) * patches)
            allowed = slot < count_ref[c]
            for h in range(0, d, LANES):
                cols = slice(h, h + LANES)
                vcols = slice(d + h, d + h + LANES)
                dq, dk, dv = attend_back(
                    q_ref[at, cols], kv_ref[keys, cols], kv_ref[keys, vcols], do[at, cols], allowed
                )
                p_ref[0, at, cols] = dq
                dkv_ref[keys, cols] = dk
                dkv_ref[keys, vcols] = dv

    @pl.when(j == 1)
    def _():
        dn, gg, gs = norm_backward(nt(p_ref[0], w_ref[...]), x_ref[...], vec_ref[row : row + 1])
        out_ref[...] = dx_ref[...] + dn
        vg_ref[0:1] = gg
        vg_ref[1:2] = gs


def feed_forward_kernel(row, x_ref, vec_ref, up_ref, down_ref, y_ref, f_ref, u_ref):
    j = pl.program_id(0)

    @pl.when(j == 0)
    def _():
        unit, _inv = unit_norm(x_ref[...])
        f_ref[0] = (unit * vec_ref[row : row + 1] + vec_ref[row + 1 : row + 2]).astype(bf16)
        y_ref[...] = x_ref[...]

    u = nn(f_ref[0], up_ref[...])
    u_ref[...] = u
    g = (0.5 * u * (1.0 + jnp.tanh(GELU_A * (u + GELU_B * u * u * u)))).astype(bf16)
    f_ref[1 + j] = g
    y_ref[...] += nn(g, down_ref[...])


def feed_backward_kernel(row, kept, x_ref, vec_ref, dx_ref, up_ref, down_ref, *refs):
    out_ref, vg_ref, p_ref = refs[1:4] if kept else refs[:3]
    acc_ref = refs[-1]
    j = pl.program_id(0)

    @pl.when(j == 0)
    def _():
        if not kept:
            unit, _inv = unit_norm(x_ref[...])
            refs[3][0] = (unit * vec_ref[row : row + 1] + vec_ref[row + 1 : row + 2]).astype(bf16)
        p_ref[0] = dx_ref[...].astype(bf16)
        acc_ref[...] = jnp.zeros_like(acc_ref)

    u = refs[0][...] if kept else nn(refs[3][0], up_ref[...])
    t = jnp.tanh(GELU_A * (u + GELU_B * u * u * u))
    if not kept:
        refs[3][1 + j] = (0.5 * u * (1.0 + t)).astype(bf16)
    slope = 0.5 * (1.0 + t) + 0.5 * u * (1.0 - t * t) * GELU_A * (1.0 + 3.0 * GELU_B * u * u)
    du = (slope * nt(p_ref[0], down_ref[...])).astype(bf16)
    p_ref[1 + j] = du
    acc_ref[...] += nt(du, up_ref[...])

    @pl.when(j == 3)
    def _():
        dn, gg, gs = norm_backward(acc_ref[...], x_ref[...], vec_ref[row : row + 1])
        out_ref[...] = dx_ref[...].astype(f32) + dn
        vg_ref[0:1] = gg
        vg_ref[1:2] = gs


def feed_out_kernel(x_ref, g_ref, down_ref, y_ref, acc_ref):
    j = pl.program_id(0)

    @pl.when(j == 0)
    def _():
        acc_ref[...] = x_ref[...]

    acc_ref[...] += nn(g_ref[0], down_ref[...])

    @pl.when(j == 3)
    def _():
        y_ref[...] = acc_ref[...].astype(bf16)


def both(own_ref, got_ref):
    return jnp.concatenate((own_ref[0], got_ref[0]), axis=0)


def emit(g, send_ref, keep_ref):
    half = keep_ref.shape[0]
    keep_ref[...] = g[:half].astype(bf16)
    send_ref[...] = g[half:].astype(bf16)


def feed_grads_kernel(
    order_ref, b_ref, b2_ref, z_ref, z2_ref, g_ref, g2_ref, u_ref, u2_ref, send_ref, keep_ref, bt_ref
):
    d = order_ref.shape[1]

    @pl.when(pl.program_id(0) == 0)
    def _():
        bt_ref[...] = nt(order_ref[...], both(b_ref, b2_ref)).astype(bf16)

    up, down = (slice(None), slice(0, d)), (slice(None), slice(d, 2 * d))
    emit(nn(bt_ref[...], both(u_ref, u2_ref)), send_ref.at[up], keep_ref.at[up])
    gt = nt(order_ref[...], both(g_ref, g2_ref)).astype(bf16)
    emit(nn(gt, both(z_ref, z2_ref)), send_ref.at[down], keep_ref.at[down])


def attend_grads_kernel(order_ref, s_ref, s2_ref, sd_ref, sd2_ref, *refs):
    send_ref, keep_ref = refs[-2:]
    j = pl.program_id(0)

    def product(a_ref, a2_ref, d_ref, d2_ref):
        at = nt(order_ref[...], both(a_ref, a2_ref)).astype(bf16)
        emit(nn(at, both(d_ref, d2_ref)), send_ref, keep_ref)

    @pl.when(j < 4)
    def _():
        product(s_ref, s2_ref, sd_ref, sd2_ref)

    if len(refs) > 2:
        c_ref, c2_ref, cd_ref, cd2_ref, pair_ref, pair2_ref = refs[:6]

        @pl.when((j == 4) | (j == 5))
        def _():
            product(c_ref, c2_ref, cd_ref, cd2_ref)

        @pl.when(j > 5)
        def _():
            emit(pair_ref[...].astype(f32) + pair2_ref[...].astype(f32), send_ref, keep_ref)


def half_sums_kernel(kept_ref, got_ref, send_ref, keep_ref):
    emit(kept_ref[...].astype(f32) + got_ref[...].astype(f32), send_ref, keep_ref)


def half_sums(kept, got):
    rows, wide = kept.shape
    steps = 2 if wide % (2 * LANES) == 0 else 1
    full = pl.BlockSpec((rows, wide // steps), lambda j: (0, j))
    half = pl.BlockSpec((rows // 2, wide // steps), lambda j: (0, j))
    outs = (sds((rows // 2, wide), bf16),) * 2
    return call(half_sums_kernel, steps, (kept, got), [full] * 2, outs, [half] * 2, vmem=24)


def pair_input_kernel(dkv_ref, k_ref, v_ref, out_ref):
    d = k_ref.shape[0]
    g = nt(dkv_ref[:, :d], k_ref[...]) + nt(dkv_ref[:, d:], v_ref[...])
    out_ref[...] = g.astype(bf16)


def pair_grads_kernel(enc_ref, dkv_ref, keep_ref, send_ref):
    emit(nn(enc_ref[...], dkv_ref[...]), send_ref, keep_ref)


def pack_kernel(u_qkv, u_out, u_up, u_down, m_qkv, m_out, m_up, m_down, c_q, c_pair, c_out, vec, out):
    rows, d = u_out.shape
    spread = spread_matrix().astype(bf16)
    i = lax.broadcasted_iota(jnp.int32, (rows, 4 * rows), 0)
    k = lax.broadcasted_iota(jnp.int32, (rows, 4 * rows), 1)

    def layer(at, qkv, w_out, up, down):
        out[:, at : at + 3 * d] = qkv[...]
        out[:, at + 3 * d : at + 4 * d] = w_out[...]
        for b in range(4 * d // 512):
            y = nn(up[:, b * 512 : (b + 1) * 512], spread).astype(bf16)
            for j in range(4):
                to = at + (4 + j) * d + b * LANES
                out[:, to : to + LANES] = y[:, j * LANES : (j + 1) * LANES]
        for j in range(4):
            y = nn((k == 4 * i + j).astype(bf16), down[...])
            out[:, at + (8 + j) * d : at + (9 + j) * d] = y.astype(bf16)

    layer(0, u_qkv, u_out, u_up, u_down)
    layer(12 * d, m_qkv, m_out, m_up, m_down)
    out[:, 24 * d : 25 * d] = c_q[...]
    out[:, 25 * d : 27 * d] = c_pair[...]
    out[:, 27 * d : 28 * d] = c_out[...]
    eye = lax.broadcasted_iota(jnp.int32, (rows, rows), 0) == lax.broadcasted_iota(jnp.int32, (rows, rows), 1)
    out[:, 28 * d :] = nt(eye.astype(bf16), vec[...]).astype(bf16)


def whole(x):
    return pl.BlockSpec(x.shape, lambda *_: (0,) * len(x.shape))


def call(kernel, steps, ins, in_specs, outs, out_specs, scratch=(), scalars=0, vmem=40):
    return pl.pallas_call(
        kernel,
        out_shape=outs,
        grid_spec=pltpu.PrefetchScalarGridSpec(
            num_scalar_prefetch=scalars,
            grid=(steps,),
            in_specs=in_specs,
            out_specs=out_specs,
            scratch_shapes=scratch,
        ),
        compiler_params=pltpu.CompilerParams(
            dimension_semantics=("arbitrary",), vmem_limit_bytes=vmem << 20
        ),
        cost_estimate=pl.CostEstimate(flops=1000, bytes_accessed=1000, transcendentals=0),
    )(*ins)


class Layers:
    def __init__(self, captions, tokens, d, w, vec, order, count):
        self.captions, self.t, self.d = captions, tokens, d
        self.w, self.vec, self.order, self.count = w, vec, order, count
        self.xs = sds((tokens, d), f32)
        self.hs = sds((tokens, d), bf16)

    def weight(self, index):
        return pl.BlockSpec((self.d, self.d), lambda j, *_: (0, index(j)))

    def self_forward(self, x, at, row):
        outs = (self.xs, sds((2, self.t, self.d), bf16), sds((3, self.t, self.d), bf16))
        return call(
            functools.partial(self_forward_kernel, self.captions, row), 4,
            (x, self.vec, self.w),
            [whole(x), whole(self.vec), self.weight(lambda j: at + j)],
            outs, [whole(o) for o in outs],
        )

    def self_backward(self, x, kept, dx, at, row, vectors=()):
        d, t = self.d, self.t
        outs = (self.xs, sds((8, d), f32), sds((4 + len(vectors), t, d), bf16))
        ins = (x, self.vec, kept, dx)
        return call(
            functools.partial(self_backward_kernel, self.captions, row), 4,
            ins + (self.w,) + vectors,
            [whole(i) for i in ins] + [self.weight(lambda j: at + (j + 3) % 4)]
            + [whole(v) for v in vectors],
            outs, [whole(i) for i in outs],
            scratch=[pltpu.VMEM((t, d), f32)],
        )

    def cross_forward(self, x, kv, at, row):
        outs = (self.xs, sds((2, self.t, self.d), bf16), self.hs)
        return call(
            functools.partial(cross_forward_kernel, self.captions, row), 2,
            (self.count, x, self.vec, kv, self.w),
            [whole(x), whole(self.vec), whole(kv), self.weight(lambda j: at + 3 * j)],
            outs, [whole(o) for o in outs], scalars=1,
        )

    def cross_backward(self, x, kept, kv, dx, at, row):
        d, t = self.d, self.t
        outs = (self.xs, sds((8, d), f32), sds((2, t, d), bf16), sds(kv.shape, bf16))
        ins = (x, self.vec, kept, kv, dx)
        return call(
            functools.partial(cross_backward_kernel, self.captions, row), 2,
            (self.count,) + ins + (self.w,),
            [whole(i) for i in ins] + [self.weight(lambda j: at + 3 - 3 * j)],
            outs, [whole(i) for i in outs], scalars=1,
        )

    def pair_grads(self, enc_t, dkv):
        d = self.d
        outs = (sds((d // 2, 2 * d), bf16),) * 2
        grad = pl.BlockSpec((d // 2, d), lambda j: (0, j))
        return call(
            pair_grads_kernel, 2, (enc_t, dkv),
            [whole(enc_t), pl.BlockSpec((dkv.shape[0], d), lambda j: (0, j))],
            outs, [grad, grad],
        )

    def pair_input(self, dkv, at):
        d, rows = self.d, dkv.shape[0] // self.captions
        out = sds((dkv.shape[0], d), bf16)
        return call(
            pair_input_kernel, self.captions, (dkv, self.w, self.w),
            [pl.BlockSpec((rows, 2 * d), lambda j: (j, 0))]
            + [self.weight(lambda j: at), self.weight(lambda j: at + 1)],
            out, pl.BlockSpec((rows, d), lambda j: (j, 0)),
        )

    def block(self, index):
        return pl.BlockSpec((1, self.t, self.d), lambda j: (index(j), 0, 0))

    def feed_grads(self, f, p):
        d, t = self.d, self.t
        outs = (sds((d // 4, 8 * d), bf16),) * 2
        first, later = self.block(lambda j: 0), self.block(lambda j: 1 + j)
        half = pl.BlockSpec((d // 2, d), lambda j: (0, 0))
        return call(
            feed_grads_kernel, 4, (self.order,) + f + p + f + p,
            [half] + [first] * 4 + [later] * 4,
            outs, [pl.BlockSpec((d // 4, 2 * d), lambda j: (0, j))] * 2,
            scratch=[pltpu.VMEM((d // 2, 2 * t), bf16)],
        )

    def attend_grads(self, f, p, cross=()):
        d, t = self.d, self.t
        steps = 8 if cross else 4
        outs = (sds((d // 4, steps * d), bf16),) * 2
        half = pl.BlockSpec((d // 2, d), lambda j: (0, 0))
        lhs = self.block(lambda j: jnp.minimum(j // 3, 1))
        rhs = self.block(lambda j: jnp.minimum(j, 3))
        ins, specs = (self.order,) + f + p, [half, lhs, lhs, rhs, rhs]
        if cross:
            f, p, pair = cross
            at = self.block(lambda j: jnp.clip(j - 4, 0, 1))
            columns = pl.BlockSpec((d // 2, d), lambda j: (0, jnp.clip(j - 6, 0, 1)))
            ins, specs = ins + f + p + pair, specs + [at] * 4 + [columns] * 2
        return call(
            attend_grads_kernel, steps, ins, specs,
            outs, [pl.BlockSpec((d // 4, d), lambda j: (0, j))] * 2,
        )

    def feed_forward(self, x, at, row):
        d, t = self.d, self.t
        outs = (self.xs, sds((5, t, d), bf16), sds((t, 4 * d), f32))
        return call(
            functools.partial(feed_forward_kernel, row), 4,
            (x, self.vec, self.w, self.w),
            [whole(x), whole(self.vec), self.weight(lambda j: at + j), self.weight(lambda j: at + 4 + j)],
            outs, [whole(outs[0]), whole(outs[1]), pl.BlockSpec((t, d), lambda j: (0, j))],
        )

    def feed_backward(self, x, kept, dx, at, row):
        d, t = self.d, self.t
        outs = (self.xs, sds((8, d), f32), sds((5, t, d), bf16))
        if not kept:
            outs = outs + (sds((5, t, d), bf16),)
        return call(
            functools.partial(feed_backward_kernel, row, bool(kept)), 4,
            (x, self.vec, dx, self.w, self.w) + kept,
            [
                whole(x), whole(self.vec), whole(dx),
                self.weight(lambda j: at + j), self.weight(lambda j: at + 4 + j),
            ] + [pl.BlockSpec((t, d), lambda j: (0, j)) for _ in kept],
            outs, [whole(i) for i in outs],
            scratch=[pltpu.VMEM((t, d), f32)],
        )

    def feed_out(self, x, p, at):
        return call(
            feed_out_kernel, 4, (x, p, self.w),
            [whole(x), self.block(lambda j: 1 + j), self.weight(lambda j: at + 4 + j)],
            self.hs, whole(self.hs), scratch=[pltpu.VMEM((self.t, self.d), f32)],
        )


def spread_matrix():
    k = lax.broadcasted_iota(jnp.int32, (512, 512), 0)
    n = lax.broadcasted_iota(jnp.int32, (512, 512), 1)
    return (k % 4) * 128 + k // 4 == n


def unspread(up):
    rows, wide = up.shape
    y = up.reshape(rows, 4, wide // 512, 128).transpose(0, 2, 1, 3)
    y = lax.dot_general(
        y.reshape(rows * (wide // 512), 512), spread_matrix().astype(f32),
        (((1,), (1,)), ((), ())), precision=lax.Precision.HIGHEST,
    )
    return y.reshape(rows, wide)


def local(
    tokens, encoder, patch_count, out_grad,
    u_ag, u_as, u_qkv, u_out, u_mg, u_ms, u_up, u_down,
    m_ag, m_as, m_qkv, m_out, c_g, c_s, c_q, c_pair, c_out, m_mg, m_ms, m_up, m_down,
):
    place = Place()
    captions, length, d = tokens.shape
    rows = u_qkv.shape[0]
    x0 = tokens.reshape(-1, d)
    enc = encoder.reshape(-1, d)
    order = place.order(d)

    vectors = (u_ag, u_as, u_mg, u_ms, m_ag, m_as, c_g, c_s, m_mg, m_ms)
    vectors = jnp.pad(jnp.stack(vectors, axis=0), ((0, LANES - len(vectors)), (0, 0)))
    parts = (u_qkv, u_out, u_up, u_down, m_qkv, m_out, m_up, m_down, c_q, c_pair, c_out, vectors)
    packed = sds((rows, 28 * d + LANES), bf16)
    shard = call(pack_kernel, 1, parts, [whole(p) for p in parts], packed, whole(packed), vmem=60)
    enc_t = nt(order, enc).astype(bf16)
    w = lax.all_gather(shard, AXES, axis=0, tiled=True)
    w, (order, enc_t) = tie(w, order, enc_t)
    vec = nt(jnp.eye(16, LANES, dtype=bf16), w[:, 28 * d :])

    net = Layers(captions, captions * length, d, w, vec, order, patch_count)

    w_pair = w[:, 25 * d : 27 * d]
    kv = nn(enc, w_pair).astype(bf16)
    x0a, f_us, k_us = net.self_forward(x0, 0, 0)
    x1, f_uf, k_uf = net.feed_forward(x0a, 4, 2)
    x1a, f_ms, k_ms = net.self_forward(x1, 12, 4)
    x1b, f_mc, k_mc = net.cross_forward(x1a, kv, 24, 6)

    def core(x):
        return place.swap(x, BIT_CORE)

    def go_on(x, sums=(), start=()):
        x = hold(x, *sums)
        for g in sums:
            g.sums()
        x = need(x, *(tuple(sums) + tuple(g for g in start if g not in sums)))
        for g in start:
            g.swap()
        return x

    def rest(x, *groups):
        for _ in range(place.outer_bits - 1):
            for g in groups:
                x = go_on(x, [g], [g])
        return x

    def pairs(x):
        return x, core(x)

    f_us, f_uf, f_ms = pairs(f_us), pairs(f_uf), pairs(f_ms)
    x1b, (f_us, f_uf, f_ms) = tie(x1b, f_us, f_uf, f_ms)
    f_mc = pairs(f_mc)
    dx, v_mf, p, f = net.feed_backward(x1b, (), out_grad.reshape(-1, d), 16, 8)
    p, f = pairs(p), pairs(f)
    x2 = net.feed_out(x1b, f[0], 16)
    p, (x2,) = tie(p, x2)
    s_mf = Sum(place, net.feed_grads(f, p))
    dx, (f_mc,) = tie(dx, f_mc)
    dx = go_on(dx, start=[s_mf])
    dx, v_mc, p_c, dkv = net.cross_backward(x1a, k_mc, kv, dx, 24, 6)
    p_c = pairs(p_c)
    pair, send = net.pair_grads(enc_t, dkv)
    dx, (send,) = tie(dx, send)
    pair = pair, core(send)
    dx, v_ms, p = net.self_backward(x1, k_ms, dx, 12, 4)
    p = pairs(p)
    dx = go_on(dx, [s_mf], [s_mf])
    dx, (p, p_c, pair) = tie(dx, p, p_c, pair)
    s_ma = Sum(place, net.attend_grads(f_ms, p, (f_mc, p_c, pair)))
    dx = go_on(dx, start=[s_ma])
    dx, v_uf, p = net.feed_backward(x0a, (k_uf,), dx, 4, 2)
    p = pairs(p)
    dx = go_on(dx, [s_ma])
    dx, (p,) = tie(dx, p)
    s_uf = Sum(place, net.feed_grads(f_uf, p))
    dx = need(dx, s_uf)
    dx = go_on(dx, [s_mf], [s_ma, s_uf, s_mf])
    v = [g[:2] for g in (v_uf, v_ms, v_mc, v_mf)]
    v = jnp.pad(jnp.concatenate(v, axis=0), ((2, 6), (0, 0)))
    dx, _v, p = net.self_backward(x0, k_us, dx, 0, 0, (v,))
    p = pairs(p)
    dx = go_on(dx, [s_mf, s_ma], [s_mf, s_ma])
    dx, (dkv,) = tie(dx, dkv)
    denc = net.pair_input(dkv, 25)
    dx, (denc,) = tie(dx, denc)
    dx, (p,) = tie(dx, p)
    send, keep = net.attend_grads(f_us, p)
    v = nt(order[: d // 2], plus(p[0][4], p[1][4])[:LANES]).astype(bf16)
    send = jnp.concatenate((send, v[d // 4 :]), axis=1)
    keep = jnp.concatenate((keep, v[: d // 4]), axis=1)
    s_us = Sum(place, (send, keep))
    dx = go_on(dx, start=[s_us])
    for _ in range(place.outer_bits - 2):
        dx = go_on(dx, [s_mf], [s_mf])
    dx = go_on(dx, [s_uf], [s_uf])
    dx = go_on(dx, [s_us], [s_us])
    dx, (r_mf,) = tie(dx, s_mf.total())
    dx = rest(dx, s_ma)
    dx = go_on(dx, [s_uf], [s_uf])
    dx, (r_ma,) = tie(dx, s_ma.total())
    dx = go_on(dx, [s_us], [s_us])
    dx = rest(dx, s_uf)
    dx, (r_uf,) = tie(dx, s_uf.total())
    dx = rest(dx, s_us)
    r_us = s_us.total()

    def columns(r, *blocks):
        parts = [r[:, b * d : (b + 1) * d] for b in blocks]
        return jnp.concatenate(parts, axis=1) if len(parts) > 1 else parts[0]

    def feed_rows(r):
        return unspread(columns(r, 0, 2, 4, 6)), columns(r, 1, 3, 5, 7).reshape(-1, d)

    r_uup, r_udown = feed_rows(r_uf)
    r_mup, r_mdown = feed_rows(r_mf)
    vs = r_us[:, 4 * d :]
    v = [vs[:, i] for i in range(10)]
    return (
        x2.reshape(tokens.shape),
        dx.astype(bf16).reshape(tokens.shape),
        denc.reshape(encoder.shape),
        v[0], v[1], r_us[:, : 3 * d], r_us[:, 3 * d : 4 * d], v[2], v[3], r_uup, r_udown,
        v[4], v[5], r_ma[:, : 3 * d], columns(r_ma, 3), v[6], v[7],
        columns(r_ma, 4), r_ma[:, 6 * d :], columns(r_ma, 5),
        v[8], v[9], r_mup, r_mdown,
    )


def solution(mesh):
    rows1 = P(AXES)
    rows2 = P(AXES, None)
    rows3 = P(AXES, None, None)
    block = (rows1, rows1, rows2, rows2)
    weights = block * 2 + block + (rows1, rows1, rows2, rows2, rows2) + block
    return jax.shard_map(
        local,
        mesh=mesh,
        in_specs=(rows3, rows3, rows1, rows3) + weights,
        out_specs=(rows3, rows3, rows3) + weights,
        check_vma=False,
    )
```

```python
import functools

import jax
import jax.numpy as jnp
from jax import lax
from jax.experimental import pallas as pl
from jax.experimental.pallas import tpu as pltpu
from jax.sharding import PartitionSpec as P

DH = 64
AXES = ("dp", "hd")
EPS = 1e-05
MASKED = -1e30
LANES = 128
bf16 = jnp.bfloat16
f32 = jnp.float32
sds = jax.ShapeDtypeStruct


BIT_PAIR, BIT_CORE, BIT_NEAR = 1, 2, 4


class Place:
    def __init__(self):
        self.count = lax.axis_size("dp") * lax.axis_size("hd")
        self.outer_size = self.count // 8
        index = lax.axis_index("dp") * lax.axis_size("hd") + lax.axis_index("hd")
        self.pair = index % 2
        self.core = (index // 2) % 2
        self.near = (index // 4) % 2
        self.outer = index // 8
        self.outer_bits = self.outer_size.bit_length() - 1

    def swap(self, x, bit):
        return lax.ppermute(x, AXES, [(i, i ^ bit) for i in range(self.count)])

    def swap_by_core(self, x, bits):
        pairs = [(i, i ^ bits[(i // BIT_CORE) % 2]) for i in range(self.count)]
        return lax.ppermute(x, AXES, pairs)

    def order(self, d):
        n, rows = self.outer_size, d // self.count
        k = lax.broadcasted_iota(jnp.int32, (d, 1), 0)
        row, place = k % rows, (k // rows) % n
        outer = jnp.zeros_like(k)
        for b in range(self.outer_bits):
            outer = outer + ((place >> (self.outer_bits - 1 - b)) & 1) * (1 << b)
        outer = outer ^ self.outer
        rest = k // (rows * n)
        low, high = rest % 2, (rest // 2) % 2
        near = jnp.where((rest // 4) ^ self.core == 0, high, low)
        pair = high + low - near
        feature = outer * 2 + (near ^ self.near)
        feature = (feature * 2 + ((rest // 4) ^ self.core)) * 2 + (pair ^ self.pair)
        feature = feature * rows + row
        return (feature == lax.broadcasted_iota(jnp.int32, (d, d), 1)).astype(bf16)


def plus(a, b):
    return (a.astype(f32) + b.astype(f32)).astype(bf16)


class Sum:
    def __init__(self, place, grads):
        self.place, self.stage = place, 0
        self.send, self.kept = grads

    def swap(self):
        if self.stage < 2:
            bits = ((BIT_NEAR, BIT_PAIR), (BIT_PAIR, BIT_NEAR))[self.stage]
            self.got = self.place.swap_by_core(self.send, bits)
        else:
            self.got = self.place.swap(self.send, 8 << (self.stage - 2))

    def sums(self):
        if self.stage < 2:
            self.send, self.kept = half_sums(self.kept, self.got)
        else:
            half = self.kept.shape[0] // 2
            self.send = plus(self.kept[half:], self.got[half:])
            self.kept = plus(self.kept[:half], self.got[:half])
        self.stage += 1

    def total(self):
        return self.kept.astype(f32) + self.got.astype(f32)


class Gather:
    def __init__(self, place, shard):
        self.place, self.x, self.stage = place, shard, 0

    def swap(self):
        outer = self.place.outer_bits
        at = self.stage - outer
        if at < 0:
            self.got = self.place.swap(self.x, 8 << (outer - 1 - self.stage))
        elif at < 2:
            bits = ((BIT_PAIR, BIT_NEAR), (BIT_NEAR, BIT_PAIR))[at]
            self.got = self.place.swap_by_core(self.x, bits)
        else:
            self.got = self.place.swap(self.x, BIT_CORE)

    def join(self):
        self.x = jnp.concatenate((self.x, self.got), axis=0)
        self.stage += 1


def tie(x, *others):
    out = lax.optimization_barrier((x,) + others)
    return out[0], out[1:]


def hold(x, *groups):
    x, terms = tie(x, *[(g.kept, g.got) for g in groups])
    for g, t in zip(groups, terms):
        g.kept, g.got = t
    return x


def need(x, *groups):
    x, send = tie(x, *[g.send for g in groups])
    for g, k in zip(groups, send):
        g.send = k
    return x


def nn(a, b):
    return jnp.dot(a, b, preferred_element_type=f32)


def nt(a, b):
    return lax.dot_general(a, b, (((1,), (1,)), ((), ())), preferred_element_type=f32)


def tn(a, b):
    return lax.dot_general(a, b, (((0,), (0,)), ((), ())), preferred_element_type=f32)


def unit_norm(x):
    centred = x - jnp.mean(x, axis=-1, keepdims=True)
    inv = lax.rsqrt(jnp.mean(centred * centred, axis=-1, keepdims=True) + EPS)
    return centred * inv, inv


def norm_backward(grad, x, gain):
    unit, inv = unit_norm(x)
    du = grad * gain
    dx = inv * (
        du
        - jnp.mean(du, axis=-1, keepdims=True)
        - unit * jnp.mean(du * unit, axis=-1, keepdims=True)
    )
    return dx, jnp.sum(grad * unit, axis=0, keepdims=True), jnp.sum(grad, axis=0, keepdims=True)


GELU_A = 0.7978845608028654
GELU_B = 0.044715


def two_heads(x):
    first = lax.broadcasted_iota(jnp.int32, x.shape, 1) < DH
    zero = jnp.zeros_like(x)
    return jnp.concatenate((jnp.where(first, x, zero), jnp.where(first, zero, x)), axis=0)


def side_by_side(x):
    n = x.shape[0] // 2
    first = lax.broadcasted_iota(jnp.int32, (n, LANES), 1) < DH
    return jnp.where(first, x[:n], x[n:])


def probabilities(qs, k2, allowed):
    s = jnp.where(allowed, nt(qs, k2) * DH ** (-0.5), MASKED)
    e = jnp.exp(s - jnp.max(s, axis=-1, keepdims=True))
    return e / jnp.sum(e, axis=-1, keepdims=True)


def causal_mask(length):
    row = lax.broadcasted_iota(jnp.int32, (2 * length, length), 0)
    col = lax.broadcasted_iota(jnp.int32, (2 * length, length), 1)
    return jnp.where(row >= length, row - length, row) >= col


def attend_back(q2, k2, v2, do2, allowed):
    scale = DH ** (-0.5)
    qs, dos = two_heads(q2), two_heads(do2)
    p = probabilities(qs, k2, allowed)
    dp = nt(dos, v2)
    ds = (p * (dp - jnp.sum(p * dp, axis=-1, keepdims=True))).astype(bf16)
    dq = side_by_side(nn(ds, k2)) * scale
    dk = tn(ds, qs) * scale
    dv = tn(p.astype(bf16), dos)
    return dq.astype(bf16), dk.astype(bf16), dv.astype(bf16)


def self_forward_kernel(captions, row, x_ref, vec_ref, w_ref, y_ref, f_ref, qkv_ref):
    j = pl.program_id(0)

    @pl.when(j == 0)
    def _():
        unit, _inv = unit_norm(x_ref[...].astype(f32))
        f_ref[0] = (unit * vec_ref[row : row + 1] + vec_ref[row + 1 : row + 2]).astype(bf16)

    @pl.when(j < 3)
    def _():
        qkv_ref[j] = nn(f_ref[0], w_ref[...]).astype(bf16)

    @pl.when(j == 3)
    def _():
        length = x_ref.shape[0] // captions
        allowed = causal_mask(length)
        for c in range(captions):
            at = slice(c * length, (c + 1) * length)
            for h in range(0, x_ref.shape[1], LANES):
                cols = slice(h, h + LANES)
                p = probabilities(two_heads(qkv_ref[0, at, cols]), qkv_ref[1, at, cols], allowed)
                o = side_by_side(nn(p.astype(bf16), qkv_ref[2, at, cols]))
                f_ref[1, at, cols] = o.astype(bf16)
        y_ref[...] = x_ref[...].astype(f32) + nn(f_ref[1], w_ref[...])


def self_backward_kernel(
    captions, row, x_ref, vec_ref, qkv_ref, dx_ref, w_ref, *refs
):
    out_ref, vg_ref, p_ref, acc_ref = refs[-4:]
    j = pl.program_id(0)

    @pl.when(j == 0)
    def _():
        dy = dx_ref[...].astype(bf16)
        p_ref[3] = dy
        do = nt(dy, w_ref[...]).astype(bf16)
        length = x_ref.shape[0] // captions
        allowed = causal_mask(length)
        for c in range(captions):
            at = slice(c * length, (c + 1) * length)
            for h in range(0, x_ref.shape[1], LANES):
                cols = slice(h, h + LANES)
                dq, dk, dv = attend_back(
                    qkv_ref[0, at, cols], qkv_ref[1, at, cols], qkv_ref[2, at, cols],
                    do[at, cols], allowed,
                )
                p_ref[0, at, cols] = dq
                p_ref[1, at, cols] = dk
                p_ref[2, at, cols] = dv
        acc_ref[...] = jnp.zeros_like(acc_ref)

    @pl.when(j > 0)
    def _():
        acc_ref[...] += nt(p_ref[j - 1], w_ref[...])

    @pl.when(j == 3)
    def _():
        dn, gg, gs = norm_backward(acc_ref[...], x_ref[...].astype(f32), vec_ref[row : row + 1])
        out_ref[...] = dx_ref[...] + dn
        vg_ref[0:1] = gg
        vg_ref[1:2] = gs
        if len(refs) > 4:
            at = lax.broadcasted_iota(jnp.int32, refs[0].shape, 0)
            rows = jnp.where(at == 0, gg, jnp.where(at == 1, gs, refs[0][...]))
            p_ref[4] = jnp.zeros_like(p_ref[4])
            p_ref[4, 0 : refs[0].shape[0]] = rows.astype(bf16)


def cross_forward_kernel(
    captions, row, count_ref, x_ref, vec_ref, kv_ref, w_ref, y_ref, f_ref, q_ref
):
    j = pl.program_id(0)
    d = x_ref.shape[1]

    @pl.when(j == 0)
    def _():
        unit, _inv = unit_norm(x_ref[...])
        c = (unit * vec_ref[row : row + 1] + vec_ref[row + 1 : row + 2]).astype(bf16)
        f_ref[0] = c
        q_ref[...] = nn(c, w_ref[...]).astype(bf16)

    @pl.when(j == 1)
    def _():
        length = x_ref.shape[0] // captions
        patches = kv_ref.shape[0] // captions
        slot = lax.broadcasted_iota(jnp.int32, (2 * length, patches), 1)
        for c in range(captions):
            at = slice(c * length, (c + 1) * length)
            keys = slice(c * patches, (c + 1) * patches)
            allowed = slot < count_ref[c]
            for h in range(0, d, LANES):
                cols = slice(h, h + LANES)
                vcols = slice(d + h, d + h + LANES)
                p = probabilities(two_heads(q_ref[at, cols]), kv_ref[keys, cols], allowed)
                o = side_by_side(nn(p.astype(bf16), kv_ref[keys, vcols]))
                f_ref[1, at, cols] = o.astype(bf16)
        y_ref[...] = x_ref[...] + nn(f_ref[1], w_ref[...])


def cross_backward_kernel(
    captions, row, count_ref, x_ref, vec_ref, q_ref, kv_ref, dx_ref, w_ref,
    out_ref, vg_ref, p_ref, dkv_ref,
):
    j = pl.program_id(0)
    d = x_ref.shape[1]

    @pl.when(j == 0)
    def _():
        dy = dx_ref[...].astype(bf16)
        p_ref[1] = dy
        do = nt(dy, w_ref[...]).astype(bf16)
        length = x_ref.shape[0] // captions
        patches = kv_ref.shape[0] // captions
        slot = lax.broadcasted_iota(jnp.int32, (2 * length, patches), 1)
        for c in range(captions):
            at = slice(c * length, (c + 1) * length)
            keys = slice(c * patches, (c + 1) * patches)
            allowed = slot < count_ref[c]
            for h in range(0, d, LANES):
                cols = slice(h, h + LANES)
                vcols = slice(d + h, d + h + LANES)
                dq, dk, dv = attend_back(
                    q_ref[at, cols], kv_ref[keys, cols], kv_ref[keys, vcols], do[at, cols], allowed
                )
                p_ref[0, at, cols] = dq
                dkv_ref[keys, cols] = dk
                dkv_ref[keys, vcols] = dv

    @pl.when(j == 1)
    def _():
        dn, gg, gs = norm_backward(nt(p_ref[0], w_ref[...]), x_ref[...], vec_ref[row : row + 1])
        out_ref[...] = dx_ref[...] + dn
        vg_ref[0:1] = gg
        vg_ref[1:2] = gs


def feed_forward_kernel(row, x_ref, vec_ref, up_ref, down_ref, y_ref, f_ref, u_ref):
    j = pl.program_id(0)

    @pl.when(j == 0)
    def _():
        unit, _inv = unit_norm(x_ref[...])
        f_ref[0] = (unit * vec_ref[row : row + 1] + vec_ref[row + 1 : row + 2]).astype(bf16)
        y_ref[...] = x_ref[...]

    u = nn(f_ref[0], up_ref[...])
    u_ref[...] = u
    g = (0.5 * u * (1.0 + jnp.tanh(GELU_A * (u + GELU_B * u * u * u)))).astype(bf16)
    f_ref[1 + j] = g
    y_ref[...] += nn(g, down_ref[...])


def gelu_terms(u):
    t = jnp.tanh(GELU_A * (u + GELU_B * u * u * u))
    slope = 0.5 * (1.0 + t) + 0.5 * u * (1.0 - t * t) * GELU_A * (1.0 + 3.0 * GELU_B * u * u)
    return 0.5 * u * (1.0 + t), slope


def feed_backward_kernel(
    row, x_ref, vec_ref, dx_ref, up_ref, down_ref, u_ref, out_ref, vg_ref, p_ref, acc_ref
):
    j = pl.program_id(0)

    @pl.when(j == 0)
    def _():
        p_ref[0] = dx_ref[...].astype(bf16)
        acc_ref[...] = jnp.zeros_like(acc_ref)

    slope = gelu_terms(u_ref[...])[1]
    du = (slope * nt(p_ref[0], down_ref[...])).astype(bf16)
    p_ref[1 + j] = du
    acc_ref[...] += nt(du, up_ref[...])

    @pl.when(j == 3)
    def _():
        dn, gg, gs = norm_backward(acc_ref[...], x_ref[...], vec_ref[row : row + 1])
        out_ref[...] = dx_ref[...] + dn
        vg_ref[0:1] = gg
        vg_ref[1:2] = gs


def by_rows(x, order_ref, top_ref, low_ref):
    half = top_ref.shape[0]
    x = nt(x, order_ref[...]).astype(bf16)
    return nn(x[:, :half], top_ref[...]) + nn(x[:, half:], low_ref[...])


def last_backward_kernel(
    row, x_ref, vec_ref, order_ref, dx_ref, up_ref, up2_ref, down_ref, down2_ref,
    out_ref, vg_ref, p_ref, f_ref, acc_ref,
):
    j = pl.program_id(0)
    half = up_ref.shape[0]

    @pl.when(j == 0)
    def _():
        unit, _inv = unit_norm(x_ref[...])
        f_ref[0] = (unit * vec_ref[row : row + 1] + vec_ref[row + 1 : row + 2]).astype(bf16)
        p_ref[0] = dx_ref[...]
        acc_ref[...] = jnp.zeros_like(acc_ref)

    g, slope = gelu_terms(by_rows(f_ref[0], order_ref, up_ref, up2_ref))
    f_ref[1 + j] = g.astype(bf16)
    dz = p_ref[0]
    dg = jnp.concatenate((nt(dz, down_ref[...]), nt(dz, down2_ref[...])), axis=1)
    du = (slope * nn(dg.astype(bf16), order_ref[...])).astype(bf16)
    p_ref[1 + j] = du
    acc_ref[:, :half] += nt(du, up_ref[...])
    acc_ref[:, half:] += nt(du, up2_ref[...])

    @pl.when(j == 3)
    def _():
        db = acc_ref[...]
        high = db.astype(bf16)
        low = (db - high.astype(f32)).astype(bf16)
        db = nn(high, order_ref[...]) + nn(low, order_ref[...])
        dn, gg, gs = norm_backward(db, x_ref[...], vec_ref[row : row + 1])
        out_ref[...] = dx_ref[...].astype(f32) + dn
        vg_ref[0:1] = gg
        vg_ref[1:2] = gs


def last_output_kernel(x_ref, order_ref, g_ref, down_ref, down2_ref, y_ref, acc_ref):
    j = pl.program_id(0)

    @pl.when(j == 0)
    def _():
        acc_ref[...] = x_ref[...]

    acc_ref[...] += by_rows(g_ref[0], order_ref, down_ref, down2_ref)

    @pl.when(j == 3)
    def _():
        y_ref[...] = acc_ref[...].astype(bf16)


def both(own_ref, got_ref):
    return jnp.concatenate((own_ref[0], got_ref[0]), axis=0)


def emit(g, send_ref, keep_ref):
    half = keep_ref.shape[0]
    keep_ref[...] = g[:half].astype(bf16)
    send_ref[...] = g[half:].astype(bf16)


def feed_grads_kernel(
    order_ref, b_ref, b2_ref, z_ref, z2_ref, g_ref, g2_ref, u_ref, u2_ref, send_ref, keep_ref, bt_ref
):
    d = order_ref.shape[1]

    @pl.when(pl.program_id(0) == 0)
    def _():
        bt_ref[...] = nt(order_ref[...], both(b_ref, b2_ref)).astype(bf16)

    up, down = (slice(None), slice(0, d)), (slice(None), slice(d, 2 * d))
    emit(nn(bt_ref[...], both(u_ref, u2_ref)), send_ref.at[up], keep_ref.at[up])
    gt = nt(order_ref[...], both(g_ref, g2_ref)).astype(bf16)
    emit(nn(gt, both(z_ref, z2_ref)), send_ref.at[down], keep_ref.at[down])


def attend_grads_kernel(order_ref, s_ref, s2_ref, sd_ref, sd2_ref, *refs):
    send_ref, keep_ref = refs[-2:]
    j = pl.program_id(0)

    def product(a_ref, a2_ref, d_ref, d2_ref):
        at = nt(order_ref[...], both(a_ref, a2_ref)).astype(bf16)
        emit(nn(at, both(d_ref, d2_ref)), send_ref, keep_ref)

    @pl.when(j < 4)
    def _():
        product(s_ref, s2_ref, sd_ref, sd2_ref)

    if len(refs) > 2:
        c_ref, c2_ref, cd_ref, cd2_ref, pair_ref, pair2_ref = refs[:6]

        @pl.when((j == 4) | (j == 5))
        def _():
            product(c_ref, c2_ref, cd_ref, cd2_ref)

        @pl.when(j > 5)
        def _():
            emit(pair_ref[...].astype(f32) + pair2_ref[...].astype(f32), send_ref, keep_ref)


def half_sums_kernel(kept_ref, got_ref, send_ref, keep_ref):
    emit(kept_ref[...].astype(f32) + got_ref[...].astype(f32), send_ref, keep_ref)


def half_sums(kept, got):
    rows, wide = kept.shape
    steps = 2 if wide % (2 * LANES) == 0 else 1
    full = pl.BlockSpec((rows, wide // steps), lambda j: (0, j))
    half = pl.BlockSpec((rows // 2, wide // steps), lambda j: (0, j))
    outs = (sds((rows // 2, wide), bf16),) * 2
    return call(half_sums_kernel, steps, (kept, got), [full] * 2, outs, [half] * 2, vmem=24)


def pair_input_kernel(dkv_ref, k_ref, v_ref, out_ref):
    d = k_ref.shape[0]
    g = nt(dkv_ref[:, :d], k_ref[...]) + nt(dkv_ref[:, d:], v_ref[...])
    out_ref[...] = g.astype(bf16)


def pair_grads_kernel(enc_ref, dkv_ref, keep_ref, send_ref):
    emit(nn(enc_ref[...], dkv_ref[...]), send_ref, keep_ref)


def pack_kernel(u_qkv, u_out, u_up, u_down, m_qkv, m_out, m_up, m_down, c_q, c_pair, c_out, vec, out, feed_out):
    rows, d = u_out.shape
    spread = spread_matrix().astype(bf16)
    i = lax.broadcasted_iota(jnp.int32, (rows, 4 * rows), 0)
    k = lax.broadcasted_iota(jnp.int32, (rows, 4 * rows), 1)

    def attend(at, qkv, w_out):
        out[:, at : at + 3 * d] = qkv[...]
        out[:, at + 3 * d : at + 4 * d] = w_out[...]

    def feed(out, at, up, down):
        for b in range(4 * d // 512):
            y = nn(up[:, b * 512 : (b + 1) * 512], spread).astype(bf16)
            for j in range(4):
                to = at + j * d + b * LANES
                out[:, to : to + LANES] = y[:, j * LANES : (j + 1) * LANES]
        for j in range(4):
            y = nn((k == 4 * i + j).astype(bf16), down[...])
            out[:, at + (4 + j) * d : at + (5 + j) * d] = y.astype(bf16)

    feed(feed_out, 0, m_up, m_down)
    attend(0, u_qkv, u_out)
    feed(out, 4 * d, u_up, u_down)
    attend(12 * d, m_qkv, m_out)
    out[:, 16 * d : 17 * d] = c_q[...]
    out[:, 17 * d : 19 * d] = c_pair[...]
    out[:, 19 * d : 20 * d] = c_out[...]
    eye = lax.broadcasted_iota(jnp.int32, (rows, rows), 0) == lax.broadcasted_iota(jnp.int32, (rows, rows), 1)
    out[:, 20 * d :] = nt(eye.astype(bf16), vec[...]).astype(bf16)


def whole(x):
    return pl.BlockSpec(x.shape, lambda *_: (0,) * len(x.shape))


def call(kernel, steps, ins, in_specs, outs, out_specs, scratch=(), scalars=0, vmem=40):
    return pl.pallas_call(
        kernel,
        out_shape=outs,
        grid_spec=pltpu.PrefetchScalarGridSpec(
            num_scalar_prefetch=scalars,
            grid=(steps,),
            in_specs=in_specs,
            out_specs=out_specs,
            scratch_shapes=scratch,
        ),
        compiler_params=pltpu.CompilerParams(
            dimension_semantics=("arbitrary",), vmem_limit_bytes=vmem << 20
        ),
        cost_estimate=pl.CostEstimate(flops=1000, bytes_accessed=1000, transcendentals=0),
    )(*ins)


class Layers:
    def __init__(self, captions, tokens, d, w, vec, order, count):
        self.captions, self.t, self.d = captions, tokens, d
        self.w, self.vec, self.order, self.count = w, vec, order, count
        self.xs = sds((tokens, d), f32)
        self.hs = sds((tokens, d), bf16)

    def weight(self, index):
        return pl.BlockSpec((self.d, self.d), lambda j, *_: (0, index(j)))

    def self_forward(self, x, at, row):
        outs = (self.xs, sds((2, self.t, self.d), bf16), sds((3, self.t, self.d), bf16))
        return call(
            functools.partial(self_forward_kernel, self.captions, row), 4,
            (x, self.vec, self.w),
            [whole(x), whole(self.vec), self.weight(lambda j: at + j)],
            outs, [whole(o) for o in outs],
        )

    def self_backward(self, x, kept, dx, at, row, vectors=()):
        d, t = self.d, self.t
        outs = (self.xs, sds((8, d), f32), sds((4 + len(vectors), t, d), bf16))
        ins = (x, self.vec, kept, dx)
        return call(
            functools.partial(self_backward_kernel, self.captions, row), 4,
            ins + (self.w,) + vectors,
            [whole(i) for i in ins] + [self.weight(lambda j: at + (j + 3) % 4)]
            + [whole(v) for v in vectors],
            outs, [whole(i) for i in outs],
            scratch=[pltpu.VMEM((t, d), f32)],
        )

    def cross_forward(self, x, kv, at, row):
        outs = (self.xs, sds((2, self.t, self.d), bf16), self.hs)
        return call(
            functools.partial(cross_forward_kernel, self.captions, row), 2,
            (self.count, x, self.vec, kv, self.w),
            [whole(x), whole(self.vec), whole(kv), self.weight(lambda j: at + 3 * j)],
            outs, [whole(o) for o in outs], scalars=1,
        )

    def cross_backward(self, x, kept, kv, dx, at, row):
        d, t = self.d, self.t
        outs = (self.xs, sds((8, d), f32), sds((2, t, d), bf16), sds(kv.shape, bf16))
        ins = (x, self.vec, kept, kv, dx)
        return call(
            functools.partial(cross_backward_kernel, self.captions, row), 2,
            (self.count,) + ins + (self.w,),
            [whole(i) for i in ins] + [self.weight(lambda j: at + 3 - 3 * j)],
            outs, [whole(i) for i in outs], scalars=1,
        )

    def pair_grads(self, enc_t, dkv):
        d = self.d
        outs = (sds((d // 2, 2 * d), bf16),) * 2
        grad = pl.BlockSpec((d // 2, d), lambda j: (0, j))
        return call(
            pair_grads_kernel, 2, (enc_t, dkv),
            [whole(enc_t), pl.BlockSpec((dkv.shape[0], d), lambda j: (0, j))],
            outs, [grad, grad],
        )

    def pair_input(self, dkv, at):
        d, rows = self.d, dkv.shape[0] // self.captions
        out = sds((dkv.shape[0], d), bf16)
        return call(
            pair_input_kernel, self.captions, (dkv, self.w, self.w),
            [pl.BlockSpec((rows, 2 * d), lambda j: (j, 0))]
            + [self.weight(lambda j: at), self.weight(lambda j: at + 1)],
            out, pl.BlockSpec((rows, d), lambda j: (j, 0)),
        )

    def block(self, index):
        return pl.BlockSpec((1, self.t, self.d), lambda j: (index(j), 0, 0))

    def feed_grads(self, f, p):
        d, t = self.d, self.t
        outs = (sds((d // 4, 8 * d), bf16),) * 2
        first, later = self.block(lambda j: 0), self.block(lambda j: 1 + j)
        half = pl.BlockSpec((d // 2, d), lambda j: (0, 0))
        return call(
            feed_grads_kernel, 4, (self.order,) + f + p + f + p,
            [half] + [first] * 4 + [later] * 4,
            outs, [pl.BlockSpec((d // 4, 2 * d), lambda j: (0, j))] * 2,
            scratch=[pltpu.VMEM((d // 2, 2 * t), bf16)],
        )

    def attend_grads(self, f, p, cross=()):
        d, t = self.d, self.t
        steps = 8 if cross else 4
        outs = (sds((d // 4, steps * d), bf16),) * 2
        half = pl.BlockSpec((d // 2, d), lambda j: (0, 0))
        lhs = self.block(lambda j: jnp.minimum(j // 3, 1))
        rhs = self.block(lambda j: jnp.minimum(j, 3))
        ins, specs = (self.order,) + f + p, [half, lhs, lhs, rhs, rhs]
        if cross:
            f, p, pair = cross
            at = self.block(lambda j: jnp.clip(j - 4, 0, 1))
            columns = pl.BlockSpec((d // 2, d), lambda j: (0, jnp.clip(j - 6, 0, 1)))
            ins, specs = ins + f + p + pair, specs + [at] * 4 + [columns] * 2
        return call(
            attend_grads_kernel, steps, ins, specs,
            outs, [pl.BlockSpec((d // 4, d), lambda j: (0, j))] * 2,
        )

    def feed_forward(self, x, at, row):
        d, t = self.d, self.t
        outs = (self.xs, sds((5, t, d), bf16), sds((t, 4 * d), f32))
        return call(
            functools.partial(feed_forward_kernel, row), 4,
            (x, self.vec, self.w, self.w),
            [whole(x), whole(self.vec), self.weight(lambda j: at + j), self.weight(lambda j: at + 4 + j)],
            outs, [whole(outs[0]), whole(outs[1]), pl.BlockSpec((t, d), lambda j: (0, j))],
        )

    def feed_backward(self, x, u, dx, at, row):
        d, t = self.d, self.t
        outs = (self.xs, sds((8, d), f32), sds((5, t, d), bf16))
        return call(
            functools.partial(feed_backward_kernel, row), 4,
            (x, self.vec, dx, self.w, self.w, u),
            [
                whole(x), whole(self.vec), whole(dx),
                self.weight(lambda j: at + j), self.weight(lambda j: at + 4 + j),
                pl.BlockSpec((t, d), lambda j: (0, j)),
            ],
            outs, [whole(i) for i in outs],
            scratch=[pltpu.VMEM((t, d), f32)],
        )

    def last_backward(self, x, dx, w, row):
        d, t = self.d, self.t
        outs = (self.xs, sds((8, d), f32)) + (sds((5, t, d), bf16),) * 2
        ins = (x, self.vec, self.order, dx)
        up = pl.BlockSpec((d // 2, d), lambda j: (0, j))
        down = pl.BlockSpec((d // 2, d), lambda j: (0, 4 + j))
        return call(
            functools.partial(last_backward_kernel, row), 4,
            ins + w + w, [whole(i) for i in ins] + [up, up, down, down],
            outs, [whole(i) for i in outs],
            scratch=[pltpu.VMEM((t, d), f32)],
        )

    def last_output(self, x, f, w):
        down = pl.BlockSpec((self.d // 2, self.d), lambda j: (0, 4 + j))
        return call(
            last_output_kernel, 4, (x, self.order, f) + w,
            [whole(x), whole(self.order), self.block(lambda j: 1 + j), down, down],
            self.hs, whole(self.hs), scratch=[pltpu.VMEM((self.t, self.d), f32)],
        )


def spread_matrix():
    k = lax.broadcasted_iota(jnp.int32, (512, 512), 0)
    n = lax.broadcasted_iota(jnp.int32, (512, 512), 1)
    return (k % 4) * 128 + k // 4 == n


def unspread(up):
    rows, wide = up.shape
    y = up.reshape(rows, 4, wide // 512, 128).transpose(0, 2, 1, 3)
    y = lax.dot_general(
        y.reshape(rows * (wide // 512), 512), spread_matrix().astype(f32),
        (((1,), (1,)), ((), ())), precision=lax.Precision.HIGHEST,
    )
    return y.reshape(rows, wide)


def local(
    tokens, encoder, patch_count, out_grad,
    u_ag, u_as, u_qkv, u_out, u_mg, u_ms, u_up, u_down,
    m_ag, m_as, m_qkv, m_out, c_g, c_s, c_q, c_pair, c_out, m_mg, m_ms, m_up, m_down,
):
    place = Place()
    captions, length, d = tokens.shape
    rows = u_qkv.shape[0]
    x0 = tokens.reshape(-1, d)
    enc = encoder.reshape(-1, d)
    order = place.order(d)

    vectors = (u_ag, u_as, u_mg, u_ms, m_ag, m_as, c_g, c_s, m_mg, m_ms)
    vectors = jnp.pad(jnp.stack(vectors, axis=0), ((0, LANES - len(vectors)), (0, 0)))
    parts = (u_qkv, u_out, u_up, u_down, m_qkv, m_out, m_up, m_down, c_q, c_pair, c_out, vectors)
    packed = sds((rows, 20 * d + LANES), bf16), sds((rows, 8 * d), bf16)
    shard, last = call(
        pack_kernel, 1, parts, [whole(p) for p in parts], packed, [whole(p) for p in packed], vmem=60
    )
    enc_t = nt(order, enc).astype(bf16)
    w = lax.all_gather(shard, AXES, axis=0, tiled=True)

    last = Gather(place, last)
    for _ in range(place.outer_bits + 2):
        last.swap()
        last.join()
    w, (order, enc_t, last.x) = tie(w, order, enc_t, last.x)
    last.swap()
    vec = nt(jnp.eye(16, LANES, dtype=bf16), w[:, 20 * d :])

    net = Layers(captions, captions * length, d, w, vec, order, patch_count)

    kv = nn(enc, w[:, 17 * d : 19 * d]).astype(bf16)
    x0a, f_us, k_us = net.self_forward(x0, 0, 0)
    x1, f_uf, k_uf = net.feed_forward(x0a, 4, 2)
    x1a, f_ms, k_ms = net.self_forward(x1, 12, 4)
    x1a, (last.x, last.got) = tie(x1a, last.x, last.got)
    w_last = last.x, last.got
    x1b, f_mc, k_mc = net.cross_forward(x1a, kv, 16, 6)

    def core(x):
        return place.swap(x, BIT_CORE)

    def go_on(x, sums=(), start=()):
        x = hold(x, *sums)
        for g in sums:
            g.sums()
        x = need(x, *(tuple(sums) + tuple(g for g in start if g not in sums)))
        for g in start:
            g.swap()
        return x

    def rest(x, *groups):
        for _ in range(place.outer_bits - 1):
            for g in groups:
                x = go_on(x, [g], [g])
        return x

    def pairs(x):
        return x, core(x)

    f_us, f_uf, f_ms = pairs(f_us), pairs(f_uf), pairs(f_ms)
    x1b, (f_us, f_uf, f_ms) = tie(x1b, f_us, f_uf, f_ms)
    f_mc = pairs(f_mc)
    dx, v_mf, p, f = net.last_backward(x1b, out_grad.reshape(-1, d), w_last, 8)
    p, f = pairs(p), pairs(f)
    x2 = net.last_output(x1b, f[0], w_last)
    p, (x2,) = tie(p, x2)
    s_mf = Sum(place, net.feed_grads(f, p))
    dx, (f_mc,) = tie(dx, f_mc)
    dx = go_on(dx, start=[s_mf])
    dx, v_mc, p_c, dkv = net.cross_backward(x1a, k_mc, kv, dx, 16, 6)
    p_c = pairs(p_c)
    pair, send = net.pair_grads(enc_t, dkv)
    dx, (send,) = tie(dx, send)
    pair = pair, core(send)
    dx, v_ms, p = net.self_backward(x1, k_ms, dx, 12, 4)
    p = pairs(p)
    dx = go_on(dx, [s_mf], [s_mf])
    dx, (p, p_c, pair) = tie(dx, p, p_c, pair)
    s_ma = Sum(place, net.attend_grads(f_ms, p, (f_mc, p_c, pair)))
    dx = go_on(dx, start=[s_ma])
    dx, v_uf, p = net.feed_backward(x0a, k_uf, dx, 4, 2)
    p = pairs(p)
    dx, (p,) = tie(dx, p)
    s_uf = Sum(place, net.feed_grads(f_uf, p))
    dx = need(dx, s_uf)
    v = [g[:2] for g in (v_uf, v_ms, v_mc, v_mf)]
    v = jnp.pad(jnp.concatenate(v, axis=0), ((2, 6), (0, 0)))
    dx, _v, p = net.self_backward(x0, k_us, dx, 0, 0, (v,))
    p = pairs(p)
    dx = go_on(dx, [s_mf], [s_uf, s_mf])
    dx = go_on(dx, [s_ma], [s_ma])
    dx, (dkv,) = tie(dx, dkv)
    denc = net.pair_input(dkv, 17)
    dx, (denc,) = tie(dx, denc)
    dx = rest(dx, s_mf)
    dx, (p,) = tie(dx, p)
    send, keep = net.attend_grads(f_us, p)
    v = nt(order[: d // 2], plus(p[0][4], p[1][4])[:LANES]).astype(bf16)
    send = jnp.concatenate((send, v[d // 4 :]), axis=1)
    keep = jnp.concatenate((keep, v[: d // 4]), axis=1)
    s_us = Sum(place, (send, keep))
    dx = need(dx, s_us)
    dx = go_on(dx, [s_ma], [s_ma])
    dx = go_on(dx, [s_uf], [s_uf, s_us])
    dx, (r_mf,) = tie(dx, s_mf.total())
    dx = rest(dx, s_ma)
    dx = go_on(dx, [s_uf], [s_uf])
    dx = go_on(dx, [s_us], [s_us])
    dx, (r_ma,) = tie(dx, s_ma.total())
    dx = rest(dx, s_uf)
    dx = go_on(dx, [s_us], [s_us])
    dx, (r_uf,) = tie(dx, s_uf.total())
    dx = rest(dx, s_us)
    r_us = s_us.total()

    def columns(r, *blocks):
        parts = [r[:, b * d : (b + 1) * d] for b in blocks]
        return jnp.concatenate(parts, axis=1) if len(parts) > 1 else parts[0]

    def feed_rows(r):
        return unspread(columns(r, 0, 2, 4, 6)), columns(r, 1, 3, 5, 7).reshape(-1, d)

    r_uup, r_udown = feed_rows(r_uf)
    r_mup, r_mdown = feed_rows(r_mf)
    vs = r_us[:, 4 * d :]
    v = [vs[:, i] for i in range(10)]
    return (
        x2.reshape(tokens.shape),
        dx.astype(bf16).reshape(tokens.shape),
        denc.reshape(encoder.shape),
        v[0], v[1], r_us[:, : 3 * d], r_us[:, 3 * d : 4 * d], v[2], v[3], r_uup, r_udown,
        v[4], v[5], r_ma[:, : 3 * d], columns(r_ma, 3), v[6], v[7],
        columns(r_ma, 4), r_ma[:, 6 * d :], columns(r_ma, 5),
        v[8], v[9], r_mup, r_mdown,
    )


def solution(mesh):
    rows1 = P(AXES)
    rows2 = P(AXES, None)
    rows3 = P(AXES, None, None)
    block = (rows1, rows1, rows2, rows2)
    weights = block * 2 + block + (rows1, rows1, rows2, rows2, rows2) + block
    return jax.shard_map(
        local,
        mesh=mesh,
        in_specs=(rows3, rows3, rows1, rows3) + weights,
        out_specs=(rows3, rows3, rows3) + weights,
        check_vma=False,
    )
```

```python
import functools

import jax
import jax.numpy as jnp
from jax import lax
from jax.experimental import pallas as pl
from jax.experimental.pallas import tpu as pltpu
from jax.sharding import PartitionSpec as P

DH = 64
AXES = ("dp", "hd")
EPS = 1e-05
MASKED = -1e30
LANES = 128
bf16 = jnp.bfloat16
f32 = jnp.float32
sds = jax.ShapeDtypeStruct


BIT_PAIR, BIT_CORE, BIT_NEAR = 1, 2, 4


class Place:
    def __init__(self):
        self.count = lax.axis_size("dp") * lax.axis_size("hd")
        self.outer_size = self.count // 8
        index = lax.axis_index("dp") * lax.axis_size("hd") + lax.axis_index("hd")
        self.pair = index % 2
        self.core = (index // 2) % 2
        self.near = (index // 4) % 2
        self.outer = index // 8
        self.outer_bits = self.outer_size.bit_length() - 1

    def swap(self, x, bit):
        return lax.ppermute(x, AXES, [(i, i ^ bit) for i in range(self.count)])

    def swap_by_core(self, x, bits):
        pairs = [(i, i ^ bits[(i // BIT_CORE) % 2]) for i in range(self.count)]
        return lax.ppermute(x, AXES, pairs)

    def order(self, d):
        n, rows = self.outer_size, d // self.count
        k = lax.broadcasted_iota(jnp.int32, (d, 1), 0)
        row, place = k % rows, (k // rows) % n
        outer = jnp.zeros_like(k)
        for b in range(self.outer_bits):
            outer = outer + ((place >> (self.outer_bits - 1 - b)) & 1) * (1 << b)
        outer = outer ^ self.outer
        rest = k // (rows * n)
        low, high = rest % 2, (rest // 2) % 2
        near = jnp.where((rest // 4) ^ self.core == 0, high, low)
        pair = high + low - near
        feature = outer * 2 + (near ^ self.near)
        feature = (feature * 2 + ((rest // 4) ^ self.core)) * 2 + (pair ^ self.pair)
        feature = feature * rows + row
        return (feature == lax.broadcasted_iota(jnp.int32, (d, d), 1)).astype(bf16)


def plus(a, b):
    return (a.astype(f32) + b.astype(f32)).astype(bf16)


class Sum:
    def __init__(self, place, grads):
        self.place, self.stage = place, 0
        self.send, self.kept = grads

    def swap(self):
        if self.stage < 2:
            bits = ((BIT_NEAR, BIT_PAIR), (BIT_PAIR, BIT_NEAR))[self.stage]
            self.got = self.place.swap_by_core(self.send, bits)
        else:
            self.got = self.place.swap(self.send, 8 << (self.stage - 2))

    def sums(self):
        if self.stage < 2:
            self.send, self.kept = half_sums(self.kept, self.got)
        else:
            half = self.kept.shape[0] // 2
            self.send = plus(self.kept[half:], self.got[half:])
            self.kept = plus(self.kept[:half], self.got[:half])
        self.stage += 1

    def total(self):
        return self.kept.astype(f32) + self.got.astype(f32)


class Gather:
    def __init__(self, place, shard):
        self.place, self.x, self.stage = place, shard, 0

    def swap(self):
        outer = self.place.outer_bits
        at = self.stage - outer
        if at < 0:
            self.got = self.place.swap(self.x, 8 << (outer - 1 - self.stage))
        elif at < 2:
            bits = ((BIT_PAIR, BIT_NEAR), (BIT_NEAR, BIT_PAIR))[at]
            self.got = self.place.swap_by_core(self.x, bits)
        else:
            self.got = self.place.swap(self.x, BIT_CORE)

    def join(self):
        self.x = jnp.concatenate((self.x, self.got), axis=0)
        self.stage += 1


def tie(x, *others):
    out = lax.optimization_barrier((x,) + others)
    return out[0], out[1:]


def hold(x, *groups):
    x, terms = tie(x, *[(g.kept, g.got) for g in groups])
    for g, t in zip(groups, terms):
        g.kept, g.got = t
    return x


def need(x, *groups):
    x, send = tie(x, *[g.send for g in groups])
    for g, k in zip(groups, send):
        g.send = k
    return x


def nn(a, b):
    return jnp.dot(a, b, preferred_element_type=f32)


def nt(a, b):
    return lax.dot_general(a, b, (((1,), (1,)), ((), ())), preferred_element_type=f32)


def tn(a, b):
    return lax.dot_general(a, b, (((0,), (0,)), ((), ())), preferred_element_type=f32)


def unit_norm(x):
    centred = x - jnp.mean(x, axis=-1, keepdims=True)
    inv = lax.rsqrt(jnp.mean(centred * centred, axis=-1, keepdims=True) + EPS)
    return centred * inv, inv


def norm_backward(grad, x, gain):
    unit, inv = unit_norm(x)
    du = grad * gain
    dx = inv * (
        du
        - jnp.mean(du, axis=-1, keepdims=True)
        - unit * jnp.mean(du * unit, axis=-1, keepdims=True)
    )
    return dx, jnp.sum(grad * unit, axis=0, keepdims=True), jnp.sum(grad, axis=0, keepdims=True)


GELU_A = 0.7978845608028654
GELU_B = 0.044715


def two_heads(x):
    first = lax.broadcasted_iota(jnp.int32, x.shape, 1) < DH
    zero = jnp.zeros_like(x)
    return jnp.concatenate((jnp.where(first, x, zero), jnp.where(first, zero, x)), axis=0)


def side_by_side(x):
    n = x.shape[0] // 2
    first = lax.broadcasted_iota(jnp.int32, (n, LANES), 1) < DH
    return jnp.where(first, x[:n], x[n:])


def probabilities(qs, k2, allowed):
    s = jnp.where(allowed, nt(qs, k2) * DH ** (-0.5), MASKED)
    e = jnp.exp(s - jnp.max(s, axis=-1, keepdims=True))
    return e / jnp.sum(e, axis=-1, keepdims=True)


def causal_mask(length):
    row = lax.broadcasted_iota(jnp.int32, (2 * length, length), 0)
    col = lax.broadcasted_iota(jnp.int32, (2 * length, length), 1)
    return jnp.where(row >= length, row - length, row) >= col


def attend_back(q2, k2, v2, do2, allowed):
    scale = DH ** (-0.5)
    qs, dos = two_heads(q2), two_heads(do2)
    p = probabilities(qs, k2, allowed)
    dp = nt(dos, v2)
    ds = (p * (dp - jnp.sum(p * dp, axis=-1, keepdims=True))).astype(bf16)
    dq = side_by_side(nn(ds, k2)) * scale
    dk = tn(ds, qs) * scale
    dv = tn(p.astype(bf16), dos)
    return dq.astype(bf16), dk.astype(bf16), dv.astype(bf16)


def relative(x, order_ref):
    return nt(x, order_ref[...]).astype(bf16)


def times(x, top_ref, low_ref):
    half = top_ref.shape[0]
    return nn(x[:, :half], top_ref[...]) + nn(x[:, half:], low_ref[...])


def times_back(g, top_ref, low_ref):
    return jnp.concatenate((nt(g, top_ref[...]), nt(g, low_ref[...])), axis=1)


def natural(x, order_ref):
    high = x.astype(bf16)
    low = (x - high.astype(f32)).astype(bf16)
    return nn(high, order_ref[...]) + nn(low, order_ref[...])


def self_forward_kernel(
    captions, row, x_ref, vec_ref, order_ref, top_ref, low_ref, y_ref, f_ref, qkv_ref, rel_ref
):
    j = pl.program_id(0)

    @pl.when(j == 0)
    def _():
        unit, _inv = unit_norm(x_ref[...].astype(f32))
        f_ref[0] = (unit * vec_ref[row : row + 1] + vec_ref[row + 1 : row + 2]).astype(bf16)
        rel_ref[...] = relative(f_ref[0], order_ref)

    @pl.when(j < 3)
    def _():
        qkv_ref[j] = times(rel_ref[...], top_ref, low_ref).astype(bf16)

    @pl.when(j == 3)
    def _():
        length = x_ref.shape[0] // captions
        allowed = causal_mask(length)
        for c in range(captions):
            at = slice(c * length, (c + 1) * length)
            for h in range(0, x_ref.shape[1], LANES):
                cols = slice(h, h + LANES)
                p = probabilities(two_heads(qkv_ref[0, at, cols]), qkv_ref[1, at, cols], allowed)
                o = side_by_side(nn(p.astype(bf16), qkv_ref[2, at, cols]))
                f_ref[1, at, cols] = o.astype(bf16)
        y_ref[...] = x_ref[...].astype(f32) + times(relative(f_ref[1], order_ref), top_ref, low_ref)


def self_backward_kernel(
    captions, row, x_ref, vec_ref, order_ref, qkv_ref, dx_ref, top_ref, low_ref, *refs
):
    out_ref, vg_ref, p_ref, acc_ref = refs[-4:]
    j = pl.program_id(0)

    @pl.when(j == 0)
    def _():
        dy = dx_ref[...].astype(bf16)
        p_ref[3] = dy
        do = times_back(dy, top_ref, low_ref).astype(bf16)
        do = nn(do, order_ref[...]).astype(bf16)
        length = x_ref.shape[0] // captions
        allowed = causal_mask(length)
        for c in range(captions):
            at = slice(c * length, (c + 1) * length)
            for h in range(0, x_ref.shape[1], LANES):
                cols = slice(h, h + LANES)
                dq, dk, dv = attend_back(
                    qkv_ref[0, at, cols], qkv_ref[1, at, cols], qkv_ref[2, at, cols],
                    do[at, cols], allowed,
                )
                p_ref[0, at, cols] = dq
                p_ref[1, at, cols] = dk
                p_ref[2, at, cols] = dv
        acc_ref[...] = jnp.zeros_like(acc_ref)

    @pl.when(j > 0)
    def _():
        acc_ref[...] += times_back(p_ref[j - 1], top_ref, low_ref)

    @pl.when(j == 3)
    def _():
        da = natural(acc_ref[...], order_ref)
        dn, gg, gs = norm_backward(da, x_ref[...].astype(f32), vec_ref[row : row + 1])
        out_ref[...] = dx_ref[...] + dn
        vg_ref[0:1] = gg
        vg_ref[1:2] = gs
        if len(refs) > 4:
            at = lax.broadcasted_iota(jnp.int32, refs[0].shape, 0)
            rows = jnp.where(at == 0, gg, jnp.where(at == 1, gs, refs[0][...]))
            p_ref[4] = jnp.zeros_like(p_ref[4])
            p_ref[4, 0 : refs[0].shape[0]] = rows.astype(bf16)


def cross_forward_kernel(
    captions, row, count_ref, x_ref, vec_ref, order_ref, kv_ref, top_ref, low_ref, y_ref, f_ref, q_ref
):
    j = pl.program_id(0)
    d = x_ref.shape[1]

    @pl.when(j == 0)
    def _():
        unit, _inv = unit_norm(x_ref[...])
        c = (unit * vec_ref[row : row + 1] + vec_ref[row + 1 : row + 2]).astype(bf16)
        f_ref[0] = c
        q_ref[...] = times(relative(c, order_ref), top_ref, low_ref).astype(bf16)

    @pl.when(j == 1)
    def _():
        length = x_ref.shape[0] // captions
        patches = kv_ref.shape[0] // captions
        slot = lax.broadcasted_iota(jnp.int32, (2 * length, patches), 1)
        for c in range(captions):
            at = slice(c * length, (c + 1) * length)
            keys = slice(c * patches, (c + 1) * patches)
            allowed = slot < count_ref[c]
            for h in range(0, d, LANES):
                cols = slice(h, h + LANES)
                vcols = slice(d + h, d + h + LANES)
                p = probabilities(two_heads(q_ref[at, cols]), kv_ref[keys, cols], allowed)
                o = side_by_side(nn(p.astype(bf16), kv_ref[keys, vcols]))
                f_ref[1, at, cols] = o.astype(bf16)
        y_ref[...] = x_ref[...] + times(relative(f_ref[1], order_ref), top_ref, low_ref)


def cross_backward_kernel(
    captions, row, count_ref, x_ref, vec_ref, order_ref, q_ref, kv_ref, dx_ref, top_ref, low_ref,
    out_ref, vg_ref, p_ref, dkv_ref,
):
    j = pl.program_id(0)
    d = x_ref.shape[1]

    @pl.when(j == 0)
    def _():
        dy = dx_ref[...].astype(bf16)
        p_ref[1] = dy
        do = times_back(dy, top_ref, low_ref).astype(bf16)
        do = nn(do, order_ref[...]).astype(bf16)
        length = x_ref.shape[0] // captions
        patches = kv_ref.shape[0] // captions
        slot = lax.broadcasted_iota(jnp.int32, (2 * length, patches), 1)
        for c in range(captions):
            at = slice(c * length, (c + 1) * length)
            keys = slice(c * patches, (c + 1) * patches)
            allowed = slot < count_ref[c]
            for h in range(0, d, LANES):
                cols = slice(h, h + LANES)
                vcols = slice(d + h, d + h + LANES)
                dq, dk, dv = attend_back(
                    q_ref[at, cols], kv_ref[keys, cols], kv_ref[keys, vcols], do[at, cols], allowed
                )
                p_ref[0, at, cols] = dq
                dkv_ref[keys, cols] = dk
                dkv_ref[keys, vcols] = dv

    @pl.when(j == 1)
    def _():
        dc = natural(times_back(p_ref[0], top_ref, low_ref), order_ref)
        dn, gg, gs = norm_backward(dc, x_ref[...], vec_ref[row : row + 1])
        out_ref[...] = dx_ref[...] + dn
        vg_ref[0:1] = gg
        vg_ref[1:2] = gs


def feed_forward_kernel(
    row, x_ref, vec_ref, order_ref, up_ref, up2_ref, down_ref, down2_ref, y_ref, f_ref, u_ref, rel_ref
):
    j = pl.program_id(0)

    @pl.when(j == 0)
    def _():
        unit, _inv = unit_norm(x_ref[...])
        f_ref[0] = (unit * vec_ref[row : row + 1] + vec_ref[row + 1 : row + 2]).astype(bf16)
        rel_ref[...] = relative(f_ref[0], order_ref)
        y_ref[...] = x_ref[...]

    u = times(rel_ref[...], up_ref, up2_ref)
    u_ref[...] = u
    g = (0.5 * u * (1.0 + jnp.tanh(GELU_A * (u + GELU_B * u * u * u)))).astype(bf16)
    f_ref[1 + j] = g
    y_ref[...] += times(relative(g, order_ref), down_ref, down2_ref)


def gelu_terms(u):
    t = jnp.tanh(GELU_A * (u + GELU_B * u * u * u))
    slope = 0.5 * (1.0 + t) + 0.5 * u * (1.0 - t * t) * GELU_A * (1.0 + 3.0 * GELU_B * u * u)
    return 0.5 * u * (1.0 + t), slope


def feed_backward_step(j, order_ref, slope, refs, p_ref, acc_ref):
    up_ref, up2_ref, down_ref, down2_ref = refs
    dg = times_back(p_ref[0], down_ref, down2_ref).astype(bf16)
    du = (slope * nn(dg, order_ref[...])).astype(bf16)
    p_ref[1 + j] = du
    acc_ref[...] += times_back(du, up_ref, up2_ref)


def feed_backward_end(row, order_ref, x_ref, vec_ref, dx_ref, acc_ref, out_ref, vg_ref):
    db = natural(acc_ref[...], order_ref)
    dn, gg, gs = norm_backward(db, x_ref[...], vec_ref[row : row + 1])
    out_ref[...] = dx_ref[...].astype(f32) + dn
    vg_ref[0:1] = gg
    vg_ref[1:2] = gs


def feed_backward_kernel(
    row, x_ref, vec_ref, order_ref, dx_ref, up_ref, up2_ref, down_ref, down2_ref, u_ref,
    out_ref, vg_ref, p_ref, acc_ref,
):
    j = pl.program_id(0)

    @pl.when(j == 0)
    def _():
        p_ref[0] = dx_ref[...].astype(bf16)
        acc_ref[...] = jnp.zeros_like(acc_ref)

    refs = up_ref, up2_ref, down_ref, down2_ref
    feed_backward_step(j, order_ref, gelu_terms(u_ref[...])[1], refs, p_ref, acc_ref)

    @pl.when(j == 3)
    def _():
        feed_backward_end(row, order_ref, x_ref, vec_ref, dx_ref, acc_ref, out_ref, vg_ref)


def last_backward_kernel(
    row, x_ref, vec_ref, order_ref, dx_ref, up_ref, up2_ref, down_ref, down2_ref,
    out_ref, vg_ref, p_ref, f_ref, acc_ref, rel_ref,
):
    j = pl.program_id(0)

    @pl.when(j == 0)
    def _():
        unit, _inv = unit_norm(x_ref[...])
        f_ref[0] = (unit * vec_ref[row : row + 1] + vec_ref[row + 1 : row + 2]).astype(bf16)
        rel_ref[...] = relative(f_ref[0], order_ref)
        p_ref[0] = dx_ref[...]
        acc_ref[...] = jnp.zeros_like(acc_ref)

    g, slope = gelu_terms(times(rel_ref[...], up_ref, up2_ref))
    f_ref[1 + j] = g.astype(bf16)
    refs = up_ref, up2_ref, down_ref, down2_ref
    feed_backward_step(j, order_ref, slope, refs, p_ref, acc_ref)

    @pl.when(j == 3)
    def _():
        feed_backward_end(row, order_ref, x_ref, vec_ref, dx_ref, acc_ref, out_ref, vg_ref)


def last_output_kernel(x_ref, order_ref, g_ref, down_ref, down2_ref, y_ref, acc_ref):
    j = pl.program_id(0)

    @pl.when(j == 0)
    def _():
        acc_ref[...] = x_ref[...]

    acc_ref[...] += times(relative(g_ref[0], order_ref), down_ref, down2_ref)

    @pl.when(j == 3)
    def _():
        y_ref[...] = acc_ref[...].astype(bf16)


def both(own_ref, got_ref):
    return jnp.concatenate((own_ref[0], got_ref[0]), axis=0)


def emit(g, send_ref, keep_ref):
    half = keep_ref.shape[0]
    keep_ref[...] = g[:half].astype(bf16)
    send_ref[...] = g[half:].astype(bf16)


def feed_grads_kernel(
    order_ref, b_ref, b2_ref, z_ref, z2_ref, g_ref, g2_ref, u_ref, u2_ref, send_ref, keep_ref, bt_ref
):
    d = order_ref.shape[1]

    @pl.when(pl.program_id(0) == 0)
    def _():
        bt_ref[...] = nt(order_ref[...], both(b_ref, b2_ref)).astype(bf16)

    up, down = (slice(None), slice(0, d)), (slice(None), slice(d, 2 * d))
    emit(nn(bt_ref[...], both(u_ref, u2_ref)), send_ref.at[up], keep_ref.at[up])
    gt = nt(order_ref[...], both(g_ref, g2_ref)).astype(bf16)
    emit(nn(gt, both(z_ref, z2_ref)), send_ref.at[down], keep_ref.at[down])


def attend_grads_kernel(order_ref, s_ref, s2_ref, sd_ref, sd2_ref, *refs):
    send_ref, keep_ref = refs[-2:]
    j = pl.program_id(0)

    def product(a_ref, a2_ref, d_ref, d2_ref):
        at = nt(order_ref[...], both(a_ref, a2_ref)).astype(bf16)
        emit(nn(at, both(d_ref, d2_ref)), send_ref, keep_ref)

    @pl.when(j < 4)
    def _():
        product(s_ref, s2_ref, sd_ref, sd2_ref)

    if len(refs) > 2:
        c_ref, c2_ref, cd_ref, cd2_ref, pair_ref, pair2_ref = refs[:6]

        @pl.when((j == 4) | (j == 5))
        def _():
            product(c_ref, c2_ref, cd_ref, cd2_ref)

        @pl.when(j > 5)
        def _():
            emit(pair_ref[...].astype(f32) + pair2_ref[...].astype(f32), send_ref, keep_ref)


def half_sums_kernel(kept_ref, got_ref, send_ref, keep_ref):
    emit(kept_ref[...].astype(f32) + got_ref[...].astype(f32), send_ref, keep_ref)


def half_sums(kept, got):
    rows, wide = kept.shape
    steps = 2 if wide % (2 * LANES) == 0 else 1
    full = pl.BlockSpec((rows, wide // steps), lambda j: (0, j))
    half = pl.BlockSpec((rows // 2, wide // steps), lambda j: (0, j))
    outs = (sds((rows // 2, wide), bf16),) * 2
    return call(half_sums_kernel, steps, (kept, got), [full] * 2, outs, [half] * 2, vmem=24)


def pair_forward_kernel(enc_ref, top_ref, low_ref, kv_ref):
    kv_ref[...] = times(enc_ref[...], top_ref, low_ref).astype(bf16)


def pair_input_kernel(dkv_ref, order_ref, top_ref, low_ref, out_ref):
    g = times_back(dkv_ref[...], top_ref, low_ref).astype(bf16)
    out_ref[...] = nn(g, order_ref[...]).astype(bf16)


def pair_grads_kernel(enc_ref, dkv_ref, keep_ref, send_ref):
    emit(nn(enc_ref[...], dkv_ref[...]), send_ref, keep_ref)


def pack_kernel(
    u_qkv, u_out, u_up, u_down, m_qkv, m_out, m_up, m_down, c_q, c_pair, c_out, vec,
    first_out, feed_out, middle_out, last_out,
):
    rows, d = u_out.shape
    spread = spread_matrix().astype(bf16)
    i = lax.broadcasted_iota(jnp.int32, (rows, 4 * rows), 0)
    k = lax.broadcasted_iota(jnp.int32, (rows, 4 * rows), 1)

    def feed(out, up, down):
        for b in range(4 * d // 512):
            y = nn(up[:, b * 512 : (b + 1) * 512], spread).astype(bf16)
            for j in range(4):
                to = j * d + b * LANES
                out[:, to : to + LANES] = y[:, j * LANES : (j + 1) * LANES]
        for j in range(4):
            y = nn((k == 4 * i + j).astype(bf16), down[...])
            out[:, (4 + j) * d : (5 + j) * d] = y.astype(bf16)

    first_out[:, : 3 * d] = u_qkv[...]
    first_out[:, 3 * d : 4 * d] = u_out[...]
    eye = lax.broadcasted_iota(jnp.int32, (rows, rows), 0) == lax.broadcasted_iota(jnp.int32, (rows, rows), 1)
    first_out[:, 4 * d :] = nt(eye.astype(bf16), vec[...]).astype(bf16)
    feed(feed_out, u_up, u_down)
    middle_out[:, : 2 * d] = c_pair[...]
    middle_out[:, 2 * d : 3 * d] = c_q[...]
    middle_out[:, 3 * d : 4 * d] = c_out[...]
    middle_out[:, 4 * d : 7 * d] = m_qkv[...]
    middle_out[:, 7 * d : 8 * d] = m_out[...]
    feed(last_out, m_up, m_down)


def whole(x):
    return pl.BlockSpec(x.shape, lambda *_: (0,) * len(x.shape))


def call(kernel, steps, ins, in_specs, outs, out_specs, scratch=(), scalars=0, vmem=40):
    return pl.pallas_call(
        kernel,
        out_shape=outs,
        grid_spec=pltpu.PrefetchScalarGridSpec(
            num_scalar_prefetch=scalars,
            grid=(steps,),
            in_specs=in_specs,
            out_specs=out_specs,
            scratch_shapes=scratch,
        ),
        compiler_params=pltpu.CompilerParams(
            dimension_semantics=("arbitrary",), vmem_limit_bytes=vmem << 20
        ),
        cost_estimate=pl.CostEstimate(flops=1000, bytes_accessed=1000, transcendentals=0),
    )(*ins)


class Layers:
    def __init__(self, captions, tokens, d, vec, order, count):
        self.captions, self.t, self.d = captions, tokens, d
        self.vec, self.order, self.count = vec, order, count
        self.xs = sds((tokens, d), f32)
        self.hs = sds((tokens, d), bf16)

    def weights(self, *columns):
        d = self.d
        specs = [pl.BlockSpec((d // 2, d), lambda j, *_, c=c: (0, c(j))) for c in columns]
        return [s for s in specs for _ in range(2)]

    def self_forward(self, x, w, at, row):
        outs = (self.xs, sds((2, self.t, self.d), bf16), sds((3, self.t, self.d), bf16))
        ins = (x, self.vec, self.order)
        return call(
            functools.partial(self_forward_kernel, self.captions, row), 4,
            ins + w, [whole(i) for i in ins] + self.weights(lambda j: at + j),
            outs, [whole(o) for o in outs], scratch=[pltpu.VMEM((self.t, self.d), bf16)],
        )

    def self_backward(self, x, kept, dx, w, at, row, vectors=()):
        d, t = self.d, self.t
        outs = (self.xs, sds((8, d), f32), sds((4 + len(vectors), t, d), bf16))
        ins = (x, self.vec, self.order, kept, dx)
        return call(
            functools.partial(self_backward_kernel, self.captions, row), 4,
            ins + w + vectors,
            [whole(i) for i in ins] + self.weights(lambda j: at + (j + 3) % 4)
            + [whole(v) for v in vectors],
            outs, [whole(i) for i in outs],
            scratch=[pltpu.VMEM((t, d), f32)],
        )

    def cross_forward(self, x, kv, w, at, row):
        outs = (self.xs, sds((2, self.t, self.d), bf16), self.hs)
        ins = (x, self.vec, self.order, kv)
        return call(
            functools.partial(cross_forward_kernel, self.captions, row), 2,
            (self.count,) + ins + w,
            [whole(i) for i in ins] + self.weights(lambda j: at + j),
            outs, [whole(o) for o in outs], scalars=1,
        )

    def cross_backward(self, x, kept, kv, dx, w, at, row):
        d, t = self.d, self.t
        outs = (self.xs, sds((8, d), f32), sds((2, t, d), bf16), sds(kv.shape, bf16))
        ins = (x, self.vec, self.order, kept, kv, dx)
        return call(
            functools.partial(cross_backward_kernel, self.captions, row), 2,
            (self.count,) + ins + w,
            [whole(i) for i in ins] + self.weights(lambda j: at + 1 - j),
            outs, [whole(i) for i in outs], scalars=1,
        )

    def pair_forward(self, enc, w):
        d, rows = self.d, enc.shape[0] // self.captions
        half = pl.BlockSpec((d // 2, 2 * d), lambda j: (0, 0))
        out = sds((enc.shape[0], 2 * d), bf16)
        return call(
            pair_forward_kernel, self.captions, (enc,) + w,
            [pl.BlockSpec((rows, d), lambda j: (j, 0)), half, half],
            out, pl.BlockSpec((rows, 2 * d), lambda j: (j, 0)),
        )

    def pair_grads(self, enc_t, dkv):
        d = self.d
        outs = (sds((d // 2, 2 * d), bf16),) * 2
        grad = pl.BlockSpec((d // 2, d), lambda j: (0, j))
        return call(
            pair_grads_kernel, 2, (enc_t, dkv),
            [whole(enc_t), pl.BlockSpec((dkv.shape[0], d), lambda j: (0, j))],
            outs, [grad, grad],
        )

    def pair_input(self, dkv, w):
        d, rows = self.d, dkv.shape[0] // self.captions
        half = pl.BlockSpec((d // 2, 2 * d), lambda j: (0, 0))
        out = sds((dkv.shape[0], d), bf16)
        return call(
            pair_input_kernel, self.captions, (dkv, self.order) + w,
            [pl.BlockSpec((rows, 2 * d), lambda j: (j, 0)), whole(self.order), half, half],
            out, pl.BlockSpec((rows, d), lambda j: (j, 0)),
        )

    def block(self, index):
        return pl.BlockSpec((1, self.t, self.d), lambda j: (index(j), 0, 0))

    def feed_grads(self, f, p):
        d, t = self.d, self.t
        outs = (sds((d // 4, 8 * d), bf16),) * 2
        first, later = self.block(lambda j: 0), self.block(lambda j: 1 + j)
        half = pl.BlockSpec((d // 2, d), lambda j: (0, 0))
        return call(
            feed_grads_kernel, 4, (self.order,) + f + p + f + p,
            [half] + [first] * 4 + [later] * 4,
            outs, [pl.BlockSpec((d // 4, 2 * d), lambda j: (0, j))] * 2,
            scratch=[pltpu.VMEM((d // 2, 2 * t), bf16)],
        )

    def attend_grads(self, f, p, cross=()):
        d, t = self.d, self.t
        steps = 8 if cross else 4
        outs = (sds((d // 4, steps * d), bf16),) * 2
        half = pl.BlockSpec((d // 2, d), lambda j: (0, 0))
        lhs = self.block(lambda j: jnp.minimum(j // 3, 1))
        rhs = self.block(lambda j: jnp.minimum(j, 3))
        ins, specs = (self.order,) + f + p, [half, lhs, lhs, rhs, rhs]
        if cross:
            f, p, pair = cross
            at = self.block(lambda j: jnp.clip(j - 4, 0, 1))
            columns = pl.BlockSpec((d // 2, d), lambda j: (0, jnp.clip(j - 6, 0, 1)))
            ins, specs = ins + f + p + pair, specs + [at] * 4 + [columns] * 2
        return call(
            attend_grads_kernel, steps, ins, specs,
            outs, [pl.BlockSpec((d // 4, d), lambda j: (0, j))] * 2,
        )

    def feed_forward(self, x, w, row):
        d, t = self.d, self.t
        outs = (self.xs, sds((5, t, d), bf16), sds((t, 4 * d), f32))
        ins = (x, self.vec, self.order)
        return call(
            functools.partial(feed_forward_kernel, row), 4,
            ins + w + w,
            [whole(i) for i in ins] + self.weights(lambda j: j, lambda j: 4 + j),
            outs, [whole(outs[0]), whole(outs[1]), pl.BlockSpec((t, d), lambda j: (0, j))],
            scratch=[pltpu.VMEM((t, d), bf16)],
        )

    def feed_backward(self, x, u, dx, w, row):
        d, t = self.d, self.t
        outs = (self.xs, sds((8, d), f32), sds((5, t, d), bf16))
        ins = (x, self.vec, self.order, dx)
        return call(
            functools.partial(feed_backward_kernel, row), 4,
            ins + w + w + (u,),
            [whole(i) for i in ins] + self.weights(lambda j: j, lambda j: 4 + j)
            + [pl.BlockSpec((t, d), lambda j: (0, j))],
            outs, [whole(i) for i in outs],
            scratch=[pltpu.VMEM((t, d), f32)],
        )

    def last_backward(self, x, dx, w, row):
        d, t = self.d, self.t
        outs = (self.xs, sds((8, d), f32)) + (sds((5, t, d), bf16),) * 2
        ins = (x, self.vec, self.order, dx)
        return call(
            functools.partial(last_backward_kernel, row), 4,
            ins + w + w,
            [whole(i) for i in ins] + self.weights(lambda j: j, lambda j: 4 + j),
            outs, [whole(i) for i in outs],
            scratch=[pltpu.VMEM((t, d), f32), pltpu.VMEM((t, d), bf16)],
        )

    def last_output(self, x, f, w):
        return call(
            last_output_kernel, 4, (x, self.order, f) + w,
            [whole(x), whole(self.order), self.block(lambda j: 1 + j)]
            + self.weights(lambda j: 4 + j),
            self.hs, whole(self.hs), scratch=[pltpu.VMEM((self.t, self.d), f32)],
        )


def spread_matrix():
    k = lax.broadcasted_iota(jnp.int32, (512, 512), 0)
    n = lax.broadcasted_iota(jnp.int32, (512, 512), 1)
    return (k % 4) * 128 + k // 4 == n


def unspread(up):
    rows, wide = up.shape
    y = up.reshape(rows, 4, wide // 512, 128).transpose(0, 2, 1, 3)
    y = lax.dot_general(
        y.reshape(rows * (wide // 512), 512), spread_matrix().astype(f32),
        (((1,), (1,)), ((), ())), precision=lax.Precision.HIGHEST,
    )
    return y.reshape(rows, wide)


def local(
    tokens, encoder, patch_count, out_grad,
    u_ag, u_as, u_qkv, u_out, u_mg, u_ms, u_up, u_down,
    m_ag, m_as, m_qkv, m_out, c_g, c_s, c_q, c_pair, c_out, m_mg, m_ms, m_up, m_down,
):
    place = Place()
    captions, length, d = tokens.shape
    rows = u_qkv.shape[0]
    x0 = tokens.reshape(-1, d)
    enc = encoder.reshape(-1, d)
    order = place.order(d)

    vectors = (u_ag, u_as, u_mg, u_ms, m_ag, m_as, c_g, c_s, m_mg, m_ms)
    vectors = jnp.pad(jnp.stack(vectors, axis=0), ((0, LANES - len(vectors)), (0, 0)))
    parts = (u_qkv, u_out, u_up, u_down, m_qkv, m_out, m_up, m_down, c_q, c_pair, c_out, vectors)
    packed = tuple(sds((rows, c), bf16) for c in (4 * d + LANES, 8 * d, 8 * d, 8 * d))
    shards = call(
        pack_kernel, 1, parts, [whole(p) for p in parts], packed, [whole(p) for p in packed], vmem=60
    )
    first, feed, middle, last = (Gather(place, x) for x in shards)

    def go(token, groups=(), start=()):
        token, got = tie(token, *[(g.x, g.got) for g in groups])
        for g, (x, y) in zip(groups, got):
            g.x, g.got = x, y
            g.join()
        every = tuple(groups) + tuple(start)
        token, xs = tie(token, *[g.x for g in every])
        for g, x in zip(every, xs):
            g.x = x
            g.swap()
        return token

    def end(token, group):
        token, (group.x, group.got) = tie(token, group.x, group.got)
        return token, (group.x, group.got)

    steps = place.outer_bits
    x0 = go(x0, start=[first])
    enc_rel = nt(enc, order).astype(bf16)
    enc_t = nt(order, enc).astype(bf16)
    for k in range(steps - 1):
        x0 = go(x0, [first], [feed] if k == 0 else [])
    x0 = go(x0, [first])
    for k in range(steps - 1):
        x0 = go(x0, [feed])
    x0 = go(x0, [first])
    x0 = go(x0, [feed], [middle])
    x0 = go(x0, [first])
    x0 = go(x0, [feed])
    for k in range(steps - 1):
        x0 = go(x0, [middle])
    x0, (order, enc_rel, enc_t) = tie(x0, order, enc_rel, enc_t)
    x0, w_first = end(x0, first)
    vec = tn(jnp.concatenate([x[:, 4 * d :] for x in w_first], axis=0), order)[:16]
    net = Layers(captions, captions * length, d, vec, order, patch_count)
    x0 = go(x0, [middle], [last])
    x0a, f_us, k_us = net.self_forward(x0, w_first, 0, 0)
    x0a = go(x0a, [feed])
    for k in range(steps - 1):
        x0a = go(x0a, [last])
    x0a = go(x0a, [middle])
    x0a, w_feed = end(x0a, feed)
    x1, f_uf, k_uf = net.feed_forward(x0a, w_feed, 2)
    x1 = go(x1, [last])
    x1 = go(x1, [middle])
    x1 = go(x1, [last])
    x1, w_middle = end(x1, middle)
    x1a, f_ms, k_ms = net.self_forward(x1, w_middle, 4, 4)
    kv = net.pair_forward(enc_rel, w_middle)
    x1b, f_mc, k_mc = net.cross_forward(x1a, kv, w_middle, 2, 6)
    x1b = go(x1b, [last])
    x1b, w_last = end(x1b, last)

    def core(x):
        return place.swap(x, BIT_CORE)

    def go_on(x, sums=(), start=()):
        x = hold(x, *sums)
        for g in sums:
            g.sums()
        x = need(x, *(tuple(sums) + tuple(g for g in start if g not in sums)))
        for g in start:
            g.swap()
        return x

    def rest(x, *groups):
        for _ in range(place.outer_bits - 1):
            for g in groups:
                x = go_on(x, [g], [g])
        return x

    def pairs(x):
        return x, core(x)

    f_us, f_uf, f_ms = pairs(f_us), pairs(f_uf), pairs(f_ms)
    x1b, (f_us, f_uf, f_ms) = tie(x1b, f_us, f_uf, f_ms)
    f_mc = pairs(f_mc)
    dx, v_mf, p, f = net.last_backward(x1b, out_grad.reshape(-1, d), w_last, 8)
    p, f = pairs(p), pairs(f)
    x2 = net.last_output(x1b, f[0], w_last)
    p, (x2,) = tie(p, x2)
    s_mf = Sum(place, net.feed_grads(f, p))
    dx, (f_mc,) = tie(dx, f_mc)
    dx = go_on(dx, start=[s_mf])
    dx, v_mc, p_c, dkv = net.cross_backward(x1a, k_mc, kv, dx, w_middle, 2, 6)
    p_c = pairs(p_c)
    pair, send = net.pair_grads(enc_t, dkv)
    dx, (send,) = tie(dx, send)
    pair = pair, core(send)
    dx, v_ms, p = net.self_backward(x1, k_ms, dx, w_middle, 4, 4)
    p = pairs(p)
    dx = go_on(dx, [s_mf], [s_mf])
    dx, (p, p_c, pair) = tie(dx, p, p_c, pair)
    s_ma = Sum(place, net.attend_grads(f_ms, p, (f_mc, p_c, pair)))
    dx = go_on(dx, start=[s_ma])
    dx, v_uf, p = net.feed_backward(x0a, k_uf, dx, w_feed, 2)
    p = pairs(p)
    dx, (p,) = tie(dx, p)
    s_uf = Sum(place, net.feed_grads(f_uf, p))
    dx = need(dx, s_uf)
    v = [g[:2] for g in (v_uf, v_ms, v_mc, v_mf)]
    v = jnp.pad(jnp.concatenate(v, axis=0), ((2, 6), (0, 0)))
    dx, _v, p = net.self_backward(x0, k_us, dx, w_first, 0, 0, (v,))
    p = pairs(p)
    dx = go_on(dx, [s_mf], [s_uf, s_mf])
    dx = go_on(dx, [s_ma], [s_ma])
    dx, (dkv,) = tie(dx, dkv)
    denc = net.pair_input(dkv, w_middle)
    dx, (denc,) = tie(dx, denc)
    dx = rest(dx, s_mf)
    dx, (p,) = tie(dx, p)
    send, keep = net.attend_grads(f_us, p)
    v = nt(order[: d // 2], plus(p[0][4], p[1][4])[:LANES]).astype(bf16)
    send = jnp.concatenate((send, v[d // 4 :]), axis=1)
    keep = jnp.concatenate((keep, v[: d // 4]), axis=1)
    s_us = Sum(place, (send, keep))
    dx = need(dx, s_us)
    dx = go_on(dx, [s_ma], [s_ma])
    dx = go_on(dx, [s_uf], [s_uf, s_us])
    dx, (r_mf,) = tie(dx, s_mf.total())
    dx = rest(dx, s_ma)
    dx = go_on(dx, [s_uf], [s_uf])
    dx = go_on(dx, [s_us], [s_us])
    dx, (r_ma,) = tie(dx, s_ma.total())
    dx = rest(dx, s_uf)
    dx = go_on(dx, [s_us], [s_us])
    dx, (r_uf,) = tie(dx, s_uf.total())
    dx = rest(dx, s_us)
    r_us = s_us.total()

    def columns(r, *blocks):
        parts = [r[:, b * d : (b + 1) * d] for b in blocks]
        return jnp.concatenate(parts, axis=1) if len(parts) > 1 else parts[0]

    def feed_rows(r):
        return unspread(columns(r, 0, 2, 4, 6)), columns(r, 1, 3, 5, 7).reshape(-1, d)

    r_uup, r_udown = feed_rows(r_uf)
    r_mup, r_mdown = feed_rows(r_mf)
    vs = r_us[:, 4 * d :]
    v = [vs[:, i] for i in range(10)]
    return (
        x2.reshape(tokens.shape),
        dx.astype(bf16).reshape(tokens.shape),
        denc.reshape(encoder.shape),
        v[0], v[1], r_us[:, : 3 * d], r_us[:, 3 * d : 4 * d], v[2], v[3], r_uup, r_udown,
        v[4], v[5], r_ma[:, : 3 * d], columns(r_ma, 3), v[6], v[7],
        columns(r_ma, 4), r_ma[:, 6 * d :], columns(r_ma, 5),
        v[8], v[9], r_mup, r_mdown,
    )


def solution(mesh):
    rows1 = P(AXES)
    rows2 = P(AXES, None)
    rows3 = P(AXES, None, None)
    block = (rows1, rows1, rows2, rows2)
    weights = block * 2 + block + (rows1, rows1, rows2, rows2, rows2) + block
    return jax.shard_map(
        local,
        mesh=mesh,
        in_specs=(rows3, rows3, rows1, rows3) + weights,
        out_specs=(rows3, rows3, rows3) + weights,
        check_vma=False,
    )
```

```python
import functools

import jax
import jax.numpy as jnp
from jax import lax
from jax.experimental import pallas as pl
from jax.experimental.pallas import tpu as pltpu
from jax.sharding import PartitionSpec as P

DH = 64
AXES = ("dp", "hd")
EPS = 1e-05
MASKED = -1e30
LANES = 128
bf16 = jnp.bfloat16
f32 = jnp.float32
sds = jax.ShapeDtypeStruct


BIT_PAIR, BIT_CORE, BIT_NEAR = 1, 2, 4


class Place:
    def __init__(self):
        self.count = lax.axis_size("dp") * lax.axis_size("hd")
        self.outer_size = self.count // 8
        index = lax.axis_index("dp") * lax.axis_size("hd") + lax.axis_index("hd")
        self.pair = index % 2
        self.core = (index // 2) % 2
        self.near = (index // 4) % 2
        self.outer = index // 8
        self.outer_bits = self.outer_size.bit_length() - 1

    def swap(self, x, bit):
        return lax.ppermute(x, AXES, [(i, i ^ bit) for i in range(self.count)])

    def swap_by_core(self, x, bits):
        pairs = [(i, i ^ bits[(i // BIT_CORE) % 2]) for i in range(self.count)]
        return lax.ppermute(x, AXES, pairs)

    def order(self, d):
        n, rows = self.outer_size, d // self.count
        k = lax.broadcasted_iota(jnp.int32, (d, 1), 0)
        row, place = k % rows, (k // rows) % n
        outer = jnp.zeros_like(k)
        for b in range(self.outer_bits):
            outer = outer + ((place >> (self.outer_bits - 1 - b)) & 1) * (1 << b)
        outer = outer ^ self.outer
        rest = k // (rows * n)
        low, high = rest % 2, (rest // 2) % 2
        near = jnp.where((rest // 4) ^ self.core == 0, high, low)
        pair = high + low - near
        feature = outer * 2 + (near ^ self.near)
        feature = (feature * 2 + ((rest // 4) ^ self.core)) * 2 + (pair ^ self.pair)
        feature = feature * rows + row
        return (feature == lax.broadcasted_iota(jnp.int32, (d, d), 1)).astype(bf16)


def plus(a, b):
    return (a.astype(f32) + b.astype(f32)).astype(bf16)


class Sum:
    def __init__(self, place, grads):
        self.place, self.stage = place, 0
        self.send, self.kept = grads

    def swap(self):
        if self.stage < 2:
            bits = ((BIT_NEAR, BIT_PAIR), (BIT_PAIR, BIT_NEAR))[self.stage]
            self.got = self.place.swap_by_core(self.send, bits)
        else:
            self.got = self.place.swap(self.send, 8 << (self.stage - 2))

    def sums(self):
        if self.stage < 2:
            self.send, self.kept = half_sums(self.kept, self.got)
        else:
            half = self.kept.shape[0] // 2
            self.send = plus(self.kept[half:], self.got[half:])
            self.kept = plus(self.kept[:half], self.got[:half])
        self.stage += 1

    def total(self):
        return self.kept.astype(f32) + self.got.astype(f32)


class Gather:
    def __init__(self, place, shard):
        self.place, self.x, self.stage = place, shard, 0

    def swap(self):
        outer = self.place.outer_bits
        at = self.stage - outer
        if at < 0:
            self.got = self.place.swap(self.x, 8 << (outer - 1 - self.stage))
        elif at < 2:
            bits = ((BIT_PAIR, BIT_NEAR), (BIT_NEAR, BIT_PAIR))[at]
            self.got = self.place.swap_by_core(self.x, bits)
        else:
            self.got = self.place.swap(self.x, BIT_CORE)

    def join(self):
        self.x = jnp.concatenate((self.x, self.got), axis=0)
        self.stage += 1


def tie(x, *others):
    out = lax.optimization_barrier((x,) + others)
    return out[0], out[1:]


def hold(x, *groups):
    x, terms = tie(x, *[(g.kept, g.got) for g in groups])
    for g, t in zip(groups, terms):
        g.kept, g.got = t
    return x


def need(x, *groups):
    x, send = tie(x, *[g.send for g in groups])
    for g, k in zip(groups, send):
        g.send = k
    return x


def nn(a, b):
    return jnp.dot(a, b, preferred_element_type=f32)


def nt(a, b):
    return lax.dot_general(a, b, (((1,), (1,)), ((), ())), preferred_element_type=f32)


def tn(a, b):
    return lax.dot_general(a, b, (((0,), (0,)), ((), ())), preferred_element_type=f32)


def unit_norm(x):
    centred = x - jnp.mean(x, axis=-1, keepdims=True)
    inv = lax.rsqrt(jnp.mean(centred * centred, axis=-1, keepdims=True) + EPS)
    return centred * inv, inv


def norm_backward(grad, x, gain):
    unit, inv = unit_norm(x)
    du = grad * gain
    dx = inv * (
        du
        - jnp.mean(du, axis=-1, keepdims=True)
        - unit * jnp.mean(du * unit, axis=-1, keepdims=True)
    )
    return dx, jnp.sum(grad * unit, axis=0, keepdims=True), jnp.sum(grad, axis=0, keepdims=True)


GELU_A = 0.7978845608028654
GELU_B = 0.044715


def two_heads(x):
    first = lax.broadcasted_iota(jnp.int32, x.shape, 1) < DH
    zero = jnp.zeros_like(x)
    return jnp.concatenate((jnp.where(first, x, zero), jnp.where(first, zero, x)), axis=0)


def side_by_side(x):
    n = x.shape[0] // 2
    first = lax.broadcasted_iota(jnp.int32, (n, LANES), 1) < DH
    return jnp.where(first, x[:n], x[n:])


def probabilities(qs, k2, allowed):
    s = jnp.where(allowed, nt(qs, k2) * DH ** (-0.5), MASKED)
    e = jnp.exp(s - jnp.max(s, axis=-1, keepdims=True))
    return e / jnp.sum(e, axis=-1, keepdims=True)


def causal_mask(length):
    row = lax.broadcasted_iota(jnp.int32, (2 * length, length), 0)
    col = lax.broadcasted_iota(jnp.int32, (2 * length, length), 1)
    return jnp.where(row >= length, row - length, row) >= col


def attend_back(q2, k2, v2, do2, allowed):
    scale = DH ** (-0.5)
    qs, dos = two_heads(q2), two_heads(do2)
    p = probabilities(qs, k2, allowed)
    dp = nt(dos, v2)
    ds = (p * (dp - jnp.sum(p * dp, axis=-1, keepdims=True))).astype(bf16)
    dq = side_by_side(nn(ds, k2)) * scale
    dk = tn(ds, qs) * scale
    dv = tn(p.astype(bf16), dos)
    return dq.astype(bf16), dk.astype(bf16), dv.astype(bf16)


def relative(x, order_ref):
    return nt(x, order_ref[...]).astype(bf16)


def times(x, top_ref, low_ref):
    half = top_ref.shape[0]
    return nn(x[:, :half], top_ref[...]) + nn(x[:, half:], low_ref[...])


def times_back(g, top_ref, low_ref):
    return jnp.concatenate((nt(g, top_ref[...]), nt(g, low_ref[...])), axis=1)


def natural(x, order_ref):
    high = x.astype(bf16)
    low = (x - high.astype(f32)).astype(bf16)
    return nn(high, order_ref[...]) + nn(low, order_ref[...])


def self_forward_kernel(
    captions, row, x_ref, vec_ref, order_ref, top_ref, low_ref, y_ref, f_ref, qkv_ref, rel_ref
):
    j = pl.program_id(0)

    @pl.when(j == 0)
    def _():
        unit, _inv = unit_norm(x_ref[...].astype(f32))
        f_ref[0] = (unit * vec_ref[row : row + 1] + vec_ref[row + 1 : row + 2]).astype(bf16)
        rel_ref[...] = relative(f_ref[0], order_ref)

    @pl.when(j < 3)
    def _():
        qkv_ref[j] = times(rel_ref[...], top_ref, low_ref).astype(bf16)

    @pl.when(j == 3)
    def _():
        length = x_ref.shape[0] // captions
        allowed = causal_mask(length)
        for c in range(captions):
            at = slice(c * length, (c + 1) * length)
            for h in range(0, x_ref.shape[1], LANES):
                cols = slice(h, h + LANES)
                p = probabilities(two_heads(qkv_ref[0, at, cols]), qkv_ref[1, at, cols], allowed)
                o = side_by_side(nn(p.astype(bf16), qkv_ref[2, at, cols]))
                f_ref[1, at, cols] = o.astype(bf16)
        y_ref[...] = x_ref[...].astype(f32) + times(relative(f_ref[1], order_ref), top_ref, low_ref)


def self_backward_kernel(
    captions, row, x_ref, vec_ref, order_ref, qkv_ref, dx_ref, top_ref, low_ref, *refs
):
    out_ref, vg_ref, p_ref, acc_ref = refs[-4:]
    j = pl.program_id(0)

    @pl.when(j == 0)
    def _():
        dy = dx_ref[...].astype(bf16)
        p_ref[3] = dy
        do = times_back(dy, top_ref, low_ref).astype(bf16)
        do = nn(do, order_ref[...]).astype(bf16)
        length = x_ref.shape[0] // captions
        allowed = causal_mask(length)
        for c in range(captions):
            at = slice(c * length, (c + 1) * length)
            for h in range(0, x_ref.shape[1], LANES):
                cols = slice(h, h + LANES)
                dq, dk, dv = attend_back(
                    qkv_ref[0, at, cols], qkv_ref[1, at, cols], qkv_ref[2, at, cols],
                    do[at, cols], allowed,
                )
                p_ref[0, at, cols] = dq
                p_ref[1, at, cols] = dk
                p_ref[2, at, cols] = dv
        acc_ref[...] = jnp.zeros_like(acc_ref)

    @pl.when(j > 0)
    def _():
        acc_ref[...] += times_back(p_ref[j - 1], top_ref, low_ref)

    @pl.when(j == 3)
    def _():
        da = natural(acc_ref[...], order_ref)
        dn, gg, gs = norm_backward(da, x_ref[...].astype(f32), vec_ref[row : row + 1])
        out_ref[...] = dx_ref[...] + dn
        vg_ref[0:1] = gg
        vg_ref[1:2] = gs
        if len(refs) > 4:
            at = lax.broadcasted_iota(jnp.int32, refs[0].shape, 0)
            rows = jnp.where(at == 0, gg, jnp.where(at == 1, gs, refs[0][...]))
            p_ref[4] = jnp.zeros_like(p_ref[4])
            p_ref[4, 0 : refs[0].shape[0]] = rows.astype(bf16)


def cross_forward_kernel(
    captions, row, count_ref, x_ref, vec_ref, order_ref, kv_ref, top_ref, low_ref, y_ref, f_ref, q_ref
):
    j = pl.program_id(0)
    d = x_ref.shape[1]

    @pl.when(j == 0)
    def _():
        unit, _inv = unit_norm(x_ref[...])
        c = (unit * vec_ref[row : row + 1] + vec_ref[row + 1 : row + 2]).astype(bf16)
        f_ref[0] = c
        q_ref[...] = times(relative(c, order_ref), top_ref, low_ref).astype(bf16)

    @pl.when(j == 1)
    def _():
        length = x_ref.shape[0] // captions
        patches = kv_ref.shape[0] // captions
        slot = lax.broadcasted_iota(jnp.int32, (2 * length, patches), 1)
        for c in range(captions):
            at = slice(c * length, (c + 1) * length)
            keys = slice(c * patches, (c + 1) * patches)
            allowed = slot < count_ref[c]
            for h in range(0, d, LANES):
                cols = slice(h, h + LANES)
                vcols = slice(d + h, d + h + LANES)
                p = probabilities(two_heads(q_ref[at, cols]), kv_ref[keys, cols], allowed)
                o = side_by_side(nn(p.astype(bf16), kv_ref[keys, vcols]))
                f_ref[1, at, cols] = o.astype(bf16)
        y_ref[...] = x_ref[...] + times(relative(f_ref[1], order_ref), top_ref, low_ref)


def cross_backward_kernel(
    captions, row, count_ref, x_ref, vec_ref, order_ref, q_ref, kv_ref, dx_ref, top_ref, low_ref,
    out_ref, vg_ref, p_ref, dkv_ref,
):
    j = pl.program_id(0)
    d = x_ref.shape[1]

    @pl.when(j == 0)
    def _():
        dy = dx_ref[...].astype(bf16)
        p_ref[1] = dy
        do = times_back(dy, top_ref, low_ref).astype(bf16)
        do = nn(do, order_ref[...]).astype(bf16)
        length = x_ref.shape[0] // captions
        patches = kv_ref.shape[0] // captions
        slot = lax.broadcasted_iota(jnp.int32, (2 * length, patches), 1)
        for c in range(captions):
            at = slice(c * length, (c + 1) * length)
            keys = slice(c * patches, (c + 1) * patches)
            allowed = slot < count_ref[c]
            for h in range(0, d, LANES):
                cols = slice(h, h + LANES)
                vcols = slice(d + h, d + h + LANES)
                dq, dk, dv = attend_back(
                    q_ref[at, cols], kv_ref[keys, cols], kv_ref[keys, vcols], do[at, cols], allowed
                )
                p_ref[0, at, cols] = dq
                dkv_ref[keys, cols] = dk
                dkv_ref[keys, vcols] = dv

    @pl.when(j == 1)
    def _():
        dc = natural(times_back(p_ref[0], top_ref, low_ref), order_ref)
        dn, gg, gs = norm_backward(dc, x_ref[...], vec_ref[row : row + 1])
        out_ref[...] = dx_ref[...] + dn
        vg_ref[0:1] = gg
        vg_ref[1:2] = gs


def feed_forward_kernel(
    row, x_ref, vec_ref, order_ref, up_ref, up2_ref, down_ref, down2_ref, y_ref, f_ref, u_ref, rel_ref
):
    j = pl.program_id(0)

    @pl.when(j == 0)
    def _():
        unit, _inv = unit_norm(x_ref[...])
        f_ref[0] = (unit * vec_ref[row : row + 1] + vec_ref[row + 1 : row + 2]).astype(bf16)
        rel_ref[...] = relative(f_ref[0], order_ref)
        y_ref[...] = x_ref[...]

    u = times(rel_ref[...], up_ref, up2_ref)
    u_ref[...] = u
    g = (0.5 * u * (1.0 + jnp.tanh(GELU_A * (u + GELU_B * u * u * u)))).astype(bf16)
    f_ref[1 + j] = g
    y_ref[...] += times(relative(g, order_ref), down_ref, down2_ref)


def gelu_terms(u):
    t = jnp.tanh(GELU_A * (u + GELU_B * u * u * u))
    slope = 0.5 * (1.0 + t) + 0.5 * u * (1.0 - t * t) * GELU_A * (1.0 + 3.0 * GELU_B * u * u)
    return 0.5 * u * (1.0 + t), slope


def feed_backward_step(j, order_ref, slope, refs, p_ref, acc_ref):
    up_ref, up2_ref, down_ref, down2_ref = refs
    dg = times_back(p_ref[0], down_ref, down2_ref).astype(bf16)
    du = (slope * nn(dg, order_ref[...])).astype(bf16)
    p_ref[1 + j] = du
    acc_ref[...] += times_back(du, up_ref, up2_ref)


def feed_backward_end(row, order_ref, x_ref, vec_ref, dx_ref, acc_ref, out_ref, vg_ref):
    db = natural(acc_ref[...], order_ref)
    dn, gg, gs = norm_backward(db, x_ref[...], vec_ref[row : row + 1])
    out_ref[...] = dx_ref[...].astype(f32) + dn
    vg_ref[0:1] = gg
    vg_ref[1:2] = gs


def feed_backward_kernel(
    row, x_ref, vec_ref, order_ref, dx_ref, up_ref, up2_ref, down_ref, down2_ref, u_ref,
    out_ref, vg_ref, p_ref, acc_ref,
):
    j = pl.program_id(0)

    @pl.when(j == 0)
    def _():
        p_ref[0] = dx_ref[...].astype(bf16)
        acc_ref[...] = jnp.zeros_like(acc_ref)

    refs = up_ref, up2_ref, down_ref, down2_ref
    feed_backward_step(j, order_ref, gelu_terms(u_ref[...])[1], refs, p_ref, acc_ref)

    @pl.when(j == 3)
    def _():
        feed_backward_end(row, order_ref, x_ref, vec_ref, dx_ref, acc_ref, out_ref, vg_ref)


def last_backward_kernel(
    row, x_ref, vec_ref, order_ref, dx_ref, up_ref, up2_ref, down_ref, down2_ref,
    out_ref, vg_ref, p_ref, f_ref, acc_ref, rel_ref,
):
    j = pl.program_id(0)

    @pl.when(j == 0)
    def _():
        unit, _inv = unit_norm(x_ref[...])
        f_ref[0] = (unit * vec_ref[row : row + 1] + vec_ref[row + 1 : row + 2]).astype(bf16)
        rel_ref[...] = relative(f_ref[0], order_ref)
        p_ref[0] = dx_ref[...]
        acc_ref[...] = jnp.zeros_like(acc_ref)

    g, slope = gelu_terms(times(rel_ref[...], up_ref, up2_ref))
    f_ref[1 + j] = g.astype(bf16)
    refs = up_ref, up2_ref, down_ref, down2_ref
    feed_backward_step(j, order_ref, slope, refs, p_ref, acc_ref)

    @pl.when(j == 3)
    def _():
        feed_backward_end(row, order_ref, x_ref, vec_ref, dx_ref, acc_ref, out_ref, vg_ref)


def last_output_kernel(x_ref, order_ref, g_ref, down_ref, down2_ref, y_ref, acc_ref):
    j = pl.program_id(0)

    @pl.when(j == 0)
    def _():
        acc_ref[...] = x_ref[...]

    acc_ref[...] += times(relative(g_ref[0], order_ref), down_ref, down2_ref)

    @pl.when(j == 3)
    def _():
        y_ref[...] = acc_ref[...].astype(bf16)


def both(own_ref, got_ref):
    return jnp.concatenate((own_ref[0], got_ref[0]), axis=0)


def emit(g, send_ref, keep_ref):
    half = keep_ref.shape[0]
    keep_ref[...] = g[:half].astype(bf16)
    send_ref[...] = g[half:].astype(bf16)


def feed_grads_kernel(
    order_ref, b_ref, b2_ref, z_ref, z2_ref, g_ref, g2_ref, u_ref, u2_ref, send_ref, keep_ref, bt_ref
):
    d = order_ref.shape[1]

    @pl.when(pl.program_id(0) == 0)
    def _():
        bt_ref[...] = nt(order_ref[...], both(b_ref, b2_ref)).astype(bf16)

    up, down = (slice(None), slice(0, d)), (slice(None), slice(d, 2 * d))
    emit(nn(bt_ref[...], both(u_ref, u2_ref)), send_ref.at[up], keep_ref.at[up])
    gt = nt(order_ref[...], both(g_ref, g2_ref)).astype(bf16)
    emit(nn(gt, both(z_ref, z2_ref)), send_ref.at[down], keep_ref.at[down])


def attend_grads_kernel(order_ref, s_ref, s2_ref, sd_ref, sd2_ref, *refs):
    send_ref, keep_ref = refs[-2:]
    j = pl.program_id(0)

    def product(a_ref, a2_ref, d_ref, d2_ref):
        at = nt(order_ref[...], both(a_ref, a2_ref)).astype(bf16)
        emit(nn(at, both(d_ref, d2_ref)), send_ref, keep_ref)

    @pl.when(j < 4)
    def _():
        product(s_ref, s2_ref, sd_ref, sd2_ref)

    if len(refs) > 2:
        c_ref, c2_ref, cd_ref, cd2_ref, pair_ref, pair2_ref = refs[:6]

        @pl.when((j == 4) | (j == 5))
        def _():
            product(c_ref, c2_ref, cd_ref, cd2_ref)

        @pl.when(j > 5)
        def _():
            emit(pair_ref[...].astype(f32) + pair2_ref[...].astype(f32), send_ref, keep_ref)


def half_sums_kernel(kept_ref, got_ref, send_ref, keep_ref):
    emit(kept_ref[...].astype(f32) + got_ref[...].astype(f32), send_ref, keep_ref)


def half_sums(kept, got):
    rows, wide = kept.shape
    steps = 2 if wide % (2 * LANES) == 0 else 1
    full = pl.BlockSpec((rows, wide // steps), lambda j: (0, j))
    half = pl.BlockSpec((rows // 2, wide // steps), lambda j: (0, j))
    outs = (sds((rows // 2, wide), bf16),) * 2
    return call(half_sums_kernel, steps, (kept, got), [full] * 2, outs, [half] * 2, vmem=24)


def pair_forward_kernel(enc_ref, top_ref, low_ref, kv_ref):
    kv_ref[...] = times(enc_ref[...], top_ref, low_ref).astype(bf16)


def pair_input_kernel(dkv_ref, order_ref, top_ref, low_ref, out_ref):
    g = times_back(dkv_ref[...], top_ref, low_ref).astype(bf16)
    out_ref[...] = nn(g, order_ref[...]).astype(bf16)


def pair_grads_kernel(enc_ref, dkv_ref, keep_ref, send_ref):
    emit(nn(enc_ref[...], dkv_ref[...]), send_ref, keep_ref)


def pack_kernel(
    u_qkv, u_out, u_up, u_down, m_qkv, m_out, m_up, m_down, c_q, c_pair, c_out, vec,
    first_out, feed_out, middle_out, last_out,
):
    rows, d = u_out.shape
    spread = spread_matrix().astype(bf16)
    i = lax.broadcasted_iota(jnp.int32, (rows, 4 * rows), 0)
    k = lax.broadcasted_iota(jnp.int32, (rows, 4 * rows), 1)

    def feed(out, up, down):
        for b in range(4 * d // 512):
            y = nn(up[:, b * 512 : (b + 1) * 512], spread).astype(bf16)
            for j in range(4):
                to = j * d + b * LANES
                out[:, to : to + LANES] = y[:, j * LANES : (j + 1) * LANES]
        for j in range(4):
            y = nn((k == 4 * i + j).astype(bf16), down[...])
            out[:, (4 + j) * d : (5 + j) * d] = y.astype(bf16)

    first_out[:, : 3 * d] = u_qkv[...]
    first_out[:, 3 * d : 4 * d] = u_out[...]
    eye = lax.broadcasted_iota(jnp.int32, (rows, rows), 0) == lax.broadcasted_iota(jnp.int32, (rows, rows), 1)
    first_out[:, 4 * d :] = nt(eye.astype(bf16), vec[...]).astype(bf16)
    feed(feed_out, u_up, u_down)
    middle_out[:, : 2 * d] = c_pair[...]
    middle_out[:, 2 * d : 3 * d] = c_q[...]
    middle_out[:, 3 * d : 4 * d] = c_out[...]
    middle_out[:, 4 * d : 7 * d] = m_qkv[...]
    middle_out[:, 7 * d : 8 * d] = m_out[...]
    feed(last_out, m_up, m_down)


def whole(x):
    return pl.BlockSpec(x.shape, lambda *_: (0,) * len(x.shape))


def call(kernel, steps, ins, in_specs, outs, out_specs, scratch=(), scalars=0, vmem=24):
    return pl.pallas_call(
        kernel,
        out_shape=outs,
        grid_spec=pltpu.PrefetchScalarGridSpec(
            num_scalar_prefetch=scalars,
            grid=(steps,),
            in_specs=in_specs,
            out_specs=out_specs,
            scratch_shapes=scratch,
        ),
        compiler_params=pltpu.CompilerParams(
            dimension_semantics=("arbitrary",), vmem_limit_bytes=vmem << 20
        ),
        cost_estimate=pl.CostEstimate(flops=1000, bytes_accessed=1000, transcendentals=0),
    )(*ins)


class Layers:
    def __init__(self, captions, tokens, d, vec, order, count):
        self.captions, self.t, self.d = captions, tokens, d
        self.vec, self.order, self.count = vec, order, count
        self.xs = sds((tokens, d), f32)
        self.hs = sds((tokens, d), bf16)

    def weights(self, *columns):
        d = self.d
        specs = [pl.BlockSpec((d // 2, d), lambda j, *_, c=c: (0, c(j))) for c in columns]
        return [s for s in specs for _ in range(2)]

    def self_forward(self, x, w, at, row):
        outs = (self.xs, sds((2, self.t, self.d), bf16), sds((3, self.t, self.d), bf16))
        ins = (x, self.vec, self.order)
        return call(
            functools.partial(self_forward_kernel, self.captions, row), 4,
            ins + w, [whole(i) for i in ins] + self.weights(lambda j: at + j),
            outs, [whole(o) for o in outs], scratch=[pltpu.VMEM((self.t, self.d), bf16)],
        )

    def self_backward(self, x, kept, dx, w, at, row, vectors=()):
        d, t = self.d, self.t
        outs = (self.xs, sds((8, d), f32), sds((4 + len(vectors), t, d), bf16))
        ins = (x, self.vec, self.order, kept, dx)
        return call(
            functools.partial(self_backward_kernel, self.captions, row), 4,
            ins + w + vectors,
            [whole(i) for i in ins] + self.weights(lambda j: at + (j + 3) % 4)
            + [whole(v) for v in vectors],
            outs, [whole(i) for i in outs],
            scratch=[pltpu.VMEM((t, d), f32)],
        )

    def cross_forward(self, x, kv, w, at, row):
        outs = (self.xs, sds((2, self.t, self.d), bf16), self.hs)
        ins = (x, self.vec, self.order, kv)
        return call(
            functools.partial(cross_forward_kernel, self.captions, row), 2,
            (self.count,) + ins + w,
            [whole(i) for i in ins] + self.weights(lambda j: at + j),
            outs, [whole(o) for o in outs], scalars=1,
        )

    def cross_backward(self, x, kept, kv, dx, w, at, row):
        d, t = self.d, self.t
        outs = (self.xs, sds((8, d), f32), sds((2, t, d), bf16), sds(kv.shape, bf16))
        ins = (x, self.vec, self.order, kept, kv, dx)
        return call(
            functools.partial(cross_backward_kernel, self.captions, row), 2,
            (self.count,) + ins + w,
            [whole(i) for i in ins] + self.weights(lambda j: at + 1 - j),
            outs, [whole(i) for i in outs], scalars=1,
        )

    def pair_forward(self, enc, w):
        d, rows = self.d, enc.shape[0] // self.captions
        half = pl.BlockSpec((d // 2, 2 * d), lambda j: (0, 0))
        out = sds((enc.shape[0], 2 * d), bf16)
        return call(
            pair_forward_kernel, self.captions, (enc,) + w,
            [pl.BlockSpec((rows, d), lambda j: (j, 0)), half, half],
            out, pl.BlockSpec((rows, 2 * d), lambda j: (j, 0)),
        )

    def pair_grads(self, enc_t, dkv):
        d = self.d
        outs = (sds((d // 2, 2 * d), bf16),) * 2
        grad = pl.BlockSpec((d // 2, d), lambda j: (0, j))
        return call(
            pair_grads_kernel, 2, (enc_t, dkv),
            [whole(enc_t), pl.BlockSpec((dkv.shape[0], d), lambda j: (0, j))],
            outs, [grad, grad],
        )

    def pair_input(self, dkv, w):
        d, rows = self.d, dkv.shape[0] // self.captions
        half = pl.BlockSpec((d // 2, 2 * d), lambda j: (0, 0))
        out = sds((dkv.shape[0], d), bf16)
        return call(
            pair_input_kernel, self.captions, (dkv, self.order) + w,
            [pl.BlockSpec((rows, 2 * d), lambda j: (j, 0)), whole(self.order), half, half],
            out, pl.BlockSpec((rows, d), lambda j: (j, 0)),
        )

    def block(self, index):
        return pl.BlockSpec((1, self.t, self.d), lambda j: (index(j), 0, 0))

    def feed_grads(self, f, p):
        d, t = self.d, self.t
        outs = (sds((d // 4, 8 * d), bf16),) * 2
        first, later = self.block(lambda j: 0), self.block(lambda j: 1 + j)
        half = pl.BlockSpec((d // 2, d), lambda j: (0, 0))
        return call(
            feed_grads_kernel, 4, (self.order,) + f + p + f + p,
            [half] + [first] * 4 + [later] * 4,
            outs, [pl.BlockSpec((d // 4, 2 * d), lambda j: (0, j))] * 2,
            scratch=[pltpu.VMEM((d // 2, 2 * t), bf16)],
        )

    def attend_grads(self, f, p, cross=()):
        d, t = self.d, self.t
        steps = 8 if cross else 4
        outs = (sds((d // 4, steps * d), bf16),) * 2
        half = pl.BlockSpec((d // 2, d), lambda j: (0, 0))
        lhs = self.block(lambda j: jnp.minimum(j // 3, 1))
        rhs = self.block(lambda j: jnp.minimum(j, 3))
        ins, specs = (self.order,) + f + p, [half, lhs, lhs, rhs, rhs]
        if cross:
            f, p, pair = cross
            at = self.block(lambda j: jnp.clip(j - 4, 0, 1))
            columns = pl.BlockSpec((d // 2, d), lambda j: (0, jnp.clip(j - 6, 0, 1)))
            ins, specs = ins + f + p + pair, specs + [at] * 4 + [columns] * 2
        return call(
            attend_grads_kernel, steps, ins, specs,
            outs, [pl.BlockSpec((d // 4, d), lambda j: (0, j))] * 2,
        )

    def feed_forward(self, x, w, row):
        d, t = self.d, self.t
        outs = (self.xs, sds((5, t, d), bf16), sds((t, 4 * d), f32))
        ins = (x, self.vec, self.order)
        return call(
            functools.partial(feed_forward_kernel, row), 4,
            ins + w + w,
            [whole(i) for i in ins] + self.weights(lambda j: j, lambda j: 4 + j),
            outs, [whole(outs[0]), whole(outs[1]), pl.BlockSpec((t, d), lambda j: (0, j))],
            scratch=[pltpu.VMEM((t, d), bf16)],
        )

    def feed_backward(self, x, u, dx, w, row):
        d, t = self.d, self.t
        outs = (self.xs, sds((8, d), f32), sds((5, t, d), bf16))
        ins = (x, self.vec, self.order, dx)
        return call(
            functools.partial(feed_backward_kernel, row), 4,
            ins + w + w + (u,),
            [whole(i) for i in ins] + self.weights(lambda j: j, lambda j: 4 + j)
            + [pl.BlockSpec((t, d), lambda j: (0, j))],
            outs, [whole(i) for i in outs],
            scratch=[pltpu.VMEM((t, d), f32)],
        )

    def last_backward(self, x, dx, w, row):
        d, t = self.d, self.t
        outs = (self.xs, sds((8, d), f32)) + (sds((5, t, d), bf16),) * 2
        ins = (x, self.vec, self.order, dx)
        return call(
            functools.partial(last_backward_kernel, row), 4,
            ins + w + w,
            [whole(i) for i in ins] + self.weights(lambda j: j, lambda j: 4 + j),
            outs, [whole(i) for i in outs],
            scratch=[pltpu.VMEM((t, d), f32), pltpu.VMEM((t, d), bf16)],
        )

    def last_output(self, x, f, w):
        return call(
            last_output_kernel, 4, (x, self.order, f) + w,
            [whole(x), whole(self.order), self.block(lambda j: 1 + j)]
            + self.weights(lambda j: 4 + j),
            self.hs, whole(self.hs), scratch=[pltpu.VMEM((self.t, self.d), f32)],
        )


def spread_matrix():
    k = lax.broadcasted_iota(jnp.int32, (512, 512), 0)
    n = lax.broadcasted_iota(jnp.int32, (512, 512), 1)
    return (k % 4) * 128 + k // 4 == n


def unspread(up):
    rows, wide = up.shape
    y = up.reshape(rows, 4, wide // 512, 128).transpose(0, 2, 1, 3)
    y = lax.dot_general(
        y.reshape(rows * (wide // 512), 512), spread_matrix().astype(f32),
        (((1,), (1,)), ((), ())), precision=lax.Precision.HIGHEST,
    )
    return y.reshape(rows, wide)


def local(
    tokens, encoder, patch_count, out_grad,
    u_ag, u_as, u_qkv, u_out, u_mg, u_ms, u_up, u_down,
    m_ag, m_as, m_qkv, m_out, c_g, c_s, c_q, c_pair, c_out, m_mg, m_ms, m_up, m_down,
):
    place = Place()
    captions, length, d = tokens.shape
    rows = u_qkv.shape[0]
    x0 = tokens.reshape(-1, d)
    enc = encoder.reshape(-1, d)
    order = place.order(d)

    vectors = (u_ag, u_as, u_mg, u_ms, m_ag, m_as, c_g, c_s, m_mg, m_ms)
    vectors = jnp.pad(jnp.stack(vectors, axis=0), ((0, LANES - len(vectors)), (0, 0)))
    parts = (u_qkv, u_out, u_up, u_down, m_qkv, m_out, m_up, m_down, c_q, c_pair, c_out, vectors)
    packed = tuple(sds((rows, c), bf16) for c in (4 * d + LANES, 8 * d, 8 * d, 8 * d))
    shards = call(
        pack_kernel, 1, parts, [whole(p) for p in parts], packed, [whole(p) for p in packed], vmem=60
    )
    first, feed, middle, last = (Gather(place, x) for x in shards)

    def go(token, groups=(), start=()):
        token, got = tie(token, *[(g.x, g.got) for g in groups])
        for g, (x, y) in zip(groups, got):
            g.x, g.got = x, y
            g.join()
        every = tuple(groups) + tuple(start)
        token, xs = tie(token, *[g.x for g in every])
        for g, x in zip(every, xs):
            g.x = x
            g.swap()
        return token

    def end(token, group):
        token, (group.x, group.got) = tie(token, group.x, group.got)
        return token, (group.x, group.got)

    steps = place.outer_bits
    x0 = go(x0, start=[first])
    enc_rel = nt(enc, order).astype(bf16)
    enc_t = nt(order, enc).astype(bf16)
    for k in range(steps - 1):
        x0 = go(x0, [first], [feed] if k == 0 else [])
    x0 = go(x0, [first])
    for k in range(steps - 1):
        x0 = go(x0, [feed])
    x0 = go(x0, [first])
    x0 = go(x0, [feed], [middle])
    x0 = go(x0, [first])
    for k in range(steps - 1):
        x0 = go(x0, [middle])
    x0 = go(x0, [feed])
    x0, (order, enc_rel, enc_t) = tie(x0, order, enc_rel, enc_t)
    x0, w_first = end(x0, first)
    vec = tn(jnp.concatenate([x[:, 4 * d :] for x in w_first], axis=0), order)[:16]
    net = Layers(captions, captions * length, d, vec, order, patch_count)
    x0 = go(x0, [middle], [last])
    x0a, f_us, k_us = net.self_forward(x0, w_first, 0, 0)
    for k in range(steps - 1):
        x0a = go(x0a, [last])
    x0a = go(x0a, [middle])
    x0a = go(x0a, [last])
    x0a = go(x0a, [feed])
    x0a, w_feed = end(x0a, feed)
    x1, f_uf, k_uf = net.feed_forward(x0a, w_feed, 2)
    x1 = go(x1, [last])
    x1 = go(x1, [middle])
    x1, w_middle = end(x1, middle)
    x1a, f_ms, k_ms = net.self_forward(x1, w_middle, 4, 4)
    kv = net.pair_forward(enc_rel, w_middle)
    x1b, f_mc, k_mc = net.cross_forward(x1a, kv, w_middle, 2, 6)
    x1b = go(x1b, [last])
    x1b, w_last = end(x1b, last)

    def core(x):
        return place.swap(x, BIT_CORE)

    def go_on(x, sums=(), start=()):
        x = hold(x, *sums)
        for g in sums:
            g.sums()
        x = need(x, *(tuple(sums) + tuple(g for g in start if g not in sums)))
        for g in start:
            g.swap()
        return x

    def rest(x, *groups):
        for _ in range(place.outer_bits - 1):
            for g in groups:
                x = go_on(x, [g], [g])
        return x

    def pairs(x):
        return x, core(x)

    f_us, f_uf, f_ms = pairs(f_us), pairs(f_uf), pairs(f_ms)
    x1b, (f_us, f_uf, f_ms) = tie(x1b, f_us, f_uf, f_ms)
    f_mc = pairs(f_mc)
    dx, v_mf, p, f = net.last_backward(x1b, out_grad.reshape(-1, d), w_last, 8)
    p, f = pairs(p), pairs(f)
    x2 = net.last_output(x1b, f[0], w_last)
    p, (x2,) = tie(p, x2)
    s_mf = Sum(place, net.feed_grads(f, p))
    dx, (f_mc,) = tie(dx, f_mc)
    dx = go_on(dx, start=[s_mf])
    dx, v_mc, p_c, dkv = net.cross_backward(x1a, k_mc, kv, dx, w_middle, 2, 6)
    p_c = pairs(p_c)
    pair, send = net.pair_grads(enc_t, dkv)
    dx, (send,) = tie(dx, send)
    pair = pair, core(send)
    dx, v_ms, p = net.self_backward(x1, k_ms, dx, w_middle, 4, 4)
    p = pairs(p)
    dx = go_on(dx, [s_mf], [s_mf])
    dx, (p, p_c, pair) = tie(dx, p, p_c, pair)
    s_ma = Sum(place, net.attend_grads(f_ms, p, (f_mc, p_c, pair)))
    dx = go_on(dx, start=[s_ma])
    dx, v_uf, p = net.feed_backward(x0a, k_uf, dx, w_feed, 2)
    p = pairs(p)
    dx, (p,) = tie(dx, p)
    s_uf = Sum(place, net.feed_grads(f_uf, p))
    dx = need(dx, s_uf)
    v = [g[:2] for g in (v_uf, v_ms, v_mc, v_mf)]
    v = jnp.pad(jnp.concatenate(v, axis=0), ((2, 6), (0, 0)))
    dx, _v, p = net.self_backward(x0, k_us, dx, w_first, 0, 0, (v,))
    p = pairs(p)
    dx = go_on(dx, [s_mf], [s_uf, s_mf])
    dx = go_on(dx, [s_ma], [s_ma])
    dx, (dkv,) = tie(dx, dkv)
    denc = net.pair_input(dkv, w_middle)
    dx, (denc,) = tie(dx, denc)
    dx = rest(dx, s_mf)
    dx, (p,) = tie(dx, p)
    send, keep = net.attend_grads(f_us, p)
    v = nt(order[: d // 2], plus(p[0][4], p[1][4])[:LANES]).astype(bf16)
    send = jnp.concatenate((send, v[d // 4 :]), axis=1)
    keep = jnp.concatenate((keep, v[: d // 4]), axis=1)
    s_us = Sum(place, (send, keep))
    dx = need(dx, s_us)
    dx = go_on(dx, [s_ma], [s_ma])
    dx = go_on(dx, [s_uf], [s_uf, s_us])
    dx, (r_mf,) = tie(dx, s_mf.total())
    dx = rest(dx, s_ma)
    dx = go_on(dx, [s_uf], [s_uf])
    dx = go_on(dx, [s_us], [s_us])
    dx, (r_ma,) = tie(dx, s_ma.total())
    dx = rest(dx, s_uf)
    dx = go_on(dx, [s_us], [s_us])
    dx, (r_uf,) = tie(dx, s_uf.total())
    dx = rest(dx, s_us)
    r_us = s_us.total()

    def columns(r, *blocks):
        parts = [r[:, b * d : (b + 1) * d] for b in blocks]
        return jnp.concatenate(parts, axis=1) if len(parts) > 1 else parts[0]

    def feed_rows(r):
        return unspread(columns(r, 0, 2, 4, 6)), columns(r, 1, 3, 5, 7).reshape(-1, d)

    r_uup, r_udown = feed_rows(r_uf)
    r_mup, r_mdown = feed_rows(r_mf)
    vs = r_us[:, 4 * d :]
    v = [vs[:, i] for i in range(10)]
    return (
        x2.reshape(tokens.shape),
        dx.astype(bf16).reshape(tokens.shape),
        denc.reshape(encoder.shape),
        v[0], v[1], r_us[:, : 3 * d], r_us[:, 3 * d : 4 * d], v[2], v[3], r_uup, r_udown,
        v[4], v[5], r_ma[:, : 3 * d], columns(r_ma, 3), v[6], v[7],
        columns(r_ma, 4), r_ma[:, 6 * d :], columns(r_ma, 5),
        v[8], v[9], r_mup, r_mdown,
    )


def solution(mesh):
    rows1 = P(AXES)
    rows2 = P(AXES, None)
    rows3 = P(AXES, None, None)
    block = (rows1, rows1, rows2, rows2)
    weights = block * 2 + block + (rows1, rows1, rows2, rows2, rows2) + block
    return jax.shard_map(
        local,
        mesh=mesh,
        in_specs=(rows3, rows3, rows1, rows3) + weights,
        out_specs=(rows3, rows3, rows3) + weights,
        check_vma=False,
    )
```

```python
import functools

import jax
import jax.numpy as jnp
from jax import lax
from jax.experimental import pallas as pl
from jax.experimental.pallas import tpu as pltpu
from jax.sharding import PartitionSpec as P

DH = 64
AXES = ("dp", "hd")
EPS = 1e-05
MASKED = -1e30
LANES = 128
bf16 = jnp.bfloat16
f32 = jnp.float32
sds = jax.ShapeDtypeStruct


BIT_PAIR, BIT_CORE, BIT_NEAR = 1, 2, 4


class Place:
    def __init__(self):
        self.count = lax.axis_size("dp") * lax.axis_size("hd")
        self.outer_size = self.count // 8
        index = lax.axis_index("dp") * lax.axis_size("hd") + lax.axis_index("hd")
        self.pair = index % 2
        self.core = (index // 2) % 2
        self.near = (index // 4) % 2
        self.outer = index // 8
        self.outer_bits = self.outer_size.bit_length() - 1

    def swap(self, x, bit):
        return lax.ppermute(x, AXES, [(i, i ^ bit) for i in range(self.count)])

    def swap_by_core(self, x, bits):
        pairs = [(i, i ^ bits[(i // BIT_CORE) % 2]) for i in range(self.count)]
        return lax.ppermute(x, AXES, pairs)

    def order(self, d):
        n, rows = self.outer_size, d // self.count
        k = lax.broadcasted_iota(jnp.int32, (d, 1), 0)
        row, place = k % rows, (k // rows) % n
        outer = jnp.zeros_like(k)
        for b in range(self.outer_bits):
            outer = outer + ((place >> (self.outer_bits - 1 - b)) & 1) * (1 << b)
        outer = outer ^ self.outer
        rest = k // (rows * n)
        low, high = rest % 2, (rest // 2) % 2
        near = jnp.where((rest // 4) ^ self.core == 0, high, low)
        pair = high + low - near
        feature = outer * 2 + (near ^ self.near)
        feature = (feature * 2 + ((rest // 4) ^ self.core)) * 2 + (pair ^ self.pair)
        feature = feature * rows + row
        return (feature == lax.broadcasted_iota(jnp.int32, (d, d), 1)).astype(bf16)


def plus(a, b):
    return (a.astype(f32) + b.astype(f32)).astype(bf16)


class Sum:
    def __init__(self, place, grads):
        self.place, self.stage = place, 0
        self.send, self.kept = grads

    def swap(self):
        if self.stage < 2:
            bits = ((BIT_NEAR, BIT_PAIR), (BIT_PAIR, BIT_NEAR))[self.stage]
            self.got = self.place.swap_by_core(self.send, bits)
        else:
            self.got = self.place.swap(self.send, 8 << (self.stage - 2))

    def sums(self):
        if self.stage < 2:
            self.send, self.kept = half_sums(self.kept, self.got)
        else:
            half = self.kept.shape[0] // 2
            self.send = plus(self.kept[half:], self.got[half:])
            self.kept = plus(self.kept[:half], self.got[:half])
        self.stage += 1

    def total(self):
        return self.kept.astype(f32) + self.got.astype(f32)


class Gather:
    def __init__(self, place, shard):
        self.place, self.x, self.stage = place, shard, 0

    def swap(self):
        outer = self.place.outer_bits
        at = self.stage - outer
        if at < 0:
            self.got = self.place.swap(self.x, 8 << (outer - 1 - self.stage))
        elif at < 2:
            bits = ((BIT_PAIR, BIT_NEAR), (BIT_NEAR, BIT_PAIR))[at]
            self.got = self.place.swap_by_core(self.x, bits)
        else:
            self.got = self.place.swap(self.x, BIT_CORE)

    def join(self):
        self.x = jnp.concatenate((self.x, self.got), axis=0)
        self.stage += 1


def tie(x, *others):
    out = lax.optimization_barrier((x,) + others)
    return out[0], out[1:]


def hold(x, *groups):
    x, terms = tie(x, *[(g.kept, g.got) for g in groups])
    for g, t in zip(groups, terms):
        g.kept, g.got = t
    return x


def need(x, *groups):
    x, send = tie(x, *[g.send for g in groups])
    for g, k in zip(groups, send):
        g.send = k
    return x


def nn(a, b):
    return jnp.dot(a, b, preferred_element_type=f32)


def nt(a, b):
    return lax.dot_general(a, b, (((1,), (1,)), ((), ())), preferred_element_type=f32)


def tn(a, b):
    return lax.dot_general(a, b, (((0,), (0,)), ((), ())), preferred_element_type=f32)


def unit_norm(x):
    centred = x - jnp.mean(x, axis=-1, keepdims=True)
    inv = lax.rsqrt(jnp.mean(centred * centred, axis=-1, keepdims=True) + EPS)
    return centred * inv, inv


def norm_backward(grad, x, gain):
    unit, inv = unit_norm(x)
    du = grad * gain
    dx = inv * (
        du
        - jnp.mean(du, axis=-1, keepdims=True)
        - unit * jnp.mean(du * unit, axis=-1, keepdims=True)
    )
    return dx, jnp.sum(grad * unit, axis=0, keepdims=True), jnp.sum(grad, axis=0, keepdims=True)


GELU_A = 0.7978845608028654
GELU_B = 0.044715


def two_heads(x):
    first = lax.broadcasted_iota(jnp.int32, x.shape, 1) < DH
    zero = jnp.zeros_like(x)
    return jnp.concatenate((jnp.where(first, x, zero), jnp.where(first, zero, x)), axis=0)


def side_by_side(x):
    n = x.shape[0] // 2
    first = lax.broadcasted_iota(jnp.int32, (n, LANES), 1) < DH
    return jnp.where(first, x[:n], x[n:])


def probabilities(qs, k2, allowed):
    s = jnp.where(allowed, nt(qs, k2) * DH ** (-0.5), MASKED)
    e = jnp.exp(s - jnp.max(s, axis=-1, keepdims=True))
    return e / jnp.sum(e, axis=-1, keepdims=True)


def causal_mask(length):
    row = lax.broadcasted_iota(jnp.int32, (2 * length, length), 0)
    col = lax.broadcasted_iota(jnp.int32, (2 * length, length), 1)
    return jnp.where(row >= length, row - length, row) >= col


def attend_back(q2, k2, v2, do2, allowed):
    scale = DH ** (-0.5)
    qs, dos = two_heads(q2), two_heads(do2)
    p = probabilities(qs, k2, allowed)
    dp = nt(dos, v2)
    ds = (p * (dp - jnp.sum(p * dp, axis=-1, keepdims=True))).astype(bf16)
    dq = side_by_side(nn(ds, k2)) * scale
    dk = tn(ds, qs) * scale
    dv = tn(p.astype(bf16), dos)
    return dq.astype(bf16), dk.astype(bf16), dv.astype(bf16)


def relative(x, order_ref):
    return nt(x, order_ref[...]).astype(bf16)


def times(x, top_ref, low_ref):
    half = top_ref.shape[0]
    return nn(x[:, :half], top_ref[...]) + nn(x[:, half:], low_ref[...])


def times_back(g, top_ref, low_ref):
    return jnp.concatenate((nt(g, top_ref[...]), nt(g, low_ref[...])), axis=1)


def natural(x, order_ref):
    high = x.astype(bf16)
    low = (x - high.astype(f32)).astype(bf16)
    return nn(high, order_ref[...]) + nn(low, order_ref[...])


def self_forward_kernel(
    captions, row, x_ref, vec_ref, order_ref, top_ref, low_ref, y_ref, f_ref, qkv_ref, rel_ref
):
    j = pl.program_id(0)

    @pl.when(j == 0)
    def _():
        unit, _inv = unit_norm(x_ref[...].astype(f32))
        f_ref[0] = (unit * vec_ref[row : row + 1] + vec_ref[row + 1 : row + 2]).astype(bf16)
        rel_ref[...] = relative(f_ref[0], order_ref)

    @pl.when(j < 3)
    def _():
        qkv_ref[j] = times(rel_ref[...], top_ref, low_ref).astype(bf16)

    @pl.when(j == 3)
    def _():
        length = x_ref.shape[0] // captions
        allowed = causal_mask(length)
        for c in range(captions):
            at = slice(c * length, (c + 1) * length)
            for h in range(0, x_ref.shape[1], LANES):
                cols = slice(h, h + LANES)
                p = probabilities(two_heads(qkv_ref[0, at, cols]), qkv_ref[1, at, cols], allowed)
                o = side_by_side(nn(p.astype(bf16), qkv_ref[2, at, cols]))
                f_ref[1, at, cols] = o.astype(bf16)
        y_ref[...] = x_ref[...].astype(f32) + times(relative(f_ref[1], order_ref), top_ref, low_ref)


def self_backward_kernel(
    captions, row, x_ref, vec_ref, order_ref, qkv_ref, dx_ref, top_ref, low_ref, *refs
):
    out_ref, vg_ref, p_ref, acc_ref = refs[-4:]
    j = pl.program_id(0)

    @pl.when(j == 0)
    def _():
        dy = dx_ref[...].astype(bf16)
        p_ref[3] = dy
        do = times_back(dy, top_ref, low_ref).astype(bf16)
        do = nn(do, order_ref[...]).astype(bf16)
        length = x_ref.shape[0] // captions
        allowed = causal_mask(length)
        for c in range(captions):
            at = slice(c * length, (c + 1) * length)
            for h in range(0, x_ref.shape[1], LANES):
                cols = slice(h, h + LANES)
                dq, dk, dv = attend_back(
                    qkv_ref[0, at, cols], qkv_ref[1, at, cols], qkv_ref[2, at, cols],
                    do[at, cols], allowed,
                )
                p_ref[0, at, cols] = dq
                p_ref[1, at, cols] = dk
                p_ref[2, at, cols] = dv
        acc_ref[...] = jnp.zeros_like(acc_ref)

    @pl.when(j > 0)
    def _():
        acc_ref[...] += times_back(p_ref[j - 1], top_ref, low_ref)

    @pl.when(j == 3)
    def _():
        da = natural(acc_ref[...], order_ref)
        dn, gg, gs = norm_backward(da, x_ref[...].astype(f32), vec_ref[row : row + 1])
        out_ref[...] = dx_ref[...] + dn
        vg_ref[0:1] = gg
        vg_ref[1:2] = gs
        if len(refs) > 4:
            at = lax.broadcasted_iota(jnp.int32, refs[0].shape, 0)
            rows = jnp.where(at == 0, gg, jnp.where(at == 1, gs, refs[0][...]))
            p_ref[4] = jnp.zeros_like(p_ref[4])
            p_ref[4, 0 : refs[0].shape[0]] = rows.astype(bf16)


def cross_forward_kernel(
    captions, row, count_ref, x_ref, vec_ref, order_ref, kv_ref, top_ref, low_ref, y_ref, f_ref, q_ref
):
    j = pl.program_id(0)
    d = x_ref.shape[1]

    @pl.when(j == 0)
    def _():
        unit, _inv = unit_norm(x_ref[...])
        c = (unit * vec_ref[row : row + 1] + vec_ref[row + 1 : row + 2]).astype(bf16)
        f_ref[0] = c
        q_ref[...] = times(relative(c, order_ref), top_ref, low_ref).astype(bf16)

    @pl.when(j == 1)
    def _():
        length = x_ref.shape[0] // captions
        patches = kv_ref.shape[0] // captions
        slot = lax.broadcasted_iota(jnp.int32, (2 * length, patches), 1)
        for c in range(captions):
            at = slice(c * length, (c + 1) * length)
            keys = slice(c * patches, (c + 1) * patches)
            allowed = slot < count_ref[c]
            for h in range(0, d, LANES):
                cols = slice(h, h + LANES)
                vcols = slice(d + h, d + h + LANES)
                p = probabilities(two_heads(q_ref[at, cols]), kv_ref[keys, cols], allowed)
                o = side_by_side(nn(p.astype(bf16), kv_ref[keys, vcols]))
                f_ref[1, at, cols] = o.astype(bf16)
        y_ref[...] = x_ref[...] + times(relative(f_ref[1], order_ref), top_ref, low_ref)


def cross_backward_kernel(
    captions, row, count_ref, x_ref, vec_ref, order_ref, q_ref, kv_ref, dx_ref, top_ref, low_ref,
    out_ref, vg_ref, p_ref, dkv_ref,
):
    j = pl.program_id(0)
    d = x_ref.shape[1]

    @pl.when(j == 0)
    def _():
        dy = dx_ref[...].astype(bf16)
        p_ref[1] = dy
        do = times_back(dy, top_ref, low_ref).astype(bf16)
        do = nn(do, order_ref[...]).astype(bf16)
        length = x_ref.shape[0] // captions
        patches = kv_ref.shape[0] // captions
        slot = lax.broadcasted_iota(jnp.int32, (2 * length, patches), 1)
        for c in range(captions):
            at = slice(c * length, (c + 1) * length)
            keys = slice(c * patches, (c + 1) * patches)
            allowed = slot < count_ref[c]
            for h in range(0, d, LANES):
                cols = slice(h, h + LANES)
                vcols = slice(d + h, d + h + LANES)
                dq, dk, dv = attend_back(
                    q_ref[at, cols], kv_ref[keys, cols], kv_ref[keys, vcols], do[at, cols], allowed
                )
                p_ref[0, at, cols] = dq
                dkv_ref[keys, cols] = dk
                dkv_ref[keys, vcols] = dv

    @pl.when(j == 1)
    def _():
        dc = natural(times_back(p_ref[0], top_ref, low_ref), order_ref)
        dn, gg, gs = norm_backward(dc, x_ref[...], vec_ref[row : row + 1])
        out_ref[...] = dx_ref[...] + dn
        vg_ref[0:1] = gg
        vg_ref[1:2] = gs


def feed_forward_kernel(
    row, x_ref, vec_ref, order_ref, up_ref, up2_ref, down_ref, down2_ref, y_ref, f_ref, u_ref, rel_ref
):
    j = pl.program_id(0)

    @pl.when(j == 0)
    def _():
        unit, _inv = unit_norm(x_ref[...])
        f_ref[0] = (unit * vec_ref[row : row + 1] + vec_ref[row + 1 : row + 2]).astype(bf16)
        rel_ref[...] = relative(f_ref[0], order_ref)
        y_ref[...] = x_ref[...]

    u = times(rel_ref[...], up_ref, up2_ref)
    u_ref[...] = u
    g = (0.5 * u * (1.0 + jnp.tanh(GELU_A * (u + GELU_B * u * u * u)))).astype(bf16)
    f_ref[1 + j] = g
    y_ref[...] += times(relative(g, order_ref), down_ref, down2_ref)


def gelu_terms(u):
    t = jnp.tanh(GELU_A * (u + GELU_B * u * u * u))
    slope = 0.5 * (1.0 + t) + 0.5 * u * (1.0 - t * t) * GELU_A * (1.0 + 3.0 * GELU_B * u * u)
    return 0.5 * u * (1.0 + t), slope


def feed_backward_step(j, order_ref, slope, refs, p_ref, acc_ref):
    up_ref, up2_ref, down_ref, down2_ref = refs
    dg = times_back(p_ref[0], down_ref, down2_ref).astype(bf16)
    du = (slope * nn(dg, order_ref[...])).astype(bf16)
    p_ref[1 + j] = du
    acc_ref[...] += times_back(du, up_ref, up2_ref)


def feed_backward_end(row, order_ref, x_ref, vec_ref, dx_ref, acc_ref, out_ref, vg_ref):
    db = natural(acc_ref[...], order_ref)
    dn, gg, gs = norm_backward(db, x_ref[...], vec_ref[row : row + 1])
    out_ref[...] = dx_ref[...].astype(f32) + dn
    vg_ref[0:1] = gg
    vg_ref[1:2] = gs


def feed_backward_kernel(
    row, x_ref, vec_ref, order_ref, dx_ref, up_ref, up2_ref, down_ref, down2_ref, u_ref,
    out_ref, vg_ref, p_ref, acc_ref,
):
    j = pl.program_id(0)

    @pl.when(j == 0)
    def _():
        p_ref[0] = dx_ref[...].astype(bf16)
        acc_ref[...] = jnp.zeros_like(acc_ref)

    refs = up_ref, up2_ref, down_ref, down2_ref
    feed_backward_step(j, order_ref, gelu_terms(u_ref[...])[1], refs, p_ref, acc_ref)

    @pl.when(j == 3)
    def _():
        feed_backward_end(row, order_ref, x_ref, vec_ref, dx_ref, acc_ref, out_ref, vg_ref)


def last_backward_kernel(
    row, x_ref, vec_ref, order_ref, dx_ref, up_ref, up2_ref, down_ref, down2_ref,
    out_ref, vg_ref, p_ref, f_ref, acc_ref, rel_ref,
):
    j = pl.program_id(0)

    @pl.when(j == 0)
    def _():
        unit, _inv = unit_norm(x_ref[...])
        f_ref[0] = (unit * vec_ref[row : row + 1] + vec_ref[row + 1 : row + 2]).astype(bf16)
        rel_ref[...] = relative(f_ref[0], order_ref)
        p_ref[0] = dx_ref[...]
        acc_ref[...] = jnp.zeros_like(acc_ref)

    g, slope = gelu_terms(times(rel_ref[...], up_ref, up2_ref))
    f_ref[1 + j] = g.astype(bf16)
    refs = up_ref, up2_ref, down_ref, down2_ref
    feed_backward_step(j, order_ref, slope, refs, p_ref, acc_ref)

    @pl.when(j == 3)
    def _():
        feed_backward_end(row, order_ref, x_ref, vec_ref, dx_ref, acc_ref, out_ref, vg_ref)


def last_output_kernel(x_ref, order_ref, g_ref, down_ref, down2_ref, y_ref, acc_ref):
    j = pl.program_id(0)

    @pl.when(j == 0)
    def _():
        acc_ref[...] = x_ref[...]

    acc_ref[...] += times(relative(g_ref[0], order_ref), down_ref, down2_ref)

    @pl.when(j == 3)
    def _():
        y_ref[...] = acc_ref[...].astype(bf16)


def both(own_ref, got_ref):
    return jnp.concatenate((own_ref[0], got_ref[0]), axis=0)


def emit(g, send_ref, keep_ref):
    half = keep_ref.shape[0]
    keep_ref[...] = g[:half].astype(bf16)
    send_ref[...] = g[half:].astype(bf16)


def feed_grads_kernel(
    order_ref, b_ref, b2_ref, z_ref, z2_ref, g_ref, g2_ref, u_ref, u2_ref, send_ref, keep_ref, bt_ref
):
    d = order_ref.shape[1]

    @pl.when(pl.program_id(0) == 0)
    def _():
        bt_ref[...] = nt(order_ref[...], both(b_ref, b2_ref)).astype(bf16)

    up, down = (slice(None), slice(0, d)), (slice(None), slice(d, 2 * d))
    emit(nn(bt_ref[...], both(u_ref, u2_ref)), send_ref.at[up], keep_ref.at[up])
    gt = nt(order_ref[...], both(g_ref, g2_ref)).astype(bf16)
    emit(nn(gt, both(z_ref, z2_ref)), send_ref.at[down], keep_ref.at[down])


def attend_grads_kernel(order_ref, s_ref, s2_ref, sd_ref, sd2_ref, *refs):
    send_ref, keep_ref = refs[-2:]
    j = pl.program_id(0)

    def product(a_ref, a2_ref, d_ref, d2_ref):
        at = nt(order_ref[...], both(a_ref, a2_ref)).astype(bf16)
        emit(nn(at, both(d_ref, d2_ref)), send_ref, keep_ref)

    @pl.when(j < 4)
    def _():
        product(s_ref, s2_ref, sd_ref, sd2_ref)

    if len(refs) > 2:
        c_ref, c2_ref, cd_ref, cd2_ref, pair_ref, pair2_ref = refs[:6]

        @pl.when((j == 4) | (j == 5))
        def _():
            product(c_ref, c2_ref, cd_ref, cd2_ref)

        @pl.when(j > 5)
        def _():
            emit(pair_ref[...].astype(f32) + pair2_ref[...].astype(f32), send_ref, keep_ref)


def half_sums_kernel(kept_ref, got_ref, send_ref, keep_ref):
    emit(kept_ref[...].astype(f32) + got_ref[...].astype(f32), send_ref, keep_ref)


def half_sums(kept, got):
    rows, wide = kept.shape
    steps = 2 if wide % (2 * LANES) == 0 else 1
    full = pl.BlockSpec((rows, wide // steps), lambda j: (0, j))
    half = pl.BlockSpec((rows // 2, wide // steps), lambda j: (0, j))
    outs = (sds((rows // 2, wide), bf16),) * 2
    return call(half_sums_kernel, steps, (kept, got), [full] * 2, outs, [half] * 2, vmem=24)


def pair_forward_kernel(enc_ref, top_ref, low_ref, kv_ref):
    kv_ref[...] = times(enc_ref[...], top_ref, low_ref).astype(bf16)


def pair_input_kernel(dkv_ref, order_ref, top_ref, low_ref, out_ref):
    g = times_back(dkv_ref[...], top_ref, low_ref).astype(bf16)
    out_ref[...] = nn(g, order_ref[...]).astype(bf16)


def pair_grads_kernel(enc_ref, dkv_ref, keep_ref, send_ref):
    emit(nn(enc_ref[...], dkv_ref[...]), send_ref, keep_ref)


def pack_kernel(
    u_qkv, u_out, u_up, u_down, m_qkv, m_out, m_up, m_down, c_q, c_pair, c_out, vec,
    first_out, feed_out, middle_out, last_out,
):
    rows, d = u_out.shape
    spread = spread_matrix().astype(bf16)
    i = lax.broadcasted_iota(jnp.int32, (rows, 4 * rows), 0)
    k = lax.broadcasted_iota(jnp.int32, (rows, 4 * rows), 1)

    def feed(out, up, down):
        for b in range(4 * d // 512):
            y = nn(up[:, b * 512 : (b + 1) * 512], spread).astype(bf16)
            for j in range(4):
                to = j * d + b * LANES
                out[:, to : to + LANES] = y[:, j * LANES : (j + 1) * LANES]
        for j in range(4):
            y = nn((k == 4 * i + j).astype(bf16), down[...])
            out[:, (4 + j) * d : (5 + j) * d] = y.astype(bf16)

    first_out[:, : 3 * d] = u_qkv[...]
    first_out[:, 3 * d : 4 * d] = u_out[...]
    eye = lax.broadcasted_iota(jnp.int32, (rows, rows), 0) == lax.broadcasted_iota(jnp.int32, (rows, rows), 1)
    first_out[:, 4 * d :] = nt(eye.astype(bf16), vec[...]).astype(bf16)
    feed(feed_out, u_up, u_down)
    middle_out[:, : 2 * d] = c_pair[...]
    middle_out[:, 2 * d : 3 * d] = c_q[...]
    middle_out[:, 3 * d : 4 * d] = c_out[...]
    middle_out[:, 4 * d : 7 * d] = m_qkv[...]
    middle_out[:, 7 * d : 8 * d] = m_out[...]
    feed(last_out, m_up, m_down)


def whole(x):
    return pl.BlockSpec(x.shape, lambda *_: (0,) * len(x.shape))


def call(kernel, steps, ins, in_specs, outs, out_specs, scratch=(), scalars=0, vmem=24):
    return pl.pallas_call(
        kernel,
        out_shape=outs,
        grid_spec=pltpu.PrefetchScalarGridSpec(
            num_scalar_prefetch=scalars,
            grid=(steps,),
            in_specs=in_specs,
            out_specs=out_specs,
            scratch_shapes=scratch,
        ),
        compiler_params=pltpu.CompilerParams(
            dimension_semantics=("arbitrary",), vmem_limit_bytes=vmem << 20
        ),
        cost_estimate=pl.CostEstimate(flops=1000, bytes_accessed=1000, transcendentals=0),
    )(*ins)


class Layers:
    def __init__(self, captions, tokens, d, vec, order, count):
        self.captions, self.t, self.d = captions, tokens, d
        self.vec, self.order, self.count = vec, order, count
        self.xs = sds((tokens, d), f32)
        self.hs = sds((tokens, d), bf16)

    def weights(self, *columns):
        d = self.d
        specs = [pl.BlockSpec((d // 2, d), lambda j, *_, c=c: (0, c(j))) for c in columns]
        return [s for s in specs for _ in range(2)]

    def self_forward(self, x, w, at, row):
        outs = (self.xs, sds((2, self.t, self.d), bf16), sds((3, self.t, self.d), bf16))
        ins = (x, self.vec, self.order)
        return call(
            functools.partial(self_forward_kernel, self.captions, row), 4,
            ins + w, [whole(i) for i in ins] + self.weights(lambda j: at + j),
            outs, [whole(o) for o in outs], scratch=[pltpu.VMEM((self.t, self.d), bf16)],
        )

    def self_backward(self, x, kept, dx, w, at, row, vectors=()):
        d, t = self.d, self.t
        outs = (self.xs, sds((8, d), f32), sds((4 + len(vectors), t, d), bf16))
        ins = (x, self.vec, self.order, kept, dx)
        return call(
            functools.partial(self_backward_kernel, self.captions, row), 4,
            ins + w + vectors,
            [whole(i) for i in ins] + self.weights(lambda j: at + (j + 3) % 4)
            + [whole(v) for v in vectors],
            outs, [whole(i) for i in outs],
            scratch=[pltpu.VMEM((t, d), f32)],
        )

    def cross_forward(self, x, kv, w, at, row):
        outs = (self.xs, sds((2, self.t, self.d), bf16), self.hs)
        ins = (x, self.vec, self.order, kv)
        return call(
            functools.partial(cross_forward_kernel, self.captions, row), 2,
            (self.count,) + ins + w,
            [whole(i) for i in ins] + self.weights(lambda j: at + j),
            outs, [whole(o) for o in outs], scalars=1,
        )

    def cross_backward(self, x, kept, kv, dx, w, at, row):
        d, t = self.d, self.t
        outs = (self.xs, sds((8, d), f32), sds((2, t, d), bf16), sds(kv.shape, bf16))
        ins = (x, self.vec, self.order, kept, kv, dx)
        return call(
            functools.partial(cross_backward_kernel, self.captions, row), 2,
            (self.count,) + ins + w,
            [whole(i) for i in ins] + self.weights(lambda j: at + 1 - j),
            outs, [whole(i) for i in outs], scalars=1,
        )

    def pair_forward(self, enc, w):
        d, rows = self.d, enc.shape[0] // self.captions
        half = pl.BlockSpec((d // 2, 2 * d), lambda j: (0, 0))
        out = sds((enc.shape[0], 2 * d), bf16)
        return call(
            pair_forward_kernel, self.captions, (enc,) + w,
            [pl.BlockSpec((rows, d), lambda j: (j, 0)), half, half],
            out, pl.BlockSpec((rows, 2 * d), lambda j: (j, 0)),
        )

    def pair_grads(self, enc_t, dkv):
        d = self.d
        outs = (sds((d // 2, 2 * d), bf16),) * 2
        grad = pl.BlockSpec((d // 2, d), lambda j: (0, j))
        return call(
            pair_grads_kernel, 2, (enc_t, dkv),
            [whole(enc_t), pl.BlockSpec((dkv.shape[0], d), lambda j: (0, j))],
            outs, [grad, grad],
        )

    def pair_input(self, dkv, w):
        d, rows = self.d, dkv.shape[0] // self.captions
        half = pl.BlockSpec((d // 2, 2 * d), lambda j: (0, 0))
        out = sds((dkv.shape[0], d), bf16)
        return call(
            pair_input_kernel, self.captions, (dkv, self.order) + w,
            [pl.BlockSpec((rows, 2 * d), lambda j: (j, 0)), whole(self.order), half, half],
            out, pl.BlockSpec((rows, d), lambda j: (j, 0)),
        )

    def block(self, index):
        return pl.BlockSpec((1, self.t, self.d), lambda j: (index(j), 0, 0))

    def feed_grads(self, f, p):
        d, t = self.d, self.t
        outs = (sds((d // 4, 8 * d), bf16),) * 2
        first, later = self.block(lambda j: 0), self.block(lambda j: 1 + j)
        half = pl.BlockSpec((d // 2, d), lambda j: (0, 0))
        return call(
            feed_grads_kernel, 4, (self.order,) + f + p + f + p,
            [half] + [first] * 4 + [later] * 4,
            outs, [pl.BlockSpec((d // 4, 2 * d), lambda j: (0, j))] * 2,
            scratch=[pltpu.VMEM((d // 2, 2 * t), bf16)],
        )

    def attend_grads(self, f, p, cross=()):
        d, t = self.d, self.t
        steps = 8 if cross else 4
        outs = (sds((d // 4, steps * d), bf16),) * 2
        half = pl.BlockSpec((d // 2, d), lambda j: (0, 0))
        lhs = self.block(lambda j: jnp.minimum(j // 3, 1))
        rhs = self.block(lambda j: jnp.minimum(j, 3))
        ins, specs = (self.order,) + f + p, [half, lhs, lhs, rhs, rhs]
        if cross:
            f, p, pair = cross
            at = self.block(lambda j: jnp.clip(j - 4, 0, 1))
            columns = pl.BlockSpec((d // 2, d), lambda j: (0, jnp.clip(j - 6, 0, 1)))
            ins, specs = ins + f + p + pair, specs + [at] * 4 + [columns] * 2
        return call(
            attend_grads_kernel, steps, ins, specs,
            outs, [pl.BlockSpec((d // 4, d), lambda j: (0, j))] * 2,
        )

    def feed_forward(self, x, w, row):
        d, t = self.d, self.t
        outs = (self.xs, sds((5, t, d), bf16), sds((t, 4 * d), f32))
        ins = (x, self.vec, self.order)
        return call(
            functools.partial(feed_forward_kernel, row), 4,
            ins + w + w,
            [whole(i) for i in ins] + self.weights(lambda j: j, lambda j: 4 + j),
            outs, [whole(outs[0]), whole(outs[1]), pl.BlockSpec((t, d), lambda j: (0, j))],
            scratch=[pltpu.VMEM((t, d), bf16)],
        )

    def feed_backward(self, x, u, dx, w, row):
        d, t = self.d, self.t
        outs = (self.xs, sds((8, d), f32), sds((5, t, d), bf16))
        ins = (x, self.vec, self.order, dx)
        return call(
            functools.partial(feed_backward_kernel, row), 4,
            ins + w + w + (u,),
            [whole(i) for i in ins] + self.weights(lambda j: j, lambda j: 4 + j)
            + [pl.BlockSpec((t, d), lambda j: (0, j))],
            outs, [whole(i) for i in outs],
            scratch=[pltpu.VMEM((t, d), f32)],
        )

    def last_backward(self, x, dx, w, row):
        d, t = self.d, self.t
        outs = (self.xs, sds((8, d), f32)) + (sds((5, t, d), bf16),) * 2
        ins = (x, self.vec, self.order, dx)
        return call(
            functools.partial(last_backward_kernel, row), 4,
            ins + w + w,
            [whole(i) for i in ins] + self.weights(lambda j: j, lambda j: 4 + j),
            outs, [whole(i) for i in outs],
            scratch=[pltpu.VMEM((t, d), f32), pltpu.VMEM((t, d), bf16)],
        )

    def last_output(self, x, f, w):
        return call(
            last_output_kernel, 4, (x, self.order, f) + w,
            [whole(x), whole(self.order), self.block(lambda j: 1 + j)]
            + self.weights(lambda j: 4 + j),
            self.hs, whole(self.hs), scratch=[pltpu.VMEM((self.t, self.d), f32)],
        )


def spread_matrix():
    k = lax.broadcasted_iota(jnp.int32, (512, 512), 0)
    n = lax.broadcasted_iota(jnp.int32, (512, 512), 1)
    return (k % 4) * 128 + k // 4 == n


def unspread(up):
    rows, wide = up.shape
    y = up.reshape(rows, 4, wide // 512, 128).transpose(0, 2, 1, 3)
    y = lax.dot_general(
        y.reshape(rows * (wide // 512), 512), spread_matrix().astype(f32),
        (((1,), (1,)), ((), ())), precision=lax.Precision.HIGHEST,
    )
    return y.reshape(rows, wide)


def local(
    tokens, encoder, patch_count, out_grad,
    u_ag, u_as, u_qkv, u_out, u_mg, u_ms, u_up, u_down,
    m_ag, m_as, m_qkv, m_out, c_g, c_s, c_q, c_pair, c_out, m_mg, m_ms, m_up, m_down,
):
    place = Place()
    captions, length, d = tokens.shape
    rows = u_qkv.shape[0]
    x0 = tokens.reshape(-1, d)
    enc = encoder.reshape(-1, d)
    order = place.order(d)

    vectors = (u_ag, u_as, u_mg, u_ms, m_ag, m_as, c_g, c_s, m_mg, m_ms)
    vectors = jnp.pad(jnp.stack(vectors, axis=0), ((0, LANES - len(vectors)), (0, 0)))
    parts = (u_qkv, u_out, u_up, u_down, m_qkv, m_out, m_up, m_down, c_q, c_pair, c_out, vectors)
    packed = tuple(sds((rows, c), bf16) for c in (4 * d + LANES, 8 * d, 8 * d, 8 * d))
    shards = call(
        pack_kernel, 1, parts, [whole(p) for p in parts], packed, [whole(p) for p in packed], vmem=60
    )
    first, feed, middle, last = (Gather(place, x) for x in shards)

    def go(token, groups=(), start=()):
        token, got = tie(token, *[(g.x, g.got) for g in groups])
        for g, (x, y) in zip(groups, got):
            g.x, g.got = x, y
            g.join()
        every = tuple(groups) + tuple(start)
        token, xs = tie(token, *[g.x for g in every])
        for g, x in zip(every, xs):
            g.x = x
            g.swap()
        return token

    def end(token, group):
        token, (group.x, group.got) = tie(token, group.x, group.got)
        return token, (group.x, group.got)

    steps = place.outer_bits
    x0 = go(x0, start=[first])
    enc_rel = nt(enc, order).astype(bf16)
    enc_t = nt(order, enc).astype(bf16)
    for k in range(steps - 1):
        x0 = go(x0, [first], [feed] if k == 0 else [])
    x0 = go(x0, [first])
    for k in range(steps - 1):
        x0 = go(x0, [feed])
    x0 = go(x0, [first])
    x0 = go(x0, [feed], [middle])
    x0 = go(x0, [first])
    for k in range(steps - 1):
        x0 = go(x0, [middle])
    x0 = go(x0, [feed])
    x0, (order, enc_rel, enc_t) = tie(x0, order, enc_rel, enc_t)
    x0, w_first = end(x0, first)
    vec = tn(jnp.concatenate([x[:, 4 * d :] for x in w_first], axis=0), order)[:16]
    net = Layers(captions, captions * length, d, vec, order, patch_count)
    x0 = go(x0, [middle], [last])
    for k in range(steps - 1):
        x0 = go(x0, [last])
    x0 = go(x0, [feed])
    x0a, f_us, k_us = net.self_forward(x0, w_first, 0, 0)
    x0a = go(x0a, [middle])
    x0a = go(x0a, [last])
    x0a, w_feed = end(x0a, feed)
    x1, f_uf, k_uf = net.feed_forward(x0a, w_feed, 2)
    x1 = go(x1, [last])
    x1 = go(x1, [middle])
    x1, w_middle = end(x1, middle)
    x1a, f_ms, k_ms = net.self_forward(x1, w_middle, 4, 4)
    kv = net.pair_forward(enc_rel, w_middle)
    x1b, f_mc, k_mc = net.cross_forward(x1a, kv, w_middle, 2, 6)
    x1b = go(x1b, [last])
    x1b, w_last = end(x1b, last)

    def core(x):
        return place.swap(x, BIT_CORE)

    def go_on(x, sums=(), start=()):
        x = hold(x, *sums)
        for g in sums:
            g.sums()
        x = need(x, *(tuple(sums) + tuple(g for g in start if g not in sums)))
        for g in start:
            g.swap()
        return x

    def rest(x, *groups):
        for _ in range(place.outer_bits - 1):
            for g in groups:
                x = go_on(x, [g], [g])
        return x

    def pairs(x):
        return x, core(x)

    f_us, f_uf, f_ms = pairs(f_us), pairs(f_uf), pairs(f_ms)
    x1b, (f_us, f_uf, f_ms) = tie(x1b, f_us, f_uf, f_ms)
    f_mc = pairs(f_mc)
    dx, v_mf, p, f = net.last_backward(x1b, out_grad.reshape(-1, d), w_last, 8)
    p, f = pairs(p), pairs(f)
    x2 = net.last_output(x1b, f[0], w_last)
    p, (x2,) = tie(p, x2)
    s_mf = Sum(place, net.feed_grads(f, p))
    dx, (f_mc,) = tie(dx, f_mc)
    dx = go_on(dx, start=[s_mf])
    dx, v_mc, p_c, dkv = net.cross_backward(x1a, k_mc, kv, dx, w_middle, 2, 6)
    p_c = pairs(p_c)
    pair, send = net.pair_grads(enc_t, dkv)
    dx, (send,) = tie(dx, send)
    pair = pair, core(send)
    dx, v_ms, p = net.self_backward(x1, k_ms, dx, w_middle, 4, 4)
    p = pairs(p)
    dx = go_on(dx, [s_mf], [s_mf])
    dx, (p, p_c, pair) = tie(dx, p, p_c, pair)
    s_ma = Sum(place, net.attend_grads(f_ms, p, (f_mc, p_c, pair)))
    dx = go_on(dx, start=[s_ma])
    dx, v_uf, p = net.feed_backward(x0a, k_uf, dx, w_feed, 2)
    p = pairs(p)
    dx, (p,) = tie(dx, p)
    s_uf = Sum(place, net.feed_grads(f_uf, p))
    dx = need(dx, s_uf)
    v = [g[:2] for g in (v_uf, v_ms, v_mc, v_mf)]
    v = jnp.pad(jnp.concatenate(v, axis=0), ((2, 6), (0, 0)))
    dx, _v, p = net.self_backward(x0, k_us, dx, w_first, 0, 0, (v,))
    p = pairs(p)
    dx = go_on(dx, [s_mf], [s_uf, s_mf])
    dx = go_on(dx, [s_ma], [s_ma])
    dx, (p,) = tie(dx, p)
    send, keep = net.attend_grads(f_us, p)
    dx, (send, keep) = tie(dx, send, keep)
    v = nt(order[: d // 2], plus(p[0][4], p[1][4])[:LANES]).astype(bf16)
    dx, (dkv,) = tie(dx, dkv)
    denc = net.pair_input(dkv, w_middle)
    dx, (denc,) = tie(dx, denc)
    dx = go_on(dx, [s_ma], [s_ma])
    send = jnp.concatenate((send, v[d // 4 :]), axis=1)
    keep = jnp.concatenate((keep, v[: d // 4]), axis=1)
    s_us = Sum(place, (send, keep))
    dx = go_on(dx, start=[s_us])
    dx = rest(dx, s_mf)
    dx = go_on(dx, [s_uf], [s_uf])
    dx, (r_mf,) = tie(dx, s_mf.total())
    dx = rest(dx, s_ma)
    dx = go_on(dx, [s_uf], [s_uf])
    dx = go_on(dx, [s_us], [s_us])
    dx, (r_ma,) = tie(dx, s_ma.total())
    dx = rest(dx, s_uf)
    dx = go_on(dx, [s_us], [s_us])
    dx, (r_uf,) = tie(dx, s_uf.total())
    dx = rest(dx, s_us)
    r_us = s_us.total()

    def columns(r, *blocks):
        parts = [r[:, b * d : (b + 1) * d] for b in blocks]
        return jnp.concatenate(parts, axis=1) if len(parts) > 1 else parts[0]

    def feed_rows(r):
        return unspread(columns(r, 0, 2, 4, 6)), columns(r, 1, 3, 5, 7).reshape(-1, d)

    r_uup, r_udown = feed_rows(r_uf)
    r_mup, r_mdown = feed_rows(r_mf)
    vs = r_us[:, 4 * d :]
    v = [vs[:, i] for i in range(10)]
    return (
        x2.reshape(tokens.shape),
        dx.astype(bf16).reshape(tokens.shape),
        denc.reshape(encoder.shape),
        v[0], v[1], r_us[:, : 3 * d], r_us[:, 3 * d : 4 * d], v[2], v[3], r_uup, r_udown,
        v[4], v[5], r_ma[:, : 3 * d], columns(r_ma, 3), v[6], v[7],
        columns(r_ma, 4), r_ma[:, 6 * d :], columns(r_ma, 5),
        v[8], v[9], r_mup, r_mdown,
    )


def solution(mesh):
    rows1 = P(AXES)
    rows2 = P(AXES, None)
    rows3 = P(AXES, None, None)
    block = (rows1, rows1, rows2, rows2)
    weights = block * 2 + block + (rows1, rows1, rows2, rows2, rows2) + block
    return jax.shard_map(
        local,
        mesh=mesh,
        in_specs=(rows3, rows3, rows1, rows3) + weights,
        out_specs=(rows3, rows3, rows3) + weights,
        check_vma=False,
    )
```

```python
import functools

import jax
import jax.numpy as jnp
from jax import lax
from jax.experimental import pallas as pl
from jax.experimental.pallas import tpu as pltpu
from jax.sharding import PartitionSpec as P

DH = 64
AXES = ("dp", "hd")
EPS = 1e-05
MASKED = -1e30
LANES = 128
bf16 = jnp.bfloat16
f32 = jnp.float32
sds = jax.ShapeDtypeStruct


BIT_PAIR, BIT_CORE, BIT_NEAR = 1, 2, 4


class Place:
    def __init__(self):
        self.count = lax.axis_size("dp") * lax.axis_size("hd")
        self.outer_size = self.count // 8
        index = lax.axis_index("dp") * lax.axis_size("hd") + lax.axis_index("hd")
        self.pair = index % 2
        self.core = (index // 2) % 2
        self.near = (index // 4) % 2
        self.outer = index // 8
        self.outer_bits = self.outer_size.bit_length() - 1

    def swap(self, x, bit):
        return lax.ppermute(x, AXES, [(i, i ^ bit) for i in range(self.count)])

    def swap_by_core(self, x, bits):
        pairs = [(i, i ^ bits[(i // BIT_CORE) % 2]) for i in range(self.count)]
        return lax.ppermute(x, AXES, pairs)

    def order(self, d):
        n, rows = self.outer_size, d // self.count
        k = lax.broadcasted_iota(jnp.int32, (d, 1), 0)
        row, place = k % rows, (k // rows) % n
        outer = jnp.zeros_like(k)
        for b in range(self.outer_bits):
            outer = outer + ((place >> (self.outer_bits - 1 - b)) & 1) * (1 << b)
        outer = outer ^ self.outer
        rest = k // (rows * n)
        low, high = rest % 2, (rest // 2) % 2
        near = jnp.where((rest // 4) ^ self.core == 0, high, low)
        pair = high + low - near
        feature = outer * 2 + (near ^ self.near)
        feature = (feature * 2 + ((rest // 4) ^ self.core)) * 2 + (pair ^ self.pair)
        feature = feature * rows + row
        return (feature == lax.broadcasted_iota(jnp.int32, (d, d), 1)).astype(bf16)


def plus(a, b):
    return (a.astype(f32) + b.astype(f32)).astype(bf16)


class Sum:
    def __init__(self, place, grads):
        self.place, self.stage = place, 0
        self.send, self.kept = grads

    def swap(self):
        if self.stage < 2:
            bits = ((BIT_NEAR, BIT_PAIR), (BIT_PAIR, BIT_NEAR))[self.stage]
            self.got = self.place.swap_by_core(self.send, bits)
        else:
            self.got = self.place.swap(self.send, 8 << (self.stage - 2))

    def sums(self):
        if self.stage < 2:
            self.send, self.kept = half_sums(self.kept, self.got)
        else:
            half = self.kept.shape[0] // 2
            self.send = plus(self.kept[half:], self.got[half:])
            self.kept = plus(self.kept[:half], self.got[:half])
        self.stage += 1

    def total(self):
        return self.kept.astype(f32) + self.got.astype(f32)


class Gather:
    def __init__(self, place, shard):
        self.place, self.x, self.stage = place, shard, 0

    def swap(self):
        outer = self.place.outer_bits
        at = self.stage - outer
        if at < 0:
            self.got = self.place.swap(self.x, 8 << (outer - 1 - self.stage))
        elif at < 2:
            bits = ((BIT_PAIR, BIT_NEAR), (BIT_NEAR, BIT_PAIR))[at]
            self.got = self.place.swap_by_core(self.x, bits)
        else:
            self.got = self.place.swap(self.x, BIT_CORE)

    def join(self):
        self.x = jnp.concatenate((self.x, self.got), axis=0)
        self.stage += 1


def tie(x, *others):
    out = lax.optimization_barrier((x,) + others)
    return out[0], out[1:]


def hold(x, *groups):
    x, terms = tie(x, *[(g.kept, g.got) for g in groups])
    for g, t in zip(groups, terms):
        g.kept, g.got = t
    return x


def need(x, *groups):
    x, send = tie(x, *[g.send for g in groups])
    for g, k in zip(groups, send):
        g.send = k
    return x


def nn(a, b):
    return jnp.dot(a, b, preferred_element_type=f32)


def nt(a, b):
    return lax.dot_general(a, b, (((1,), (1,)), ((), ())), preferred_element_type=f32)


def tn(a, b):
    return lax.dot_general(a, b, (((0,), (0,)), ((), ())), preferred_element_type=f32)


def unit_norm(x):
    centred = x - jnp.mean(x, axis=-1, keepdims=True)
    inv = lax.rsqrt(jnp.mean(centred * centred, axis=-1, keepdims=True) + EPS)
    return centred * inv, inv


def norm_backward(grad, x, gain):
    unit, inv = unit_norm(x)
    du = grad * gain
    dx = inv * (
        du
        - jnp.mean(du, axis=-1, keepdims=True)
        - unit * jnp.mean(du * unit, axis=-1, keepdims=True)
    )
    return dx, jnp.sum(grad * unit, axis=0, keepdims=True), jnp.sum(grad, axis=0, keepdims=True)


GELU_A = 0.7978845608028654
GELU_B = 0.044715


def two_heads(x):
    first = lax.broadcasted_iota(jnp.int32, x.shape, 1) < DH
    zero = jnp.zeros_like(x)
    return jnp.concatenate((jnp.where(first, x, zero), jnp.where(first, zero, x)), axis=0)


def side_by_side(x):
    n = x.shape[0] // 2
    first = lax.broadcasted_iota(jnp.int32, (n, LANES), 1) < DH
    return jnp.where(first, x[:n], x[n:])


def probabilities(qs, k2, allowed):
    s = jnp.where(allowed, nt(qs, k2) * DH ** (-0.5), MASKED)
    e = jnp.exp(s - jnp.max(s, axis=-1, keepdims=True))
    return e / jnp.sum(e, axis=-1, keepdims=True)


def causal_mask(length):
    row = lax.broadcasted_iota(jnp.int32, (2 * length, length), 0)
    col = lax.broadcasted_iota(jnp.int32, (2 * length, length), 1)
    return jnp.where(row >= length, row - length, row) >= col


def attend_back(q2, k2, v2, do2, allowed):
    scale = DH ** (-0.5)
    qs, dos = two_heads(q2), two_heads(do2)
    p = probabilities(qs, k2, allowed)
    dp = nt(dos, v2)
    ds = (p * (dp - jnp.sum(p * dp, axis=-1, keepdims=True))).astype(bf16)
    dq = side_by_side(nn(ds, k2)) * scale
    dk = tn(ds, qs) * scale
    dv = tn(p.astype(bf16), dos)
    return dq.astype(bf16), dk.astype(bf16), dv.astype(bf16)


def relative(x, order_ref):
    return nt(x, order_ref[...]).astype(bf16)


def times(x, top_ref, low_ref):
    half = top_ref.shape[0]
    return nn(x[:, :half], top_ref[...]) + nn(x[:, half:], low_ref[...])


def times_back(g, top_ref, low_ref):
    return jnp.concatenate((nt(g, top_ref[...]), nt(g, low_ref[...])), axis=1)


def natural(x, order_ref):
    high = x.astype(bf16)
    low = (x - high.astype(f32)).astype(bf16)
    return nn(high, order_ref[...]) + nn(low, order_ref[...])


def self_forward_kernel(
    captions, row, x_ref, vec_ref, order_ref, top_ref, low_ref, y_ref, f_ref, qkv_ref, rel_ref
):
    j = pl.program_id(0)

    @pl.when(j == 0)
    def _():
        unit, _inv = unit_norm(x_ref[...].astype(f32))
        f_ref[0] = (unit * vec_ref[row : row + 1] + vec_ref[row + 1 : row + 2]).astype(bf16)
        rel_ref[...] = relative(f_ref[0], order_ref)

    @pl.when(j < 3)
    def _():
        qkv_ref[j] = times(rel_ref[...], top_ref, low_ref).astype(bf16)

    @pl.when(j == 3)
    def _():
        length = x_ref.shape[0] // captions
        allowed = causal_mask(length)
        for c in range(captions):
            at = slice(c * length, (c + 1) * length)
            for h in range(0, x_ref.shape[1], LANES):
                cols = slice(h, h + LANES)
                p = probabilities(two_heads(qkv_ref[0, at, cols]), qkv_ref[1, at, cols], allowed)
                o = side_by_side(nn(p.astype(bf16), qkv_ref[2, at, cols]))
                f_ref[1, at, cols] = o.astype(bf16)
        y_ref[...] = x_ref[...].astype(f32) + times(relative(f_ref[1], order_ref), top_ref, low_ref)


def self_backward_kernel(
    captions, row, x_ref, vec_ref, order_ref, qkv_ref, dx_ref, top_ref, low_ref, *refs
):
    out_ref, vg_ref, p_ref, acc_ref = refs[-4:]
    j = pl.program_id(0)

    @pl.when(j == 0)
    def _():
        dy = dx_ref[...].astype(bf16)
        p_ref[3] = dy
        do = times_back(dy, top_ref, low_ref).astype(bf16)
        do = nn(do, order_ref[...]).astype(bf16)
        length = x_ref.shape[0] // captions
        allowed = causal_mask(length)
        for c in range(captions):
            at = slice(c * length, (c + 1) * length)
            for h in range(0, x_ref.shape[1], LANES):
                cols = slice(h, h + LANES)
                dq, dk, dv = attend_back(
                    qkv_ref[0, at, cols], qkv_ref[1, at, cols], qkv_ref[2, at, cols],
                    do[at, cols], allowed,
                )
                p_ref[0, at, cols] = dq
                p_ref[1, at, cols] = dk
                p_ref[2, at, cols] = dv
        acc_ref[...] = jnp.zeros_like(acc_ref)

    @pl.when(j > 0)
    def _():
        acc_ref[...] += times_back(p_ref[j - 1], top_ref, low_ref)

    @pl.when(j == 3)
    def _():
        da = natural(acc_ref[...], order_ref)
        dn, gg, gs = norm_backward(da, x_ref[...].astype(f32), vec_ref[row : row + 1])
        out_ref[...] = dx_ref[...] + dn
        vg_ref[0:1] = gg
        vg_ref[1:2] = gs
        if len(refs) > 4:
            at = lax.broadcasted_iota(jnp.int32, refs[0].shape, 0)
            rows = jnp.where(at == 0, gg, jnp.where(at == 1, gs, refs[0][...]))
            p_ref[4] = jnp.zeros_like(p_ref[4])
            p_ref[4, 0 : refs[0].shape[0]] = rows.astype(bf16)


def cross_forward_kernel(
    captions, row, count_ref, x_ref, vec_ref, order_ref, kv_ref, top_ref, low_ref, y_ref, f_ref, q_ref
):
    j = pl.program_id(0)
    d = x_ref.shape[1]

    @pl.when(j == 0)
    def _():
        unit, _inv = unit_norm(x_ref[...])
        c = (unit * vec_ref[row : row + 1] + vec_ref[row + 1 : row + 2]).astype(bf16)
        f_ref[0] = c
        q_ref[...] = times(relative(c, order_ref), top_ref, low_ref).astype(bf16)

    @pl.when(j == 1)
    def _():
        length = x_ref.shape[0] // captions
        patches = kv_ref.shape[0] // captions
        slot = lax.broadcasted_iota(jnp.int32, (2 * length, patches), 1)
        for c in range(captions):
            at = slice(c * length, (c + 1) * length)
            keys = slice(c * patches, (c + 1) * patches)
            allowed = slot < count_ref[c]
            for h in range(0, d, LANES):
                cols = slice(h, h + LANES)
                vcols = slice(d + h, d + h + LANES)
                p = probabilities(two_heads(q_ref[at, cols]), kv_ref[keys, cols], allowed)
                o = side_by_side(nn(p.astype(bf16), kv_ref[keys, vcols]))
                f_ref[1, at, cols] = o.astype(bf16)
        y_ref[...] = x_ref[...] + times(relative(f_ref[1], order_ref), top_ref, low_ref)


def cross_backward_kernel(
    captions, row, count_ref, x_ref, vec_ref, order_ref, q_ref, kv_ref, dx_ref, top_ref, low_ref,
    out_ref, vg_ref, p_ref, dkv_ref,
):
    j = pl.program_id(0)
    d = x_ref.shape[1]

    @pl.when(j == 0)
    def _():
        dy = dx_ref[...].astype(bf16)
        p_ref[1] = dy
        do = times_back(dy, top_ref, low_ref).astype(bf16)
        do = nn(do, order_ref[...]).astype(bf16)
        length = x_ref.shape[0] // captions
        patches = kv_ref.shape[0] // captions
        slot = lax.broadcasted_iota(jnp.int32, (2 * length, patches), 1)
        for c in range(captions):
            at = slice(c * length, (c + 1) * length)
            keys = slice(c * patches, (c + 1) * patches)
            allowed = slot < count_ref[c]
            for h in range(0, d, LANES):
                cols = slice(h, h + LANES)
                vcols = slice(d + h, d + h + LANES)
                dq, dk, dv = attend_back(
                    q_ref[at, cols], kv_ref[keys, cols], kv_ref[keys, vcols], do[at, cols], allowed
                )
                p_ref[0, at, cols] = dq
                dkv_ref[keys, cols] = dk
                dkv_ref[keys, vcols] = dv

    @pl.when(j == 1)
    def _():
        dc = natural(times_back(p_ref[0], top_ref, low_ref), order_ref)
        dn, gg, gs = norm_backward(dc, x_ref[...], vec_ref[row : row + 1])
        out_ref[...] = dx_ref[...] + dn
        vg_ref[0:1] = gg
        vg_ref[1:2] = gs


def feed_forward_kernel(
    row, x_ref, vec_ref, order_ref, up_ref, up2_ref, down_ref, down2_ref, y_ref, f_ref, u_ref, rel_ref
):
    j = pl.program_id(0)

    @pl.when(j == 0)
    def _():
        unit, _inv = unit_norm(x_ref[...])
        f_ref[0] = (unit * vec_ref[row : row + 1] + vec_ref[row + 1 : row + 2]).astype(bf16)
        rel_ref[...] = relative(f_ref[0], order_ref)
        y_ref[...] = x_ref[...]

    u = times(rel_ref[...], up_ref, up2_ref)
    u_ref[...] = u
    g = (0.5 * u * (1.0 + jnp.tanh(GELU_A * (u + GELU_B * u * u * u)))).astype(bf16)
    f_ref[1 + j] = g
    y_ref[...] += times(relative(g, order_ref), down_ref, down2_ref)


def gelu_terms(u):
    t = jnp.tanh(GELU_A * (u + GELU_B * u * u * u))
    slope = 0.5 * (1.0 + t) + 0.5 * u * (1.0 - t * t) * GELU_A * (1.0 + 3.0 * GELU_B * u * u)
    return 0.5 * u * (1.0 + t), slope


def feed_backward_step(j, order_ref, slope, refs, p_ref, acc_ref):
    up_ref, up2_ref, down_ref, down2_ref = refs
    dg = times_back(p_ref[0], down_ref, down2_ref).astype(bf16)
    du = (slope * nn(dg, order_ref[...])).astype(bf16)
    p_ref[1 + j] = du
    acc_ref[...] += times_back(du, up_ref, up2_ref)


def feed_backward_end(row, order_ref, x_ref, vec_ref, dx_ref, acc_ref, out_ref, vg_ref):
    db = natural(acc_ref[...], order_ref)
    dn, gg, gs = norm_backward(db, x_ref[...], vec_ref[row : row + 1])
    out_ref[...] = dx_ref[...].astype(f32) + dn
    vg_ref[0:1] = gg
    vg_ref[1:2] = gs


def feed_backward_kernel(
    row, x_ref, vec_ref, order_ref, dx_ref, up_ref, up2_ref, down_ref, down2_ref, u_ref,
    out_ref, vg_ref, p_ref, acc_ref,
):
    j = pl.program_id(0)

    @pl.when(j == 0)
    def _():
        p_ref[0] = dx_ref[...].astype(bf16)
        acc_ref[...] = jnp.zeros_like(acc_ref)

    refs = up_ref, up2_ref, down_ref, down2_ref
    feed_backward_step(j, order_ref, gelu_terms(u_ref[...])[1], refs, p_ref, acc_ref)

    @pl.when(j == 3)
    def _():
        feed_backward_end(row, order_ref, x_ref, vec_ref, dx_ref, acc_ref, out_ref, vg_ref)


def last_backward_kernel(
    row, x_ref, vec_ref, order_ref, dx_ref, up_ref, up2_ref, down_ref, down2_ref,
    out_ref, vg_ref, p_ref, f_ref, acc_ref, rel_ref,
):
    j = pl.program_id(0)

    @pl.when(j == 0)
    def _():
        unit, _inv = unit_norm(x_ref[...])
        f_ref[0] = (unit * vec_ref[row : row + 1] + vec_ref[row + 1 : row + 2]).astype(bf16)
        rel_ref[...] = relative(f_ref[0], order_ref)
        p_ref[0] = dx_ref[...]
        acc_ref[...] = jnp.zeros_like(acc_ref)

    g, slope = gelu_terms(times(rel_ref[...], up_ref, up2_ref))
    f_ref[1 + j] = g.astype(bf16)
    refs = up_ref, up2_ref, down_ref, down2_ref
    feed_backward_step(j, order_ref, slope, refs, p_ref, acc_ref)

    @pl.when(j == 3)
    def _():
        feed_backward_end(row, order_ref, x_ref, vec_ref, dx_ref, acc_ref, out_ref, vg_ref)


def last_output_kernel(x_ref, order_ref, g_ref, down_ref, down2_ref, y_ref, acc_ref):
    j = pl.program_id(0)

    @pl.when(j == 0)
    def _():
        acc_ref[...] = x_ref[...]

    acc_ref[...] += times(relative(g_ref[0], order_ref), down_ref, down2_ref)

    @pl.when(j == 3)
    def _():
        y_ref[...] = acc_ref[...].astype(bf16)


def both(own_ref, got_ref):
    return jnp.concatenate((own_ref[0], got_ref[0]), axis=0)


def emit(g, send_ref, keep_ref):
    half = keep_ref.shape[0]
    keep_ref[...] = g[:half].astype(bf16)
    send_ref[...] = g[half:].astype(bf16)


def feed_grads_kernel(
    order_ref, b_ref, b2_ref, z_ref, z2_ref, g_ref, g2_ref, u_ref, u2_ref, send_ref, keep_ref, bt_ref
):
    d = order_ref.shape[1]

    @pl.when(pl.program_id(0) == 0)
    def _():
        bt_ref[...] = nt(order_ref[...], both(b_ref, b2_ref)).astype(bf16)

    up, down = (slice(None), slice(0, d)), (slice(None), slice(d, 2 * d))
    emit(nn(bt_ref[...], both(u_ref, u2_ref)), send_ref.at[up], keep_ref.at[up])
    gt = nt(order_ref[...], both(g_ref, g2_ref)).astype(bf16)
    emit(nn(gt, both(z_ref, z2_ref)), send_ref.at[down], keep_ref.at[down])


def attend_grads_kernel(order_ref, s_ref, s2_ref, sd_ref, sd2_ref, *refs):
    send_ref, keep_ref = refs[-2:]
    j = pl.program_id(0)

    def product(a_ref, a2_ref, d_ref, d2_ref):
        at = nt(order_ref[...], both(a_ref, a2_ref)).astype(bf16)
        emit(nn(at, both(d_ref, d2_ref)), send_ref, keep_ref)

    @pl.when(j < 4)
    def _():
        product(s_ref, s2_ref, sd_ref, sd2_ref)

    if len(refs) > 2:
        c_ref, c2_ref, cd_ref, cd2_ref, pair_ref, pair2_ref = refs[:6]

        @pl.when((j == 4) | (j == 5))
        def _():
            product(c_ref, c2_ref, cd_ref, cd2_ref)

        @pl.when(j > 5)
        def _():
            emit(pair_ref[...].astype(f32) + pair2_ref[...].astype(f32), send_ref, keep_ref)


def half_sums_kernel(kept_ref, got_ref, send_ref, keep_ref):
    emit(kept_ref[...].astype(f32) + got_ref[...].astype(f32), send_ref, keep_ref)


def half_sums(kept, got):
    rows, wide = kept.shape
    steps = 2 if wide % (2 * LANES) == 0 else 1
    full = pl.BlockSpec((rows, wide // steps), lambda j: (0, j))
    half = pl.BlockSpec((rows // 2, wide // steps), lambda j: (0, j))
    outs = (sds((rows // 2, wide), bf16),) * 2
    return call(half_sums_kernel, steps, (kept, got), [full] * 2, outs, [half] * 2, vmem=24)


def feed_rows_kernel(kept_ref, got_ref, up_ref, down_ref):
    rows, wide = up_ref.shape
    d = wide // 4
    spread = spread_matrix().astype(bf16)
    i = lax.broadcasted_iota(jnp.int32, (4 * rows, rows), 0)
    k = lax.broadcasted_iota(jnp.int32, (4 * rows, rows), 1)

    def part(at, size):
        x = kept_ref[:, at : at + size].astype(f32) + got_ref[:, at : at + size].astype(f32)
        high = x.astype(bf16)
        return high, (x - high.astype(f32)).astype(bf16)

    for b in range(wide // 512):
        parts = [part(2 * j * d + b * LANES, LANES) for j in range(4)]
        high, low = (jnp.concatenate(p, axis=1) for p in zip(*parts))
        up_ref[:, b * 512 : (b + 1) * 512] = nt(high, spread) + nt(low, spread)
    down = jnp.zeros(down_ref.shape, f32)
    for j in range(4):
        place = (i == 4 * k + j).astype(bf16)
        high, low = part((2 * j + 1) * d, d)
        down = down + nn(place, high) + nn(place, low)
    down_ref[...] = down


def feed_rows(kept, got):
    rows, wide = kept.shape
    outs = sds((rows, wide // 2), f32), sds((4 * rows, wide // 8), f32)
    ins = kept, got
    return call(feed_rows_kernel, 1, ins, [whole(x) for x in ins], outs, [whole(x) for x in outs])


def pair_forward_kernel(enc_ref, top_ref, low_ref, kv_ref):
    kv_ref[...] = times(enc_ref[...], top_ref, low_ref).astype(bf16)


def pair_input_kernel(dkv_ref, order_ref, top_ref, low_ref, out_ref):
    g = times_back(dkv_ref[...], top_ref, low_ref).astype(bf16)
    out_ref[...] = nn(g, order_ref[...]).astype(bf16)


def pair_grads_kernel(enc_ref, dkv_ref, keep_ref, send_ref):
    emit(nn(enc_ref[...], dkv_ref[...]), send_ref, keep_ref)


def pack_kernel(
    u_qkv, u_out, u_up, u_down, m_qkv, m_out, m_up, m_down, c_q, c_pair, c_out, vec,
    first_out, feed_out, middle_out, last_out,
):
    rows, d = u_out.shape
    spread = spread_matrix().astype(bf16)
    i = lax.broadcasted_iota(jnp.int32, (rows, 4 * rows), 0)
    k = lax.broadcasted_iota(jnp.int32, (rows, 4 * rows), 1)

    def feed(out, up, down):
        for b in range(4 * d // 512):
            y = nn(up[:, b * 512 : (b + 1) * 512], spread).astype(bf16)
            for j in range(4):
                to = j * d + b * LANES
                out[:, to : to + LANES] = y[:, j * LANES : (j + 1) * LANES]
        for j in range(4):
            y = nn((k == 4 * i + j).astype(bf16), down[...])
            out[:, (4 + j) * d : (5 + j) * d] = y.astype(bf16)

    first_out[:, : 3 * d] = u_qkv[...]
    first_out[:, 3 * d : 4 * d] = u_out[...]
    eye = lax.broadcasted_iota(jnp.int32, (rows, rows), 0) == lax.broadcasted_iota(jnp.int32, (rows, rows), 1)
    first_out[:, 4 * d :] = nt(eye.astype(bf16), vec[...]).astype(bf16)
    feed(feed_out, u_up, u_down)
    middle_out[:, : 2 * d] = c_pair[...]
    middle_out[:, 2 * d : 3 * d] = c_q[...]
    middle_out[:, 3 * d : 4 * d] = c_out[...]
    middle_out[:, 4 * d : 7 * d] = m_qkv[...]
    middle_out[:, 7 * d : 8 * d] = m_out[...]
    feed(last_out, m_up, m_down)


def whole(x):
    return pl.BlockSpec(x.shape, lambda *_: (0,) * len(x.shape))


def call(kernel, steps, ins, in_specs, outs, out_specs, scratch=(), scalars=0, vmem=24):
    return pl.pallas_call(
        kernel,
        out_shape=outs,
        grid_spec=pltpu.PrefetchScalarGridSpec(
            num_scalar_prefetch=scalars,
            grid=(steps,),
            in_specs=in_specs,
            out_specs=out_specs,
            scratch_shapes=scratch,
        ),
        compiler_params=pltpu.CompilerParams(
            dimension_semantics=("arbitrary",), vmem_limit_bytes=vmem << 20
        ),
        cost_estimate=pl.CostEstimate(flops=1000, bytes_accessed=1000, transcendentals=0),
    )(*ins)


class Layers:
    def __init__(self, captions, tokens, d, vec, order, count):
        self.captions, self.t, self.d = captions, tokens, d
        self.vec, self.order, self.count = vec, order, count
        self.xs = sds((tokens, d), f32)
        self.hs = sds((tokens, d), bf16)

    def weights(self, *columns):
        d = self.d
        specs = [pl.BlockSpec((d // 2, d), lambda j, *_, c=c: (0, c(j))) for c in columns]
        return [s for s in specs for _ in range(2)]

    def self_forward(self, x, w, at, row):
        outs = (self.xs, sds((2, self.t, self.d), bf16), sds((3, self.t, self.d), bf16))
        ins = (x, self.vec, self.order)
        return call(
            functools.partial(self_forward_kernel, self.captions, row), 4,
            ins + w, [whole(i) for i in ins] + self.weights(lambda j: at + j),
            outs, [whole(o) for o in outs], scratch=[pltpu.VMEM((self.t, self.d), bf16)],
        )

    def self_backward(self, x, kept, dx, w, at, row, vectors=()):
        d, t = self.d, self.t
        outs = (self.xs, sds((8, d), f32), sds((4 + len(vectors), t, d), bf16))
        ins = (x, self.vec, self.order, kept, dx)
        return call(
            functools.partial(self_backward_kernel, self.captions, row), 4,
            ins + w + vectors,
            [whole(i) for i in ins] + self.weights(lambda j: at + (j + 3) % 4)
            + [whole(v) for v in vectors],
            outs, [whole(i) for i in outs],
            scratch=[pltpu.VMEM((t, d), f32)],
        )

    def cross_forward(self, x, kv, w, at, row):
        outs = (self.xs, sds((2, self.t, self.d), bf16), self.hs)
        ins = (x, self.vec, self.order, kv)
        return call(
            functools.partial(cross_forward_kernel, self.captions, row), 2,
            (self.count,) + ins + w,
            [whole(i) for i in ins] + self.weights(lambda j: at + j),
            outs, [whole(o) for o in outs], scalars=1,
        )

    def cross_backward(self, x, kept, kv, dx, w, at, row):
        d, t = self.d, self.t
        outs = (self.xs, sds((8, d), f32), sds((2, t, d), bf16), sds(kv.shape, bf16))
        ins = (x, self.vec, self.order, kept, kv, dx)
        return call(
            functools.partial(cross_backward_kernel, self.captions, row), 2,
            (self.count,) + ins + w,
            [whole(i) for i in ins] + self.weights(lambda j: at + 1 - j),
            outs, [whole(i) for i in outs], scalars=1,
        )

    def pair_forward(self, enc, w):
        d, rows = self.d, enc.shape[0] // self.captions
        half = pl.BlockSpec((d // 2, 2 * d), lambda j: (0, 0))
        out = sds((enc.shape[0], 2 * d), bf16)
        return call(
            pair_forward_kernel, self.captions, (enc,) + w,
            [pl.BlockSpec((rows, d), lambda j: (j, 0)), half, half],
            out, pl.BlockSpec((rows, 2 * d), lambda j: (j, 0)),
        )

    def pair_grads(self, enc_t, dkv):
        d = self.d
        outs = (sds((d // 2, 2 * d), bf16),) * 2
        grad = pl.BlockSpec((d // 2, d), lambda j: (0, j))
        return call(
            pair_grads_kernel, 2, (enc_t, dkv),
            [whole(enc_t), pl.BlockSpec((dkv.shape[0], d), lambda j: (0, j))],
            outs, [grad, grad],
        )

    def pair_input(self, dkv, w):
        d, rows = self.d, dkv.shape[0] // self.captions
        half = pl.BlockSpec((d // 2, 2 * d), lambda j: (0, 0))
        out = sds((dkv.shape[0], d), bf16)
        return call(
            pair_input_kernel, self.captions, (dkv, self.order) + w,
            [pl.BlockSpec((rows, 2 * d), lambda j: (j, 0)), whole(self.order), half, half],
            out, pl.BlockSpec((rows, d), lambda j: (j, 0)),
        )

    def block(self, index):
        return pl.BlockSpec((1, self.t, self.d), lambda j: (index(j), 0, 0))

    def feed_grads(self, f, p):
        d, t = self.d, self.t
        outs = (sds((d // 4, 8 * d), bf16),) * 2
        first, later = self.block(lambda j: 0), self.block(lambda j: 1 + j)
        half = pl.BlockSpec((d // 2, d), lambda j: (0, 0))
        return call(
            feed_grads_kernel, 4, (self.order,) + f + p + f + p,
            [half] + [first] * 4 + [later] * 4,
            outs, [pl.BlockSpec((d // 4, 2 * d), lambda j: (0, j))] * 2,
            scratch=[pltpu.VMEM((d // 2, 2 * t), bf16)],
        )

    def attend_grads(self, f, p, cross=()):
        d, t = self.d, self.t
        steps = 8 if cross else 4
        outs = (sds((d // 4, steps * d), bf16),) * 2
        half = pl.BlockSpec((d // 2, d), lambda j: (0, 0))
        lhs = self.block(lambda j: jnp.minimum(j // 3, 1))
        rhs = self.block(lambda j: jnp.minimum(j, 3))
        ins, specs = (self.order,) + f + p, [half, lhs, lhs, rhs, rhs]
        if cross:
            f, p, pair = cross
            at = self.block(lambda j: jnp.clip(j - 4, 0, 1))
            columns = pl.BlockSpec((d // 2, d), lambda j: (0, jnp.clip(j - 6, 0, 1)))
            ins, specs = ins + f + p + pair, specs + [at] * 4 + [columns] * 2
        return call(
            attend_grads_kernel, steps, ins, specs,
            outs, [pl.BlockSpec((d // 4, d), lambda j: (0, j))] * 2,
        )

    def feed_forward(self, x, w, row):
        d, t = self.d, self.t
        outs = (self.xs, sds((5, t, d), bf16), sds((t, 4 * d), f32))
        ins = (x, self.vec, self.order)
        return call(
            functools.partial(feed_forward_kernel, row), 4,
            ins + w + w,
            [whole(i) for i in ins] + self.weights(lambda j: j, lambda j: 4 + j),
            outs, [whole(outs[0]), whole(outs[1]), pl.BlockSpec((t, d), lambda j: (0, j))],
            scratch=[pltpu.VMEM((t, d), bf16)],
        )

    def feed_backward(self, x, u, dx, w, row):
        d, t = self.d, self.t
        outs = (self.xs, sds((8, d), f32), sds((5, t, d), bf16))
        ins = (x, self.vec, self.order, dx)
        return call(
            functools.partial(feed_backward_kernel, row), 4,
            ins + w + w + (u,),
            [whole(i) for i in ins] + self.weights(lambda j: j, lambda j: 4 + j)
            + [pl.BlockSpec((t, d), lambda j: (0, j))],
            outs, [whole(i) for i in outs],
            scratch=[pltpu.VMEM((t, d), f32)],
        )

    def last_backward(self, x, dx, w, row):
        d, t = self.d, self.t
        outs = (self.xs, sds((8, d), f32)) + (sds((5, t, d), bf16),) * 2
        ins = (x, self.vec, self.order, dx)
        return call(
            functools.partial(last_backward_kernel, row), 4,
            ins + w + w,
            [whole(i) for i in ins] + self.weights(lambda j: j, lambda j: 4 + j),
            outs, [whole(i) for i in outs],
            scratch=[pltpu.VMEM((t, d), f32), pltpu.VMEM((t, d), bf16)],
        )

    def last_output(self, x, f, w):
        return call(
            last_output_kernel, 4, (x, self.order, f) + w,
            [whole(x), whole(self.order), self.block(lambda j: 1 + j)]
            + self.weights(lambda j: 4 + j),
            self.hs, whole(self.hs), scratch=[pltpu.VMEM((self.t, self.d), f32)],
        )


def spread_matrix():
    k = lax.broadcasted_iota(jnp.int32, (512, 512), 0)
    n = lax.broadcasted_iota(jnp.int32, (512, 512), 1)
    return (k % 4) * 128 + k // 4 == n


def local(
    tokens, encoder, patch_count, out_grad,
    u_ag, u_as, u_qkv, u_out, u_mg, u_ms, u_up, u_down,
    m_ag, m_as, m_qkv, m_out, c_g, c_s, c_q, c_pair, c_out, m_mg, m_ms, m_up, m_down,
):
    place = Place()
    captions, length, d = tokens.shape
    rows = u_qkv.shape[0]
    x0 = tokens.reshape(-1, d)
    enc = encoder.reshape(-1, d)
    order = place.order(d)

    vectors = (u_ag, u_as, u_mg, u_ms, m_ag, m_as, c_g, c_s, m_mg, m_ms)
    vectors = jnp.pad(jnp.stack(vectors, axis=0), ((0, LANES - len(vectors)), (0, 0)))
    parts = (u_qkv, u_out, u_up, u_down, m_qkv, m_out, m_up, m_down, c_q, c_pair, c_out, vectors)
    packed = tuple(sds((rows, c), bf16) for c in (4 * d + LANES, 8 * d, 8 * d, 8 * d))
    shards = call(
        pack_kernel, 1, parts, [whole(p) for p in parts], packed, [whole(p) for p in packed], vmem=60
    )
    first, feed, middle, last = (Gather(place, x) for x in shards)

    def go(token, groups=(), start=()):
        token, got = tie(token, *[(g.x, g.got) for g in groups])
        for g, (x, y) in zip(groups, got):
            g.x, g.got = x, y
            g.join()
        every = tuple(groups) + tuple(start)
        token, xs = tie(token, *[g.x for g in every])
        for g, x in zip(every, xs):
            g.x = x
            g.swap()
        return token

    def end(token, group):
        token, (group.x, group.got) = tie(token, group.x, group.got)
        return token, (group.x, group.got)

    steps = place.outer_bits
    x0 = go(x0, start=[first])
    enc_rel = nt(enc, order).astype(bf16)
    enc_t = nt(order, enc).astype(bf16)
    for k in range(steps - 1):
        x0 = go(x0, [first], [feed] if k == 0 else [])
    x0 = go(x0, [first])
    for k in range(steps - 1):
        x0 = go(x0, [feed])
    x0 = go(x0, [first])
    x0 = go(x0, [feed], [middle])
    x0 = go(x0, [first, middle])
    x0 = go(x0, [feed])
    for k in range(steps - 2):
        x0 = go(x0, [middle])
    x0, (order, enc_rel, enc_t) = tie(x0, order, enc_rel, enc_t)
    x0, w_first = end(x0, first)
    vec = tn(jnp.concatenate([x[:, 4 * d :] for x in w_first], axis=0), order)[:16]
    net = Layers(captions, captions * length, d, vec, order, patch_count)
    x0 = go(x0, [middle], [last])
    for k in range(steps - 1):
        x0 = go(x0, [last])
    x0 = go(x0, [feed])
    x0a, f_us, k_us = net.self_forward(x0, w_first, 0, 0)
    x0a = go(x0a, [middle])
    x0a = go(x0a, [last])
    x0a, w_feed = end(x0a, feed)
    x1, f_uf, k_uf = net.feed_forward(x0a, w_feed, 2)
    x1 = go(x1, [last])
    x1 = go(x1, [middle])
    x1, w_middle = end(x1, middle)
    x1a, f_ms, k_ms = net.self_forward(x1, w_middle, 4, 4)
    kv = net.pair_forward(enc_rel, w_middle)
    x1b, f_mc, k_mc = net.cross_forward(x1a, kv, w_middle, 2, 6)
    x1b = go(x1b, [last])
    x1b, w_last = end(x1b, last)

    def core(x):
        return place.swap(x, BIT_CORE)

    def go_on(x, sums=(), start=()):
        x = hold(x, *sums)
        for g in sums:
            g.sums()
        x = need(x, *(tuple(sums) + tuple(g for g in start if g not in sums)))
        for g in start:
            g.swap()
        return x

    def rest(x, *groups):
        for _ in range(place.outer_bits - 1):
            for g in groups:
                x = go_on(x, [g], [g])
        return x

    def pairs(x):
        return x, core(x)

    f_us, f_uf, f_ms = pairs(f_us), pairs(f_uf), pairs(f_ms)
    x1b, (f_us, f_uf, f_ms) = tie(x1b, f_us, f_uf, f_ms)
    f_mc = pairs(f_mc)
    dx, v_mf, p, f = net.last_backward(x1b, out_grad.reshape(-1, d), w_last, 8)
    p, f = pairs(p), pairs(f)
    x2 = net.last_output(x1b, f[0], w_last)
    p, (x2,) = tie(p, x2)
    s_mf = Sum(place, net.feed_grads(f, p))
    dx, (f_mc,) = tie(dx, f_mc)
    dx = go_on(dx, start=[s_mf])
    dx, v_mc, p_c, dkv = net.cross_backward(x1a, k_mc, kv, dx, w_middle, 2, 6)
    p_c = pairs(p_c)
    pair, send = net.pair_grads(enc_t, dkv)
    dx, (send,) = tie(dx, send)
    pair = pair, core(send)
    dx, v_ms, p = net.self_backward(x1, k_ms, dx, w_middle, 4, 4)
    p = pairs(p)
    dx = go_on(dx, [s_mf], [s_mf])
    dx, (p, p_c, pair) = tie(dx, p, p_c, pair)
    s_ma = Sum(place, net.attend_grads(f_ms, p, (f_mc, p_c, pair)))
    dx = go_on(dx, start=[s_ma])
    dx, v_uf, p = net.feed_backward(x0a, k_uf, dx, w_feed, 2)
    p = pairs(p)
    dx, (p,) = tie(dx, p)
    s_uf = Sum(place, net.feed_grads(f_uf, p))
    dx = need(dx, s_uf)
    v = [g[:2] for g in (v_uf, v_ms, v_mc, v_mf)]
    v = jnp.pad(jnp.concatenate(v, axis=0), ((2, 6), (0, 0)))
    dx, _v, p = net.self_backward(x0, k_us, dx, w_first, 0, 0, (v,))
    p = pairs(p)
    dx = go_on(dx, [s_mf], [s_uf, s_mf])
    dx = go_on(dx, [s_ma], [s_ma])
    dx, (p,) = tie(dx, p)
    send, keep = net.attend_grads(f_us, p)
    dx, (send, keep) = tie(dx, send, keep)
    v = nt(order[: d // 2], plus(p[0][4], p[1][4])[:LANES]).astype(bf16)
    dx, (dkv,) = tie(dx, dkv)
    denc = net.pair_input(dkv, w_middle)
    dx, (denc,) = tie(dx, denc)
    dx = go_on(dx, [s_ma], [s_ma])
    send = jnp.concatenate((send, v[d // 4 :]), axis=1)
    keep = jnp.concatenate((keep, v[: d // 4]), axis=1)
    s_us = Sum(place, (send, keep))
    dx = go_on(dx, start=[s_us])
    dx = rest(dx, s_mf)
    dx = go_on(dx, [s_uf], [s_uf])
    dx, (r_mf,) = tie(dx, feed_rows(s_mf.kept, s_mf.got))
    dx = rest(dx, s_ma)
    dx = go_on(dx, [s_uf, s_us], [s_uf, s_us])
    dx, (r_ma,) = tie(dx, s_ma.total())
    dx = rest(dx, s_uf)
    dx = go_on(dx, [s_us], [s_us])
    dx, (r_uf,) = tie(dx, feed_rows(s_uf.kept, s_uf.got))
    dx = rest(dx, s_us)
    r_us = s_us.total()

    def columns(r, *blocks):
        parts = [r[:, b * d : (b + 1) * d] for b in blocks]
        return jnp.concatenate(parts, axis=1) if len(parts) > 1 else parts[0]

    r_uup, r_udown = r_uf
    r_mup, r_mdown = r_mf
    vs = r_us[:, 4 * d :]
    v = [vs[:, i] for i in range(10)]
    return (
        x2.reshape(tokens.shape),
        dx.astype(bf16).reshape(tokens.shape),
        denc.reshape(encoder.shape),
        v[0], v[1], r_us[:, : 3 * d], r_us[:, 3 * d : 4 * d], v[2], v[3], r_uup, r_udown,
        v[4], v[5], r_ma[:, : 3 * d], columns(r_ma, 3), v[6], v[7],
        columns(r_ma, 4), r_ma[:, 6 * d :], columns(r_ma, 5),
        v[8], v[9], r_mup, r_mdown,
    )


def solution(mesh):
    rows1 = P(AXES)
    rows2 = P(AXES, None)
    rows3 = P(AXES, None, None)
    block = (rows1, rows1, rows2, rows2)
    weights = block * 2 + block + (rows1, rows1, rows2, rows2, rows2) + block
    return jax.shard_map(
        local,
        mesh=mesh,
        in_specs=(rows3, rows3, rows1, rows3) + weights,
        out_specs=(rows3, rows3, rows3) + weights,
        check_vma=False,
    )
```

```python
import functools

import jax
import jax.numpy as jnp
from jax import lax
from jax.experimental import pallas as pl
from jax.experimental.pallas import tpu as pltpu
from jax.sharding import PartitionSpec as P

DH = 64
AXES = ("dp", "hd")
EPS = 1e-05
MASKED = -1e30
LANES = 128
bf16 = jnp.bfloat16
f32 = jnp.float32
sds = jax.ShapeDtypeStruct


BIT_PAIR, BIT_CORE, BIT_NEAR = 1, 2, 4


class Place:
    def __init__(self):
        self.count = lax.axis_size("dp") * lax.axis_size("hd")
        self.outer_size = self.count // 8
        index = lax.axis_index("dp") * lax.axis_size("hd") + lax.axis_index("hd")
        self.pair = index % 2
        self.core = (index // 2) % 2
        self.near = (index // 4) % 2
        self.outer = index // 8
        self.outer_bits = self.outer_size.bit_length() - 1

    def swap(self, x, bit):
        return lax.ppermute(x, AXES, [(i, i ^ bit) for i in range(self.count)])

    def swap_by_core(self, x, bits):
        pairs = [(i, i ^ bits[(i // BIT_CORE) % 2]) for i in range(self.count)]
        return lax.ppermute(x, AXES, pairs)

    def order(self, d):
        n, rows = self.outer_size, d // self.count
        k = lax.broadcasted_iota(jnp.int32, (d, 1), 0)
        row, place = k % rows, (k // rows) % n
        outer = jnp.zeros_like(k)
        for b in range(self.outer_bits):
            outer = outer + ((place >> (self.outer_bits - 1 - b)) & 1) * (1 << b)
        outer = outer ^ self.outer
        rest = k // (rows * n)
        low, high = rest % 2, (rest // 2) % 2
        near = jnp.where((rest // 4) ^ self.core == 0, high, low)
        pair = high + low - near
        feature = outer * 2 + (near ^ self.near)
        feature = (feature * 2 + ((rest // 4) ^ self.core)) * 2 + (pair ^ self.pair)
        feature = feature * rows + row
        return (feature == lax.broadcasted_iota(jnp.int32, (d, d), 1)).astype(bf16)


def plus(a, b):
    return (a.astype(f32) + b.astype(f32)).astype(bf16)


class Sum:
    def __init__(self, place, grads):
        self.place, self.stage = place, 0
        self.send, self.kept = grads

    def swap(self):
        if self.stage < 2:
            bits = ((BIT_NEAR, BIT_PAIR), (BIT_PAIR, BIT_NEAR))[self.stage]
            self.got = self.place.swap_by_core(self.send, bits)
        else:
            self.got = self.place.swap(self.send, 8 << (self.stage - 2))

    def sums(self):
        if self.stage < 2:
            self.send, self.kept = half_sums(self.kept, self.got)
        else:
            half = self.kept.shape[0] // 2
            self.send = plus(self.kept[half:], self.got[half:])
            self.kept = plus(self.kept[:half], self.got[:half])
        self.stage += 1

    def total(self):
        return self.kept.astype(f32) + self.got.astype(f32)


class Gather:
    def __init__(self, place, shard):
        self.place, self.x, self.stage = place, shard, 0

    def swap(self):
        outer = self.place.outer_bits
        at = self.stage - outer
        if at < 0:
            self.got = self.place.swap(self.x, 8 << (outer - 1 - self.stage))
        elif at < 2:
            bits = ((BIT_PAIR, BIT_NEAR), (BIT_NEAR, BIT_PAIR))[at]
            self.got = self.place.swap_by_core(self.x, bits)
        else:
            self.got = self.place.swap(self.x, BIT_CORE)

    def join(self):
        self.x = jnp.concatenate((self.x, self.got), axis=0)
        self.stage += 1


def tie(x, *others):
    out = lax.optimization_barrier((x,) + others)
    return out[0], out[1:]


def hold(x, *groups):
    x, terms = tie(x, *[(g.kept, g.got) for g in groups])
    for g, t in zip(groups, terms):
        g.kept, g.got = t
    return x


def need(x, *groups):
    x, send = tie(x, *[g.send for g in groups])
    for g, k in zip(groups, send):
        g.send = k
    return x


def nn(a, b):
    return jnp.dot(a, b, preferred_element_type=f32)


def nt(a, b):
    return lax.dot_general(a, b, (((1,), (1,)), ((), ())), preferred_element_type=f32)


def tn(a, b):
    return lax.dot_general(a, b, (((0,), (0,)), ((), ())), preferred_element_type=f32)


def unit_norm(x):
    centred = x - jnp.mean(x, axis=-1, keepdims=True)
    inv = lax.rsqrt(jnp.mean(centred * centred, axis=-1, keepdims=True) + EPS)
    return centred * inv, inv


def norm_backward(grad, x, gain):
    unit, inv = unit_norm(x)
    du = grad * gain
    dx = inv * (
        du
        - jnp.mean(du, axis=-1, keepdims=True)
        - unit * jnp.mean(du * unit, axis=-1, keepdims=True)
    )
    return dx, jnp.sum(grad * unit, axis=0, keepdims=True), jnp.sum(grad, axis=0, keepdims=True)


GELU_A = 0.7978845608028654
GELU_B = 0.044715


def two_heads(x):
    first = lax.broadcasted_iota(jnp.int32, x.shape, 1) < DH
    zero = jnp.zeros_like(x)
    return jnp.concatenate((jnp.where(first, x, zero), jnp.where(first, zero, x)), axis=0)


def side_by_side(x):
    n = x.shape[0] // 2
    first = lax.broadcasted_iota(jnp.int32, (n, LANES), 1) < DH
    return jnp.where(first, x[:n], x[n:])


def probabilities(qs, k2, allowed):
    s = jnp.where(allowed, nt(qs, k2) * DH ** (-0.5), MASKED)
    e = jnp.exp(s - jnp.max(s, axis=-1, keepdims=True))
    return e / jnp.sum(e, axis=-1, keepdims=True)


def causal_mask(length):
    row = lax.broadcasted_iota(jnp.int32, (2 * length, length), 0)
    col = lax.broadcasted_iota(jnp.int32, (2 * length, length), 1)
    return jnp.where(row >= length, row - length, row) >= col


def attend_back(q2, k2, v2, do2, allowed):
    scale = DH ** (-0.5)
    qs, dos = two_heads(q2), two_heads(do2)
    p = probabilities(qs, k2, allowed)
    dp = nt(dos, v2)
    ds = (p * (dp - jnp.sum(p * dp, axis=-1, keepdims=True))).astype(bf16)
    dq = side_by_side(nn(ds, k2)) * scale
    dk = tn(ds, qs) * scale
    dv = tn(p.astype(bf16), dos)
    return dq.astype(bf16), dk.astype(bf16), dv.astype(bf16)


def relative(x, order_ref):
    return nt(x, order_ref[...]).astype(bf16)


def times(x, top_ref, low_ref):
    half = top_ref.shape[0]
    return nn(x[:, :half], top_ref[...]) + nn(x[:, half:], low_ref[...])


def times_back(g, top_ref, low_ref):
    return jnp.concatenate((nt(g, top_ref[...]), nt(g, low_ref[...])), axis=1)


def natural(x, order_ref):
    high = x.astype(bf16)
    low = (x - high.astype(f32)).astype(bf16)
    return nn(high, order_ref[...]) + nn(low, order_ref[...])


def self_forward_kernel(
    captions, row, x_ref, vec_ref, order_ref, top_ref, low_ref, y_ref, f_ref, qkv_ref, rel_ref
):
    j = pl.program_id(0)

    @pl.when(j == 0)
    def _():
        unit, _inv = unit_norm(x_ref[...].astype(f32))
        f_ref[0] = (unit * vec_ref[row : row + 1] + vec_ref[row + 1 : row + 2]).astype(bf16)
        rel_ref[...] = relative(f_ref[0], order_ref)

    @pl.when(j < 3)
    def _():
        qkv_ref[j] = times(rel_ref[...], top_ref, low_ref).astype(bf16)

    @pl.when(j == 3)
    def _():
        length = x_ref.shape[0] // captions
        allowed = causal_mask(length)
        for c in range(captions):
            at = slice(c * length, (c + 1) * length)
            for h in range(0, x_ref.shape[1], LANES):
                cols = slice(h, h + LANES)
                p = probabilities(two_heads(qkv_ref[0, at, cols]), qkv_ref[1, at, cols], allowed)
                o = side_by_side(nn(p.astype(bf16), qkv_ref[2, at, cols]))
                f_ref[1, at, cols] = o.astype(bf16)
        y_ref[...] = x_ref[...].astype(f32) + times(relative(f_ref[1], order_ref), top_ref, low_ref)


def self_backward_kernel(
    captions, row, x_ref, vec_ref, order_ref, qkv_ref, dx_ref, top_ref, low_ref, *refs
):
    out_ref, vg_ref, p_ref, acc_ref = refs[-4:]
    j = pl.program_id(0)

    @pl.when(j == 0)
    def _():
        dy = dx_ref[...].astype(bf16)
        p_ref[3] = dy
        do = times_back(dy, top_ref, low_ref).astype(bf16)
        do = nn(do, order_ref[...]).astype(bf16)
        length = x_ref.shape[0] // captions
        allowed = causal_mask(length)
        for c in range(captions):
            at = slice(c * length, (c + 1) * length)
            for h in range(0, x_ref.shape[1], LANES):
                cols = slice(h, h + LANES)
                dq, dk, dv = attend_back(
                    qkv_ref[0, at, cols], qkv_ref[1, at, cols], qkv_ref[2, at, cols],
                    do[at, cols], allowed,
                )
                p_ref[0, at, cols] = dq
                p_ref[1, at, cols] = dk
                p_ref[2, at, cols] = dv
        acc_ref[...] = jnp.zeros_like(acc_ref)

    @pl.when(j > 0)
    def _():
        acc_ref[...] += times_back(p_ref[j - 1], top_ref, low_ref)

    @pl.when(j == 3)
    def _():
        da = natural(acc_ref[...], order_ref)
        dn, gg, gs = norm_backward(da, x_ref[...].astype(f32), vec_ref[row : row + 1])
        out_ref[...] = dx_ref[...] + dn
        vg_ref[0:1] = gg
        vg_ref[1:2] = gs
        if len(refs) > 4:
            at = lax.broadcasted_iota(jnp.int32, refs[0].shape, 0)
            rows = jnp.where(at == 0, gg, jnp.where(at == 1, gs, refs[0][...]))
            p_ref[4] = jnp.zeros_like(p_ref[4])
            p_ref[4, 0 : refs[0].shape[0]] = rows.astype(bf16)


def cross_forward_kernel(
    captions, row, count_ref, x_ref, vec_ref, order_ref, kv_ref, top_ref, low_ref, y_ref, f_ref, q_ref
):
    j = pl.program_id(0)
    d = x_ref.shape[1]

    @pl.when(j == 0)
    def _():
        unit, _inv = unit_norm(x_ref[...])
        c = (unit * vec_ref[row : row + 1] + vec_ref[row + 1 : row + 2]).astype(bf16)
        f_ref[0] = c
        q_ref[...] = times(relative(c, order_ref), top_ref, low_ref).astype(bf16)

    @pl.when(j == 1)
    def _():
        length = x_ref.shape[0] // captions
        patches = kv_ref.shape[0] // captions
        slot = lax.broadcasted_iota(jnp.int32, (2 * length, patches), 1)
        for c in range(captions):
            at = slice(c * length, (c + 1) * length)
            keys = slice(c * patches, (c + 1) * patches)
            allowed = slot < count_ref[c]
            for h in range(0, d, LANES):
                cols = slice(h, h + LANES)
                vcols = slice(d + h, d + h + LANES)
                p = probabilities(two_heads(q_ref[at, cols]), kv_ref[keys, cols], allowed)
                o = side_by_side(nn(p.astype(bf16), kv_ref[keys, vcols]))
                f_ref[1, at, cols] = o.astype(bf16)
        y_ref[...] = x_ref[...] + times(relative(f_ref[1], order_ref), top_ref, low_ref)


def cross_backward_kernel(
    captions, row, count_ref, x_ref, vec_ref, order_ref, q_ref, kv_ref, dx_ref, top_ref, low_ref,
    out_ref, vg_ref, p_ref, dkv_ref,
):
    j = pl.program_id(0)
    d = x_ref.shape[1]

    @pl.when(j == 0)
    def _():
        dy = dx_ref[...].astype(bf16)
        p_ref[1] = dy
        do = times_back(dy, top_ref, low_ref).astype(bf16)
        do = nn(do, order_ref[...]).astype(bf16)
        length = x_ref.shape[0] // captions
        patches = kv_ref.shape[0] // captions
        slot = lax.broadcasted_iota(jnp.int32, (2 * length, patches), 1)
        for c in range(captions):
            at = slice(c * length, (c + 1) * length)
            keys = slice(c * patches, (c + 1) * patches)
            allowed = slot < count_ref[c]
            for h in range(0, d, LANES):
                cols = slice(h, h + LANES)
                vcols = slice(d + h, d + h + LANES)
                dq, dk, dv = attend_back(
                    q_ref[at, cols], kv_ref[keys, cols], kv_ref[keys, vcols], do[at, cols], allowed
                )
                p_ref[0, at, cols] = dq
                dkv_ref[keys, cols] = dk
                dkv_ref[keys, vcols] = dv

    @pl.when(j == 1)
    def _():
        dc = natural(times_back(p_ref[0], top_ref, low_ref), order_ref)
        dn, gg, gs = norm_backward(dc, x_ref[...], vec_ref[row : row + 1])
        out_ref[...] = dx_ref[...] + dn
        vg_ref[0:1] = gg
        vg_ref[1:2] = gs


def feed_forward_kernel(
    row, x_ref, vec_ref, order_ref, up_ref, up2_ref, down_ref, down2_ref, y_ref, f_ref, u_ref, rel_ref
):
    j = pl.program_id(0)

    @pl.when(j == 0)
    def _():
        unit, _inv = unit_norm(x_ref[...])
        f_ref[0] = (unit * vec_ref[row : row + 1] + vec_ref[row + 1 : row + 2]).astype(bf16)
        rel_ref[...] = relative(f_ref[0], order_ref)
        y_ref[...] = x_ref[...]

    u = times(rel_ref[...], up_ref, up2_ref)
    u_ref[...] = u
    g = (0.5 * u * (1.0 + jnp.tanh(GELU_A * (u + GELU_B * u * u * u)))).astype(bf16)
    f_ref[1 + j] = g
    y_ref[...] += times(relative(g, order_ref), down_ref, down2_ref)


def gelu_terms(u):
    t = jnp.tanh(GELU_A * (u + GELU_B * u * u * u))
    slope = 0.5 * (1.0 + t) + 0.5 * u * (1.0 - t * t) * GELU_A * (1.0 + 3.0 * GELU_B * u * u)
    return 0.5 * u * (1.0 + t), slope


def feed_backward_step(j, order_ref, slope, refs, p_ref, acc_ref):
    up_ref, up2_ref, down_ref, down2_ref = refs
    dg = times_back(p_ref[0], down_ref, down2_ref).astype(bf16)
    du = (slope * nn(dg, order_ref[...])).astype(bf16)
    p_ref[1 + j] = du
    acc_ref[...] += times_back(du, up_ref, up2_ref)


def feed_backward_end(row, order_ref, x_ref, vec_ref, dx_ref, acc_ref, out_ref, vg_ref):
    db = natural(acc_ref[...], order_ref)
    dn, gg, gs = norm_backward(db, x_ref[...], vec_ref[row : row + 1])
    out_ref[...] = dx_ref[...].astype(f32) + dn
    vg_ref[0:1] = gg
    vg_ref[1:2] = gs


def feed_backward_kernel(
    row, x_ref, vec_ref, order_ref, dx_ref, up_ref, up2_ref, down_ref, down2_ref, u_ref,
    out_ref, vg_ref, p_ref, acc_ref,
):
    j = pl.program_id(0)

    @pl.when(j == 0)
    def _():
        p_ref[0] = dx_ref[...].astype(bf16)
        acc_ref[...] = jnp.zeros_like(acc_ref)

    refs = up_ref, up2_ref, down_ref, down2_ref
    feed_backward_step(j, order_ref, gelu_terms(u_ref[...])[1], refs, p_ref, acc_ref)

    @pl.when(j == 3)
    def _():
        feed_backward_end(row, order_ref, x_ref, vec_ref, dx_ref, acc_ref, out_ref, vg_ref)


def last_backward_kernel(
    row, x_ref, vec_ref, order_ref, dx_ref, up_ref, up2_ref, down_ref, down2_ref,
    out_ref, vg_ref, p_ref, f_ref, acc_ref, rel_ref,
):
    j = pl.program_id(0)

    @pl.when(j == 0)
    def _():
        unit, _inv = unit_norm(x_ref[...])
        f_ref[0] = (unit * vec_ref[row : row + 1] + vec_ref[row + 1 : row + 2]).astype(bf16)
        rel_ref[...] = relative(f_ref[0], order_ref)
        p_ref[0] = dx_ref[...]
        acc_ref[...] = jnp.zeros_like(acc_ref)

    g, slope = gelu_terms(times(rel_ref[...], up_ref, up2_ref))
    f_ref[1 + j] = g.astype(bf16)
    refs = up_ref, up2_ref, down_ref, down2_ref
    feed_backward_step(j, order_ref, slope, refs, p_ref, acc_ref)

    @pl.when(j == 3)
    def _():
        feed_backward_end(row, order_ref, x_ref, vec_ref, dx_ref, acc_ref, out_ref, vg_ref)


def last_output_kernel(x_ref, order_ref, g_ref, down_ref, down2_ref, y_ref, acc_ref):
    j = pl.program_id(0)

    @pl.when(j == 0)
    def _():
        acc_ref[...] = x_ref[...]

    acc_ref[...] += times(relative(g_ref[0], order_ref), down_ref, down2_ref)

    @pl.when(j == 3)
    def _():
        y_ref[...] = acc_ref[...].astype(bf16)


def both(own_ref, got_ref):
    return jnp.concatenate((own_ref[0], got_ref[0]), axis=0)


def emit(g, send_ref, keep_ref):
    half = keep_ref.shape[0]
    keep_ref[...] = g[:half].astype(bf16)
    send_ref[...] = g[half:].astype(bf16)


def feed_grads_kernel(
    order_ref, b_ref, b2_ref, z_ref, z2_ref, g_ref, g2_ref, u_ref, u2_ref, send_ref, keep_ref, bt_ref
):
    d = order_ref.shape[1]

    @pl.when(pl.program_id(0) == 0)
    def _():
        bt_ref[...] = nt(order_ref[...], both(b_ref, b2_ref)).astype(bf16)

    up, down = (slice(None), slice(0, d)), (slice(None), slice(d, 2 * d))
    emit(nn(bt_ref[...], both(u_ref, u2_ref)), send_ref.at[up], keep_ref.at[up])
    gt = nt(order_ref[...], both(g_ref, g2_ref)).astype(bf16)
    emit(nn(gt, both(z_ref, z2_ref)), send_ref.at[down], keep_ref.at[down])


def attend_grads_kernel(order_ref, s_ref, s2_ref, sd_ref, sd2_ref, *refs):
    send_ref, keep_ref = refs[-2:]
    j = pl.program_id(0)

    def product(a_ref, a2_ref, d_ref, d2_ref):
        at = nt(order_ref[...], both(a_ref, a2_ref)).astype(bf16)
        emit(nn(at, both(d_ref, d2_ref)), send_ref, keep_ref)

    @pl.when(j < 4)
    def _():
        product(s_ref, s2_ref, sd_ref, sd2_ref)

    if len(refs) > 2:
        c_ref, c2_ref, cd_ref, cd2_ref, pair_ref, pair2_ref = refs[:6]

        @pl.when((j == 4) | (j == 5))
        def _():
            product(c_ref, c2_ref, cd_ref, cd2_ref)

        @pl.when(j > 5)
        def _():
            emit(pair_ref[...].astype(f32) + pair2_ref[...].astype(f32), send_ref, keep_ref)


def half_sums_kernel(kept_ref, got_ref, send_ref, keep_ref):
    emit(kept_ref[...].astype(f32) + got_ref[...].astype(f32), send_ref, keep_ref)


def half_sums(kept, got):
    rows, wide = kept.shape
    steps = 2 if wide % (2 * LANES) == 0 else 1
    full = pl.BlockSpec((rows, wide // steps), lambda j: (0, j))
    half = pl.BlockSpec((rows // 2, wide // steps), lambda j: (0, j))
    outs = (sds((rows // 2, wide), bf16),) * 2
    return call(half_sums_kernel, steps, (kept, got), [full] * 2, outs, [half] * 2, vmem=24)


def feed_rows_kernel(kept_ref, got_ref, up_ref, down_ref):
    rows, wide = up_ref.shape
    d = wide // 4
    spread = spread_matrix().astype(bf16)
    i = lax.broadcasted_iota(jnp.int32, (4 * rows, rows), 0)
    k = lax.broadcasted_iota(jnp.int32, (4 * rows, rows), 1)

    def part(at, size):
        x = kept_ref[:, at : at + size].astype(f32) + got_ref[:, at : at + size].astype(f32)
        high = x.astype(bf16)
        return high, (x - high.astype(f32)).astype(bf16)

    for b in range(wide // 512):
        parts = [part(2 * j * d + b * LANES, LANES) for j in range(4)]
        high, low = (jnp.concatenate(p, axis=1) for p in zip(*parts))
        up_ref[:, b * 512 : (b + 1) * 512] = nt(high, spread) + nt(low, spread)
    down = jnp.zeros(down_ref.shape, f32)
    for j in range(4):
        place = (i == 4 * k + j).astype(bf16)
        high, low = part((2 * j + 1) * d, d)
        down = down + nn(place, high) + nn(place, low)
    down_ref[...] = down


def feed_rows(kept, got):
    rows, wide = kept.shape
    outs = sds((rows, wide // 2), f32), sds((4 * rows, wide // 8), f32)
    ins = kept, got
    return call(feed_rows_kernel, 1, ins, [whole(x) for x in ins], outs, [whole(x) for x in outs])


def pair_forward_kernel(enc_ref, top_ref, low_ref, kv_ref):
    kv_ref[...] = times(enc_ref[...], top_ref, low_ref).astype(bf16)


def pair_input_kernel(dkv_ref, order_ref, top_ref, low_ref, out_ref):
    g = times_back(dkv_ref[...], top_ref, low_ref).astype(bf16)
    out_ref[...] = nn(g, order_ref[...]).astype(bf16)


def pair_grads_kernel(enc_ref, dkv_ref, keep_ref, send_ref):
    emit(nn(enc_ref[...], dkv_ref[...]), send_ref, keep_ref)


def first_pack_kernel(u_qkv, u_out, vec, out):
    rows, d = u_out.shape
    out[:, : 3 * d] = u_qkv[...]
    out[:, 3 * d : 4 * d] = u_out[...]
    eye = lax.broadcasted_iota(jnp.int32, (rows, rows), 0) == lax.broadcasted_iota(jnp.int32, (rows, rows), 1)
    out[:, 4 * d :] = nt(eye.astype(bf16), vec[...]).astype(bf16)


def pack_kernel(
    u_up, u_down, m_qkv, m_out, m_up, m_down, c_q, c_pair, c_out, feed_out, middle_out, last_out
):
    rows, d = m_out.shape
    spread = spread_matrix().astype(bf16)
    i = lax.broadcasted_iota(jnp.int32, (rows, 4 * rows), 0)
    k = lax.broadcasted_iota(jnp.int32, (rows, 4 * rows), 1)

    def feed(out, up, down):
        for b in range(4 * d // 512):
            y = nn(up[:, b * 512 : (b + 1) * 512], spread).astype(bf16)
            for j in range(4):
                to = j * d + b * LANES
                out[:, to : to + LANES] = y[:, j * LANES : (j + 1) * LANES]
        for j in range(4):
            y = nn((k == 4 * i + j).astype(bf16), down[...])
            out[:, (4 + j) * d : (5 + j) * d] = y.astype(bf16)

    feed(feed_out, u_up, u_down)
    middle_out[:, : 2 * d] = c_pair[...]
    middle_out[:, 2 * d : 3 * d] = c_q[...]
    middle_out[:, 3 * d : 4 * d] = c_out[...]
    middle_out[:, 4 * d : 7 * d] = m_qkv[...]
    middle_out[:, 7 * d : 8 * d] = m_out[...]
    feed(last_out, m_up, m_down)


def whole(x):
    return pl.BlockSpec(x.shape, lambda *_: (0,) * len(x.shape))


def call(kernel, steps, ins, in_specs, outs, out_specs, scratch=(), scalars=0, vmem=24):
    return pl.pallas_call(
        kernel,
        out_shape=outs,
        grid_spec=pltpu.PrefetchScalarGridSpec(
            num_scalar_prefetch=scalars,
            grid=(steps,),
            in_specs=in_specs,
            out_specs=out_specs,
            scratch_shapes=scratch,
        ),
        compiler_params=pltpu.CompilerParams(
            dimension_semantics=("arbitrary",), vmem_limit_bytes=vmem << 20
        ),
        cost_estimate=pl.CostEstimate(flops=1000, bytes_accessed=1000, transcendentals=0),
    )(*ins)


class Layers:
    def __init__(self, captions, tokens, d, vec, order, count):
        self.captions, self.t, self.d = captions, tokens, d
        self.vec, self.order, self.count = vec, order, count
        self.xs = sds((tokens, d), f32)
        self.hs = sds((tokens, d), bf16)

    def weights(self, *columns):
        d = self.d
        specs = [pl.BlockSpec((d // 2, d), lambda j, *_, c=c: (0, c(j))) for c in columns]
        return [s for s in specs for _ in range(2)]

    def self_forward(self, x, w, at, row):
        outs = (self.xs, sds((2, self.t, self.d), bf16), sds((3, self.t, self.d), bf16))
        ins = (x, self.vec, self.order)
        return call(
            functools.partial(self_forward_kernel, self.captions, row), 4,
            ins + w, [whole(i) for i in ins] + self.weights(lambda j: at + j),
            outs, [whole(o) for o in outs], scratch=[pltpu.VMEM((self.t, self.d), bf16)],
        )

    def self_backward(self, x, kept, dx, w, at, row, vectors=()):
        d, t = self.d, self.t
        outs = (self.xs, sds((8, d), f32), sds((4 + len(vectors), t, d), bf16))
        ins = (x, self.vec, self.order, kept, dx)
        return call(
            functools.partial(self_backward_kernel, self.captions, row), 4,
            ins + w + vectors,
            [whole(i) for i in ins] + self.weights(lambda j: at + (j + 3) % 4)
            + [whole(v) for v in vectors],
            outs, [whole(i) for i in outs],
            scratch=[pltpu.VMEM((t, d), f32)],
        )

    def cross_forward(self, x, kv, w, at, row):
        outs = (self.xs, sds((2, self.t, self.d), bf16), self.hs)
        ins = (x, self.vec, self.order, kv)
        return call(
            functools.partial(cross_forward_kernel, self.captions, row), 2,
            (self.count,) + ins + w,
            [whole(i) for i in ins] + self.weights(lambda j: at + j),
            outs, [whole(o) for o in outs], scalars=1,
        )

    def cross_backward(self, x, kept, kv, dx, w, at, row):
        d, t = self.d, self.t
        outs = (self.xs, sds((8, d), f32), sds((2, t, d), bf16), sds(kv.shape, bf16))
        ins = (x, self.vec, self.order, kept, kv, dx)
        return call(
            functools.partial(cross_backward_kernel, self.captions, row), 2,
            (self.count,) + ins + w,
            [whole(i) for i in ins] + self.weights(lambda j: at + 1 - j),
            outs, [whole(i) for i in outs], scalars=1,
        )

    def pair_forward(self, enc, w):
        d, rows = self.d, enc.shape[0] // self.captions
        half = pl.BlockSpec((d // 2, 2 * d), lambda j: (0, 0))
        out = sds((enc.shape[0], 2 * d), bf16)
        return call(
            pair_forward_kernel, self.captions, (enc,) + w,
            [pl.BlockSpec((rows, d), lambda j: (j, 0)), half, half],
            out, pl.BlockSpec((rows, 2 * d), lambda j: (j, 0)),
        )

    def pair_grads(self, enc_t, dkv):
        d = self.d
        outs = (sds((d // 2, 2 * d), bf16),) * 2
        grad = pl.BlockSpec((d // 2, d), lambda j: (0, j))
        return call(
            pair_grads_kernel, 2, (enc_t, dkv),
            [whole(enc_t), pl.BlockSpec((dkv.shape[0], d), lambda j: (0, j))],
            outs, [grad, grad],
        )

    def pair_input(self, dkv, w):
        d, rows = self.d, dkv.shape[0] // self.captions
        half = pl.BlockSpec((d // 2, 2 * d), lambda j: (0, 0))
        out = sds((dkv.shape[0], d), bf16)
        return call(
            pair_input_kernel, self.captions, (dkv, self.order) + w,
            [pl.BlockSpec((rows, 2 * d), lambda j: (j, 0)), whole(self.order), half, half],
            out, pl.BlockSpec((rows, d), lambda j: (j, 0)),
        )

    def block(self, index):
        return pl.BlockSpec((1, self.t, self.d), lambda j: (index(j), 0, 0))

    def feed_grads(self, f, p):
        d, t = self.d, self.t
        outs = (sds((d // 4, 8 * d), bf16),) * 2
        first, later = self.block(lambda j: 0), self.block(lambda j: 1 + j)
        half = pl.BlockSpec((d // 2, d), lambda j: (0, 0))
        return call(
            feed_grads_kernel, 4, (self.order,) + f + p + f + p,
            [half] + [first] * 4 + [later] * 4,
            outs, [pl.BlockSpec((d // 4, 2 * d), lambda j: (0, j))] * 2,
            scratch=[pltpu.VMEM((d // 2, 2 * t), bf16)],
        )

    def attend_grads(self, f, p, cross=()):
        d, t = self.d, self.t
        steps = 8 if cross else 4
        outs = (sds((d // 4, steps * d), bf16),) * 2
        half = pl.BlockSpec((d // 2, d), lambda j: (0, 0))
        lhs = self.block(lambda j: jnp.minimum(j // 3, 1))
        rhs = self.block(lambda j: jnp.minimum(j, 3))
        ins, specs = (self.order,) + f + p, [half, lhs, lhs, rhs, rhs]
        if cross:
            f, p, pair = cross
            at = self.block(lambda j: jnp.clip(j - 4, 0, 1))
            columns = pl.BlockSpec((d // 2, d), lambda j: (0, jnp.clip(j - 6, 0, 1)))
            ins, specs = ins + f + p + pair, specs + [at] * 4 + [columns] * 2
        return call(
            attend_grads_kernel, steps, ins, specs,
            outs, [pl.BlockSpec((d // 4, d), lambda j: (0, j))] * 2,
        )

    def feed_forward(self, x, w, row):
        d, t = self.d, self.t
        outs = (self.xs, sds((5, t, d), bf16), sds((t, 4 * d), f32))
        ins = (x, self.vec, self.order)
        return call(
            functools.partial(feed_forward_kernel, row), 4,
            ins + w + w,
            [whole(i) for i in ins] + self.weights(lambda j: j, lambda j: 4 + j),
            outs, [whole(outs[0]), whole(outs[1]), pl.BlockSpec((t, d), lambda j: (0, j))],
            scratch=[pltpu.VMEM((t, d), bf16)],
        )

    def feed_backward(self, x, u, dx, w, row):
        d, t = self.d, self.t
        outs = (self.xs, sds((8, d), f32), sds((5, t, d), bf16))
        ins = (x, self.vec, self.order, dx)
        return call(
            functools.partial(feed_backward_kernel, row), 4,
            ins + w + w + (u,),
            [whole(i) for i in ins] + self.weights(lambda j: j, lambda j: 4 + j)
            + [pl.BlockSpec((t, d), lambda j: (0, j))],
            outs, [whole(i) for i in outs],
            scratch=[pltpu.VMEM((t, d), f32)],
        )

    def last_backward(self, x, dx, w, row):
        d, t = self.d, self.t
        outs = (self.xs, sds((8, d), f32)) + (sds((5, t, d), bf16),) * 2
        ins = (x, self.vec, self.order, dx)
        return call(
            functools.partial(last_backward_kernel, row), 4,
            ins + w + w,
            [whole(i) for i in ins] + self.weights(lambda j: j, lambda j: 4 + j),
            outs, [whole(i) for i in outs],
            scratch=[pltpu.VMEM((t, d), f32), pltpu.VMEM((t, d), bf16)],
        )

    def last_output(self, x, f, w):
        return call(
            last_output_kernel, 4, (x, self.order, f) + w,
            [whole(x), whole(self.order), self.block(lambda j: 1 + j)]
            + self.weights(lambda j: 4 + j),
            self.hs, whole(self.hs), scratch=[pltpu.VMEM((self.t, self.d), f32)],
        )


def spread_matrix():
    k = lax.broadcasted_iota(jnp.int32, (512, 512), 0)
    n = lax.broadcasted_iota(jnp.int32, (512, 512), 1)
    return (k % 4) * 128 + k // 4 == n


def local(
    tokens, encoder, patch_count, out_grad,
    u_ag, u_as, u_qkv, u_out, u_mg, u_ms, u_up, u_down,
    m_ag, m_as, m_qkv, m_out, c_g, c_s, c_q, c_pair, c_out, m_mg, m_ms, m_up, m_down,
):
    place = Place()
    captions, length, d = tokens.shape
    rows = u_qkv.shape[0]
    x0 = tokens.reshape(-1, d)
    enc = encoder.reshape(-1, d)
    order = place.order(d)

    vectors = (u_ag, u_as, u_mg, u_ms, m_ag, m_as, c_g, c_s, m_mg, m_ms)
    vectors = jnp.pad(jnp.stack(vectors, axis=0), ((0, LANES - len(vectors)), (0, 0)))
    def packed(kernel, parts, *widths):
        outs = tuple(sds((rows, c), bf16) for c in widths)
        shards = call(kernel, 1, parts, [whole(p) for p in parts], outs, [whole(o) for o in outs], vmem=60)
        return [Gather(place, x) for x in shards]

    (first,) = packed(first_pack_kernel, (u_qkv, u_out, vectors), 4 * d + LANES)
    parts = (u_up, u_down, m_qkv, m_out, m_up, m_down, c_q, c_pair, c_out)
    feed, middle, last = packed(pack_kernel, parts, 8 * d, 8 * d, 8 * d)

    def go(token, groups=(), start=()):
        token, got = tie(token, *[(g.x, g.got) for g in groups])
        for g, (x, y) in zip(groups, got):
            g.x, g.got = x, y
            g.join()
        every = tuple(groups) + tuple(start)
        token, xs = tie(token, *[g.x for g in every])
        for g, x in zip(every, xs):
            g.x = x
            g.swap()
        return token

    def end(token, group):
        token, (group.x, group.got) = tie(token, group.x, group.got)
        return token, (group.x, group.got)

    steps = place.outer_bits
    x0 = go(x0, start=[first])
    enc_rel = nt(enc, order).astype(bf16)
    enc_t = nt(order, enc).astype(bf16)
    for k in range(steps - 1):
        x0 = go(x0, [first], [feed] if k == 0 else [])
    x0 = go(x0, [first])
    for k in range(steps - 1):
        x0 = go(x0, [feed])
    x0 = go(x0, [first])
    x0 = go(x0, [feed], [middle])
    x0 = go(x0, [first, middle])
    x0 = go(x0, [feed])
    for k in range(steps - 2):
        x0 = go(x0, [middle])
    x0, (order, enc_rel, enc_t) = tie(x0, order, enc_rel, enc_t)
    x0, w_first = end(x0, first)
    vec = tn(jnp.concatenate([x[:, 4 * d :] for x in w_first], axis=0), order)[:16]
    net = Layers(captions, captions * length, d, vec, order, patch_count)
    x0 = go(x0, [middle], [last])
    for k in range(steps - 1):
        x0 = go(x0, [last])
    x0 = go(x0, [feed])
    x0a, f_us, k_us = net.self_forward(x0, w_first, 0, 0)
    x0a = go(x0a, [middle])
    x0a, w_feed = end(x0a, feed)
    x1, f_uf, k_uf = net.feed_forward(x0a, w_feed, 2)
    x1 = go(x1, [middle, last])
    x1, w_middle = end(x1, middle)
    kv = net.pair_forward(enc_rel, w_middle)
    x1, (kv,) = tie(x1, kv)
    x1 = go(x1, [last])
    x1a, f_ms, k_ms = net.self_forward(x1, w_middle, 4, 4)
    x1b, f_mc, k_mc = net.cross_forward(x1a, kv, w_middle, 2, 6)
    x1b = go(x1b, [last])
    x1b, w_last = end(x1b, last)

    def core(x):
        return place.swap(x, BIT_CORE)

    def go_on(x, sums=(), start=()):
        x = hold(x, *sums)
        for g in sums:
            g.sums()
        x = need(x, *(tuple(sums) + tuple(g for g in start if g not in sums)))
        for g in start:
            g.swap()
        return x

    def rest(x, *groups):
        for _ in range(place.outer_bits - 1):
            for g in groups:
                x = go_on(x, [g], [g])
        return x

    def pairs(x):
        return x, core(x)

    f_us, f_uf, f_ms = pairs(f_us), pairs(f_uf), pairs(f_ms)
    x1b, (f_us, f_uf, f_ms) = tie(x1b, f_us, f_uf, f_ms)
    f_mc = pairs(f_mc)
    dx, v_mf, p, f = net.last_backward(x1b, out_grad.reshape(-1, d), w_last, 8)
    p, f = pairs(p), pairs(f)
    x2 = net.last_output(x1b, f[0], w_last)
    p, (x2,) = tie(p, x2)
    s_mf = Sum(place, net.feed_grads(f, p))
    dx, (f_mc,) = tie(dx, f_mc)
    dx = go_on(dx, start=[s_mf])
    dx, v_mc, p_c, dkv = net.cross_backward(x1a, k_mc, kv, dx, w_middle, 2, 6)
    p_c = pairs(p_c)
    pair, send = net.pair_grads(enc_t, dkv)
    dx, (send,) = tie(dx, send)
    pair = pair, core(send)
    dx, v_ms, p = net.self_backward(x1, k_ms, dx, w_middle, 4, 4)
    p = pairs(p)
    dx = go_on(dx, [s_mf], [s_mf])
    dx, (p, p_c, pair) = tie(dx, p, p_c, pair)
    s_ma = Sum(place, net.attend_grads(f_ms, p, (f_mc, p_c, pair)))
    dx = go_on(dx, start=[s_ma])
    dx, v_uf, p = net.feed_backward(x0a, k_uf, dx, w_feed, 2)
    p = pairs(p)
    dx, (p,) = tie(dx, p)
    s_uf = Sum(place, net.feed_grads(f_uf, p))
    dx = need(dx, s_uf)
    v = [g[:2] for g in (v_uf, v_ms, v_mc, v_mf)]
    v = jnp.pad(jnp.concatenate(v, axis=0), ((2, 6), (0, 0)))
    dx, _v, p = net.self_backward(x0, k_us, dx, w_first, 0, 0, (v,))
    p = pairs(p)
    dx = go_on(dx, [s_mf], [s_uf, s_mf])
    dx = go_on(dx, [s_ma], [s_ma])
    dx, (p,) = tie(dx, p)
    send, keep = net.attend_grads(f_us, p)
    dx, (send, keep) = tie(dx, send, keep)
    v = nt(order[: d // 2], plus(p[0][4], p[1][4])[:LANES]).astype(bf16)
    dx, (dkv,) = tie(dx, dkv)
    denc = net.pair_input(dkv, w_middle)
    dx, (denc,) = tie(dx, denc)
    dx = go_on(dx, [s_ma], [s_ma])
    send = jnp.concatenate((send, v[d // 4 :]), axis=1)
    keep = jnp.concatenate((keep, v[: d // 4]), axis=1)
    s_us = Sum(place, (send, keep))
    dx = go_on(dx, start=[s_us])
    dx = rest(dx, s_mf)
    dx = go_on(dx, [s_uf], [s_uf])
    dx = hold(dx, s_mf)
    dx, (r_mf,) = tie(dx, feed_rows(s_mf.kept, s_mf.got))
    dx = rest(dx, s_ma)
    dx = go_on(dx, [s_uf, s_us], [s_uf, s_us])
    dx, (r_ma,) = tie(dx, s_ma.total())
    dx = go_on(dx, [s_us], [s_us])
    dx = rest(dx, s_uf, s_us)
    dx = hold(dx, s_uf)
    dx, (r_uf,) = tie(dx, feed_rows(s_uf.kept, s_uf.got))
    r_us = s_us.total()

    def columns(r, *blocks):
        parts = [r[:, b * d : (b + 1) * d] for b in blocks]
        return jnp.concatenate(parts, axis=1) if len(parts) > 1 else parts[0]

    r_uup, r_udown = r_uf
    r_mup, r_mdown = r_mf
    vs = r_us[:, 4 * d :]
    v = [vs[:, i] for i in range(10)]
    return (
        x2.reshape(tokens.shape),
        dx.astype(bf16).reshape(tokens.shape),
        denc.reshape(encoder.shape),
        v[0], v[1], r_us[:, : 3 * d], r_us[:, 3 * d : 4 * d], v[2], v[3], r_uup, r_udown,
        v[4], v[5], r_ma[:, : 3 * d], columns(r_ma, 3), v[6], v[7],
        columns(r_ma, 4), r_ma[:, 6 * d :], columns(r_ma, 5),
        v[8], v[9], r_mup, r_mdown,
    )


def solution(mesh):
    rows1 = P(AXES)
    rows2 = P(AXES, None)
    rows3 = P(AXES, None, None)
    block = (rows1, rows1, rows2, rows2)
    weights = block * 2 + block + (rows1, rows1, rows2, rows2, rows2) + block
    return jax.shard_map(
        local,
        mesh=mesh,
        in_specs=(rows3, rows3, rows1, rows3) + weights,
        out_specs=(rows3, rows3, rows3) + weights,
        check_vma=False,
    )
```

```python
import functools

import jax
import jax.numpy as jnp
from jax import lax
from jax.experimental import pallas as pl
from jax.experimental.pallas import tpu as pltpu
from jax.sharding import PartitionSpec as P

DH = 64
AXES = ("dp", "hd")
EPS = 1e-05
MASKED = -1e30
LANES = 128
bf16 = jnp.bfloat16
f32 = jnp.float32
sds = jax.ShapeDtypeStruct


BIT_PAIR, BIT_CORE, BIT_NEAR = 1, 2, 4


class Place:
    def __init__(self):
        self.count = lax.axis_size("dp") * lax.axis_size("hd")
        self.outer_size = self.count // 8
        index = lax.axis_index("dp") * lax.axis_size("hd") + lax.axis_index("hd")
        self.pair = index % 2
        self.core = (index // 2) % 2
        self.near = (index // 4) % 2
        self.outer = index // 8
        self.outer_bits = self.outer_size.bit_length() - 1

    def swap(self, x, bit):
        return lax.ppermute(x, AXES, [(i, i ^ bit) for i in range(self.count)])

    def swap_by_core(self, x, bits):
        pairs = [(i, i ^ bits[(i // BIT_CORE) % 2]) for i in range(self.count)]
        return lax.ppermute(x, AXES, pairs)

    def order(self, d):
        n, rows = self.outer_size, d // self.count
        k = lax.broadcasted_iota(jnp.int32, (d, 1), 0)
        row, place = k % rows, (k // rows) % n
        outer = jnp.zeros_like(k)
        for b in range(self.outer_bits):
            outer = outer + ((place >> (self.outer_bits - 1 - b)) & 1) * (1 << b)
        outer = outer ^ self.outer
        rest = k // (rows * n)
        low, high = rest % 2, (rest // 2) % 2
        near = jnp.where((rest // 4) ^ self.core == 0, high, low)
        pair = high + low - near
        feature = outer * 2 + (near ^ self.near)
        feature = (feature * 2 + ((rest // 4) ^ self.core)) * 2 + (pair ^ self.pair)
        feature = feature * rows + row
        return (feature == lax.broadcasted_iota(jnp.int32, (d, d), 1)).astype(bf16)


def plus(a, b):
    return (a.astype(f32) + b.astype(f32)).astype(bf16)


class Sum:
    def __init__(self, place, grads):
        self.place, self.stage = place, 0
        self.send, self.kept = grads

    def swap(self):
        if self.stage < 2:
            bits = ((BIT_NEAR, BIT_PAIR), (BIT_PAIR, BIT_NEAR))[self.stage]
            self.got = self.place.swap_by_core(self.send, bits)
        else:
            self.got = self.place.swap(self.send, 8 << (self.stage - 2))

    def sums(self):
        if self.stage < 2:
            self.send, self.kept = half_sums(self.kept, self.got)
        else:
            half = self.kept.shape[0] // 2
            self.send = plus(self.kept[half:], self.got[half:])
            self.kept = plus(self.kept[:half], self.got[:half])
        self.stage += 1

    def total(self):
        return self.kept.astype(f32) + self.got.astype(f32)


class Gather:
    def __init__(self, place, shard):
        self.place, self.x, self.stage = place, shard, 0

    def swap(self):
        outer = self.place.outer_bits
        at = self.stage - outer
        if at < 0:
            self.got = self.place.swap(self.x, 8 << (outer - 1 - self.stage))
        elif at < 2:
            bits = ((BIT_PAIR, BIT_NEAR), (BIT_NEAR, BIT_PAIR))[at]
            self.got = self.place.swap_by_core(self.x, bits)
        else:
            self.got = self.place.swap(self.x, BIT_CORE)

    def join(self):
        self.x = jnp.concatenate((self.x, self.got), axis=0)
        self.stage += 1


def tie(x, *others):
    out = lax.optimization_barrier((x,) + others)
    return out[0], out[1:]


def hold(x, *groups):
    x, terms = tie(x, *[(g.kept, g.got) for g in groups])
    for g, t in zip(groups, terms):
        g.kept, g.got = t
    return x


def need(x, *groups):
    x, send = tie(x, *[g.send for g in groups])
    for g, k in zip(groups, send):
        g.send = k
    return x


def nn(a, b):
    return jnp.dot(a, b, preferred_element_type=f32)


def nt(a, b):
    return lax.dot_general(a, b, (((1,), (1,)), ((), ())), preferred_element_type=f32)


def tn(a, b):
    return lax.dot_general(a, b, (((0,), (0,)), ((), ())), preferred_element_type=f32)


def unit_norm(x):
    centred = x - jnp.mean(x, axis=-1, keepdims=True)
    inv = lax.rsqrt(jnp.mean(centred * centred, axis=-1, keepdims=True) + EPS)
    return centred * inv, inv


def norm_backward(grad, x, gain):
    unit, inv = unit_norm(x)
    du = grad * gain
    dx = inv * (
        du
        - jnp.mean(du, axis=-1, keepdims=True)
        - unit * jnp.mean(du * unit, axis=-1, keepdims=True)
    )
    return dx, jnp.sum(grad * unit, axis=0, keepdims=True), jnp.sum(grad, axis=0, keepdims=True)


GELU_A = 0.7978845608028654
GELU_B = 0.044715


def two_heads(x):
    first = lax.broadcasted_iota(jnp.int32, x.shape, 1) < DH
    zero = jnp.zeros_like(x)
    return jnp.concatenate((jnp.where(first, x, zero), jnp.where(first, zero, x)), axis=0)


def side_by_side(x):
    n = x.shape[0] // 2
    first = lax.broadcasted_iota(jnp.int32, (n, LANES), 1) < DH
    return jnp.where(first, x[:n], x[n:])


def probabilities(qs, k2, allowed):
    s = jnp.where(allowed, nt(qs, k2) * DH ** (-0.5), MASKED)
    e = jnp.exp(s - jnp.max(s, axis=-1, keepdims=True))
    return e / jnp.sum(e, axis=-1, keepdims=True)


def causal_mask(length):
    row = lax.broadcasted_iota(jnp.int32, (2 * length, length), 0)
    col = lax.broadcasted_iota(jnp.int32, (2 * length, length), 1)
    return jnp.where(row >= length, row - length, row) >= col


def attend_back(q2, k2, v2, do2, allowed):
    scale = DH ** (-0.5)
    qs, dos = two_heads(q2), two_heads(do2)
    p = probabilities(qs, k2, allowed)
    dp = nt(dos, v2)
    ds = (p * (dp - jnp.sum(p * dp, axis=-1, keepdims=True))).astype(bf16)
    dq = side_by_side(nn(ds, k2)) * scale
    dk = tn(ds, qs) * scale
    dv = tn(p.astype(bf16), dos)
    return dq.astype(bf16), dk.astype(bf16), dv.astype(bf16)


def relative(x, order_ref):
    return nt(x, order_ref[...]).astype(bf16)


def times(x, top_ref, low_ref):
    half = top_ref.shape[0]
    return nn(x[:, :half], top_ref[...]) + nn(x[:, half:], low_ref[...])


def times_back(g, top_ref, low_ref):
    return jnp.concatenate((nt(g, top_ref[...]), nt(g, low_ref[...])), axis=1)


def natural(x, order_ref):
    high = x.astype(bf16)
    low = (x - high.astype(f32)).astype(bf16)
    return nn(high, order_ref[...]) + nn(low, order_ref[...])


def self_forward_kernel(
    captions, row, x_ref, vec_ref, order_ref, top_ref, low_ref, y_ref, f_ref, qkv_ref, rel_ref
):
    j = pl.program_id(0)

    @pl.when(j == 0)
    def _():
        unit, _inv = unit_norm(x_ref[...].astype(f32))
        f_ref[0] = (unit * vec_ref[row : row + 1] + vec_ref[row + 1 : row + 2]).astype(bf16)
        rel_ref[...] = relative(f_ref[0], order_ref)

    @pl.when(j < 3)
    def _():
        qkv_ref[j] = times(rel_ref[...], top_ref, low_ref).astype(bf16)

    @pl.when(j == 3)
    def _():
        length = x_ref.shape[0] // captions
        allowed = causal_mask(length)
        for c in range(captions):
            at = slice(c * length, (c + 1) * length)
            for h in range(0, x_ref.shape[1], LANES):
                cols = slice(h, h + LANES)
                p = probabilities(two_heads(qkv_ref[0, at, cols]), qkv_ref[1, at, cols], allowed)
                o = side_by_side(nn(p.astype(bf16), qkv_ref[2, at, cols]))
                f_ref[1, at, cols] = o.astype(bf16)
        y_ref[...] = x_ref[...].astype(f32) + times(relative(f_ref[1], order_ref), top_ref, low_ref)


def self_backward_kernel(
    captions, row, x_ref, vec_ref, order_ref, qkv_ref, dx_ref, top_ref, low_ref, *refs
):
    out_ref, vg_ref, p_ref, acc_ref = refs[-4:]
    j = pl.program_id(0)

    @pl.when(j == 0)
    def _():
        dy = dx_ref[...].astype(bf16)
        p_ref[3] = dy
        do = times_back(dy, top_ref, low_ref).astype(bf16)
        do = nn(do, order_ref[...]).astype(bf16)
        length = x_ref.shape[0] // captions
        allowed = causal_mask(length)
        for c in range(captions):
            at = slice(c * length, (c + 1) * length)
            for h in range(0, x_ref.shape[1], LANES):
                cols = slice(h, h + LANES)
                dq, dk, dv = attend_back(
                    qkv_ref[0, at, cols], qkv_ref[1, at, cols], qkv_ref[2, at, cols],
                    do[at, cols], allowed,
                )
                p_ref[0, at, cols] = dq
                p_ref[1, at, cols] = dk
                p_ref[2, at, cols] = dv
        acc_ref[...] = jnp.zeros_like(acc_ref)

    @pl.when(j > 0)
    def _():
        acc_ref[...] += times_back(p_ref[j - 1], top_ref, low_ref)

    @pl.when(j == 3)
    def _():
        da = natural(acc_ref[...], order_ref)
        dn, gg, gs = norm_backward(da, x_ref[...].astype(f32), vec_ref[row : row + 1])
        out_ref[...] = dx_ref[...] + dn
        vg_ref[0:1] = gg
        vg_ref[1:2] = gs
        if len(refs) > 4:
            at = lax.broadcasted_iota(jnp.int32, refs[0].shape, 0)
            rows = jnp.where(at == 0, gg, jnp.where(at == 1, gs, refs[0][...]))
            p_ref[4] = jnp.zeros_like(p_ref[4])
            p_ref[4, 0 : refs[0].shape[0]] = rows.astype(bf16)


def cross_forward_kernel(
    captions, row, count_ref, x_ref, vec_ref, order_ref, kv_ref, top_ref, low_ref, y_ref, f_ref, q_ref
):
    j = pl.program_id(0)
    d = x_ref.shape[1]

    @pl.when(j == 0)
    def _():
        unit, _inv = unit_norm(x_ref[...])
        c = (unit * vec_ref[row : row + 1] + vec_ref[row + 1 : row + 2]).astype(bf16)
        f_ref[0] = c
        q_ref[...] = times(relative(c, order_ref), top_ref, low_ref).astype(bf16)

    @pl.when(j == 1)
    def _():
        length = x_ref.shape[0] // captions
        patches = kv_ref.shape[0] // captions
        slot = lax.broadcasted_iota(jnp.int32, (2 * length, patches), 1)
        for c in range(captions):
            at = slice(c * length, (c + 1) * length)
            keys = slice(c * patches, (c + 1) * patches)
            allowed = slot < count_ref[c]
            for h in range(0, d, LANES):
                cols = slice(h, h + LANES)
                vcols = slice(d + h, d + h + LANES)
                p = probabilities(two_heads(q_ref[at, cols]), kv_ref[keys, cols], allowed)
                o = side_by_side(nn(p.astype(bf16), kv_ref[keys, vcols]))
                f_ref[1, at, cols] = o.astype(bf16)
        y_ref[...] = x_ref[...] + times(relative(f_ref[1], order_ref), top_ref, low_ref)


def cross_backward_kernel(
    captions, row, count_ref, x_ref, vec_ref, order_ref, q_ref, kv_ref, dx_ref, top_ref, low_ref,
    out_ref, vg_ref, p_ref, dkv_ref,
):
    j = pl.program_id(0)
    d = x_ref.shape[1]

    @pl.when(j == 0)
    def _():
        dy = dx_ref[...].astype(bf16)
        p_ref[1] = dy
        do = times_back(dy, top_ref, low_ref).astype(bf16)
        do = nn(do, order_ref[...]).astype(bf16)
        length = x_ref.shape[0] // captions
        patches = kv_ref.shape[0] // captions
        slot = lax.broadcasted_iota(jnp.int32, (2 * length, patches), 1)
        for c in range(captions):
            at = slice(c * length, (c + 1) * length)
            keys = slice(c * patches, (c + 1) * patches)
            allowed = slot < count_ref[c]
            for h in range(0, d, LANES):
                cols = slice(h, h + LANES)
                vcols = slice(d + h, d + h + LANES)
                dq, dk, dv = attend_back(
                    q_ref[at, cols], kv_ref[keys, cols], kv_ref[keys, vcols], do[at, cols], allowed
                )
                p_ref[0, at, cols] = dq
                dkv_ref[keys, cols] = dk
                dkv_ref[keys, vcols] = dv

    @pl.when(j == 1)
    def _():
        dc = natural(times_back(p_ref[0], top_ref, low_ref), order_ref)
        dn, gg, gs = norm_backward(dc, x_ref[...], vec_ref[row : row + 1])
        out_ref[...] = dx_ref[...] + dn
        vg_ref[0:1] = gg
        vg_ref[1:2] = gs


def feed_forward_kernel(
    row, x_ref, vec_ref, order_ref, up_ref, up2_ref, down_ref, down2_ref, y_ref, f_ref, u_ref, rel_ref
):
    j = pl.program_id(0)

    @pl.when(j == 0)
    def _():
        unit, _inv = unit_norm(x_ref[...])
        f_ref[0] = (unit * vec_ref[row : row + 1] + vec_ref[row + 1 : row + 2]).astype(bf16)
        rel_ref[...] = relative(f_ref[0], order_ref)
        y_ref[...] = x_ref[...]

    u = times(rel_ref[...], up_ref, up2_ref)
    u_ref[...] = u
    g = (0.5 * u * (1.0 + jnp.tanh(GELU_A * (u + GELU_B * u * u * u)))).astype(bf16)
    f_ref[1 + j] = g
    y_ref[...] += times(relative(g, order_ref), down_ref, down2_ref)


def gelu_terms(u):
    t = jnp.tanh(GELU_A * (u + GELU_B * u * u * u))
    slope = 0.5 * (1.0 + t) + 0.5 * u * (1.0 - t * t) * GELU_A * (1.0 + 3.0 * GELU_B * u * u)
    return 0.5 * u * (1.0 + t), slope


def feed_backward_step(j, order_ref, slope, refs, p_ref, acc_ref):
    up_ref, up2_ref, down_ref, down2_ref = refs
    dg = times_back(p_ref[0], down_ref, down2_ref).astype(bf16)
    du = (slope * nn(dg, order_ref[...])).astype(bf16)
    p_ref[1 + j] = du
    acc_ref[...] += times_back(du, up_ref, up2_ref)


def feed_backward_end(row, order_ref, x_ref, vec_ref, dx_ref, acc_ref, out_ref, vg_ref):
    db = natural(acc_ref[...], order_ref)
    dn, gg, gs = norm_backward(db, x_ref[...], vec_ref[row : row + 1])
    out_ref[...] = dx_ref[...].astype(f32) + dn
    vg_ref[0:1] = gg
    vg_ref[1:2] = gs


def feed_backward_kernel(
    row, x_ref, vec_ref, order_ref, dx_ref, up_ref, up2_ref, down_ref, down2_ref, u_ref,
    out_ref, vg_ref, p_ref, acc_ref,
):
    j = pl.program_id(0)

    @pl.when(j == 0)
    def _():
        p_ref[0] = dx_ref[...].astype(bf16)
        acc_ref[...] = jnp.zeros_like(acc_ref)

    refs = up_ref, up2_ref, down_ref, down2_ref
    feed_backward_step(j, order_ref, gelu_terms(u_ref[...])[1], refs, p_ref, acc_ref)

    @pl.when(j == 3)
    def _():
        feed_backward_end(row, order_ref, x_ref, vec_ref, dx_ref, acc_ref, out_ref, vg_ref)


def last_backward_kernel(
    row, x_ref, vec_ref, order_ref, dx_ref, up_ref, up2_ref, down_ref, down2_ref,
    out_ref, vg_ref, p_ref, f_ref, acc_ref, rel_ref,
):
    j = pl.program_id(0)

    @pl.when(j == 0)
    def _():
        unit, _inv = unit_norm(x_ref[...])
        f_ref[0] = (unit * vec_ref[row : row + 1] + vec_ref[row + 1 : row + 2]).astype(bf16)
        rel_ref[...] = relative(f_ref[0], order_ref)
        p_ref[0] = dx_ref[...]
        acc_ref[...] = jnp.zeros_like(acc_ref)

    g, slope = gelu_terms(times(rel_ref[...], up_ref, up2_ref))
    f_ref[1 + j] = g.astype(bf16)
    refs = up_ref, up2_ref, down_ref, down2_ref
    feed_backward_step(j, order_ref, slope, refs, p_ref, acc_ref)

    @pl.when(j == 3)
    def _():
        feed_backward_end(row, order_ref, x_ref, vec_ref, dx_ref, acc_ref, out_ref, vg_ref)


def last_output_kernel(x_ref, order_ref, g_ref, down_ref, down2_ref, y_ref, acc_ref):
    j = pl.program_id(0)

    @pl.when(j == 0)
    def _():
        acc_ref[...] = x_ref[...]

    acc_ref[...] += times(relative(g_ref[0], order_ref), down_ref, down2_ref)

    @pl.when(j == 3)
    def _():
        y_ref[...] = acc_ref[...].astype(bf16)


def both(own_ref, got_ref):
    return jnp.concatenate((own_ref[0], got_ref[0]), axis=0)


def emit(g, send_ref, keep_ref):
    half = keep_ref.shape[0]
    keep_ref[...] = g[:half].astype(bf16)
    send_ref[...] = g[half:].astype(bf16)


def feed_grads_kernel(
    order_ref, b_ref, b2_ref, z_ref, z2_ref, g_ref, g2_ref, u_ref, u2_ref, send_ref, keep_ref, bt_ref
):
    d = order_ref.shape[1]

    @pl.when(pl.program_id(0) == 0)
    def _():
        bt_ref[...] = nt(order_ref[...], both(b_ref, b2_ref)).astype(bf16)

    up, down = (slice(None), slice(0, d)), (slice(None), slice(d, 2 * d))
    emit(nn(bt_ref[...], both(u_ref, u2_ref)), send_ref.at[up], keep_ref.at[up])
    gt = nt(order_ref[...], both(g_ref, g2_ref)).astype(bf16)
    emit(nn(gt, both(z_ref, z2_ref)), send_ref.at[down], keep_ref.at[down])


def attend_grads_kernel(order_ref, s_ref, s2_ref, sd_ref, sd2_ref, *refs):
    send_ref, keep_ref = refs[-2:]
    j = pl.program_id(0)

    def product(a_ref, a2_ref, d_ref, d2_ref):
        at = nt(order_ref[...], both(a_ref, a2_ref)).astype(bf16)
        emit(nn(at, both(d_ref, d2_ref)), send_ref, keep_ref)

    @pl.when(j < 4)
    def _():
        product(s_ref, s2_ref, sd_ref, sd2_ref)

    if len(refs) > 2:
        c_ref, c2_ref, cd_ref, cd2_ref, pair_ref, pair2_ref = refs[:6]

        @pl.when((j == 4) | (j == 5))
        def _():
            product(c_ref, c2_ref, cd_ref, cd2_ref)

        @pl.when(j > 5)
        def _():
            emit(pair_ref[...].astype(f32) + pair2_ref[...].astype(f32), send_ref, keep_ref)


def half_sums_kernel(kept_ref, got_ref, send_ref, keep_ref):
    emit(kept_ref[...].astype(f32) + got_ref[...].astype(f32), send_ref, keep_ref)


def half_sums(kept, got):
    rows, wide = kept.shape
    steps = 2 if wide % (2 * LANES) == 0 else 1
    full = pl.BlockSpec((rows, wide // steps), lambda j: (0, j))
    half = pl.BlockSpec((rows // 2, wide // steps), lambda j: (0, j))
    outs = (sds((rows // 2, wide), bf16),) * 2
    return call(half_sums_kernel, steps, (kept, got), [full] * 2, outs, [half] * 2, vmem=24)


def feed_rows_kernel(kept_ref, got_ref, up_ref, down_ref):
    rows, wide = up_ref.shape
    d = wide // 4
    spread = spread_matrix().astype(bf16)
    i = lax.broadcasted_iota(jnp.int32, (4 * rows, rows), 0)
    k = lax.broadcasted_iota(jnp.int32, (4 * rows, rows), 1)

    def part(at, size):
        x = kept_ref[:, at : at + size].astype(f32) + got_ref[:, at : at + size].astype(f32)
        high = x.astype(bf16)
        return high, (x - high.astype(f32)).astype(bf16)

    for b in range(wide // 512):
        parts = [part(2 * j * d + b * LANES, LANES) for j in range(4)]
        high, low = (jnp.concatenate(p, axis=1) for p in zip(*parts))
        up_ref[:, b * 512 : (b + 1) * 512] = nt(high, spread) + nt(low, spread)
    down = jnp.zeros(down_ref.shape, f32)
    for j in range(4):
        place = (i == 4 * k + j).astype(bf16)
        high, low = part((2 * j + 1) * d, d)
        down = down + nn(place, high) + nn(place, low)
    down_ref[...] = down


def feed_rows(kept, got):
    rows, wide = kept.shape
    outs = sds((rows, wide // 2), f32), sds((4 * rows, wide // 8), f32)
    ins = kept, got
    return call(feed_rows_kernel, 1, ins, [whole(x) for x in ins], outs, [whole(x) for x in outs])


def pair_forward_kernel(enc_ref, top_ref, low_ref, kv_ref):
    kv_ref[...] = times(enc_ref[...], top_ref, low_ref).astype(bf16)


def pair_input_kernel(dkv_ref, order_ref, top_ref, low_ref, out_ref):
    g = times_back(dkv_ref[...], top_ref, low_ref).astype(bf16)
    out_ref[...] = nn(g, order_ref[...]).astype(bf16)


def pair_grads_kernel(enc_ref, dkv_ref, keep_ref, send_ref):
    emit(nn(enc_ref[...], dkv_ref[...]), send_ref, keep_ref)


def first_pack_kernel(u_qkv, u_out, vec, out):
    rows, d = u_out.shape
    out[:, : 3 * d] = u_qkv[...]
    out[:, 3 * d : 4 * d] = u_out[...]
    eye = lax.broadcasted_iota(jnp.int32, (rows, rows), 0) == lax.broadcasted_iota(jnp.int32, (rows, rows), 1)
    out[:, 4 * d :] = nt(eye.astype(bf16), vec[...]).astype(bf16)


def pack_kernel(
    u_up, u_down, m_qkv, m_out, m_up, m_down, c_q, c_pair, c_out, feed_out, middle_out, last_out
):
    rows, d = m_out.shape
    spread = spread_matrix().astype(bf16)
    i = lax.broadcasted_iota(jnp.int32, (rows, 4 * rows), 0)
    k = lax.broadcasted_iota(jnp.int32, (rows, 4 * rows), 1)

    def feed(out, up, down):
        for b in range(4 * d // 512):
            y = nn(up[:, b * 512 : (b + 1) * 512], spread).astype(bf16)
            for j in range(4):
                to = j * d + b * LANES
                out[:, to : to + LANES] = y[:, j * LANES : (j + 1) * LANES]
        for j in range(4):
            y = nn((k == 4 * i + j).astype(bf16), down[...])
            out[:, (4 + j) * d : (5 + j) * d] = y.astype(bf16)

    feed(feed_out, u_up, u_down)
    middle_out[:, : 2 * d] = c_pair[...]
    middle_out[:, 2 * d : 3 * d] = c_q[...]
    middle_out[:, 3 * d : 4 * d] = c_out[...]
    middle_out[:, 4 * d : 7 * d] = m_qkv[...]
    middle_out[:, 7 * d : 8 * d] = m_out[...]
    feed(last_out, m_up, m_down)


def whole(x):
    return pl.BlockSpec(x.shape, lambda *_: (0,) * len(x.shape))


def call(kernel, steps, ins, in_specs, outs, out_specs, scratch=(), scalars=0, vmem=24):
    return pl.pallas_call(
        kernel,
        out_shape=outs,
        grid_spec=pltpu.PrefetchScalarGridSpec(
            num_scalar_prefetch=scalars,
            grid=(steps,),
            in_specs=in_specs,
            out_specs=out_specs,
            scratch_shapes=scratch,
        ),
        compiler_params=pltpu.CompilerParams(
            dimension_semantics=("arbitrary",), vmem_limit_bytes=vmem << 20
        ),
        cost_estimate=pl.CostEstimate(flops=1000, bytes_accessed=1000, transcendentals=0),
    )(*ins)


class Layers:
    def __init__(self, captions, tokens, d, vec, order, count):
        self.captions, self.t, self.d = captions, tokens, d
        self.vec, self.order, self.count = vec, order, count
        self.xs = sds((tokens, d), f32)
        self.hs = sds((tokens, d), bf16)

    def weights(self, *columns):
        d = self.d
        specs = [pl.BlockSpec((d // 2, d), lambda j, *_, c=c: (0, c(j))) for c in columns]
        return [s for s in specs for _ in range(2)]

    def self_forward(self, x, w, at, row):
        outs = (self.xs, sds((2, self.t, self.d), bf16), sds((3, self.t, self.d), bf16))
        ins = (x, self.vec, self.order)
        return call(
            functools.partial(self_forward_kernel, self.captions, row), 4,
            ins + w, [whole(i) for i in ins] + self.weights(lambda j: at + j),
            outs, [whole(o) for o in outs], scratch=[pltpu.VMEM((self.t, self.d), bf16)],
        )

    def self_backward(self, x, kept, dx, w, at, row, vectors=()):
        d, t = self.d, self.t
        outs = (self.xs, sds((8, d), f32), sds((4 + len(vectors), t, d), bf16))
        ins = (x, self.vec, self.order, kept, dx)
        return call(
            functools.partial(self_backward_kernel, self.captions, row), 4,
            ins + w + vectors,
            [whole(i) for i in ins] + self.weights(lambda j: at + (j + 3) % 4)
            + [whole(v) for v in vectors],
            outs, [whole(i) for i in outs],
            scratch=[pltpu.VMEM((t, d), f32)],
        )

    def cross_forward(self, x, kv, w, at, row):
        outs = (self.xs, sds((2, self.t, self.d), bf16), self.hs)
        ins = (x, self.vec, self.order, kv)
        return call(
            functools.partial(cross_forward_kernel, self.captions, row), 2,
            (self.count,) + ins + w,
            [whole(i) for i in ins] + self.weights(lambda j: at + j),
            outs, [whole(o) for o in outs], scalars=1,
        )

    def cross_backward(self, x, kept, kv, dx, w, at, row):
        d, t = self.d, self.t
        outs = (self.xs, sds((8, d), f32), sds((2, t, d), bf16), sds(kv.shape, bf16))
        ins = (x, self.vec, self.order, kept, kv, dx)
        return call(
            functools.partial(cross_backward_kernel, self.captions, row), 2,
            (self.count,) + ins + w,
            [whole(i) for i in ins] + self.weights(lambda j: at + 1 - j),
            outs, [whole(i) for i in outs], scalars=1,
        )

    def pair_forward(self, enc, w):
        d, rows = self.d, enc.shape[0] // self.captions
        half = pl.BlockSpec((d // 2, 2 * d), lambda j: (0, 0))
        out = sds((enc.shape[0], 2 * d), bf16)
        return call(
            pair_forward_kernel, self.captions, (enc,) + w,
            [pl.BlockSpec((rows, d), lambda j: (j, 0)), half, half],
            out, pl.BlockSpec((rows, 2 * d), lambda j: (j, 0)),
        )

    def pair_grads(self, enc_t, dkv):
        d = self.d
        outs = (sds((d // 2, 2 * d), bf16),) * 2
        grad = pl.BlockSpec((d // 2, d), lambda j: (0, j))
        return call(
            pair_grads_kernel, 2, (enc_t, dkv),
            [whole(enc_t), pl.BlockSpec((dkv.shape[0], d), lambda j: (0, j))],
            outs, [grad, grad],
        )

    def pair_input(self, dkv, w):
        d, rows = self.d, dkv.shape[0] // self.captions
        half = pl.BlockSpec((d // 2, 2 * d), lambda j: (0, 0))
        out = sds((dkv.shape[0], d), bf16)
        return call(
            pair_input_kernel, self.captions, (dkv, self.order) + w,
            [pl.BlockSpec((rows, 2 * d), lambda j: (j, 0)), whole(self.order), half, half],
            out, pl.BlockSpec((rows, d), lambda j: (j, 0)),
        )

    def block(self, index):
        return pl.BlockSpec((1, self.t, self.d), lambda j: (index(j), 0, 0))

    def feed_grads(self, f, p):
        d, t = self.d, self.t
        outs = (sds((d // 4, 8 * d), bf16),) * 2
        first, later = self.block(lambda j: 0), self.block(lambda j: 1 + j)
        half = pl.BlockSpec((d // 2, d), lambda j: (0, 0))
        return call(
            feed_grads_kernel, 4, (self.order,) + f + p + f + p,
            [half] + [first] * 4 + [later] * 4,
            outs, [pl.BlockSpec((d // 4, 2 * d), lambda j: (0, j))] * 2,
            scratch=[pltpu.VMEM((d // 2, 2 * t), bf16)],
        )

    def attend_grads(self, f, p, cross=()):
        d, t = self.d, self.t
        steps = 8 if cross else 4
        outs = (sds((d // 4, steps * d), bf16),) * 2
        half = pl.BlockSpec((d // 2, d), lambda j: (0, 0))
        lhs = self.block(lambda j: jnp.minimum(j // 3, 1))
        rhs = self.block(lambda j: jnp.minimum(j, 3))
        ins, specs = (self.order,) + f + p, [half, lhs, lhs, rhs, rhs]
        if cross:
            f, p, pair = cross
            at = self.block(lambda j: jnp.clip(j - 4, 0, 1))
            columns = pl.BlockSpec((d // 2, d), lambda j: (0, jnp.clip(j - 6, 0, 1)))
            ins, specs = ins + f + p + pair, specs + [at] * 4 + [columns] * 2
        return call(
            attend_grads_kernel, steps, ins, specs,
            outs, [pl.BlockSpec((d // 4, d), lambda j: (0, j))] * 2,
        )

    def feed_forward(self, x, w, row):
        d, t = self.d, self.t
        outs = (self.xs, sds((5, t, d), bf16), sds((t, 4 * d), f32))
        ins = (x, self.vec, self.order)
        return call(
            functools.partial(feed_forward_kernel, row), 4,
            ins + w + w,
            [whole(i) for i in ins] + self.weights(lambda j: j, lambda j: 4 + j),
            outs, [whole(outs[0]), whole(outs[1]), pl.BlockSpec((t, d), lambda j: (0, j))],
            scratch=[pltpu.VMEM((t, d), bf16)],
        )

    def feed_backward(self, x, u, dx, w, row):
        d, t = self.d, self.t
        outs = (self.xs, sds((8, d), f32), sds((5, t, d), bf16))
        ins = (x, self.vec, self.order, dx)
        return call(
            functools.partial(feed_backward_kernel, row), 4,
            ins + w + w + (u,),
            [whole(i) for i in ins] + self.weights(lambda j: j, lambda j: 4 + j)
            + [pl.BlockSpec((t, d), lambda j: (0, j))],
            outs, [whole(i) for i in outs],
            scratch=[pltpu.VMEM((t, d), f32)],
        )

    def last_backward(self, x, dx, w, row):
        d, t = self.d, self.t
        outs = (self.xs, sds((8, d), f32)) + (sds((5, t, d), bf16),) * 2
        ins = (x, self.vec, self.order, dx)
        return call(
            functools.partial(last_backward_kernel, row), 4,
            ins + w + w,
            [whole(i) for i in ins] + self.weights(lambda j: j, lambda j: 4 + j),
            outs, [whole(i) for i in outs],
            scratch=[pltpu.VMEM((t, d), f32), pltpu.VMEM((t, d), bf16)],
        )

    def last_output(self, x, f, w):
        return call(
            last_output_kernel, 4, (x, self.order, f) + w,
            [whole(x), whole(self.order), self.block(lambda j: 1 + j)]
            + self.weights(lambda j: 4 + j),
            self.hs, whole(self.hs), scratch=[pltpu.VMEM((self.t, self.d), f32)],
        )


def spread_matrix():
    k = lax.broadcasted_iota(jnp.int32, (512, 512), 0)
    n = lax.broadcasted_iota(jnp.int32, (512, 512), 1)
    return (k % 4) * 128 + k // 4 == n


def local(
    tokens, encoder, patch_count, out_grad,
    u_ag, u_as, u_qkv, u_out, u_mg, u_ms, u_up, u_down,
    m_ag, m_as, m_qkv, m_out, c_g, c_s, c_q, c_pair, c_out, m_mg, m_ms, m_up, m_down,
):
    place = Place()
    captions, length, d = tokens.shape
    rows = u_qkv.shape[0]
    x0 = tokens.reshape(-1, d)
    enc = encoder.reshape(-1, d)
    order = place.order(d)

    vectors = (u_ag, u_as, u_mg, u_ms, m_ag, m_as, c_g, c_s, m_mg, m_ms)
    vectors = jnp.pad(jnp.stack(vectors, axis=0), ((0, LANES - len(vectors)), (0, 0)))
    def core(x):
        return place.swap(x, BIT_CORE)

    def pairs(x):
        return x, core(x)

    def packed(kernel, parts, *widths):
        outs = tuple(sds((rows, c), bf16) for c in widths)
        shards = call(kernel, 1, parts, [whole(p) for p in parts], outs, [whole(o) for o in outs], vmem=60)
        return [Gather(place, x) for x in shards]

    (first,) = packed(first_pack_kernel, (u_qkv, u_out, vectors), 4 * d + LANES)
    parts = (u_up, u_down, m_qkv, m_out, m_up, m_down, c_q, c_pair, c_out)
    feed, middle, last = packed(pack_kernel, parts, 8 * d, 8 * d, 8 * d)

    def go(token, groups=(), start=()):
        token, got = tie(token, *[(g.x, g.got) for g in groups])
        for g, (x, y) in zip(groups, got):
            g.x, g.got = x, y
            g.join()
        every = tuple(groups) + tuple(start)
        token, xs = tie(token, *[g.x for g in every])
        for g, x in zip(every, xs):
            g.x = x
            g.swap()
        return token

    def end(token, group):
        token, (group.x, group.got) = tie(token, group.x, group.got)
        return token, (group.x, group.got)

    steps = place.outer_bits
    x0 = go(x0, start=[first])
    enc_rel = nt(enc, order).astype(bf16)
    enc_t = nt(order, enc).astype(bf16)
    for k in range(steps - 1):
        x0 = go(x0, [first], [feed] if k == 0 else [])
    x0 = go(x0, [first])
    for k in range(steps - 1):
        x0 = go(x0, [feed])
    x0 = go(x0, [first])
    x0 = go(x0, [feed], [middle])
    x0 = go(x0, [first, middle])
    x0 = go(x0, [feed])
    for k in range(steps - 2):
        x0 = go(x0, [middle])
    x0, (order, enc_rel, enc_t) = tie(x0, order, enc_rel, enc_t)
    x0, w_first = end(x0, first)
    vec = tn(jnp.concatenate([x[:, 4 * d :] for x in w_first], axis=0), order)[:16]
    net = Layers(captions, captions * length, d, vec, order, patch_count)
    x0 = go(x0, [middle], [last])
    for k in range(steps - 1):
        x0 = go(x0, [last])
    x0 = go(x0, [feed])
    x0a, f_us, k_us = net.self_forward(x0, w_first, 0, 0)
    x0a = go(x0a, [middle])
    x0a = go(x0a, [last])
    x0a, w_feed = end(x0a, feed)
    x1, f_uf, k_uf = net.feed_forward(x0a, w_feed, 2)
    x1 = go(x1, [last])
    x1 = go(x1, [middle])
    x1, w_middle = end(x1, middle)
    x1a, f_ms, k_ms = net.self_forward(x1, w_middle, 4, 4)
    kv = net.pair_forward(enc_rel, w_middle)
    f_us, f_uf, f_ms = pairs(f_us), pairs(f_uf), pairs(f_ms)
    x1a, (f_us, f_uf, f_ms, kv) = tie(x1a, f_us, f_uf, f_ms, kv)
    x1a = go(x1a, [last])
    x1b, f_mc, k_mc = net.cross_forward(x1a, kv, w_middle, 2, 6)
    x1b, w_last = end(x1b, last)

    def go_on(x, sums=(), start=()):
        x = hold(x, *sums)
        for g in sums:
            g.sums()
        x = need(x, *(tuple(sums) + tuple(g for g in start if g not in sums)))
        for g in start:
            g.swap()
        return x

    def rest(x, *groups):
        for _ in range(place.outer_bits - 1):
            for g in groups:
                x = go_on(x, [g], [g])
        return x

    f_mc = pairs(f_mc)
    dx, v_mf, p, f = net.last_backward(x1b, out_grad.reshape(-1, d), w_last, 8)
    p, f = pairs(p), pairs(f)
    x2 = net.last_output(x1b, f[0], w_last)
    p, (x2,) = tie(p, x2)
    s_mf = Sum(place, net.feed_grads(f, p))
    dx, (f_mc,) = tie(dx, f_mc)
    dx = go_on(dx, start=[s_mf])
    dx, v_mc, p_c, dkv = net.cross_backward(x1a, k_mc, kv, dx, w_middle, 2, 6)
    p_c = pairs(p_c)
    pair, send = net.pair_grads(enc_t, dkv)
    dx, (send,) = tie(dx, send)
    pair = pair, core(send)
    dx, v_ms, p = net.self_backward(x1, k_ms, dx, w_middle, 4, 4)
    p = pairs(p)
    dx = go_on(dx, [s_mf], [s_mf])
    dx, (p, p_c, pair) = tie(dx, p, p_c, pair)
    s_ma = Sum(place, net.attend_grads(f_ms, p, (f_mc, p_c, pair)))
    dx = go_on(dx, start=[s_ma])
    dx, v_uf, p = net.feed_backward(x0a, k_uf, dx, w_feed, 2)
    p = pairs(p)
    dx, (p,) = tie(dx, p)
    s_uf = Sum(place, net.feed_grads(f_uf, p))
    dx = need(dx, s_uf)
    v = [g[:2] for g in (v_uf, v_ms, v_mc, v_mf)]
    v = jnp.pad(jnp.concatenate(v, axis=0), ((2, 6), (0, 0)))
    dx, _v, p = net.self_backward(x0, k_us, dx, w_first, 0, 0, (v,))
    p = pairs(p)
    dx = go_on(dx, [s_mf], [s_uf, s_mf])
    dx = go_on(dx, [s_ma], [s_ma])
    dx, (p,) = tie(dx, p)
    send, keep = net.attend_grads(f_us, p)
    dx, (send, keep) = tie(dx, send, keep)
    v = nt(order[: d // 2], plus(p[0][4], p[1][4])[:LANES]).astype(bf16)
    dx, (dkv,) = tie(dx, dkv)
    denc = net.pair_input(dkv, w_middle)
    dx, (denc,) = tie(dx, denc)
    dx = go_on(dx, [s_ma], [s_ma])
    send = jnp.concatenate((send, v[d // 4 :]), axis=1)
    keep = jnp.concatenate((keep, v[: d // 4]), axis=1)
    s_us = Sum(place, (send, keep))
    dx = go_on(dx, start=[s_us])
    dx = rest(dx, s_mf)
    dx = go_on(dx, [s_uf], [s_uf])
    dx = hold(dx, s_mf)
    dx, (r_mf,) = tie(dx, feed_rows(s_mf.kept, s_mf.got))
    dx = rest(dx, s_ma)
    dx = go_on(dx, [s_uf, s_us], [s_uf, s_us])
    dx, (r_ma,) = tie(dx, s_ma.total())
    dx = rest(dx, s_uf)
    dx = go_on(dx, [s_us], [s_us])
    dx = rest(dx, s_us)
    dx = hold(dx, s_uf)
    dx, (r_uf,) = tie(dx, feed_rows(s_uf.kept, s_uf.got))
    r_us = s_us.total()

    def columns(r, *blocks):
        parts = [r[:, b * d : (b + 1) * d] for b in blocks]
        return jnp.concatenate(parts, axis=1) if len(parts) > 1 else parts[0]

    r_uup, r_udown = r_uf
    r_mup, r_mdown = r_mf
    vs = r_us[:, 4 * d :]
    v = [vs[:, i] for i in range(10)]
    return (
        x2.reshape(tokens.shape),
        dx.astype(bf16).reshape(tokens.shape),
        denc.reshape(encoder.shape),
        v[0], v[1], r_us[:, : 3 * d], r_us[:, 3 * d : 4 * d], v[2], v[3], r_uup, r_udown,
        v[4], v[5], r_ma[:, : 3 * d], columns(r_ma, 3), v[6], v[7],
        columns(r_ma, 4), r_ma[:, 6 * d :], columns(r_ma, 5),
        v[8], v[9], r_mup, r_mdown,
    )


def solution(mesh):
    rows1 = P(AXES)
    rows2 = P(AXES, None)
    rows3 = P(AXES, None, None)
    block = (rows1, rows1, rows2, rows2)
    weights = block * 2 + block + (rows1, rows1, rows2, rows2, rows2) + block
    return jax.shard_map(
        local,
        mesh=mesh,
        in_specs=(rows3, rows3, rows1, rows3) + weights,
        out_specs=(rows3, rows3, rows3) + weights,
        check_vma=False,
    )
```

```python
import functools

import jax
import jax.numpy as jnp
from jax import lax
from jax.experimental import pallas as pl
from jax.experimental.pallas import tpu as pltpu
from jax.sharding import PartitionSpec as P

DH = 64
AXES = ("dp", "hd")
EPS = 1e-05
MASKED = -1e30
LANES = 128
bf16 = jnp.bfloat16
f32 = jnp.float32
sds = jax.ShapeDtypeStruct


BIT_PAIR, BIT_CORE, BIT_NEAR = 1, 2, 4


class Place:
    def __init__(self):
        self.count = lax.axis_size("dp") * lax.axis_size("hd")
        self.outer_size = self.count // 8
        index = lax.axis_index("dp") * lax.axis_size("hd") + lax.axis_index("hd")
        self.pair = index % 2
        self.core = (index // 2) % 2
        self.near = (index // 4) % 2
        self.outer = index // 8
        self.outer_bits = self.outer_size.bit_length() - 1

    def swap(self, x, bit):
        return lax.ppermute(x, AXES, [(i, i ^ bit) for i in range(self.count)])

    def swap_by_core(self, x, bits):
        pairs = [(i, i ^ bits[(i // BIT_CORE) % 2]) for i in range(self.count)]
        return lax.ppermute(x, AXES, pairs)

    def order(self, d):
        n, rows = self.outer_size, d // self.count
        k = lax.broadcasted_iota(jnp.int32, (d, 1), 0)
        row, place = k % rows, (k // rows) % n
        outer = jnp.zeros_like(k)
        for b in range(self.outer_bits):
            outer = outer + ((place >> (self.outer_bits - 1 - b)) & 1) * (1 << b)
        outer = outer ^ self.outer
        rest = k // (rows * n)
        low, high = rest % 2, (rest // 2) % 2
        near = jnp.where((rest // 4) ^ self.core == 0, high, low)
        pair = high + low - near
        feature = outer * 2 + (near ^ self.near)
        feature = (feature * 2 + ((rest // 4) ^ self.core)) * 2 + (pair ^ self.pair)
        feature = feature * rows + row
        return (feature == lax.broadcasted_iota(jnp.int32, (d, d), 1)).astype(bf16)


def plus(a, b):
    return (a.astype(f32) + b.astype(f32)).astype(bf16)


class Sum:
    def __init__(self, place, grads):
        self.place, self.stage = place, 0
        self.send, self.kept = grads

    def swap(self):
        if self.stage < 2:
            bits = ((BIT_NEAR, BIT_PAIR), (BIT_PAIR, BIT_NEAR))[self.stage]
            self.got = self.place.swap_by_core(self.send, bits)
        else:
            self.got = self.place.swap(self.send, 8 << (self.stage - 2))

    def sums(self):
        if self.stage < 2:
            self.send, self.kept = half_sums(self.kept, self.got)
        else:
            half = self.kept.shape[0] // 2
            self.send = plus(self.kept[half:], self.got[half:])
            self.kept = plus(self.kept[:half], self.got[:half])
        self.stage += 1

    def total(self):
        return self.kept.astype(f32) + self.got.astype(f32)


class Gather:
    def __init__(self, place, shard):
        self.place, self.x, self.stage = place, shard, 0

    def swap(self):
        outer = self.place.outer_bits
        at = self.stage - outer
        if at < 0:
            self.got = self.place.swap(self.x, 8 << (outer - 1 - self.stage))
        elif at < 2:
            bits = ((BIT_PAIR, BIT_NEAR), (BIT_NEAR, BIT_PAIR))[at]
            self.got = self.place.swap_by_core(self.x, bits)
        else:
            self.got = self.place.swap(self.x, BIT_CORE)

    def join(self):
        self.x = jnp.concatenate((self.x, self.got), axis=0)
        self.stage += 1


def tie(x, *others):
    out = lax.optimization_barrier((x,) + others)
    return out[0], out[1:]


def hold(x, *groups):
    x, terms = tie(x, *[(g.kept, g.got) for g in groups])
    for g, t in zip(groups, terms):
        g.kept, g.got = t
    return x


def need(x, *groups):
    x, send = tie(x, *[g.send for g in groups])
    for g, k in zip(groups, send):
        g.send = k
    return x


def nn(a, b):
    return jnp.dot(a, b, preferred_element_type=f32)


def nt(a, b):
    return lax.dot_general(a, b, (((1,), (1,)), ((), ())), preferred_element_type=f32)


def tn(a, b):
    return lax.dot_general(a, b, (((0,), (0,)), ((), ())), preferred_element_type=f32)


def unit_norm(x):
    centred = x - jnp.mean(x, axis=-1, keepdims=True)
    inv = lax.rsqrt(jnp.mean(centred * centred, axis=-1, keepdims=True) + EPS)
    return centred * inv, inv


def norm_backward(grad, x, gain):
    unit, inv = unit_norm(x)
    du = grad * gain
    dx = inv * (
        du
        - jnp.mean(du, axis=-1, keepdims=True)
        - unit * jnp.mean(du * unit, axis=-1, keepdims=True)
    )
    return dx, jnp.sum(grad * unit, axis=0, keepdims=True), jnp.sum(grad, axis=0, keepdims=True)


GELU_A = 0.7978845608028654
GELU_B = 0.044715


def two_heads(x):
    first = lax.broadcasted_iota(jnp.int32, x.shape, 1) < DH
    zero = jnp.zeros_like(x)
    return jnp.concatenate((jnp.where(first, x, zero), jnp.where(first, zero, x)), axis=0)


def side_by_side(x):
    n = x.shape[0] // 2
    first = lax.broadcasted_iota(jnp.int32, (n, LANES), 1) < DH
    return jnp.where(first, x[:n], x[n:])


def probabilities(qs, k2, allowed):
    s = jnp.where(allowed, nt(qs, k2) * DH ** (-0.5), MASKED)
    e = jnp.exp(s - jnp.max(s, axis=-1, keepdims=True))
    return e / jnp.sum(e, axis=-1, keepdims=True)


def causal_mask(length):
    row = lax.broadcasted_iota(jnp.int32, (2 * length, length), 0)
    col = lax.broadcasted_iota(jnp.int32, (2 * length, length), 1)
    return jnp.where(row >= length, row - length, row) >= col


def attend_back(q2, k2, v2, do2, allowed):
    scale = DH ** (-0.5)
    qs, dos = two_heads(q2), two_heads(do2)
    p = probabilities(qs, k2, allowed)
    dp = nt(dos, v2)
    ds = (p * (dp - jnp.sum(p * dp, axis=-1, keepdims=True))).astype(bf16)
    dq = side_by_side(nn(ds, k2)) * scale
    dk = tn(ds, qs) * scale
    dv = tn(p.astype(bf16), dos)
    return dq.astype(bf16), dk.astype(bf16), dv.astype(bf16)


def relative(x, order_ref):
    return nt(x, order_ref[...]).astype(bf16)


def times(x, top_ref, low_ref):
    half = top_ref.shape[0]
    return nn(x[:, :half], top_ref[...]) + nn(x[:, half:], low_ref[...])


def times_back(g, top_ref, low_ref):
    return jnp.concatenate((nt(g, top_ref[...]), nt(g, low_ref[...])), axis=1)


def natural(x, order_ref):
    high = x.astype(bf16)
    low = (x - high.astype(f32)).astype(bf16)
    return nn(high, order_ref[...]) + nn(low, order_ref[...])


def self_forward_kernel(
    captions, row, x_ref, vec_ref, order_ref, top_ref, low_ref, y_ref, f_ref, qkv_ref, rel_ref
):
    j = pl.program_id(0)

    @pl.when(j == 0)
    def _():
        unit, _inv = unit_norm(x_ref[...].astype(f32))
        f_ref[0] = (unit * vec_ref[row : row + 1] + vec_ref[row + 1 : row + 2]).astype(bf16)
        rel_ref[...] = relative(f_ref[0], order_ref)

    @pl.when(j < 3)
    def _():
        qkv_ref[j] = times(rel_ref[...], top_ref, low_ref).astype(bf16)

    @pl.when(j == 3)
    def _():
        length = x_ref.shape[0] // captions
        allowed = causal_mask(length)
        for c in range(captions):
            at = slice(c * length, (c + 1) * length)
            for h in range(0, x_ref.shape[1], LANES):
                cols = slice(h, h + LANES)
                p = probabilities(two_heads(qkv_ref[0, at, cols]), qkv_ref[1, at, cols], allowed)
                o = side_by_side(nn(p.astype(bf16), qkv_ref[2, at, cols]))
                f_ref[1, at, cols] = o.astype(bf16)
        y_ref[...] = x_ref[...].astype(f32) + times(relative(f_ref[1], order_ref), top_ref, low_ref)


def self_backward_kernel(
    captions, row, x_ref, vec_ref, order_ref, qkv_ref, dx_ref, top_ref, low_ref, *refs
):
    out_ref, vg_ref, p_ref, acc_ref = refs[-4:]
    j = pl.program_id(0)

    @pl.when(j == 0)
    def _():
        dy = dx_ref[...].astype(bf16)
        p_ref[3] = dy
        do = times_back(dy, top_ref, low_ref).astype(bf16)
        do = nn(do, order_ref[...]).astype(bf16)
        length = x_ref.shape[0] // captions
        allowed = causal_mask(length)
        for c in range(captions):
            at = slice(c * length, (c + 1) * length)
            for h in range(0, x_ref.shape[1], LANES):
                cols = slice(h, h + LANES)
                dq, dk, dv = attend_back(
                    qkv_ref[0, at, cols], qkv_ref[1, at, cols], qkv_ref[2, at, cols],
                    do[at, cols], allowed,
                )
                p_ref[0, at, cols] = dq
                p_ref[1, at, cols] = dk
                p_ref[2, at, cols] = dv
        acc_ref[...] = jnp.zeros_like(acc_ref)

    @pl.when(j > 0)
    def _():
        acc_ref[...] += times_back(p_ref[j - 1], top_ref, low_ref)

    @pl.when(j == 3)
    def _():
        da = natural(acc_ref[...], order_ref)
        dn, gg, gs = norm_backward(da, x_ref[...].astype(f32), vec_ref[row : row + 1])
        out_ref[...] = dx_ref[...] + dn
        vg_ref[0:1] = gg
        vg_ref[1:2] = gs
        if len(refs) > 4:
            at = lax.broadcasted_iota(jnp.int32, refs[0].shape, 0)
            rows = jnp.where(at == 0, gg, jnp.where(at == 1, gs, refs[0][...]))
            p_ref[4] = jnp.zeros_like(p_ref[4])
            p_ref[4, 0 : refs[0].shape[0]] = rows.astype(bf16)


def cross_forward_kernel(
    captions, row, count_ref, x_ref, vec_ref, order_ref, kv_ref, top_ref, low_ref, y_ref, f_ref, q_ref
):
    j = pl.program_id(0)
    d = x_ref.shape[1]

    @pl.when(j == 0)
    def _():
        unit, _inv = unit_norm(x_ref[...])
        c = (unit * vec_ref[row : row + 1] + vec_ref[row + 1 : row + 2]).astype(bf16)
        f_ref[0] = c
        q_ref[...] = times(relative(c, order_ref), top_ref, low_ref).astype(bf16)

    @pl.when(j == 1)
    def _():
        length = x_ref.shape[0] // captions
        patches = kv_ref.shape[0] // captions
        slot = lax.broadcasted_iota(jnp.int32, (2 * length, patches), 1)
        for c in range(captions):
            at = slice(c * length, (c + 1) * length)
            keys = slice(c * patches, (c + 1) * patches)
            allowed = slot < count_ref[c]
            for h in range(0, d, LANES):
                cols = slice(h, h + LANES)
                vcols = slice(d + h, d + h + LANES)
                p = probabilities(two_heads(q_ref[at, cols]), kv_ref[keys, cols], allowed)
                o = side_by_side(nn(p.astype(bf16), kv_ref[keys, vcols]))
                f_ref[1, at, cols] = o.astype(bf16)
        y_ref[...] = x_ref[...] + times(relative(f_ref[1], order_ref), top_ref, low_ref)


def cross_backward_kernel(
    captions, row, count_ref, x_ref, vec_ref, order_ref, q_ref, kv_ref, dx_ref, top_ref, low_ref,
    out_ref, vg_ref, p_ref, dkv_ref,
):
    j = pl.program_id(0)
    d = x_ref.shape[1]

    @pl.when(j == 0)
    def _():
        dy = dx_ref[...].astype(bf16)
        p_ref[1] = dy
        do = times_back(dy, top_ref, low_ref).astype(bf16)
        do = nn(do, order_ref[...]).astype(bf16)
        length = x_ref.shape[0] // captions
        patches = kv_ref.shape[0] // captions
        slot = lax.broadcasted_iota(jnp.int32, (2 * length, patches), 1)
        for c in range(captions):
            at = slice(c * length, (c + 1) * length)
            keys = slice(c * patches, (c + 1) * patches)
            allowed = slot < count_ref[c]
            for h in range(0, d, LANES):
                cols = slice(h, h + LANES)
                vcols = slice(d + h, d + h + LANES)
                dq, dk, dv = attend_back(
                    q_ref[at, cols], kv_ref[keys, cols], kv_ref[keys, vcols], do[at, cols], allowed
                )
                p_ref[0, at, cols] = dq
                dkv_ref[keys, cols] = dk
                dkv_ref[keys, vcols] = dv

    @pl.when(j == 1)
    def _():
        dc = natural(times_back(p_ref[0], top_ref, low_ref), order_ref)
        dn, gg, gs = norm_backward(dc, x_ref[...], vec_ref[row : row + 1])
        out_ref[...] = dx_ref[...] + dn
        vg_ref[0:1] = gg
        vg_ref[1:2] = gs


def feed_forward_kernel(
    row, x_ref, vec_ref, order_ref, up_ref, up2_ref, down_ref, down2_ref, y_ref, f_ref, u_ref, rel_ref
):
    j = pl.program_id(0)

    @pl.when(j == 0)
    def _():
        unit, _inv = unit_norm(x_ref[...])
        f_ref[0] = (unit * vec_ref[row : row + 1] + vec_ref[row + 1 : row + 2]).astype(bf16)
        rel_ref[...] = relative(f_ref[0], order_ref)
        y_ref[...] = x_ref[...]

    u = times(rel_ref[...], up_ref, up2_ref)
    u_ref[...] = u
    g = (0.5 * u * (1.0 + jnp.tanh(GELU_A * (u + GELU_B * u * u * u)))).astype(bf16)
    f_ref[1 + j] = g
    y_ref[...] += times(relative(g, order_ref), down_ref, down2_ref)


def gelu_terms(u):
    t = jnp.tanh(GELU_A * (u + GELU_B * u * u * u))
    slope = 0.5 * (1.0 + t) + 0.5 * u * (1.0 - t * t) * GELU_A * (1.0 + 3.0 * GELU_B * u * u)
    return 0.5 * u * (1.0 + t), slope


def feed_backward_step(j, order_ref, slope, refs, p_ref, acc_ref):
    up_ref, up2_ref, down_ref, down2_ref = refs
    dg = times_back(p_ref[0], down_ref, down2_ref).astype(bf16)
    du = (slope * nn(dg, order_ref[...])).astype(bf16)
    p_ref[1 + j] = du
    acc_ref[...] += times_back(du, up_ref, up2_ref)


def feed_backward_end(row, order_ref, x_ref, vec_ref, dx_ref, acc_ref, out_ref, vg_ref):
    db = natural(acc_ref[...], order_ref)
    dn, gg, gs = norm_backward(db, x_ref[...], vec_ref[row : row + 1])
    out_ref[...] = dx_ref[...].astype(f32) + dn
    vg_ref[0:1] = gg
    vg_ref[1:2] = gs


def feed_backward_kernel(
    row, x_ref, vec_ref, order_ref, dx_ref, up_ref, up2_ref, down_ref, down2_ref, u_ref,
    out_ref, vg_ref, p_ref, acc_ref,
):
    j = pl.program_id(0)

    @pl.when(j == 0)
    def _():
        p_ref[0] = dx_ref[...].astype(bf16)
        acc_ref[...] = jnp.zeros_like(acc_ref)

    refs = up_ref, up2_ref, down_ref, down2_ref
    feed_backward_step(j, order_ref, gelu_terms(u_ref[...])[1], refs, p_ref, acc_ref)

    @pl.when(j == 3)
    def _():
        feed_backward_end(row, order_ref, x_ref, vec_ref, dx_ref, acc_ref, out_ref, vg_ref)


def last_backward_kernel(
    row, x_ref, vec_ref, order_ref, dx_ref, up_ref, up2_ref, down_ref, down2_ref,
    out_ref, vg_ref, p_ref, f_ref, acc_ref, rel_ref,
):
    j = pl.program_id(0)

    @pl.when(j == 0)
    def _():
        unit, _inv = unit_norm(x_ref[...])
        f_ref[0] = (unit * vec_ref[row : row + 1] + vec_ref[row + 1 : row + 2]).astype(bf16)
        rel_ref[...] = relative(f_ref[0], order_ref)
        p_ref[0] = dx_ref[...]
        acc_ref[...] = jnp.zeros_like(acc_ref)

    g, slope = gelu_terms(times(rel_ref[...], up_ref, up2_ref))
    f_ref[1 + j] = g.astype(bf16)
    refs = up_ref, up2_ref, down_ref, down2_ref
    feed_backward_step(j, order_ref, slope, refs, p_ref, acc_ref)

    @pl.when(j == 3)
    def _():
        feed_backward_end(row, order_ref, x_ref, vec_ref, dx_ref, acc_ref, out_ref, vg_ref)


def last_output_kernel(x_ref, order_ref, g_ref, down_ref, down2_ref, y_ref, acc_ref):
    j = pl.program_id(0)

    @pl.when(j == 0)
    def _():
        acc_ref[...] = x_ref[...]

    acc_ref[...] += times(relative(g_ref[0], order_ref), down_ref, down2_ref)

    @pl.when(j == 3)
    def _():
        y_ref[...] = acc_ref[...].astype(bf16)


def both(own_ref, got_ref):
    return jnp.concatenate((own_ref[0], got_ref[0]), axis=0)


def emit(g, send_ref, keep_ref):
    half = keep_ref.shape[0]
    keep_ref[...] = g[:half].astype(bf16)
    send_ref[...] = g[half:].astype(bf16)


def feed_grads_kernel(
    order_ref, b_ref, b2_ref, z_ref, z2_ref, g_ref, g2_ref, u_ref, u2_ref, send_ref, keep_ref, bt_ref
):
    d = order_ref.shape[1]

    @pl.when(pl.program_id(0) == 0)
    def _():
        bt_ref[...] = nt(order_ref[...], both(b_ref, b2_ref)).astype(bf16)

    up, down = (slice(None), slice(0, d)), (slice(None), slice(d, 2 * d))
    emit(nn(bt_ref[...], both(u_ref, u2_ref)), send_ref.at[up], keep_ref.at[up])
    gt = nt(order_ref[...], both(g_ref, g2_ref)).astype(bf16)
    emit(nn(gt, both(z_ref, z2_ref)), send_ref.at[down], keep_ref.at[down])


def attend_grads_kernel(order_ref, s_ref, s2_ref, sd_ref, sd2_ref, *refs):
    send_ref, keep_ref = refs[-2:]
    j = pl.program_id(0)

    def product(a_ref, a2_ref, d_ref, d2_ref):
        at = nt(order_ref[...], both(a_ref, a2_ref)).astype(bf16)
        emit(nn(at, both(d_ref, d2_ref)), send_ref, keep_ref)

    @pl.when(j < 4)
    def _():
        product(s_ref, s2_ref, sd_ref, sd2_ref)

    if len(refs) > 2:
        c_ref, c2_ref, cd_ref, cd2_ref, pair_ref, pair2_ref = refs[:6]

        @pl.when((j == 4) | (j == 5))
        def _():
            product(c_ref, c2_ref, cd_ref, cd2_ref)

        @pl.when(j > 5)
        def _():
            emit(pair_ref[...].astype(f32) + pair2_ref[...].astype(f32), send_ref, keep_ref)


def half_sums_kernel(kept_ref, got_ref, send_ref, keep_ref):
    emit(kept_ref[...].astype(f32) + got_ref[...].astype(f32), send_ref, keep_ref)


def half_sums(kept, got):
    rows, wide = kept.shape
    steps = 2 if wide % (2 * LANES) == 0 else 1
    full = pl.BlockSpec((rows, wide // steps), lambda j: (0, j))
    half = pl.BlockSpec((rows // 2, wide // steps), lambda j: (0, j))
    outs = (sds((rows // 2, wide), bf16),) * 2
    return call(half_sums_kernel, steps, (kept, got), [full] * 2, outs, [half] * 2, vmem=24)


def feed_rows_kernel(kept_ref, got_ref, up_ref, down_ref):
    rows, wide = up_ref.shape
    d = wide // 4
    spread = spread_matrix().astype(bf16)
    i = lax.broadcasted_iota(jnp.int32, (4 * rows, rows), 0)
    k = lax.broadcasted_iota(jnp.int32, (4 * rows, rows), 1)

    def part(at, size):
        x = kept_ref[:, at : at + size].astype(f32) + got_ref[:, at : at + size].astype(f32)
        high = x.astype(bf16)
        return high, (x - high.astype(f32)).astype(bf16)

    for b in range(wide // 512):
        parts = [part(2 * j * d + b * LANES, LANES) for j in range(4)]
        high, low = (jnp.concatenate(p, axis=1) for p in zip(*parts))
        up_ref[:, b * 512 : (b + 1) * 512] = nt(high, spread) + nt(low, spread)
    down = jnp.zeros(down_ref.shape, f32)
    for j in range(4):
        place = (i == 4 * k + j).astype(bf16)
        high, low = part((2 * j + 1) * d, d)
        down = down + nn(place, high) + nn(place, low)
    down_ref[...] = down


def feed_rows(kept, got):
    rows, wide = kept.shape
    outs = sds((rows, wide // 2), f32), sds((4 * rows, wide // 8), f32)
    ins = kept, got
    return call(feed_rows_kernel, 1, ins, [whole(x) for x in ins], outs, [whole(x) for x in outs])


def pair_forward_kernel(enc_ref, top_ref, low_ref, kv_ref):
    kv_ref[...] = times(enc_ref[...], top_ref, low_ref).astype(bf16)


def pair_input_kernel(dkv_ref, order_ref, top_ref, low_ref, out_ref):
    g = times_back(dkv_ref[...], top_ref, low_ref).astype(bf16)
    out_ref[...] = nn(g, order_ref[...]).astype(bf16)


def pair_grads_kernel(enc_ref, dkv_ref, keep_ref, send_ref):
    emit(nn(enc_ref[...], dkv_ref[...]), send_ref, keep_ref)


def first_pack_kernel(u_qkv, u_out, vec, out):
    rows, d = u_out.shape
    out[:, : 3 * d] = u_qkv[...]
    out[:, 3 * d : 4 * d] = u_out[...]
    eye = lax.broadcasted_iota(jnp.int32, (rows, rows), 0) == lax.broadcasted_iota(jnp.int32, (rows, rows), 1)
    out[:, 4 * d :] = nt(eye.astype(bf16), vec[...]).astype(bf16)


def pack_kernel(
    u_up, u_down, m_qkv, m_out, m_up, m_down, c_q, c_pair, c_out, feed_out, middle_out, last_out
):
    rows, d = m_out.shape
    spread = spread_matrix().astype(bf16)
    i = lax.broadcasted_iota(jnp.int32, (rows, 4 * rows), 0)
    k = lax.broadcasted_iota(jnp.int32, (rows, 4 * rows), 1)

    def feed(out, up, down):
        for b in range(4 * d // 512):
            y = nn(up[:, b * 512 : (b + 1) * 512], spread).astype(bf16)
            for j in range(4):
                to = j * d + b * LANES
                out[:, to : to + LANES] = y[:, j * LANES : (j + 1) * LANES]
        for j in range(4):
            y = nn((k == 4 * i + j).astype(bf16), down[...])
            out[:, (4 + j) * d : (5 + j) * d] = y.astype(bf16)

    feed(feed_out, u_up, u_down)
    middle_out[:, : 2 * d] = c_pair[...]
    middle_out[:, 2 * d : 3 * d] = c_q[...]
    middle_out[:, 3 * d : 4 * d] = c_out[...]
    middle_out[:, 4 * d : 7 * d] = m_qkv[...]
    middle_out[:, 7 * d : 8 * d] = m_out[...]
    feed(last_out, m_up, m_down)


def whole(x):
    return pl.BlockSpec(x.shape, lambda *_: (0,) * len(x.shape))


def call(kernel, steps, ins, in_specs, outs, out_specs, scratch=(), scalars=0, vmem=24):
    return pl.pallas_call(
        kernel,
        out_shape=outs,
        grid_spec=pltpu.PrefetchScalarGridSpec(
            num_scalar_prefetch=scalars,
            grid=(steps,),
            in_specs=in_specs,
            out_specs=out_specs,
            scratch_shapes=scratch,
        ),
        compiler_params=pltpu.CompilerParams(
            dimension_semantics=("arbitrary",), vmem_limit_bytes=vmem << 20
        ),
        cost_estimate=pl.CostEstimate(flops=1000, bytes_accessed=1000, transcendentals=0),
    )(*ins)


class Layers:
    def __init__(self, captions, tokens, d, vec, order, count):
        self.captions, self.t, self.d = captions, tokens, d
        self.vec, self.order, self.count = vec, order, count
        self.xs = sds((tokens, d), f32)
        self.hs = sds((tokens, d), bf16)

    def weights(self, *columns):
        d = self.d
        specs = [pl.BlockSpec((d // 2, d), lambda j, *_, c=c: (0, c(j))) for c in columns]
        return [s for s in specs for _ in range(2)]

    def self_forward(self, x, w, at, row):
        outs = (self.xs, sds((2, self.t, self.d), bf16), sds((3, self.t, self.d), bf16))
        ins = (x, self.vec, self.order)
        return call(
            functools.partial(self_forward_kernel, self.captions, row), 4,
            ins + w, [whole(i) for i in ins] + self.weights(lambda j: at + j),
            outs, [whole(o) for o in outs], scratch=[pltpu.VMEM((self.t, self.d), bf16)],
        )

    def self_backward(self, x, kept, dx, w, at, row, vectors=()):
        d, t = self.d, self.t
        outs = (self.xs, sds((8, d), f32), sds((4 + len(vectors), t, d), bf16))
        ins = (x, self.vec, self.order, kept, dx)
        return call(
            functools.partial(self_backward_kernel, self.captions, row), 4,
            ins + w + vectors,
            [whole(i) for i in ins] + self.weights(lambda j: at + (j + 3) % 4)
            + [whole(v) for v in vectors],
            outs, [whole(i) for i in outs],
            scratch=[pltpu.VMEM((t, d), f32)],
        )

    def cross_forward(self, x, kv, w, at, row):
        outs = (self.xs, sds((2, self.t, self.d), bf16), self.hs)
        ins = (x, self.vec, self.order, kv)
        return call(
            functools.partial(cross_forward_kernel, self.captions, row), 2,
            (self.count,) + ins + w,
            [whole(i) for i in ins] + self.weights(lambda j: at + j),
            outs, [whole(o) for o in outs], scalars=1,
        )

    def cross_backward(self, x, kept, kv, dx, w, at, row):
        d, t = self.d, self.t
        outs = (self.xs, sds((8, d), f32), sds((2, t, d), bf16), sds(kv.shape, bf16))
        ins = (x, self.vec, self.order, kept, kv, dx)
        return call(
            functools.partial(cross_backward_kernel, self.captions, row), 2,
            (self.count,) + ins + w,
            [whole(i) for i in ins] + self.weights(lambda j: at + 1 - j),
            outs, [whole(i) for i in outs], scalars=1,
        )

    def pair_forward(self, enc, w):
        d, rows = self.d, enc.shape[0] // self.captions
        half = pl.BlockSpec((d // 2, 2 * d), lambda j: (0, 0))
        out = sds((enc.shape[0], 2 * d), bf16)
        return call(
            pair_forward_kernel, self.captions, (enc,) + w,
            [pl.BlockSpec((rows, d), lambda j: (j, 0)), half, half],
            out, pl.BlockSpec((rows, 2 * d), lambda j: (j, 0)),
        )

    def pair_grads(self, enc_t, dkv):
        d = self.d
        outs = (sds((d // 2, 2 * d), bf16),) * 2
        grad = pl.BlockSpec((d // 2, d), lambda j: (0, j))
        return call(
            pair_grads_kernel, 2, (enc_t, dkv),
            [whole(enc_t), pl.BlockSpec((dkv.shape[0], d), lambda j: (0, j))],
            outs, [grad, grad],
        )

    def pair_input(self, dkv, w):
        d, rows = self.d, dkv.shape[0] // self.captions
        half = pl.BlockSpec((d // 2, 2 * d), lambda j: (0, 0))
        out = sds((dkv.shape[0], d), bf16)
        return call(
            pair_input_kernel, self.captions, (dkv, self.order) + w,
            [pl.BlockSpec((rows, 2 * d), lambda j: (j, 0)), whole(self.order), half, half],
            out, pl.BlockSpec((rows, d), lambda j: (j, 0)),
        )

    def block(self, index):
        return pl.BlockSpec((1, self.t, self.d), lambda j: (index(j), 0, 0))

    def feed_grads(self, f, p):
        d, t = self.d, self.t
        outs = (sds((d // 4, 8 * d), bf16),) * 2
        first, later = self.block(lambda j: 0), self.block(lambda j: 1 + j)
        half = pl.BlockSpec((d // 2, d), lambda j: (0, 0))
        return call(
            feed_grads_kernel, 4, (self.order,) + f + p + f + p,
            [half] + [first] * 4 + [later] * 4,
            outs, [pl.BlockSpec((d // 4, 2 * d), lambda j: (0, j))] * 2,
            scratch=[pltpu.VMEM((d // 2, 2 * t), bf16)],
        )

    def attend_grads(self, f, p, cross=()):
        d, t = self.d, self.t
        steps = 8 if cross else 4
        outs = (sds((d // 4, steps * d), bf16),) * 2
        half = pl.BlockSpec((d // 2, d), lambda j: (0, 0))
        lhs = self.block(lambda j: jnp.minimum(j // 3, 1))
        rhs = self.block(lambda j: jnp.minimum(j, 3))
        ins, specs = (self.order,) + f + p, [half, lhs, lhs, rhs, rhs]
        if cross:
            f, p, pair = cross
            at = self.block(lambda j: jnp.clip(j - 4, 0, 1))
            columns = pl.BlockSpec((d // 2, d), lambda j: (0, jnp.clip(j - 6, 0, 1)))
            ins, specs = ins + f + p + pair, specs + [at] * 4 + [columns] * 2
        return call(
            attend_grads_kernel, steps, ins, specs,
            outs, [pl.BlockSpec((d // 4, d), lambda j: (0, j))] * 2,
        )

    def feed_forward(self, x, w, row):
        d, t = self.d, self.t
        outs = (self.xs, sds((5, t, d), bf16), sds((t, 4 * d), f32))
        ins = (x, self.vec, self.order)
        return call(
            functools.partial(feed_forward_kernel, row), 4,
            ins + w + w,
            [whole(i) for i in ins] + self.weights(lambda j: j, lambda j: 4 + j),
            outs, [whole(outs[0]), whole(outs[1]), pl.BlockSpec((t, d), lambda j: (0, j))],
            scratch=[pltpu.VMEM((t, d), bf16)],
        )

    def feed_backward(self, x, u, dx, w, row):
        d, t = self.d, self.t
        outs = (self.xs, sds((8, d), f32), sds((5, t, d), bf16))
        ins = (x, self.vec, self.order, dx)
        return call(
            functools.partial(feed_backward_kernel, row), 4,
            ins + w + w + (u,),
            [whole(i) for i in ins] + self.weights(lambda j: j, lambda j: 4 + j)
            + [pl.BlockSpec((t, d), lambda j: (0, j))],
            outs, [whole(i) for i in outs],
            scratch=[pltpu.VMEM((t, d), f32)],
        )

    def last_backward(self, x, dx, w, row):
        d, t = self.d, self.t
        outs = (self.xs, sds((8, d), f32)) + (sds((5, t, d), bf16),) * 2
        ins = (x, self.vec, self.order, dx)
        return call(
            functools.partial(last_backward_kernel, row), 4,
            ins + w + w,
            [whole(i) for i in ins] + self.weights(lambda j: j, lambda j: 4 + j),
            outs, [whole(i) for i in outs],
            scratch=[pltpu.VMEM((t, d), f32), pltpu.VMEM((t, d), bf16)],
        )

    def last_output(self, x, f, w):
        return call(
            last_output_kernel, 4, (x, self.order, f) + w,
            [whole(x), whole(self.order), self.block(lambda j: 1 + j)]
            + self.weights(lambda j: 4 + j),
            self.hs, whole(self.hs), scratch=[pltpu.VMEM((self.t, self.d), f32)],
        )


def spread_matrix():
    k = lax.broadcasted_iota(jnp.int32, (512, 512), 0)
    n = lax.broadcasted_iota(jnp.int32, (512, 512), 1)
    return (k % 4) * 128 + k // 4 == n


def local(
    tokens, encoder, patch_count, out_grad,
    u_ag, u_as, u_qkv, u_out, u_mg, u_ms, u_up, u_down,
    m_ag, m_as, m_qkv, m_out, c_g, c_s, c_q, c_pair, c_out, m_mg, m_ms, m_up, m_down,
):
    place = Place()
    captions, length, d = tokens.shape
    rows = u_qkv.shape[0]
    x0 = tokens.reshape(-1, d)
    enc = encoder.reshape(-1, d)
    order = place.order(d)

    vectors = (u_ag, u_as, u_mg, u_ms, m_ag, m_as, c_g, c_s, m_mg, m_ms)
    vectors = jnp.pad(jnp.stack(vectors, axis=0), ((0, LANES - len(vectors)), (0, 0)))
    def packed(kernel, parts, *widths):
        outs = tuple(sds((rows, c), bf16) for c in widths)
        shards = call(kernel, 1, parts, [whole(p) for p in parts], outs, [whole(o) for o in outs], vmem=60)
        return [Gather(place, x) for x in shards]

    (first,) = packed(first_pack_kernel, (u_qkv, u_out, vectors), 4 * d + LANES)
    parts = (u_up, u_down, m_qkv, m_out, m_up, m_down, c_q, c_pair, c_out)
    feed, middle, last = packed(pack_kernel, parts, 8 * d, 8 * d, 8 * d)

    def go(token, groups=(), start=()):
        token, got = tie(token, *[(g.x, g.got) for g in groups])
        for g, (x, y) in zip(groups, got):
            g.x, g.got = x, y
            g.join()
        every = tuple(groups) + tuple(start)
        token, xs = tie(token, *[g.x for g in every])
        for g, x in zip(every, xs):
            g.x = x
            g.swap()
        return token

    def end(token, group):
        token, (group.x, group.got) = tie(token, group.x, group.got)
        return token, (group.x, group.got)

    steps = place.outer_bits
    x0 = go(x0, start=[first])
    enc_rel = nt(enc, order).astype(bf16)
    enc_t = nt(order, enc).astype(bf16)
    for k in range(steps - 1):
        x0 = go(x0, [first], [feed] if k == 0 else [])
    x0 = go(x0, [first])
    for k in range(steps - 1):
        x0 = go(x0, [feed])
    x0 = go(x0, [first])
    x0 = go(x0, [feed], [middle])
    x0 = go(x0, [first, middle])
    x0 = go(x0, [feed])
    for k in range(steps - 2):
        x0 = go(x0, [middle])
    x0, (order, enc_rel, enc_t) = tie(x0, order, enc_rel, enc_t)
    x0, w_first = end(x0, first)
    vec = tn(jnp.concatenate([x[:, 4 * d :] for x in w_first], axis=0), order)[:16]
    net = Layers(captions, captions * length, d, vec, order, patch_count)
    x0 = go(x0, [middle], [last])
    for k in range(steps - 1):
        x0 = go(x0, [last])
    x0 = go(x0, [feed])
    x0a, f_us, k_us = net.self_forward(x0, w_first, 0, 0)
    x0a = go(x0a, [middle])
    x0a = go(x0a, [last])
    x0a, w_feed = end(x0a, feed)
    x1, f_uf, k_uf = net.feed_forward(x0a, w_feed, 2)
    x1 = go(x1, [last])
    x1 = go(x1, [middle])
    x1, w_middle = end(x1, middle)
    x1a, f_ms, k_ms = net.self_forward(x1, w_middle, 4, 4)
    kv = net.pair_forward(enc_rel, w_middle)
    x1b, f_mc, k_mc = net.cross_forward(x1a, kv, w_middle, 2, 6)
    x1b = go(x1b, [last])
    x1b, w_last = end(x1b, last)

    def core(x):
        return place.swap(x, BIT_CORE)

    def go_on(x, sums=(), start=()):
        x = hold(x, *sums)
        for g in sums:
            g.sums()
        x = need(x, *(tuple(sums) + tuple(g for g in start if g not in sums)))
        for g in start:
            g.swap()
        return x

    def rest(x, *groups):
        for _ in range(place.outer_bits - 1):
            for g in groups:
                x = go_on(x, [g], [g])
        return x

    def pairs(x):
        return x, core(x)

    f_us, f_uf, f_ms = pairs(f_us), pairs(f_uf), pairs(f_ms)
    x1b, (f_us, f_uf, f_ms) = tie(x1b, f_us, f_uf, f_ms)
    f_mc = pairs(f_mc)
    dx, v_mf, p, f = net.last_backward(x1b, out_grad.reshape(-1, d), w_last, 8)
    p, f = pairs(p), pairs(f)
    x2 = net.last_output(x1b, f[0], w_last)
    p, (x2,) = tie(p, x2)
    s_mf = Sum(place, net.feed_grads(f, p))
    dx, (f_mc,) = tie(dx, f_mc)
    dx = go_on(dx, start=[s_mf])
    dx, v_mc, p_c, dkv = net.cross_backward(x1a, k_mc, kv, dx, w_middle, 2, 6)
    p_c = pairs(p_c)
    pair, send = net.pair_grads(enc_t, dkv)
    dx, (send,) = tie(dx, send)
    pair = pair, core(send)
    dx, v_ms, p = net.self_backward(x1, k_ms, dx, w_middle, 4, 4)
    p = pairs(p)
    dx = go_on(dx, [s_mf], [s_mf])
    dx, (p, p_c, pair) = tie(dx, p, p_c, pair)
    s_ma = Sum(place, net.attend_grads(f_ms, p, (f_mc, p_c, pair)))
    dx = go_on(dx, start=[s_ma])
    dx, v_uf, p = net.feed_backward(x0a, k_uf, dx, w_feed, 2)
    p = pairs(p)
    dx, (p,) = tie(dx, p)
    s_uf = Sum(place, net.feed_grads(f_uf, p))
    dx = need(dx, s_uf)
    v = [g[:2] for g in (v_uf, v_ms, v_mc, v_mf)]
    v = jnp.pad(jnp.concatenate(v, axis=0), ((2, 6), (0, 0)))
    dx, _v, p = net.self_backward(x0, k_us, dx, w_first, 0, 0, (v,))
    p = pairs(p)
    dx = go_on(dx, [s_mf], [s_uf, s_mf])
    dx = go_on(dx, [s_ma], [s_ma])
    dx, (p,) = tie(dx, p)
    send, keep = net.attend_grads(f_us, p)
    dx, (send, keep) = tie(dx, send, keep)
    v = nt(order[: d // 2], plus(p[0][4], p[1][4])[:LANES]).astype(bf16)
    dx, (dkv,) = tie(dx, dkv)
    denc = net.pair_input(dkv, w_middle)
    dx, (denc,) = tie(dx, denc)
    dx = go_on(dx, [s_ma], [s_ma])
    send = jnp.concatenate((send, v[d // 4 :]), axis=1)
    keep = jnp.concatenate((keep, v[: d // 4]), axis=1)
    s_us = Sum(place, (send, keep))
    dx = go_on(dx, start=[s_us])
    dx = rest(dx, s_mf)
    dx = go_on(dx, [s_uf], [s_uf])
    dx, (r_mf,) = tie(dx, feed_rows(s_mf.kept, s_mf.got))
    dx = rest(dx, s_ma)
    dx = go_on(dx, [s_uf, s_us], [s_uf, s_us])
    dx, (r_ma,) = tie(dx, s_ma.total())
    dx = rest(dx, s_uf)
    dx = go_on(dx, [s_us], [s_us])
    dx = rest(dx, s_us)
    dx = hold(dx, s_uf)
    dx, (r_uf,) = tie(dx, feed_rows(s_uf.kept, s_uf.got))
    r_us = s_us.total()

    def columns(r, *blocks):
        parts = [r[:, b * d : (b + 1) * d] for b in blocks]
        return jnp.concatenate(parts, axis=1) if len(parts) > 1 else parts[0]

    r_uup, r_udown = r_uf
    r_mup, r_mdown = r_mf
    vs = r_us[:, 4 * d :]
    v = [vs[:, i] for i in range(10)]
    return (
        x2.reshape(tokens.shape),
        dx.astype(bf16).reshape(tokens.shape),
        denc.reshape(encoder.shape),
        v[0], v[1], r_us[:, : 3 * d], r_us[:, 3 * d : 4 * d], v[2], v[3], r_uup, r_udown,
        v[4], v[5], r_ma[:, : 3 * d], columns(r_ma, 3), v[6], v[7],
        columns(r_ma, 4), r_ma[:, 6 * d :], columns(r_ma, 5),
        v[8], v[9], r_mup, r_mdown,
    )


def solution(mesh):
    rows1 = P(AXES)
    rows2 = P(AXES, None)
    rows3 = P(AXES, None, None)
    block = (rows1, rows1, rows2, rows2)
    weights = block * 2 + block + (rows1, rows1, rows2, rows2, rows2) + block
    return jax.shard_map(
        local,
        mesh=mesh,
        in_specs=(rows3, rows3, rows1, rows3) + weights,
        out_specs=(rows3, rows3, rows3) + weights,
        check_vma=False,
    )
```

```python
import functools

import jax
import jax.numpy as jnp
from jax import lax
from jax.experimental import pallas as pl
from jax.experimental.pallas import tpu as pltpu
from jax.sharding import PartitionSpec as P

DH = 64
AXES = ("dp", "hd")
EPS = 1e-05
MASKED = -1e30
LANES = 128
bf16 = jnp.bfloat16
f32 = jnp.float32
sds = jax.ShapeDtypeStruct


BIT_PAIR, BIT_CORE, BIT_NEAR = 1, 2, 4


class Place:
    def __init__(self):
        self.count = lax.axis_size("dp") * lax.axis_size("hd")
        self.outer_size = self.count // 8
        index = lax.axis_index("dp") * lax.axis_size("hd") + lax.axis_index("hd")
        self.pair = index % 2
        self.core = (index // 2) % 2
        self.near = (index // 4) % 2
        self.outer = index // 8
        self.outer_bits = self.outer_size.bit_length() - 1

    def swap(self, x, bit):
        return lax.ppermute(x, AXES, [(i, i ^ bit) for i in range(self.count)])

    def swap_by_core(self, x, bits):
        pairs = [(i, i ^ bits[(i // BIT_CORE) % 2]) for i in range(self.count)]
        return lax.ppermute(x, AXES, pairs)

    def order(self, d):
        n, rows = self.outer_size, d // self.count
        k = lax.broadcasted_iota(jnp.int32, (d, 1), 0)
        row, place = k % rows, (k // rows) % n
        outer = jnp.zeros_like(k)
        for b in range(self.outer_bits):
            outer = outer + ((place >> (self.outer_bits - 1 - b)) & 1) * (1 << b)
        outer = outer ^ self.outer
        rest = k // (rows * n)
        low, high = rest % 2, (rest // 2) % 2
        near = jnp.where((rest // 4) ^ self.core == 0, high, low)
        pair = high + low - near
        feature = outer * 2 + (near ^ self.near)
        feature = (feature * 2 + ((rest // 4) ^ self.core)) * 2 + (pair ^ self.pair)
        feature = feature * rows + row
        return (feature == lax.broadcasted_iota(jnp.int32, (d, d), 1)).astype(bf16)


def plus(a, b):
    return (a.astype(f32) + b.astype(f32)).astype(bf16)


class Sum:
    def __init__(self, place, grads):
        self.place, self.stage = place, 0
        self.send, self.kept = grads

    def swap(self):
        if self.stage < 2:
            bits = ((BIT_NEAR, BIT_PAIR), (BIT_PAIR, BIT_NEAR))[self.stage]
            self.got = self.place.swap_by_core(self.send, bits)
        else:
            self.got = self.place.swap(self.send, 8 << (self.stage - 2))

    def sums(self):
        if self.stage < 2:
            self.send, self.kept = half_sums(self.kept, self.got)
        else:
            half = self.kept.shape[0] // 2
            self.send = plus(self.kept[half:], self.got[half:])
            self.kept = plus(self.kept[:half], self.got[:half])
        self.stage += 1

    def total(self):
        return self.kept.astype(f32) + self.got.astype(f32)


class Gather:
    def __init__(self, place, shard):
        self.place, self.x, self.stage = place, shard, 0

    def swap(self):
        outer = self.place.outer_bits
        at = self.stage - outer
        if at < 0:
            self.got = self.place.swap(self.x, 8 << (outer - 1 - self.stage))
        elif at < 2:
            bits = ((BIT_PAIR, BIT_NEAR), (BIT_NEAR, BIT_PAIR))[at]
            self.got = self.place.swap_by_core(self.x, bits)
        else:
            self.got = self.place.swap(self.x, BIT_CORE)

    def join(self):
        self.x = jnp.concatenate((self.x, self.got), axis=0)
        self.stage += 1


def tie(x, *others):
    out = lax.optimization_barrier((x,) + others)
    return out[0], out[1:]


def hold(x, *groups):
    x, terms = tie(x, *[(g.kept, g.got) for g in groups])
    for g, t in zip(groups, terms):
        g.kept, g.got = t
    return x


def need(x, *groups):
    x, send = tie(x, *[g.send for g in groups])
    for g, k in zip(groups, send):
        g.send = k
    return x


def nn(a, b):
    return jnp.dot(a, b, preferred_element_type=f32)


def nt(a, b):
    return lax.dot_general(a, b, (((1,), (1,)), ((), ())), preferred_element_type=f32)


def tn(a, b):
    return lax.dot_general(a, b, (((0,), (0,)), ((), ())), preferred_element_type=f32)


def unit_norm(x):
    centred = x - jnp.mean(x, axis=-1, keepdims=True)
    inv = lax.rsqrt(jnp.mean(centred * centred, axis=-1, keepdims=True) + EPS)
    return centred * inv, inv


def norm_backward(grad, x, gain):
    unit, inv = unit_norm(x)
    du = grad * gain
    dx = inv * (
        du
        - jnp.mean(du, axis=-1, keepdims=True)
        - unit * jnp.mean(du * unit, axis=-1, keepdims=True)
    )
    return dx, jnp.sum(grad * unit, axis=0, keepdims=True), jnp.sum(grad, axis=0, keepdims=True)


GELU_A = 0.7978845608028654
GELU_B = 0.044715


def two_heads(x):
    first = lax.broadcasted_iota(jnp.int32, x.shape, 1) < DH
    zero = jnp.zeros_like(x)
    return jnp.concatenate((jnp.where(first, x, zero), jnp.where(first, zero, x)), axis=0)


def side_by_side(x):
    n = x.shape[0] // 2
    first = lax.broadcasted_iota(jnp.int32, (n, LANES), 1) < DH
    return jnp.where(first, x[:n], x[n:])


def probabilities(qs, k2, allowed):
    s = jnp.where(allowed, nt(qs, k2) * DH ** (-0.5), MASKED)
    e = jnp.exp(s - jnp.max(s, axis=-1, keepdims=True))
    return e / jnp.sum(e, axis=-1, keepdims=True)


def causal_mask(length):
    row = lax.broadcasted_iota(jnp.int32, (2 * length, length), 0)
    col = lax.broadcasted_iota(jnp.int32, (2 * length, length), 1)
    return jnp.where(row >= length, row - length, row) >= col


def attend_back(q2, k2, v2, do2, allowed):
    scale = DH ** (-0.5)
    qs, dos = two_heads(q2), two_heads(do2)
    p = probabilities(qs, k2, allowed)
    dp = nt(dos, v2)
    ds = (p * (dp - jnp.sum(p * dp, axis=-1, keepdims=True))).astype(bf16)
    dq = side_by_side(nn(ds, k2)) * scale
    dk = tn(ds, qs) * scale
    dv = tn(p.astype(bf16), dos)
    return dq.astype(bf16), dk.astype(bf16), dv.astype(bf16)


def relative(x, order_ref):
    return nt(x, order_ref[...]).astype(bf16)


def times(x, top_ref, low_ref):
    half = top_ref.shape[0]
    return nn(x[:, :half], top_ref[...]) + nn(x[:, half:], low_ref[...])


def times_back(g, top_ref, low_ref):
    return jnp.concatenate((nt(g, top_ref[...]), nt(g, low_ref[...])), axis=1)


def natural(x, order_ref):
    high = x.astype(bf16)
    low = (x - high.astype(f32)).astype(bf16)
    return nn(high, order_ref[...]) + nn(low, order_ref[...])


def self_forward_kernel(
    captions, row, x_ref, vec_ref, order_ref, top_ref, low_ref, y_ref, f_ref, qkv_ref, rel_ref
):
    j = pl.program_id(0)

    @pl.when(j == 0)
    def _():
        unit, _inv = unit_norm(x_ref[...].astype(f32))
        f_ref[0] = (unit * vec_ref[row : row + 1] + vec_ref[row + 1 : row + 2]).astype(bf16)
        rel_ref[...] = relative(f_ref[0], order_ref)

    @pl.when(j < 3)
    def _():
        qkv_ref[j] = times(rel_ref[...], top_ref, low_ref).astype(bf16)

    @pl.when(j == 3)
    def _():
        length = x_ref.shape[0] // captions
        allowed = causal_mask(length)
        for c in range(captions):
            at = slice(c * length, (c + 1) * length)
            for h in range(0, x_ref.shape[1], LANES):
                cols = slice(h, h + LANES)
                p = probabilities(two_heads(qkv_ref[0, at, cols]), qkv_ref[1, at, cols], allowed)
                o = side_by_side(nn(p.astype(bf16), qkv_ref[2, at, cols]))
                f_ref[1, at, cols] = o.astype(bf16)
        y_ref[...] = x_ref[...].astype(f32) + times(relative(f_ref[1], order_ref), top_ref, low_ref)


def self_backward_kernel(
    captions, row, x_ref, vec_ref, order_ref, qkv_ref, dx_ref, top_ref, low_ref, *refs
):
    out_ref, vg_ref, p_ref, acc_ref = refs[-4:]
    j = pl.program_id(0)

    @pl.when(j == 0)
    def _():
        dy = dx_ref[...].astype(bf16)
        p_ref[3] = dy
        do = times_back(dy, top_ref, low_ref).astype(bf16)
        do = nn(do, order_ref[...]).astype(bf16)
        length = x_ref.shape[0] // captions
        allowed = causal_mask(length)
        for c in range(captions):
            at = slice(c * length, (c + 1) * length)
            for h in range(0, x_ref.shape[1], LANES):
                cols = slice(h, h + LANES)
                dq, dk, dv = attend_back(
                    qkv_ref[0, at, cols], qkv_ref[1, at, cols], qkv_ref[2, at, cols],
                    do[at, cols], allowed,
                )
                p_ref[0, at, cols] = dq
                p_ref[1, at, cols] = dk
                p_ref[2, at, cols] = dv
        acc_ref[...] = jnp.zeros_like(acc_ref)

    @pl.when(j > 0)
    def _():
        acc_ref[...] += times_back(p_ref[j - 1], top_ref, low_ref)

    @pl.when(j == 3)
    def _():
        da = natural(acc_ref[...], order_ref)
        dn, gg, gs = norm_backward(da, x_ref[...].astype(f32), vec_ref[row : row + 1])
        out_ref[...] = dx_ref[...] + dn
        vg_ref[0:1] = gg
        vg_ref[1:2] = gs
        if len(refs) > 4:
            at = lax.broadcasted_iota(jnp.int32, refs[0].shape, 0)
            rows = jnp.where(at == 0, gg, jnp.where(at == 1, gs, refs[0][...]))
            p_ref[4] = jnp.zeros_like(p_ref[4])
            p_ref[4, 0 : refs[0].shape[0]] = rows.astype(bf16)


def cross_forward_kernel(
    captions, row, count_ref, x_ref, vec_ref, order_ref, kv_ref, top_ref, low_ref, y_ref, f_ref, q_ref
):
    j = pl.program_id(0)
    d = x_ref.shape[1]

    @pl.when(j == 0)
    def _():
        unit, _inv = unit_norm(x_ref[...])
        c = (unit * vec_ref[row : row + 1] + vec_ref[row + 1 : row + 2]).astype(bf16)
        f_ref[0] = c
        q_ref[...] = times(relative(c, order_ref), top_ref, low_ref).astype(bf16)

    @pl.when(j == 1)
    def _():
        length = x_ref.shape[0] // captions
        patches = kv_ref.shape[0] // captions
        slot = lax.broadcasted_iota(jnp.int32, (2 * length, patches), 1)
        for c in range(captions):
            at = slice(c * length, (c + 1) * length)
            keys = slice(c * patches, (c + 1) * patches)
            allowed = slot < count_ref[c]
            for h in range(0, d, LANES):
                cols = slice(h, h + LANES)
                vcols = slice(d + h, d + h + LANES)
                p = probabilities(two_heads(q_ref[at, cols]), kv_ref[keys, cols], allowed)
                o = side_by_side(nn(p.astype(bf16), kv_ref[keys, vcols]))
                f_ref[1, at, cols] = o.astype(bf16)
        y_ref[...] = x_ref[...] + times(relative(f_ref[1], order_ref), top_ref, low_ref)


def cross_backward_kernel(
    captions, row, count_ref, x_ref, vec_ref, order_ref, q_ref, kv_ref, dx_ref, top_ref, low_ref,
    out_ref, vg_ref, p_ref, dkv_ref,
):
    j = pl.program_id(0)
    d = x_ref.shape[1]

    @pl.when(j == 0)
    def _():
        dy = dx_ref[...].astype(bf16)
        p_ref[1] = dy
        do = times_back(dy, top_ref, low_ref).astype(bf16)
        do = nn(do, order_ref[...]).astype(bf16)
        length = x_ref.shape[0] // captions
        patches = kv_ref.shape[0] // captions
        slot = lax.broadcasted_iota(jnp.int32, (2 * length, patches), 1)
        for c in range(captions):
            at = slice(c * length, (c + 1) * length)
            keys = slice(c * patches, (c + 1) * patches)
            allowed = slot < count_ref[c]
            for h in range(0, d, LANES):
                cols = slice(h, h + LANES)
                vcols = slice(d + h, d + h + LANES)
                dq, dk, dv = attend_back(
                    q_ref[at, cols], kv_ref[keys, cols], kv_ref[keys, vcols], do[at, cols], allowed
                )
                p_ref[0, at, cols] = dq
                dkv_ref[keys, cols] = dk
                dkv_ref[keys, vcols] = dv

    @pl.when(j == 1)
    def _():
        dc = natural(times_back(p_ref[0], top_ref, low_ref), order_ref)
        dn, gg, gs = norm_backward(dc, x_ref[...], vec_ref[row : row + 1])
        out_ref[...] = dx_ref[...] + dn
        vg_ref[0:1] = gg
        vg_ref[1:2] = gs


def feed_forward_kernel(
    row, x_ref, vec_ref, order_ref, up_ref, up2_ref, down_ref, down2_ref, y_ref, f_ref, u_ref, rel_ref
):
    j = pl.program_id(0)

    @pl.when(j == 0)
    def _():
        unit, _inv = unit_norm(x_ref[...])
        f_ref[0] = (unit * vec_ref[row : row + 1] + vec_ref[row + 1 : row + 2]).astype(bf16)
        rel_ref[...] = relative(f_ref[0], order_ref)
        y_ref[...] = x_ref[...]

    u = times(rel_ref[...], up_ref, up2_ref)
    u_ref[...] = u
    g = (0.5 * u * (1.0 + jnp.tanh(GELU_A * (u + GELU_B * u * u * u)))).astype(bf16)
    f_ref[1 + j] = g
    y_ref[...] += times(relative(g, order_ref), down_ref, down2_ref)


def gelu_terms(u):
    t = jnp.tanh(GELU_A * (u + GELU_B * u * u * u))
    slope = 0.5 * (1.0 + t) + 0.5 * u * (1.0 - t * t) * GELU_A * (1.0 + 3.0 * GELU_B * u * u)
    return 0.5 * u * (1.0 + t), slope


def feed_backward_step(j, order_ref, slope, refs, p_ref, acc_ref):
    up_ref, up2_ref, down_ref, down2_ref = refs
    dg = times_back(p_ref[0], down_ref, down2_ref).astype(bf16)
    du = (slope * nn(dg, order_ref[...])).astype(bf16)
    p_ref[1 + j] = du
    acc_ref[...] += times_back(du, up_ref, up2_ref)


def feed_backward_end(row, order_ref, x_ref, vec_ref, dx_ref, acc_ref, out_ref, vg_ref):
    db = natural(acc_ref[...], order_ref)
    dn, gg, gs = norm_backward(db, x_ref[...], vec_ref[row : row + 1])
    out_ref[...] = dx_ref[...].astype(f32) + dn
    vg_ref[0:1] = gg
    vg_ref[1:2] = gs


def feed_backward_kernel(
    row, x_ref, vec_ref, order_ref, dx_ref, up_ref, up2_ref, down_ref, down2_ref, u_ref,
    out_ref, vg_ref, p_ref, acc_ref,
):
    j = pl.program_id(0)

    @pl.when(j == 0)
    def _():
        p_ref[0] = dx_ref[...].astype(bf16)
        acc_ref[...] = jnp.zeros_like(acc_ref)

    refs = up_ref, up2_ref, down_ref, down2_ref
    feed_backward_step(j, order_ref, gelu_terms(u_ref[...])[1], refs, p_ref, acc_ref)

    @pl.when(j == 3)
    def _():
        feed_backward_end(row, order_ref, x_ref, vec_ref, dx_ref, acc_ref, out_ref, vg_ref)


def last_backward_kernel(
    row, x_ref, vec_ref, order_ref, dx_ref, up_ref, up2_ref, down_ref, down2_ref,
    out_ref, vg_ref, p_ref, f_ref, acc_ref, rel_ref,
):
    j = pl.program_id(0)

    @pl.when(j == 0)
    def _():
        unit, _inv = unit_norm(x_ref[...])
        f_ref[0] = (unit * vec_ref[row : row + 1] + vec_ref[row + 1 : row + 2]).astype(bf16)
        rel_ref[...] = relative(f_ref[0], order_ref)
        p_ref[0] = dx_ref[...]
        acc_ref[...] = jnp.zeros_like(acc_ref)

    g, slope = gelu_terms(times(rel_ref[...], up_ref, up2_ref))
    f_ref[1 + j] = g.astype(bf16)
    refs = up_ref, up2_ref, down_ref, down2_ref
    feed_backward_step(j, order_ref, slope, refs, p_ref, acc_ref)

    @pl.when(j == 3)
    def _():
        feed_backward_end(row, order_ref, x_ref, vec_ref, dx_ref, acc_ref, out_ref, vg_ref)


def last_output_kernel(x_ref, order_ref, g_ref, down_ref, down2_ref, y_ref, acc_ref):
    j = pl.program_id(0)

    @pl.when(j == 0)
    def _():
        acc_ref[...] = x_ref[...]

    acc_ref[...] += times(relative(g_ref[0], order_ref), down_ref, down2_ref)

    @pl.when(j == 3)
    def _():
        y_ref[...] = acc_ref[...].astype(bf16)


def both(own_ref, got_ref):
    return jnp.concatenate((own_ref[0], got_ref[0]), axis=0)


def emit(g, send_ref, keep_ref):
    half = keep_ref.shape[0]
    keep_ref[...] = g[:half].astype(bf16)
    send_ref[...] = g[half:].astype(bf16)


def feed_grads_kernel(
    order_ref, b_ref, b2_ref, z_ref, z2_ref, g_ref, g2_ref, u_ref, u2_ref, send_ref, keep_ref, bt_ref
):
    d = order_ref.shape[1]

    @pl.when(pl.program_id(0) == 0)
    def _():
        bt_ref[...] = nt(order_ref[...], both(b_ref, b2_ref)).astype(bf16)

    up, down = (slice(None), slice(0, d)), (slice(None), slice(d, 2 * d))
    emit(nn(bt_ref[...], both(u_ref, u2_ref)), send_ref.at[up], keep_ref.at[up])
    gt = nt(order_ref[...], both(g_ref, g2_ref)).astype(bf16)
    emit(nn(gt, both(z_ref, z2_ref)), send_ref.at[down], keep_ref.at[down])


def attend_grads_kernel(order_ref, s_ref, s2_ref, sd_ref, sd2_ref, *refs):
    send_ref, keep_ref = refs[-2:]
    j = pl.program_id(0)

    def product(a_ref, a2_ref, d_ref, d2_ref):
        at = nt(order_ref[...], both(a_ref, a2_ref)).astype(bf16)
        emit(nn(at, both(d_ref, d2_ref)), send_ref, keep_ref)

    @pl.when(j < 4)
    def _():
        product(s_ref, s2_ref, sd_ref, sd2_ref)

    if len(refs) > 2:
        c_ref, c2_ref, cd_ref, cd2_ref, pair_ref, pair2_ref = refs[:6]

        @pl.when((j == 4) | (j == 5))
        def _():
            product(c_ref, c2_ref, cd_ref, cd2_ref)

        @pl.when(j > 5)
        def _():
            emit(pair_ref[...].astype(f32) + pair2_ref[...].astype(f32), send_ref, keep_ref)


def half_sums_kernel(kept_ref, got_ref, send_ref, keep_ref):
    emit(kept_ref[...].astype(f32) + got_ref[...].astype(f32), send_ref, keep_ref)


def half_sums(kept, got):
    rows, wide = kept.shape
    steps = 2 if wide % (2 * LANES) == 0 else 1
    full = pl.BlockSpec((rows, wide // steps), lambda j: (0, j))
    half = pl.BlockSpec((rows // 2, wide // steps), lambda j: (0, j))
    outs = (sds((rows // 2, wide), bf16),) * 2
    return call(half_sums_kernel, steps, (kept, got), [full] * 2, outs, [half] * 2, vmem=24)


def feed_rows_kernel(kept_ref, got_ref, up_ref, down_ref):
    rows, wide = up_ref.shape
    d = wide // 4
    spread = spread_matrix().astype(bf16)
    i = lax.broadcasted_iota(jnp.int32, (4 * rows, rows), 0)
    k = lax.broadcasted_iota(jnp.int32, (4 * rows, rows), 1)

    def part(at, size):
        x = kept_ref[:, at : at + size].astype(f32) + got_ref[:, at : at + size].astype(f32)
        high = x.astype(bf16)
        return high, (x - high.astype(f32)).astype(bf16)

    for b in range(wide // 512):
        parts = [part(2 * j * d + b * LANES, LANES) for j in range(4)]
        high, low = (jnp.concatenate(p, axis=1) for p in zip(*parts))
        up_ref[:, b * 512 : (b + 1) * 512] = nt(high, spread) + nt(low, spread)
    down = jnp.zeros(down_ref.shape, f32)
    for j in range(4):
        place = (i == 4 * k + j).astype(bf16)
        high, low = part((2 * j + 1) * d, d)
        down = down + nn(place, high) + nn(place, low)
    down_ref[...] = down


def feed_rows(kept, got):
    rows, wide = kept.shape
    outs = sds((rows, wide // 2), f32), sds((4 * rows, wide // 8), f32)
    ins = kept, got
    return call(feed_rows_kernel, 1, ins, [whole(x) for x in ins], outs, [whole(x) for x in outs])


def pair_forward_kernel(enc_ref, top_ref, low_ref, kv_ref):
    kv_ref[...] = times(enc_ref[...], top_ref, low_ref).astype(bf16)


def pair_input_kernel(dkv_ref, order_ref, top_ref, low_ref, out_ref):
    g = times_back(dkv_ref[...], top_ref, low_ref).astype(bf16)
    out_ref[...] = nn(g, order_ref[...]).astype(bf16)


def pair_grads_kernel(enc_ref, dkv_ref, keep_ref, send_ref):
    emit(nn(enc_ref[...], dkv_ref[...]), send_ref, keep_ref)


def first_pack_kernel(u_qkv, u_out, vec, out):
    rows, d = u_out.shape
    out[:, : 3 * d] = u_qkv[...]
    out[:, 3 * d : 4 * d] = u_out[...]
    eye = lax.broadcasted_iota(jnp.int32, (rows, rows), 0) == lax.broadcasted_iota(jnp.int32, (rows, rows), 1)
    out[:, 4 * d :] = nt(eye.astype(bf16), vec[...]).astype(bf16)


def pack_kernel(
    u_up, u_down, m_qkv, m_out, m_up, m_down, c_q, c_pair, c_out, feed_out, middle_out, last_out
):
    rows, d = m_out.shape
    spread = spread_matrix().astype(bf16)
    i = lax.broadcasted_iota(jnp.int32, (rows, 4 * rows), 0)
    k = lax.broadcasted_iota(jnp.int32, (rows, 4 * rows), 1)

    def feed(out, up, down):
        for b in range(4 * d // 512):
            y = nn(up[:, b * 512 : (b + 1) * 512], spread).astype(bf16)
            for j in range(4):
                to = j * d + b * LANES
                out[:, to : to + LANES] = y[:, j * LANES : (j + 1) * LANES]
        for j in range(4):
            y = nn((k == 4 * i + j).astype(bf16), down[...])
            out[:, (4 + j) * d : (5 + j) * d] = y.astype(bf16)

    feed(feed_out, u_up, u_down)
    middle_out[:, : 2 * d] = c_pair[...]
    middle_out[:, 2 * d : 3 * d] = c_q[...]
    middle_out[:, 3 * d : 4 * d] = c_out[...]
    middle_out[:, 4 * d : 7 * d] = m_qkv[...]
    middle_out[:, 7 * d : 8 * d] = m_out[...]
    feed(last_out, m_up, m_down)


def whole(x):
    return pl.BlockSpec(x.shape, lambda *_: (0,) * len(x.shape))


def call(kernel, steps, ins, in_specs, outs, out_specs, scratch=(), scalars=0, vmem=24):
    return pl.pallas_call(
        kernel,
        out_shape=outs,
        grid_spec=pltpu.PrefetchScalarGridSpec(
            num_scalar_prefetch=scalars,
            grid=(steps,),
            in_specs=in_specs,
            out_specs=out_specs,
            scratch_shapes=scratch,
        ),
        compiler_params=pltpu.CompilerParams(
            dimension_semantics=("arbitrary",), vmem_limit_bytes=vmem << 20
        ),
        cost_estimate=pl.CostEstimate(flops=1000, bytes_accessed=1000, transcendentals=0),
    )(*ins)


class Layers:
    def __init__(self, captions, tokens, d, vec, order, count):
        self.captions, self.t, self.d = captions, tokens, d
        self.vec, self.order, self.count = vec, order, count
        self.xs = sds((tokens, d), f32)
        self.hs = sds((tokens, d), bf16)

    def weights(self, *columns):
        d = self.d
        specs = [pl.BlockSpec((d // 2, d), lambda j, *_, c=c: (0, c(j))) for c in columns]
        return [s for s in specs for _ in range(2)]

    def self_forward(self, x, w, at, row):
        outs = (self.xs, sds((2, self.t, self.d), bf16), sds((3, self.t, self.d), bf16))
        ins = (x, self.vec, self.order)
        return call(
            functools.partial(self_forward_kernel, self.captions, row), 4,
            ins + w, [whole(i) for i in ins] + self.weights(lambda j: at + j),
            outs, [whole(o) for o in outs], scratch=[pltpu.VMEM((self.t, self.d), bf16)],
        )

    def self_backward(self, x, kept, dx, w, at, row, vectors=()):
        d, t = self.d, self.t
        outs = (self.xs, sds((8, d), f32), sds((4 + len(vectors), t, d), bf16))
        ins = (x, self.vec, self.order, kept, dx)
        return call(
            functools.partial(self_backward_kernel, self.captions, row), 4,
            ins + w + vectors,
            [whole(i) for i in ins] + self.weights(lambda j: at + (j + 3) % 4)
            + [whole(v) for v in vectors],
            outs, [whole(i) for i in outs],
            scratch=[pltpu.VMEM((t, d), f32)],
        )

    def cross_forward(self, x, kv, w, at, row):
        outs = (self.xs, sds((2, self.t, self.d), bf16), self.hs)
        ins = (x, self.vec, self.order, kv)
        return call(
            functools.partial(cross_forward_kernel, self.captions, row), 2,
            (self.count,) + ins + w,
            [whole(i) for i in ins] + self.weights(lambda j: at + j),
            outs, [whole(o) for o in outs], scalars=1,
        )

    def cross_backward(self, x, kept, kv, dx, w, at, row):
        d, t = self.d, self.t
        outs = (self.xs, sds((8, d), f32), sds((2, t, d), bf16), sds(kv.shape, bf16))
        ins = (x, self.vec, self.order, kept, kv, dx)
        return call(
            functools.partial(cross_backward_kernel, self.captions, row), 2,
            (self.count,) + ins + w,
            [whole(i) for i in ins] + self.weights(lambda j: at + 1 - j),
            outs, [whole(i) for i in outs], scalars=1,
        )

    def pair_forward(self, enc, w):
        d, rows = self.d, enc.shape[0] // self.captions
        half = pl.BlockSpec((d // 2, 2 * d), lambda j: (0, 0))
        out = sds((enc.shape[0], 2 * d), bf16)
        return call(
            pair_forward_kernel, self.captions, (enc,) + w,
            [pl.BlockSpec((rows, d), lambda j: (j, 0)), half, half],
            out, pl.BlockSpec((rows, 2 * d), lambda j: (j, 0)),
        )

    def pair_grads(self, enc_t, dkv):
        d = self.d
        outs = (sds((d // 2, 2 * d), bf16),) * 2
        grad = pl.BlockSpec((d // 2, d), lambda j: (0, j))
        return call(
            pair_grads_kernel, 2, (enc_t, dkv),
            [whole(enc_t), pl.BlockSpec((dkv.shape[0], d), lambda j: (0, j))],
            outs, [grad, grad],
        )

    def pair_input(self, dkv, w):
        d, rows = self.d, dkv.shape[0] // self.captions
        half = pl.BlockSpec((d // 2, 2 * d), lambda j: (0, 0))
        out = sds((dkv.shape[0], d), bf16)
        return call(
            pair_input_kernel, self.captions, (dkv, self.order) + w,
            [pl.BlockSpec((rows, 2 * d), lambda j: (j, 0)), whole(self.order), half, half],
            out, pl.BlockSpec((rows, d), lambda j: (j, 0)),
        )

    def block(self, index):
        return pl.BlockSpec((1, self.t, self.d), lambda j: (index(j), 0, 0))

    def feed_grads(self, f, p):
        d, t = self.d, self.t
        outs = (sds((d // 4, 8 * d), bf16),) * 2
        first, later = self.block(lambda j: 0), self.block(lambda j: 1 + j)
        half = pl.BlockSpec((d // 2, d), lambda j: (0, 0))
        return call(
            feed_grads_kernel, 4, (self.order,) + f + p + f + p,
            [half] + [first] * 4 + [later] * 4,
            outs, [pl.BlockSpec((d // 4, 2 * d), lambda j: (0, j))] * 2,
            scratch=[pltpu.VMEM((d // 2, 2 * t), bf16)],
        )

    def attend_grads(self, f, p, cross=()):
        d, t = self.d, self.t
        steps = 8 if cross else 4
        outs = (sds((d // 4, steps * d), bf16),) * 2
        half = pl.BlockSpec((d // 2, d), lambda j: (0, 0))
        lhs = self.block(lambda j: jnp.minimum(j // 3, 1))
        rhs = self.block(lambda j: jnp.minimum(j, 3))
        ins, specs = (self.order,) + f + p, [half, lhs, lhs, rhs, rhs]
        if cross:
            f, p, pair = cross
            at = self.block(lambda j: jnp.clip(j - 4, 0, 1))
            columns = pl.BlockSpec((d // 2, d), lambda j: (0, jnp.clip(j - 6, 0, 1)))
            ins, specs = ins + f + p + pair, specs + [at] * 4 + [columns] * 2
        return call(
            attend_grads_kernel, steps, ins, specs,
            outs, [pl.BlockSpec((d // 4, d), lambda j: (0, j))] * 2,
        )

    def feed_forward(self, x, w, row):
        d, t = self.d, self.t
        outs = (self.xs, sds((5, t, d), bf16), sds((t, 4 * d), f32))
        ins = (x, self.vec, self.order)
        return call(
            functools.partial(feed_forward_kernel, row), 4,
            ins + w + w,
            [whole(i) for i in ins] + self.weights(lambda j: j, lambda j: 4 + j),
            outs, [whole(outs[0]), whole(outs[1]), pl.BlockSpec((t, d), lambda j: (0, j))],
            scratch=[pltpu.VMEM((t, d), bf16)],
        )

    def feed_backward(self, x, u, dx, w, row):
        d, t = self.d, self.t
        outs = (self.xs, sds((8, d), f32), sds((5, t, d), bf16))
        ins = (x, self.vec, self.order, dx)
        return call(
            functools.partial(feed_backward_kernel, row), 4,
            ins + w + w + (u,),
            [whole(i) for i in ins] + self.weights(lambda j: j, lambda j: 4 + j)
            + [pl.BlockSpec((t, d), lambda j: (0, j))],
            outs, [whole(i) for i in outs],
            scratch=[pltpu.VMEM((t, d), f32)],
        )

    def last_backward(self, x, dx, w, row):
        d, t = self.d, self.t
        outs = (self.xs, sds((8, d), f32)) + (sds((5, t, d), bf16),) * 2
        ins = (x, self.vec, self.order, dx)
        return call(
            functools.partial(last_backward_kernel, row), 4,
            ins + w + w,
            [whole(i) for i in ins] + self.weights(lambda j: j, lambda j: 4 + j),
            outs, [whole(i) for i in outs],
            scratch=[pltpu.VMEM((t, d), f32), pltpu.VMEM((t, d), bf16)],
        )

    def last_output(self, x, f, w):
        return call(
            last_output_kernel, 4, (x, self.order, f) + w,
            [whole(x), whole(self.order), self.block(lambda j: 1 + j)]
            + self.weights(lambda j: 4 + j),
            self.hs, whole(self.hs), scratch=[pltpu.VMEM((self.t, self.d), f32)],
        )


def spread_matrix():
    k = lax.broadcasted_iota(jnp.int32, (512, 512), 0)
    n = lax.broadcasted_iota(jnp.int32, (512, 512), 1)
    return (k % 4) * 128 + k // 4 == n


def local(
    tokens, encoder, patch_count, out_grad,
    u_ag, u_as, u_qkv, u_out, u_mg, u_ms, u_up, u_down,
    m_ag, m_as, m_qkv, m_out, c_g, c_s, c_q, c_pair, c_out, m_mg, m_ms, m_up, m_down,
):
    place = Place()
    captions, length, d = tokens.shape
    rows = u_qkv.shape[0]
    x0 = tokens.reshape(-1, d)
    enc = encoder.reshape(-1, d)
    order = place.order(d)

    vectors = (u_ag, u_as, u_mg, u_ms, m_ag, m_as, c_g, c_s, m_mg, m_ms)
    vectors = jnp.pad(jnp.stack(vectors, axis=0), ((0, LANES - len(vectors)), (0, 0)))
    def packed(kernel, parts, *widths):
        outs = tuple(sds((rows, c), bf16) for c in widths)
        shards = call(kernel, 1, parts, [whole(p) for p in parts], outs, [whole(o) for o in outs], vmem=60)
        return [Gather(place, x) for x in shards]

    (first,) = packed(first_pack_kernel, (u_qkv, u_out, vectors), 4 * d + LANES)
    parts = (u_up, u_down, m_qkv, m_out, m_up, m_down, c_q, c_pair, c_out)
    feed, middle, last = packed(pack_kernel, parts, 8 * d, 8 * d, 8 * d)

    def go(token, groups=(), start=()):
        token, got = tie(token, *[(g.x, g.got) for g in groups])
        for g, (x, y) in zip(groups, got):
            g.x, g.got = x, y
            g.join()
        every = tuple(groups) + tuple(start)
        token, xs = tie(token, *[g.x for g in every])
        for g, x in zip(every, xs):
            g.x = x
            g.swap()
        return token

    def end(token, group):
        token, (group.x, group.got) = tie(token, group.x, group.got)
        return token, (group.x, group.got)

    steps = place.outer_bits
    x0 = go(x0, start=[first])
    enc_rel = nt(enc, order).astype(bf16)
    enc_t = nt(order, enc).astype(bf16)
    for k in range(steps - 1):
        x0 = go(x0, [first], [feed] if k == 0 else [])
    x0 = go(x0, [first])
    for k in range(steps - 1):
        x0 = go(x0, [feed])
    x0 = go(x0, [first])
    x0 = go(x0, [feed], [middle])
    x0 = go(x0, [first, middle])
    x0 = go(x0, [feed])
    for k in range(steps - 2):
        x0 = go(x0, [middle])
    x0, (order, enc_rel, enc_t) = tie(x0, order, enc_rel, enc_t)
    x0, w_first = end(x0, first)
    vec = tn(jnp.concatenate([x[:, 4 * d :] for x in w_first], axis=0), order)[:16]
    net = Layers(captions, captions * length, d, vec, order, patch_count)
    x0 = go(x0, [middle], [last])
    for k in range(steps - 1):
        x0 = go(x0, [last])
    x0 = go(x0, [feed])
    x0a, f_us, k_us = net.self_forward(x0, w_first, 0, 0)
    x0a = go(x0a, [middle])
    x0a = go(x0a, [last])
    x0a, w_feed = end(x0a, feed)
    x1, f_uf, k_uf = net.feed_forward(x0a, w_feed, 2)
    x1 = go(x1, [last])
    x1 = go(x1, [middle])
    x1, w_middle = end(x1, middle)
    kv = net.pair_forward(enc_rel, w_middle)
    x1, (kv,) = tie(x1, kv)
    x1a, f_ms, k_ms = net.self_forward(x1, w_middle, 4, 4)
    x1a = go(x1a, [last])
    x1b, f_mc, k_mc = net.cross_forward(x1a, kv, w_middle, 2, 6)
    x1b, w_last = end(x1b, last)

    def core(x):
        return place.swap(x, BIT_CORE)

    def go_on(x, sums=(), start=()):
        x = hold(x, *sums)
        for g in sums:
            g.sums()
        x = need(x, *(tuple(sums) + tuple(g for g in start if g not in sums)))
        for g in start:
            g.swap()
        return x

    def rest(x, *groups):
        for _ in range(place.outer_bits - 1):
            for g in groups:
                x = go_on(x, [g], [g])
        return x

    def pairs(x):
        return x, core(x)

    f_us, f_uf, f_ms = pairs(f_us), pairs(f_uf), pairs(f_ms)
    x1b, (f_us, f_uf, f_ms) = tie(x1b, f_us, f_uf, f_ms)
    f_mc = pairs(f_mc)
    dx, v_mf, p, f = net.last_backward(x1b, out_grad.reshape(-1, d), w_last, 8)
    p, f = pairs(p), pairs(f)
    x2 = net.last_output(x1b, f[0], w_last)
    p, (x2,) = tie(p, x2)
    s_mf = Sum(place, net.feed_grads(f, p))
    dx, (f_mc,) = tie(dx, f_mc)
    dx = go_on(dx, start=[s_mf])
    dx, v_mc, p_c, dkv = net.cross_backward(x1a, k_mc, kv, dx, w_middle, 2, 6)
    p_c = pairs(p_c)
    pair, send = net.pair_grads(enc_t, dkv)
    dx, (send,) = tie(dx, send)
    pair = pair, core(send)
    dx, v_ms, p = net.self_backward(x1, k_ms, dx, w_middle, 4, 4)
    p = pairs(p)
    dx = go_on(dx, [s_mf], [s_mf])
    dx, (p, p_c, pair) = tie(dx, p, p_c, pair)
    s_ma = Sum(place, net.attend_grads(f_ms, p, (f_mc, p_c, pair)))
    dx = go_on(dx, start=[s_ma])
    dx, v_uf, p = net.feed_backward(x0a, k_uf, dx, w_feed, 2)
    p = pairs(p)
    dx, (p,) = tie(dx, p)
    s_uf = Sum(place, net.feed_grads(f_uf, p))
    dx = need(dx, s_uf)
    v = [g[:2] for g in (v_uf, v_ms, v_mc, v_mf)]
    v = jnp.pad(jnp.concatenate(v, axis=0), ((2, 6), (0, 0)))
    dx, _v, p = net.self_backward(x0, k_us, dx, w_first, 0, 0, (v,))
    p = pairs(p)
    dx = go_on(dx, [s_mf], [s_uf, s_mf])
    dx = go_on(dx, [s_ma], [s_ma])
    dx, (p,) = tie(dx, p)
    send, keep = net.attend_grads(f_us, p)
    dx, (send, keep) = tie(dx, send, keep)
    v = nt(order[: d // 2], plus(p[0][4], p[1][4])[:LANES]).astype(bf16)
    dx, (dkv,) = tie(dx, dkv)
    denc = net.pair_input(dkv, w_middle)
    dx, (denc,) = tie(dx, denc)
    dx = go_on(dx, [s_ma], [s_ma])
    send = jnp.concatenate((send, v[d // 4 :]), axis=1)
    keep = jnp.concatenate((keep, v[: d // 4]), axis=1)
    s_us = Sum(place, (send, keep))
    dx = go_on(dx, start=[s_us])
    dx = rest(dx, s_mf)
    dx = go_on(dx, [s_uf], [s_uf])
    dx, (r_mf,) = tie(dx, feed_rows(s_mf.kept, s_mf.got))
    dx = rest(dx, s_ma)
    dx = go_on(dx, [s_uf, s_us], [s_uf, s_us])
    dx, (r_ma,) = tie(dx, s_ma.total())
    dx = rest(dx, s_uf)
    dx = go_on(dx, [s_us], [s_us])
    dx = rest(dx, s_us)
    dx = hold(dx, s_uf)
    dx, (r_uf,) = tie(dx, feed_rows(s_uf.kept, s_uf.got))
    r_us = s_us.total()

    def columns(r, *blocks):
        parts = [r[:, b * d : (b + 1) * d] for b in blocks]
        return jnp.concatenate(parts, axis=1) if len(parts) > 1 else parts[0]

    r_uup, r_udown = r_uf
    r_mup, r_mdown = r_mf
    vs = r_us[:, 4 * d :]
    v = [vs[:, i] for i in range(10)]
    return (
        x2.reshape(tokens.shape),
        dx.astype(bf16).reshape(tokens.shape),
        denc.reshape(encoder.shape),
        v[0], v[1], r_us[:, : 3 * d], r_us[:, 3 * d : 4 * d], v[2], v[3], r_uup, r_udown,
        v[4], v[5], r_ma[:, : 3 * d], columns(r_ma, 3), v[6], v[7],
        columns(r_ma, 4), r_ma[:, 6 * d :], columns(r_ma, 5),
        v[8], v[9], r_mup, r_mdown,
    )


def solution(mesh):
    rows1 = P(AXES)
    rows2 = P(AXES, None)
    rows3 = P(AXES, None, None)
    block = (rows1, rows1, rows2, rows2)
    weights = block * 2 + block + (rows1, rows1, rows2, rows2, rows2) + block
    return jax.shard_map(
        local,
        mesh=mesh,
        in_specs=(rows3, rows3, rows1, rows3) + weights,
        out_specs=(rows3, rows3, rows3) + weights,
        check_vma=False,
    )
```

```python
import functools

import jax
import jax.numpy as jnp
from jax import lax
from jax.experimental import pallas as pl
from jax.experimental.pallas import tpu as pltpu
from jax.sharding import PartitionSpec as P

DH = 64
AXES = ("dp", "hd")
EPS = 1e-05
MASKED = -1e30
LANES = 128
bf16 = jnp.bfloat16
f32 = jnp.float32
sds = jax.ShapeDtypeStruct


BIT_PAIR, BIT_CORE, BIT_NEAR = 1, 2, 4


class Place:
    def __init__(self):
        self.count = lax.axis_size("dp") * lax.axis_size("hd")
        self.outer_size = self.count // 8
        index = lax.axis_index("dp") * lax.axis_size("hd") + lax.axis_index("hd")
        self.pair = index % 2
        self.core = (index // 2) % 2
        self.near = (index // 4) % 2
        self.outer = index // 8
        self.outer_bits = self.outer_size.bit_length() - 1

    def swap(self, x, bit):
        return lax.ppermute(x, AXES, [(i, i ^ bit) for i in range(self.count)])

    def swap_by_core(self, x, bits):
        pairs = [(i, i ^ bits[(i // BIT_CORE) % 2]) for i in range(self.count)]
        return lax.ppermute(x, AXES, pairs)

    def order(self, d):
        n, rows = self.outer_size, d // self.count
        k = lax.broadcasted_iota(jnp.int32, (d, 1), 0)
        row, place = k % rows, (k // rows) % n
        outer = jnp.zeros_like(k)
        for b in range(self.outer_bits):
            outer = outer + ((place >> (self.outer_bits - 1 - b)) & 1) * (1 << b)
        outer = outer ^ self.outer
        rest = k // (rows * n)
        low, high = rest % 2, (rest // 2) % 2
        near = jnp.where((rest // 4) ^ self.core == 0, high, low)
        pair = high + low - near
        feature = outer * 2 + (near ^ self.near)
        feature = (feature * 2 + ((rest // 4) ^ self.core)) * 2 + (pair ^ self.pair)
        feature = feature * rows + row
        return (feature == lax.broadcasted_iota(jnp.int32, (d, d), 1)).astype(bf16)


def plus(a, b):
    return (a.astype(f32) + b.astype(f32)).astype(bf16)


class Sum:
    def __init__(self, place, grads):
        self.place, self.stage = place, 0
        self.send, self.kept = grads

    def swap(self):
        if self.stage < 2:
            bits = ((BIT_NEAR, BIT_PAIR), (BIT_PAIR, BIT_NEAR))[self.stage]
            self.got = self.place.swap_by_core(self.send, bits)
        else:
            self.got = self.place.swap(self.send, 8 << (self.stage - 2))

    def sums(self):
        if self.stage < 2:
            self.send, self.kept = half_sums(self.kept, self.got)
        else:
            half = self.kept.shape[0] // 2
            self.send = plus(self.kept[half:], self.got[half:])
            self.kept = plus(self.kept[:half], self.got[:half])
        self.stage += 1

    def total(self):
        return self.kept.astype(f32) + self.got.astype(f32)


class Gather:
    def __init__(self, place, shard):
        self.place, self.x, self.stage = place, shard, 0

    def swap(self):
        outer = self.place.outer_bits
        at = self.stage - outer
        if at < 0:
            self.got = self.place.swap(self.x, 8 << (outer - 1 - self.stage))
        elif at < 2:
            bits = ((BIT_PAIR, BIT_NEAR), (BIT_NEAR, BIT_PAIR))[at]
            self.got = self.place.swap_by_core(self.x, bits)
        else:
            self.got = self.place.swap(self.x, BIT_CORE)

    def join(self):
        self.x = jnp.concatenate((self.x, self.got), axis=0)
        self.stage += 1


def tie(x, *others):
    out = lax.optimization_barrier((x,) + others)
    return out[0], out[1:]


def hold(x, *groups):
    x, terms = tie(x, *[(g.kept, g.got) for g in groups])
    for g, t in zip(groups, terms):
        g.kept, g.got = t
    return x


def need(x, *groups):
    x, send = tie(x, *[g.send for g in groups])
    for g, k in zip(groups, send):
        g.send = k
    return x


def nn(a, b):
    return jnp.dot(a, b, preferred_element_type=f32)


def nt(a, b):
    return lax.dot_general(a, b, (((1,), (1,)), ((), ())), preferred_element_type=f32)


def tn(a, b):
    return lax.dot_general(a, b, (((0,), (0,)), ((), ())), preferred_element_type=f32)


def unit_norm(x):
    centred = x - jnp.mean(x, axis=-1, keepdims=True)
    inv = lax.rsqrt(jnp.mean(centred * centred, axis=-1, keepdims=True) + EPS)
    return centred * inv, inv


def norm_backward(grad, x, gain):
    unit, inv = unit_norm(x)
    du = grad * gain
    dx = inv * (
        du
        - jnp.mean(du, axis=-1, keepdims=True)
        - unit * jnp.mean(du * unit, axis=-1, keepdims=True)
    )
    return dx, jnp.sum(grad * unit, axis=0, keepdims=True), jnp.sum(grad, axis=0, keepdims=True)


GELU_A = 0.7978845608028654
GELU_B = 0.044715


def two_heads(x):
    first = lax.broadcasted_iota(jnp.int32, x.shape, 1) < DH
    zero = jnp.zeros_like(x)
    return jnp.concatenate((jnp.where(first, x, zero), jnp.where(first, zero, x)), axis=0)


def side_by_side(x):
    n = x.shape[0] // 2
    first = lax.broadcasted_iota(jnp.int32, (n, LANES), 1) < DH
    return jnp.where(first, x[:n], x[n:])


def probabilities(qs, k2, allowed):
    s = jnp.where(allowed, nt(qs, k2) * DH ** (-0.5), MASKED)
    e = jnp.exp(s - jnp.max(s, axis=-1, keepdims=True))
    return e / jnp.sum(e, axis=-1, keepdims=True)


def causal_mask(length):
    row = lax.broadcasted_iota(jnp.int32, (2 * length, length), 0)
    col = lax.broadcasted_iota(jnp.int32, (2 * length, length), 1)
    return jnp.where(row >= length, row - length, row) >= col


def attend_back(q2, k2, v2, do2, allowed):
    scale = DH ** (-0.5)
    qs, dos = two_heads(q2), two_heads(do2)
    p = probabilities(qs, k2, allowed)
    dp = nt(dos, v2)
    ds = (p * (dp - jnp.sum(p * dp, axis=-1, keepdims=True))).astype(bf16)
    dq = side_by_side(nn(ds, k2)) * scale
    dk = tn(ds, qs) * scale
    dv = tn(p.astype(bf16), dos)
    return dq.astype(bf16), dk.astype(bf16), dv.astype(bf16)


def relative(x, order_ref):
    return nt(x, order_ref[...]).astype(bf16)


def times(x, top_ref, low_ref):
    half = top_ref.shape[0]
    return nn(x[:, :half], top_ref[...]) + nn(x[:, half:], low_ref[...])


def times_back(g, top_ref, low_ref):
    return jnp.concatenate((nt(g, top_ref[...]), nt(g, low_ref[...])), axis=1)


def natural(x, order_ref):
    high = x.astype(bf16)
    low = (x - high.astype(f32)).astype(bf16)
    return nn(high, order_ref[...]) + nn(low, order_ref[...])


def self_forward_kernel(
    captions, row, x_ref, vec_ref, order_ref, top_ref, low_ref, y_ref, f_ref, qkv_ref, rel_ref
):
    j = pl.program_id(0)

    @pl.when(j == 0)
    def _():
        unit, _inv = unit_norm(x_ref[...].astype(f32))
        f_ref[0] = (unit * vec_ref[row : row + 1] + vec_ref[row + 1 : row + 2]).astype(bf16)
        rel_ref[...] = relative(f_ref[0], order_ref)

    @pl.when(j < 3)
    def _():
        qkv_ref[j] = times(rel_ref[...], top_ref, low_ref).astype(bf16)

    @pl.when(j == 3)
    def _():
        length = x_ref.shape[0] // captions
        allowed = causal_mask(length)
        for c in range(captions):
            at = slice(c * length, (c + 1) * length)
            for h in range(0, x_ref.shape[1], LANES):
                cols = slice(h, h + LANES)
                p = probabilities(two_heads(qkv_ref[0, at, cols]), qkv_ref[1, at, cols], allowed)
                o = side_by_side(nn(p.astype(bf16), qkv_ref[2, at, cols]))
                f_ref[1, at, cols] = o.astype(bf16)
        y_ref[...] = x_ref[...].astype(f32) + times(relative(f_ref[1], order_ref), top_ref, low_ref)


def self_backward_kernel(
    captions, row, x_ref, vec_ref, order_ref, qkv_ref, dx_ref, top_ref, low_ref, *refs
):
    out_ref, vg_ref, p_ref, acc_ref = refs[-4:]
    j = pl.program_id(0)

    @pl.when(j == 0)
    def _():
        dy = dx_ref[...].astype(bf16)
        p_ref[3] = dy
        do = times_back(dy, top_ref, low_ref).astype(bf16)
        do = nn(do, order_ref[...]).astype(bf16)
        length = x_ref.shape[0] // captions
        allowed = causal_mask(length)
        for c in range(captions):
            at = slice(c * length, (c + 1) * length)
            for h in range(0, x_ref.shape[1], LANES):
                cols = slice(h, h + LANES)
                dq, dk, dv = attend_back(
                    qkv_ref[0, at, cols], qkv_ref[1, at, cols], qkv_ref[2, at, cols],
                    do[at, cols], allowed,
                )
                p_ref[0, at, cols] = dq
                p_ref[1, at, cols] = dk
                p_ref[2, at, cols] = dv
        acc_ref[...] = jnp.zeros_like(acc_ref)

    @pl.when(j > 0)
    def _():
        acc_ref[...] += times_back(p_ref[j - 1], top_ref, low_ref)

    @pl.when(j == 3)
    def _():
        da = natural(acc_ref[...], order_ref)
        dn, gg, gs = norm_backward(da, x_ref[...].astype(f32), vec_ref[row : row + 1])
        out_ref[...] = dx_ref[...] + dn
        vg_ref[0:1] = gg
        vg_ref[1:2] = gs
        if len(refs) > 4:
            at = lax.broadcasted_iota(jnp.int32, refs[0].shape, 0)
            rows = jnp.where(at == 0, gg, jnp.where(at == 1, gs, refs[0][...]))
            p_ref[4] = jnp.zeros_like(p_ref[4])
            p_ref[4, 0 : refs[0].shape[0]] = rows.astype(bf16)


def cross_forward_kernel(
    captions, row, count_ref, x_ref, vec_ref, order_ref, kv_ref, top_ref, low_ref, y_ref, f_ref, q_ref
):
    j = pl.program_id(0)
    d = x_ref.shape[1]

    @pl.when(j == 0)
    def _():
        unit, _inv = unit_norm(x_ref[...])
        c = (unit * vec_ref[row : row + 1] + vec_ref[row + 1 : row + 2]).astype(bf16)
        f_ref[0] = c
        q_ref[...] = times(relative(c, order_ref), top_ref, low_ref).astype(bf16)

    @pl.when(j == 1)
    def _():
        length = x_ref.shape[0] // captions
        patches = kv_ref.shape[0] // captions
        slot = lax.broadcasted_iota(jnp.int32, (2 * length, patches), 1)
        for c in range(captions):
            at = slice(c * length, (c + 1) * length)
            keys = slice(c * patches, (c + 1) * patches)
            allowed = slot < count_ref[c]
            for h in range(0, d, LANES):
                cols = slice(h, h + LANES)
                vcols = slice(d + h, d + h + LANES)
                p = probabilities(two_heads(q_ref[at, cols]), kv_ref[keys, cols], allowed)
                o = side_by_side(nn(p.astype(bf16), kv_ref[keys, vcols]))
                f_ref[1, at, cols] = o.astype(bf16)
        y_ref[...] = x_ref[...] + times(relative(f_ref[1], order_ref), top_ref, low_ref)


def cross_backward_kernel(
    captions, row, count_ref, x_ref, vec_ref, order_ref, q_ref, kv_ref, dx_ref, top_ref, low_ref,
    out_ref, vg_ref, p_ref, dkv_ref,
):
    j = pl.program_id(0)
    d = x_ref.shape[1]

    @pl.when(j == 0)
    def _():
        dy = dx_ref[...].astype(bf16)
        p_ref[1] = dy
        do = times_back(dy, top_ref, low_ref).astype(bf16)
        do = nn(do, order_ref[...]).astype(bf16)
        length = x_ref.shape[0] // captions
        patches = kv_ref.shape[0] // captions
        slot = lax.broadcasted_iota(jnp.int32, (2 * length, patches), 1)
        for c in range(captions):
            at = slice(c * length, (c + 1) * length)
            keys = slice(c * patches, (c + 1) * patches)
            allowed = slot < count_ref[c]
            for h in range(0, d, LANES):
                cols = slice(h, h + LANES)
                vcols = slice(d + h, d + h + LANES)
                dq, dk, dv = attend_back(
                    q_ref[at, cols], kv_ref[keys, cols], kv_ref[keys, vcols], do[at, cols], allowed
                )
                p_ref[0, at, cols] = dq
                dkv_ref[keys, cols] = dk
                dkv_ref[keys, vcols] = dv

    @pl.when(j == 1)
    def _():
        dc = natural(times_back(p_ref[0], top_ref, low_ref), order_ref)
        dn, gg, gs = norm_backward(dc, x_ref[...], vec_ref[row : row + 1])
        out_ref[...] = dx_ref[...] + dn
        vg_ref[0:1] = gg
        vg_ref[1:2] = gs


def feed_forward_kernel(
    row, x_ref, vec_ref, order_ref, up_ref, up2_ref, down_ref, down2_ref, y_ref, f_ref, u_ref, rel_ref
):
    j = pl.program_id(0)

    @pl.when(j == 0)
    def _():
        unit, _inv = unit_norm(x_ref[...])
        f_ref[0] = (unit * vec_ref[row : row + 1] + vec_ref[row + 1 : row + 2]).astype(bf16)
        rel_ref[...] = relative(f_ref[0], order_ref)
        y_ref[...] = x_ref[...]

    u = times(rel_ref[...], up_ref, up2_ref)
    u_ref[...] = u
    g = (0.5 * u * (1.0 + jnp.tanh(GELU_A * (u + GELU_B * u * u * u)))).astype(bf16)
    f_ref[1 + j] = g
    y_ref[...] += times(relative(g, order_ref), down_ref, down2_ref)


def gelu_terms(u):
    t = jnp.tanh(GELU_A * (u + GELU_B * u * u * u))
    slope = 0.5 * (1.0 + t) + 0.5 * u * (1.0 - t * t) * GELU_A * (1.0 + 3.0 * GELU_B * u * u)
    return 0.5 * u * (1.0 + t), slope


def feed_backward_step(j, order_ref, slope, refs, p_ref, acc_ref):
    up_ref, up2_ref, down_ref, down2_ref = refs
    dg = times_back(p_ref[0], down_ref, down2_ref).astype(bf16)
    du = (slope * nn(dg, order_ref[...])).astype(bf16)
    p_ref[1 + j] = du
    acc_ref[...] += times_back(du, up_ref, up2_ref)


def feed_backward_end(row, order_ref, x_ref, vec_ref, dx_ref, acc_ref, out_ref, vg_ref):
    db = natural(acc_ref[...], order_ref)
    dn, gg, gs = norm_backward(db, x_ref[...], vec_ref[row : row + 1])
    out_ref[...] = dx_ref[...].astype(f32) + dn
    vg_ref[0:1] = gg
    vg_ref[1:2] = gs


def feed_backward_kernel(
    row, x_ref, vec_ref, order_ref, dx_ref, up_ref, up2_ref, down_ref, down2_ref, u_ref,
    out_ref, vg_ref, p_ref, acc_ref,
):
    j = pl.program_id(0)

    @pl.when(j == 0)
    def _():
        p_ref[0] = dx_ref[...].astype(bf16)
        acc_ref[...] = jnp.zeros_like(acc_ref)

    refs = up_ref, up2_ref, down_ref, down2_ref
    feed_backward_step(j, order_ref, gelu_terms(u_ref[...])[1], refs, p_ref, acc_ref)

    @pl.when(j == 3)
    def _():
        feed_backward_end(row, order_ref, x_ref, vec_ref, dx_ref, acc_ref, out_ref, vg_ref)


def last_backward_kernel(
    row, x_ref, vec_ref, order_ref, dx_ref, up_ref, up2_ref, down_ref, down2_ref,
    out_ref, vg_ref, p_ref, f_ref, acc_ref, rel_ref,
):
    j = pl.program_id(0)

    @pl.when(j == 0)
    def _():
        unit, _inv = unit_norm(x_ref[...])
        f_ref[0] = (unit * vec_ref[row : row + 1] + vec_ref[row + 1 : row + 2]).astype(bf16)
        rel_ref[...] = relative(f_ref[0], order_ref)
        p_ref[0] = dx_ref[...]
        acc_ref[...] = jnp.zeros_like(acc_ref)

    g, slope = gelu_terms(times(rel_ref[...], up_ref, up2_ref))
    f_ref[1 + j] = g.astype(bf16)
    refs = up_ref, up2_ref, down_ref, down2_ref
    feed_backward_step(j, order_ref, slope, refs, p_ref, acc_ref)

    @pl.when(j == 3)
    def _():
        feed_backward_end(row, order_ref, x_ref, vec_ref, dx_ref, acc_ref, out_ref, vg_ref)


def last_output_kernel(x_ref, order_ref, g_ref, down_ref, down2_ref, y_ref, acc_ref):
    j = pl.program_id(0)

    @pl.when(j == 0)
    def _():
        acc_ref[...] = x_ref[...]

    acc_ref[...] += times(relative(g_ref[0], order_ref), down_ref, down2_ref)

    @pl.when(j == 3)
    def _():
        y_ref[...] = acc_ref[...].astype(bf16)


def both(own_ref, got_ref):
    return jnp.concatenate((own_ref[0], got_ref[0]), axis=0)


def emit(g, send_ref, keep_ref):
    half = keep_ref.shape[0]
    keep_ref[...] = g[:half].astype(bf16)
    send_ref[...] = g[half:].astype(bf16)


def feed_grads_kernel(
    order_ref, b_ref, b2_ref, z_ref, z2_ref, g_ref, g2_ref, u_ref, u2_ref, send_ref, keep_ref, bt_ref
):
    d = order_ref.shape[1]

    @pl.when(pl.program_id(0) == 0)
    def _():
        bt_ref[...] = nt(order_ref[...], both(b_ref, b2_ref)).astype(bf16)

    up, down = (slice(None), slice(0, d)), (slice(None), slice(d, 2 * d))
    emit(nn(bt_ref[...], both(u_ref, u2_ref)), send_ref.at[up], keep_ref.at[up])
    gt = nt(order_ref[...], both(g_ref, g2_ref)).astype(bf16)
    emit(nn(gt, both(z_ref, z2_ref)), send_ref.at[down], keep_ref.at[down])


def attend_grads_kernel(order_ref, s_ref, s2_ref, sd_ref, sd2_ref, *refs):
    send_ref, keep_ref = refs[-2:]
    j = pl.program_id(0)

    def product(a_ref, a2_ref, d_ref, d2_ref):
        at = nt(order_ref[...], both(a_ref, a2_ref)).astype(bf16)
        emit(nn(at, both(d_ref, d2_ref)), send_ref, keep_ref)

    @pl.when(j < 4)
    def _():
        product(s_ref, s2_ref, sd_ref, sd2_ref)

    if len(refs) > 2:
        c_ref, c2_ref, cd_ref, cd2_ref, pair_ref, pair2_ref = refs[:6]

        @pl.when((j == 4) | (j == 5))
        def _():
            product(c_ref, c2_ref, cd_ref, cd2_ref)

        @pl.when(j > 5)
        def _():
            emit(pair_ref[...].astype(f32) + pair2_ref[...].astype(f32), send_ref, keep_ref)


def half_sums_kernel(kept_ref, got_ref, send_ref, keep_ref):
    emit(kept_ref[...].astype(f32) + got_ref[...].astype(f32), send_ref, keep_ref)


def half_sums(kept, got):
    rows, wide = kept.shape
    steps = 2 if wide % (2 * LANES) == 0 else 1
    full = pl.BlockSpec((rows, wide // steps), lambda j: (0, j))
    half = pl.BlockSpec((rows // 2, wide // steps), lambda j: (0, j))
    outs = (sds((rows // 2, wide), bf16),) * 2
    return call(half_sums_kernel, steps, (kept, got), [full] * 2, outs, [half] * 2, vmem=24)


def feed_rows_kernel(kept_ref, got_ref, up_ref, down_ref):
    rows, wide = up_ref.shape
    d = wide // 4
    spread = spread_matrix().astype(bf16)
    i = lax.broadcasted_iota(jnp.int32, (4 * rows, rows), 0)
    k = lax.broadcasted_iota(jnp.int32, (4 * rows, rows), 1)

    def part(at, size):
        x = kept_ref[:, at : at + size].astype(f32) + got_ref[:, at : at + size].astype(f32)
        high = x.astype(bf16)
        return high, (x - high.astype(f32)).astype(bf16)

    for b in range(wide // 512):
        parts = [part(2 * j * d + b * LANES, LANES) for j in range(4)]
        high, low = (jnp.concatenate(p, axis=1) for p in zip(*parts))
        up_ref[:, b * 512 : (b + 1) * 512] = nt(high, spread) + nt(low, spread)
    down = jnp.zeros(down_ref.shape, f32)
    for j in range(4):
        place = (i == 4 * k + j).astype(bf16)
        high, low = part((2 * j + 1) * d, d)
        down = down + nn(place, high) + nn(place, low)
    down_ref[...] = down


def feed_rows(kept, got):
    rows, wide = kept.shape
    outs = sds((rows, wide // 2), f32), sds((4 * rows, wide // 8), f32)
    ins = kept, got
    return call(feed_rows_kernel, 1, ins, [whole(x) for x in ins], outs, [whole(x) for x in outs])


def pair_forward_kernel(enc_ref, top_ref, low_ref, kv_ref):
    kv_ref[...] = times(enc_ref[...], top_ref, low_ref).astype(bf16)


def pair_input_kernel(dkv_ref, order_ref, top_ref, low_ref, out_ref):
    g = times_back(dkv_ref[...], top_ref, low_ref).astype(bf16)
    out_ref[...] = nn(g, order_ref[...]).astype(bf16)


def pair_grads_kernel(enc_ref, dkv_ref, keep_ref, send_ref):
    emit(nn(enc_ref[...], dkv_ref[...]), send_ref, keep_ref)


def first_pack_kernel(u_qkv, u_out, vec, out):
    rows, d = u_out.shape
    out[:, : 3 * d] = u_qkv[...]
    out[:, 3 * d : 4 * d] = u_out[...]
    eye = lax.broadcasted_iota(jnp.int32, (rows, rows), 0) == lax.broadcasted_iota(jnp.int32, (rows, rows), 1)
    out[:, 4 * d :] = nt(eye.astype(bf16), vec[...]).astype(bf16)


def pack_kernel(
    u_up, u_down, m_qkv, m_out, m_up, m_down, c_q, c_pair, c_out, feed_out, middle_out, last_out
):
    rows, d = m_out.shape
    spread = spread_matrix().astype(bf16)
    i = lax.broadcasted_iota(jnp.int32, (rows, 4 * rows), 0)
    k = lax.broadcasted_iota(jnp.int32, (rows, 4 * rows), 1)

    def feed(out, up, down):
        for b in range(4 * d // 512):
            y = nn(up[:, b * 512 : (b + 1) * 512], spread).astype(bf16)
            for j in range(4):
                to = j * d + b * LANES
                out[:, to : to + LANES] = y[:, j * LANES : (j + 1) * LANES]
        for j in range(4):
            y = nn((k == 4 * i + j).astype(bf16), down[...])
            out[:, (4 + j) * d : (5 + j) * d] = y.astype(bf16)

    feed(feed_out, u_up, u_down)
    middle_out[:, : 2 * d] = c_pair[...]
    middle_out[:, 2 * d : 3 * d] = c_q[...]
    middle_out[:, 3 * d : 4 * d] = c_out[...]
    middle_out[:, 4 * d : 7 * d] = m_qkv[...]
    middle_out[:, 7 * d : 8 * d] = m_out[...]
    feed(last_out, m_up, m_down)


def whole(x):
    return pl.BlockSpec(x.shape, lambda *_: (0,) * len(x.shape))


def call(kernel, steps, ins, in_specs, outs, out_specs, scratch=(), scalars=0, vmem=16):
    return pl.pallas_call(
        kernel,
        out_shape=outs,
        grid_spec=pltpu.PrefetchScalarGridSpec(
            num_scalar_prefetch=scalars,
            grid=(steps,),
            in_specs=in_specs,
            out_specs=out_specs,
            scratch_shapes=scratch,
        ),
        compiler_params=pltpu.CompilerParams(
            dimension_semantics=("arbitrary",), vmem_limit_bytes=vmem << 20
        ),
        cost_estimate=pl.CostEstimate(flops=1000, bytes_accessed=1000, transcendentals=0),
    )(*ins)


class Layers:
    def __init__(self, captions, tokens, d, vec, order, count):
        self.captions, self.t, self.d = captions, tokens, d
        self.vec, self.order, self.count = vec, order, count
        self.xs = sds((tokens, d), f32)
        self.hs = sds((tokens, d), bf16)

    def weights(self, *columns):
        d = self.d
        specs = [pl.BlockSpec((d // 2, d), lambda j, *_, c=c: (0, c(j))) for c in columns]
        return [s for s in specs for _ in range(2)]

    def self_forward(self, x, w, at, row):
        outs = (self.xs, sds((2, self.t, self.d), bf16), sds((3, self.t, self.d), bf16))
        ins = (x, self.vec, self.order)
        return call(
            functools.partial(self_forward_kernel, self.captions, row), 4,
            ins + w, [whole(i) for i in ins] + self.weights(lambda j: at + j),
            outs, [whole(o) for o in outs], scratch=[pltpu.VMEM((self.t, self.d), bf16)],
        )

    def self_backward(self, x, kept, dx, w, at, row, vectors=()):
        d, t = self.d, self.t
        outs = (self.xs, sds((8, d), f32), sds((4 + len(vectors), t, d), bf16))
        ins = (x, self.vec, self.order, kept, dx)
        return call(
            functools.partial(self_backward_kernel, self.captions, row), 4,
            ins + w + vectors,
            [whole(i) for i in ins] + self.weights(lambda j: at + (j + 3) % 4)
            + [whole(v) for v in vectors],
            outs, [whole(i) for i in outs],
            scratch=[pltpu.VMEM((t, d), f32)],
        )

    def cross_forward(self, x, kv, w, at, row):
        outs = (self.xs, sds((2, self.t, self.d), bf16), self.hs)
        ins = (x, self.vec, self.order, kv)
        return call(
            functools.partial(cross_forward_kernel, self.captions, row), 2,
            (self.count,) + ins + w,
            [whole(i) for i in ins] + self.weights(lambda j: at + j),
            outs, [whole(o) for o in outs], scalars=1, vmem=24,
        )

    def cross_backward(self, x, kept, kv, dx, w, at, row):
        d, t = self.d, self.t
        outs = (self.xs, sds((8, d), f32), sds((2, t, d), bf16), sds(kv.shape, bf16))
        ins = (x, self.vec, self.order, kept, kv, dx)
        return call(
            functools.partial(cross_backward_kernel, self.captions, row), 2,
            (self.count,) + ins + w,
            [whole(i) for i in ins] + self.weights(lambda j: at + 1 - j),
            outs, [whole(i) for i in outs], scalars=1, vmem=24,
        )

    def pair_forward(self, enc, w):
        d, rows = self.d, enc.shape[0] // self.captions
        half = pl.BlockSpec((d // 2, 2 * d), lambda j: (0, 0))
        out = sds((enc.shape[0], 2 * d), bf16)
        return call(
            pair_forward_kernel, self.captions, (enc,) + w,
            [pl.BlockSpec((rows, d), lambda j: (j, 0)), half, half],
            out, pl.BlockSpec((rows, 2 * d), lambda j: (j, 0)),
        )

    def pair_grads(self, enc_t, dkv):
        d = self.d
        outs = (sds((d // 2, 2 * d), bf16),) * 2
        grad = pl.BlockSpec((d // 2, d), lambda j: (0, j))
        return call(
            pair_grads_kernel, 2, (enc_t, dkv),
            [whole(enc_t), pl.BlockSpec((dkv.shape[0], d), lambda j: (0, j))],
            outs, [grad, grad],
        )

    def pair_input(self, dkv, w):
        d, rows = self.d, dkv.shape[0] // self.captions
        half = pl.BlockSpec((d // 2, 2 * d), lambda j: (0, 0))
        out = sds((dkv.shape[0], d), bf16)
        return call(
            pair_input_kernel, self.captions, (dkv, self.order) + w,
            [pl.BlockSpec((rows, 2 * d), lambda j: (j, 0)), whole(self.order), half, half],
            out, pl.BlockSpec((rows, d), lambda j: (j, 0)),
        )

    def block(self, index):
        return pl.BlockSpec((1, self.t, self.d), lambda j: (index(j), 0, 0))

    def feed_grads(self, f, p):
        d, t = self.d, self.t
        outs = (sds((d // 4, 8 * d), bf16),) * 2
        first, later = self.block(lambda j: 0), self.block(lambda j: 1 + j)
        half = pl.BlockSpec((d // 2, d), lambda j: (0, 0))
        return call(
            feed_grads_kernel, 4, (self.order,) + f + p + f + p,
            [half] + [first] * 4 + [later] * 4,
            outs, [pl.BlockSpec((d // 4, 2 * d), lambda j: (0, j))] * 2,
            scratch=[pltpu.VMEM((d // 2, 2 * t), bf16)],
        )

    def attend_grads(self, f, p, cross=()):
        d, t = self.d, self.t
        steps = 8 if cross else 4
        outs = (sds((d // 4, steps * d), bf16),) * 2
        half = pl.BlockSpec((d // 2, d), lambda j: (0, 0))
        lhs = self.block(lambda j: jnp.minimum(j // 3, 1))
        rhs = self.block(lambda j: jnp.minimum(j, 3))
        ins, specs = (self.order,) + f + p, [half, lhs, lhs, rhs, rhs]
        if cross:
            f, p, pair = cross
            at = self.block(lambda j: jnp.clip(j - 4, 0, 1))
            columns = pl.BlockSpec((d // 2, d), lambda j: (0, jnp.clip(j - 6, 0, 1)))
            ins, specs = ins + f + p + pair, specs + [at] * 4 + [columns] * 2
        return call(
            attend_grads_kernel, steps, ins, specs,
            outs, [pl.BlockSpec((d // 4, d), lambda j: (0, j))] * 2,
        )

    def feed_forward(self, x, w, row):
        d, t = self.d, self.t
        outs = (self.xs, sds((5, t, d), bf16), sds((t, 4 * d), f32))
        ins = (x, self.vec, self.order)
        return call(
            functools.partial(feed_forward_kernel, row), 4,
            ins + w + w,
            [whole(i) for i in ins] + self.weights(lambda j: j, lambda j: 4 + j),
            outs, [whole(outs[0]), whole(outs[1]), pl.BlockSpec((t, d), lambda j: (0, j))],
            scratch=[pltpu.VMEM((t, d), bf16)],
        )

    def feed_backward(self, x, u, dx, w, row):
        d, t = self.d, self.t
        outs = (self.xs, sds((8, d), f32), sds((5, t, d), bf16))
        ins = (x, self.vec, self.order, dx)
        return call(
            functools.partial(feed_backward_kernel, row), 4,
            ins + w + w + (u,),
            [whole(i) for i in ins] + self.weights(lambda j: j, lambda j: 4 + j)
            + [pl.BlockSpec((t, d), lambda j: (0, j))],
            outs, [whole(i) for i in outs],
            scratch=[pltpu.VMEM((t, d), f32)],
        )

    def last_backward(self, x, dx, w, row):
        d, t = self.d, self.t
        outs = (self.xs, sds((8, d), f32)) + (sds((5, t, d), bf16),) * 2
        ins = (x, self.vec, self.order, dx)
        return call(
            functools.partial(last_backward_kernel, row), 4,
            ins + w + w,
            [whole(i) for i in ins] + self.weights(lambda j: j, lambda j: 4 + j),
            outs, [whole(i) for i in outs],
            scratch=[pltpu.VMEM((t, d), f32), pltpu.VMEM((t, d), bf16)],
        )

    def last_output(self, x, f, w):
        return call(
            last_output_kernel, 4, (x, self.order, f) + w,
            [whole(x), whole(self.order), self.block(lambda j: 1 + j)]
            + self.weights(lambda j: 4 + j),
            self.hs, whole(self.hs), scratch=[pltpu.VMEM((self.t, self.d), f32)],
        )


def spread_matrix():
    k = lax.broadcasted_iota(jnp.int32, (512, 512), 0)
    n = lax.broadcasted_iota(jnp.int32, (512, 512), 1)
    return (k % 4) * 128 + k // 4 == n


def local(
    tokens, encoder, patch_count, out_grad,
    u_ag, u_as, u_qkv, u_out, u_mg, u_ms, u_up, u_down,
    m_ag, m_as, m_qkv, m_out, c_g, c_s, c_q, c_pair, c_out, m_mg, m_ms, m_up, m_down,
):
    place = Place()
    captions, length, d = tokens.shape
    rows = u_qkv.shape[0]
    x0 = tokens.reshape(-1, d)
    enc = encoder.reshape(-1, d)
    order = place.order(d)

    vectors = (u_ag, u_as, u_mg, u_ms, m_ag, m_as, c_g, c_s, m_mg, m_ms)
    vectors = jnp.pad(jnp.stack(vectors, axis=0), ((0, LANES - len(vectors)), (0, 0)))
    def packed(kernel, parts, *widths):
        outs = tuple(sds((rows, c), bf16) for c in widths)
        shards = call(kernel, 1, parts, [whole(p) for p in parts], outs, [whole(o) for o in outs], vmem=60)
        return [Gather(place, x) for x in shards]

    (first,) = packed(first_pack_kernel, (u_qkv, u_out, vectors), 4 * d + LANES)
    parts = (u_up, u_down, m_qkv, m_out, m_up, m_down, c_q, c_pair, c_out)
    feed, middle, last = packed(pack_kernel, parts, 8 * d, 8 * d, 8 * d)

    def go(token, groups=(), start=()):
        token, got = tie(token, *[(g.x, g.got) for g in groups])
        for g, (x, y) in zip(groups, got):
            g.x, g.got = x, y
            g.join()
        every = tuple(groups) + tuple(start)
        token, xs = tie(token, *[g.x for g in every])
        for g, x in zip(every, xs):
            g.x = x
            g.swap()
        return token

    def end(token, group):
        token, (group.x, group.got) = tie(token, group.x, group.got)
        return token, (group.x, group.got)

    steps = place.outer_bits
    x0 = go(x0, start=[first])
    enc_rel = nt(enc, order).astype(bf16)
    enc_t = nt(order, enc).astype(bf16)
    for k in range(steps - 1):
        x0 = go(x0, [first], [feed] if k == 0 else [])
    x0 = go(x0, [first])
    for k in range(steps - 1):
        x0 = go(x0, [feed])
    x0 = go(x0, [first])
    x0 = go(x0, [feed], [middle])
    x0 = go(x0, [first, middle])
    x0 = go(x0, [feed])
    for k in range(steps - 2):
        x0 = go(x0, [middle])
    x0, (order, enc_rel, enc_t) = tie(x0, order, enc_rel, enc_t)
    x0, w_first = end(x0, first)
    vec = tn(jnp.concatenate([x[:, 4 * d :] for x in w_first], axis=0), order)[:16]
    net = Layers(captions, captions * length, d, vec, order, patch_count)
    x0 = go(x0, [middle], [last])
    for k in range(steps - 1):
        x0 = go(x0, [last])
    x0 = go(x0, [feed])
    x0a, f_us, k_us = net.self_forward(x0, w_first, 0, 0)
    x0a = go(x0a, [middle])
    x0a = go(x0a, [last])
    x0a, w_feed = end(x0a, feed)
    x1, f_uf, k_uf = net.feed_forward(x0a, w_feed, 2)
    x1 = go(x1, [last])
    x1 = go(x1, [middle])
    x1, w_middle = end(x1, middle)
    x1a, f_ms, k_ms = net.self_forward(x1, w_middle, 4, 4)
    kv = net.pair_forward(enc_rel, w_middle)
    x1b, f_mc, k_mc = net.cross_forward(x1a, kv, w_middle, 2, 6)
    x1b = go(x1b, [last])
    x1b, w_last = end(x1b, last)

    def core(x):
        return place.swap(x, BIT_CORE)

    def go_on(x, sums=(), start=()):
        x = hold(x, *sums)
        for g in sums:
            g.sums()
        x = need(x, *(tuple(sums) + tuple(g for g in start if g not in sums)))
        for g in start:
            g.swap()
        return x

    def rest(x, *groups):
        for _ in range(place.outer_bits - 1):
            for g in groups:
                x = go_on(x, [g], [g])
        return x

    def pairs(x):
        return x, core(x)

    f_us, f_uf, f_ms = pairs(f_us), pairs(f_uf), pairs(f_ms)
    x1b, (f_us, f_uf, f_ms) = tie(x1b, f_us, f_uf, f_ms)
    f_mc = pairs(f_mc)
    dx, v_mf, p, f = net.last_backward(x1b, out_grad.reshape(-1, d), w_last, 8)
    p, f = pairs(p), pairs(f)
    x2 = net.last_output(x1b, f[0], w_last)
    p, (x2,) = tie(p, x2)
    s_mf = Sum(place, net.feed_grads(f, p))
    dx, (f_mc,) = tie(dx, f_mc)
    dx = go_on(dx, start=[s_mf])
    dx, v_mc, p_c, dkv = net.cross_backward(x1a, k_mc, kv, dx, w_middle, 2, 6)
    p_c = pairs(p_c)
    pair, send = net.pair_grads(enc_t, dkv)
    dx, (send,) = tie(dx, send)
    pair = pair, core(send)
    dx, v_ms, p = net.self_backward(x1, k_ms, dx, w_middle, 4, 4)
    p = pairs(p)
    dx = go_on(dx, [s_mf], [s_mf])
    dx, (p, p_c, pair) = tie(dx, p, p_c, pair)
    s_ma = Sum(place, net.attend_grads(f_ms, p, (f_mc, p_c, pair)))
    dx = go_on(dx, start=[s_ma])
    dx, v_uf, p = net.feed_backward(x0a, k_uf, dx, w_feed, 2)
    p = pairs(p)
    dx, (p,) = tie(dx, p)
    s_uf = Sum(place, net.feed_grads(f_uf, p))
    dx = need(dx, s_uf)
    v = [g[:2] for g in (v_uf, v_ms, v_mc, v_mf)]
    v = jnp.pad(jnp.concatenate(v, axis=0), ((2, 6), (0, 0)))
    dx, _v, p = net.self_backward(x0, k_us, dx, w_first, 0, 0, (v,))
    p = pairs(p)
    dx = go_on(dx, [s_mf], [s_uf, s_mf])
    dx = go_on(dx, [s_ma], [s_ma])
    dx, (p,) = tie(dx, p)
    send, keep = net.attend_grads(f_us, p)
    dx, (send, keep) = tie(dx, send, keep)
    v = nt(order[: d // 2], plus(p[0][4], p[1][4])[:LANES]).astype(bf16)
    dx, (dkv,) = tie(dx, dkv)
    denc = net.pair_input(dkv, w_middle)
    dx, (denc,) = tie(dx, denc)
    dx = go_on(dx, [s_ma], [s_ma])
    send = jnp.concatenate((send, v[d // 4 :]), axis=1)
    keep = jnp.concatenate((keep, v[: d // 4]), axis=1)
    s_us = Sum(place, (send, keep))
    dx = go_on(dx, start=[s_us])
    dx = rest(dx, s_mf)
    dx = go_on(dx, [s_uf], [s_uf])
    dx, (r_mf,) = tie(dx, feed_rows(s_mf.kept, s_mf.got))
    dx = rest(dx, s_ma)
    dx = go_on(dx, [s_uf, s_us], [s_uf, s_us])
    dx, (r_ma,) = tie(dx, s_ma.total())
    dx = rest(dx, s_uf)
    dx = go_on(dx, [s_us], [s_us])
    dx = rest(dx, s_us)
    dx = hold(dx, s_uf)
    dx, (r_uf,) = tie(dx, feed_rows(s_uf.kept, s_uf.got))
    r_us = s_us.total()

    def columns(r, *blocks):
        parts = [r[:, b * d : (b + 1) * d] for b in blocks]
        return jnp.concatenate(parts, axis=1) if len(parts) > 1 else parts[0]

    r_uup, r_udown = r_uf
    r_mup, r_mdown = r_mf
    vs = r_us[:, 4 * d :]
    v = [vs[:, i] for i in range(10)]
    return (
        x2.reshape(tokens.shape),
        dx.astype(bf16).reshape(tokens.shape),
        denc.reshape(encoder.shape),
        v[0], v[1], r_us[:, : 3 * d], r_us[:, 3 * d : 4 * d], v[2], v[3], r_uup, r_udown,
        v[4], v[5], r_ma[:, : 3 * d], columns(r_ma, 3), v[6], v[7],
        columns(r_ma, 4), r_ma[:, 6 * d :], columns(r_ma, 5),
        v[8], v[9], r_mup, r_mdown,
    )


def solution(mesh):
    rows1 = P(AXES)
    rows2 = P(AXES, None)
    rows3 = P(AXES, None, None)
    block = (rows1, rows1, rows2, rows2)
    weights = block * 2 + block + (rows1, rows1, rows2, rows2, rows2) + block
    return jax.shard_map(
        local,
        mesh=mesh,
        in_specs=(rows3, rows3, rows1, rows3) + weights,
        out_specs=(rows3, rows3, rows3) + weights,
        check_vma=False,
    )
```
